32 devices in a mesh: dp: 8 (over z, x), mp: 4 (over y, core).
Axes of the slice: x: 2, y: 2, z: 4, core: 2. Of those that a mesh axis runs over, the one named last changes fastest.
Arguments:
- tokens: bfloat16 [2, 16384, 768], P(None, ('dp', 'mp')), may hold values from -6 to 6
- norm_gains: bfloat16 [768, 2], P('dp'), may hold values from 0.5 to 1.5
- norm_biases: bfloat16 [768, 2], P('dp'), may hold values from -3 to 3
- w_query: bfloat16 [768, 768], P('dp', 'mp'), may hold values from -0.21875 to 0.21875
- w_keyval: bfloat16 [768, 128], P('dp'), may hold values from -0.21875 to 0.21875
- w_output: bfloat16 [768, 768], P('dp', 'mp'), may hold values from -1.5 to 1.5
- w_up: bfloat16 [768, 3072], P('dp', 'mp'), may hold values from -0.21875 to 0.21875
- w_down: bfloat16 [768, 3072], P('dp', 'mp'), may hold values from -0.109375 to 0.109375
- cotangent: bfloat16 [2, 16384, 768], P(None, ('dp', 'mp')), may hold values from -6 to 6
- subset_ids: int32 [32768], P('dp'), may hold values from 0 to 21
- subset_weights: float32 [22], replicated, may hold values from 0.25 to 4
Outputs:
- output: bfloat16 [2, 16384, 768], P(None, ('dp', 'mp'))
- kv_cache: bfloat16 [32768, 128], P('dp')
- input_grad: bfloat16 [2, 16384, 768], P(None, ('dp', 'mp'))
- grad_gains: float32 [768, 2], P('dp')
- grad_biases: float32 [768, 2], P('dp')
- grad_query: float32 [768, 768], P('dp', 'mp')
- grad_keyval: float32 [768, 128], P('dp')
- grad_output: float32 [768, 768], P('dp', 'mp')
- grad_up: float32 [768, 3072], P('dp', 'mp')
- grad_down: float32 [768, 3072], P('dp', 'mp')
The draws below stay inside these ranges and needn't reach their ends.
All inputs are finite; a program needn't handle non-finite values.
Results may differ from the reference program's by a relative error of at most 0.012.
Values may be sent and summed in bfloat16 or wider, within the bound.
A program may use at most 256 MiB of HBM per device.

```python
import math
import jax
import jax.numpy as jnp
import numpy as np
from jax import lax

D = 768
H = 12
HD = 64
ROT = 16
FF = 3072
SEQ_LEN = 2048
QB = 512
MICRO = 2
SEQ_MB = 1
NSUB = 22
TOK_DEV = 4096
TOKENS = 32768
N_DP = 8


def touch_ends(drawn, key, low, high):
    longest = drawn.shape.index(max(drawn.shape))
    spots = []
    for shift in (0, 1):
        where = [jax.random.randint(jax.random.fold_in(key, axis), (), 0, length) for axis, length in enumerate(drawn.shape)]
        where[longest] = (where[longest] + shift) % drawn.shape[longest]
        spots.append(tuple(where))
    return drawn.at[spots[0]].set(low).at[spots[1]].set(high)


def block_scale(own_key, extent, split, least, largest):
    level = 1.0
    for axis_at, shards_of in split:
        draws = jax.random.uniform(jax.random.fold_in(jax.random.fold_in(own_key, 6), axis_at), (shards_of,), jnp.float32, least / len(split), largest / len(split))
        level = level * jnp.repeat(jnp.exp(draws), extent[axis_at] // shards_of).reshape((-1,) + (1,) * (len(extent) - 1 - axis_at))
    return level


def rank_bounds(count, slope):
    weights = [(1 << 20) // math.isqrt(rank ** slope) + 1 for rank in range(1, count + 1)]
    deviation = 1 + sum(weights) // (1 << 30)
    return np.cumsum(np.array([max(1, weight // deviation) for weight in weights]))


def skewed_ids(own_key, dims, number_of, lean):
    grid = rank_bounds(number_of, lean)
    lot = jax.random.randint(jax.random.fold_in(own_key, 1), dims, 0, int(grid[number_of - 1]))
    grade = jnp.searchsorted(jnp.asarray(grid, jnp.int32), lot, side="right")
    return jax.random.permutation(jax.random.fold_in(own_key, 2), number_of)[grade].astype(jnp.int32)


def noise(rng, shape, spread, limit, cuts=(), kind=jnp.bfloat16):
    entries = spread * jax.random.normal(rng, shape, jnp.float32)
    if cuts:
        entries = entries * block_scale(rng, shape, cuts, -0.22, 0.18)
    return jnp.clip(entries, -limit, limit).astype(kind)


def setup_inputs(seed: int = 0) -> dict:
    key_list = jax.random.split(jax.random.key(seed), 12)
    return {
        "tokens": noise(key_list[0], (MICRO, TOKENS // MICRO, D), 1.0, 6.0, ((1, 32),)),
        "norm_gains": jnp.clip(1.0 + 0.1 * jax.random.normal(key_list[1], (D, 2), jnp.float32), 0.5, 1.5).astype(jnp.bfloat16),
        "norm_biases": noise(key_list[2], (D, 2), 0.5, 3.0, ((0, 8),)),
        "w_query": noise(key_list[3], (D, H * HD), D ** -0.5, 0.21875, ((0, 8), (1, 4))),
        "w_keyval": noise(key_list[4], (D, 2 * HD), D ** -0.5, 0.21875, ((0, 8),)),
        "w_output": noise(key_list[5], (D, H * HD), (HD // 4) ** -0.5, 1.5, ((0, 8), (1, 4))),
        "w_up": noise(key_list[6], (D, FF), D ** -0.5, 0.21875, ((0, 8), (1, 4))),
        "w_down": noise(key_list[7], (D, FF), FF ** -0.5, 0.109375, ((0, 8), (1, 4))),
        "cotangent": noise(key_list[8], (MICRO, TOKENS // MICRO, D), 1.0, 6.0, ((1, 32),)),
        "subset_ids": touch_ends(skewed_ids(key_list[9], (TOKENS,), NSUB, 2), jax.random.fold_in(key_list[9], 3), 0, NSUB - 1).astype(jnp.int32),
        "subset_weights": jnp.clip(jnp.exp(jax.random.uniform(key_list[10], (NSUB,), jnp.float32, math.log(0.25), math.log(4.0))), 0.25, 4.0),
    }


@jax.custom_vjp
def low(v):
    return lax.optimization_barrier(v.astype(jnp.bfloat16)).astype(jnp.float32)

@jax.custom_vjp
def low_back(v):
    return v

def low_keep(v):
    return (low(v), None)

def low_pass(kept, grad):
    return (grad,)

def back_keep(v):
    return (v, None)

def back_low(kept, grad):
    return (low(grad),)
low.defvjp(low_keep, low_pass)
low_back.defvjp(back_keep, back_low)
epsilon = 1e-05
highest = lax.Precision.HIGHEST

def rotary_tables():
    position = jnp.arange(SEQ_LEN, dtype=jnp.float32)
    frequency = 10000.0 ** (-2.0 * jnp.arange(ROT // 2, dtype=jnp.float32) / ROT)
    angles = position[:, None] * frequency[None, :]
    return (jnp.cos(angles), jnp.sin(angles))

def rotate(vectors, cosine, sine_table):
    first_half = vectors[..., :ROT // 2]
    second_half = vectors[..., ROT // 2:ROT]
    cos_wide = cosine[:, None, :]
    sin_wide = sine_table[:, None, :]
    return jnp.concatenate([first_half * cos_wide - second_half * sin_wide, second_half * cos_wide + first_half * sin_wide, vectors[..., ROT:]], axis=-1)

def attend_block(query_block, key_rows, value_rows, start):
    scores = low_back(jnp.einsum('qhd,kd->hqk', query_block, key_rows, precision=highest))
    row_ids = start + jnp.arange(QB, dtype=jnp.int32)
    col_ids = jnp.arange(SEQ_LEN, dtype=jnp.int32)
    causal = col_ids[None, :] <= row_ids[:, None]
    scores = jnp.where(causal[None], scores, -1e+30)
    probability = low(jax.nn.softmax(scores, axis=-1))
    return jnp.einsum('hqk,kd->qhd', probability, value_rows, precision=highest)

def attend_sequence(queries, key_rows, value_rows):
    blocks = queries.reshape(SEQ_LEN // QB, QB, H, HD)
    starts = jnp.arange(SEQ_LEN // QB, dtype=jnp.int32) * QB

    def one_block(block_pair):
        return attend_block(block_pair[0], key_rows, value_rows, block_pair[1])
    mixed_heads = lax.map(jax.checkpoint(one_block), (blocks, starts))
    return mixed_heads.reshape(SEQ_LEN, H * HD)

def layer(tokens, gains, biases, w_query, w_keyval, w_output, w_up, w_down):
    seq_count = tokens.shape[0] // SEQ_LEN
    mean_row = lax.optimization_barrier(jnp.mean(tokens, axis=1, keepdims=True))
    centered = tokens - mean_row
    normed = centered * lax.rsqrt(lax.optimization_barrier(jnp.mean(centered * centered, axis=1, keepdims=True)) + epsilon)
    attn_in = low(normed * gains[:, 0] + biases[:, 0])
    mlp_in = low(normed * gains[:, 1] + biases[:, 1])
    query_pre = low_back(jnp.dot(attn_in, w_query, precision=highest))
    keyval_pre = low_back(jnp.dot(attn_in, w_keyval, precision=highest))
    cosine, sine_table = rotary_tables()
    queries = low(rotate(query_pre.reshape(seq_count, SEQ_LEN, H, HD), cosine, sine_table) * HD ** (-0.5))
    key_rows = low(rotate(keyval_pre[:, :HD].reshape(seq_count, SEQ_LEN, 1, HD), cosine, sine_table)).reshape(seq_count, SEQ_LEN, HD)
    value_rows = low(keyval_pre[:, HD:]).reshape(seq_count, SEQ_LEN, HD)
    heads_out = jax.vmap(attend_sequence)(queries, key_rows, value_rows).reshape(-1, H * HD)
    heads_out = low(low_back(heads_out))
    hidden_pre = low_back(jnp.dot(mlp_in, w_up, precision=highest))
    hidden = low(jax.nn.gelu(hidden_pre, approximate=False))
    branch_attn = jnp.dot(heads_out, w_output.T, precision=highest)
    branch_mlp = jnp.dot(hidden, w_down.T, precision=highest)
    output = tokens + low_back(branch_attn) + low_back(branch_mlp)
    kv_cache = jnp.concatenate([key_rows, value_rows], axis=-1).reshape(-1, 2 * HD)
    return (output, kv_cache)

def to_groups(array_in):
    return jnp.transpose(array_in.reshape(MICRO, N_DP, SEQ_MB * SEQ_LEN, D), (1, 0, 2, 3)).reshape(N_DP, TOK_DEV, D)

def from_groups(array_in):
    return jnp.transpose(array_in.reshape(N_DP, MICRO, SEQ_MB * SEQ_LEN, D), (1, 0, 2, 3)).reshape(MICRO, TOKENS // MICRO, D)

def reference(tokens, norm_gains, norm_biases, w_query, w_keyval, w_output, w_up, w_down, cotangent, subset_ids, subset_weights):
    params = tuple((array_in.astype(jnp.float32) for array_in in (norm_gains, norm_biases, w_query, w_keyval, w_output, w_up, w_down)))
    inputs = to_groups(tokens.astype(jnp.float32))
    grads_in = to_groups(cotangent.astype(jnp.float32))
    scales = subset_weights.astype(jnp.float32)[subset_ids].reshape(N_DP, TOK_DEV, 1)

    def scan_step(totals, scan_item):
        rows_in, cot_rows, scale_rows = scan_item
        output, pullback, kv_cache = jax.vjp(layer, rows_in, *params, has_aux=True)
        gradients = pullback(cot_rows * scale_rows)
        totals = tuple((running + added for running, added in zip(totals, gradients[1:])))
        return (totals, (output.astype(jnp.bfloat16), kv_cache.astype(jnp.bfloat16), gradients[0].astype(jnp.bfloat16)))
    zero_sums = tuple((jnp.zeros_like(array_in) for array_in in params))
    totals, results = lax.scan(scan_step, zero_sums, (inputs, grads_in, scales))
    output, kv_cache, input_grad = results
    return (from_groups(output), kv_cache.reshape(TOKENS, 2 * HD), from_groups(input_grad), totals[0], totals[1], totals[2], totals[3], totals[4], totals[5], totals[6])
```

```python
import functools

import jax
import jax.numpy as jnp
from jax import lax
from jax.experimental import pallas as pl
from jax.experimental.pallas import tpu as pltpu
from jax.sharding import PartitionSpec as P

f32 = jnp.float32
bf = jnp.bfloat16
MESH = pl.DeviceIdType.MESH
HD = 64
ROT = 16
SEQ_LEN = 2048
epsilon = 1e-05
sqrt_half = 0.7071067811865476
inv_sqrt_two_pi = 0.3989422804014327


def coords(nz):
    d=lax.axis_index("dp"); m=lax.axis_index("mp")
    return d//2, d%2, m//2, m%2

def peer(pos,kind,nz):
    z,x,y,c=pos
    if kind[0]=="z": z=lax.rem(z+int(kind[1:]),nz)
    if kind=="x": x=1-x
    if kind=="y": y=1-y
    if kind=="c": c=1-c
    return (z*2+x, y*2+c)

def greet(pos,kinds,nz):
    bar=pltpu.get_barrier_semaphore()
    for k in kinds:
        pl.semaphore_signal(bar,inc=1,device_id=peer(pos,k,nz),device_id_type=MESH)
    pl.semaphore_wait(bar,len(kinds))

def gather_routes(order,nz):
    zs=[f"z{k}" for k in range(1,nz)]
    out=[]
    if order=="zyx":
        out.append(((0,0,0),zs+["y","x","c"]))
        out+=[((k,0,0),["y","x","c"]) for k in range(1,nz)]
        out+=[((k,0,1),["x","c"]) for k in range(nz)]
        out+=[((k,1,r),["c"]) for r in (0,1) for k in range(nz)]
    elif order=="xzy":
        out.append(((0,0,0),["x"]+zs+["y","c"]))
        out.append(((0,1,0),zs+["y","c"]))
        out+=[((k,r,0),["y","c"]) for k in range(1,nz) for r in (0,1)]
        out+=[((k,r,1),["c"]) for k in range(nz) for r in (0,1)]
    elif order=="zx":
        out.append(((0,0,0),zs+["x"]))
        out+=[((k,0,0),["x"]) for k in range(1,nz)]
        out+=[((k,1,0),[]) for k in range(nz)]
    return out

def gather_kernel(nz,plan,n,*refs):
    shards=refs[:n]; full=refs[n:2*n]; send,recv,local=refs[2*n:]
    pos=coords(nz); z,x,y,c=pos
    kinds=[f"z{k}" for k in range(1,nz)]+["x","y","c"]
    greet(pos,kinds,nz)
    sent=[]
    def block(i,lo,hi,zz,xx,yy,cc,both):
        d=zz*2+xx
        return full[i].at[yy*2+cc,d,:,lo:hi] if both else full[i].at[d,:,lo:hi]
    locs=[]
    for i in range(n):
        both=len(full[i].shape)==4
        dst=full[i].at[y*2+c,z*2+x] if both else full[i].at[z*2+x]
        cp=pltpu.make_async_copy(shards[i],dst,local.at[i]); cp.start(); locs.append(cp)
    chunks=[]
    count=0
    for ci,(i,lo,hi,order) in enumerate(plan):
        both=len(full[i].shape)==4
        chunks.append((ci,i,lo,hi,both,gather_routes(order,nz)))
    def act(chunk,step):
        nonlocal count
        ci,i,lo,hi,both,routes=chunk
        (k,rx,ry),fw=routes[step]
        zz=lax.rem(z+nz-k,nz); xx=1-x if rx else x; yy=1-y if ry else y
        dst=block(i,lo,hi,zz,xx,yy,c,both)
        midx=yy*2+c if both else 0
        if step>0:
            pltpu.make_async_remote_copy(dst,dst,send.at[0],recv.at[ci,midx,zz*2+xx],device_id=peer(pos,"c",nz),device_id_type=MESH).wait_recv()
        src=shards[i].at[:,lo:hi] if step==0 else dst
        for f in fw:
            cp=pltpu.make_async_remote_copy(src,dst,send.at[count],recv.at[ci,midx,zz*2+xx],device_id=peer(pos,f,nz),device_id_type=MESH)
            cp.start(); sent.append(cp); count+=1
    for ch in chunks: act(ch,0)
    longest=max(len(ch[5]) for ch in chunks)
    done=[1]*len(chunks)
    for s in range(1,longest):
        for j,ch in enumerate(chunks):
            if s<len(ch[5]): act(ch,s)
    for ci,i,lo,hi,both,routes in chunks:
        if not both: continue
        for (k,rx,ry),_ in routes:
            zz=lax.rem(z+nz-k,nz); xx=1-x if rx else x; yy=1-y if ry else y
            dst=block(i,lo,hi,zz,xx,yy,1-c,both)
            pltpu.make_async_remote_copy(dst,dst,send.at[0],recv.at[ci,yy*2+1-c,zz*2+xx],device_id=peer(pos,"c",nz),device_id_type=MESH).wait_recv()
    for cp in sent: cp.wait_send()
    for cp in locs: cp.wait()

def gather(shards,plan,dp,mp,cid,interp=False):
    nz=dp//2; n=len(shards)
    inside={i for i,_,_,o in plan if o=="zx"}
    outs=[jax.ShapeDtypeStruct(((dp,) if i in inside else (mp,dp))+s.shape,s.dtype) for i,s in enumerate(shards)]
    sends=sum(len(f) for _,_,_,o in plan for _,f in gather_routes(o,nz))
    return pl.pallas_call(functools.partial(gather_kernel,nz,plan,n),
        in_specs=[pl.BlockSpec(memory_space=pltpu.VMEM)]*n,
        out_specs=[pl.BlockSpec(memory_space=pl.ANY)]*n,
        out_shape=outs,
        scratch_shapes=[pltpu.SemaphoreType.DMA((sends,)),pltpu.SemaphoreType.DMA((len(plan),mp,dp)),pltpu.SemaphoreType.DMA((n,))],
        compiler_params=pltpu.CompilerParams(collective_id=cid,has_side_effects=True),name="gather_weights")(*shards)

def scatter_kernel(nz,plan,n,*refs):
    parts=refs[:n]; outs=refs[n:2*n]
    np_=len(plan)
    per=refs[2*n:2*n+5*np_]
    send,csem,xsem,ysem,zsem=refs[2*n+5*np_:]
    pos=coords(nz); z,x,y,c=pos
    kinds=[f"z{k}" for k in range(1,nz)]+["x","y","c"]
    greet(pos,kinds,nz)
    sent=[]
    def start(src,dst,rsem,kind):
        cp=pltpu.make_async_remote_copy(src,dst,send.at[len(sent)],rsem,device_id=peer(pos,kind,nz),device_id_type=MESH)
        cp.start(); sent.append(cp)
    def wait(dst,rsem):
        pltpu.make_async_remote_copy(dst,dst,send.at[0],rsem,device_id=peer(pos,"c",nz),device_id_type=MESH).wait_recv()
    def part(i,lo,hi,r,cc):
        rz,rx,ry=r
        zz=lax.rem(z+rz,nz); xx=1-x if rx else x; yy=1-y if ry else y
        if len(parts[i].shape)==4: return parts[i].at[yy*2+cc,zz*2+xx,:,lo:hi]
        return parts[i].at[zz*2+xx,:,lo:hi]
    def ordering(order):
        if order=="xyz":
            return [(k,1,r) for r in (1,0) for k in range(nz-1,-1,-1)]+[(k,0,1) for k in range(nz-1,-1,-1)]+[(k,0,0) for k in range(nz-1,-1,-1)]
        if order=="yzx":
            return [(k,r,1) for r in (1,0) for k in range(nz-1,-1,-1)]+[(k,1,0) for k in range(nz-1,-1,-1)]+[(k,0,0) for k in range(nz-1,-1,-1)]
        return [(k,1,0) for k in range(nz-1,-1,-1)]+[(k,0,0) for k in range(nz-1,-1,-1)]
    state=[]
    for p,(i,lo,hi,order) in enumerate(plan):
        acc,cb,xb,yb,zb=per[5*p:5*p+5]
        state.append((p,i,lo,hi,order,ordering(order),acc,cb,xb,yb,zb))
    def slot(order,r):
        return (r[0]*2+r[1])*2+r[2] if order!="xz" else r[0]*2+r[1]
    L=max(len(s[5]) for s in state)
    for t in range(L):
        for p,i,lo,hi,order,seq,acc,cb,xb,yb,zb in state:
            if t<len(seq):
                r=seq[t]; s=slot(order,r)
                start(part(i,lo,hi,r,1-c) if order!="xz" else part(i,lo,hi,r,c),cb.at[s],csem.at[p,s],"c")
    def add(acc_ref,*others):
        v=acc_ref[...].astype(f32)
        for o in others: v=v+o[...].astype(f32)
        return v
    def first_phase(st,t):
        p,i,lo,hi,order,seq,acc,cb,xb,yb,zb=st
        r=seq[t]; s=slot(order,r)
        wait(cb.at[s],csem.at[p,s])
        acc[s]=add(part(i,lo,hi,r,c),cb.at[s]).astype(bf)
        rz,rx,ry=r
        if order in ("xyz","xz") and rx: start(acc.at[s],xb.at[rz*2+ry],xsem.at[p,rz*2+ry],"x")
        if order=="yzx" and ry: start(acc.at[s],yb.at[rz*2+rx],ysem.at[p,rz*2+rx],"y")
    for t in range(L):
        for st in state:
            if t<len(st[5]): first_phase(st,t)
    def later(st):
        p,i,lo,hi,order,seq,acc,cb,xb,yb,zb=st
        A=lambda r: acc.at[slot(order,r)]
        if order=="xyz":
            for k in range(nz-1,-1,-1):
                r=(k,0,1); j=k*2+1
                wait(xb.at[j],xsem.at[p,j]); A(r)[...]=add(A(r),xb.at[j]).astype(bf)
                start(A(r),yb.at[k*2],ysem.at[p,k*2],"y")
            yield
            for k in range(nz-1,-1,-1):
                r=(k,0,0); j=k*2
                wait(xb.at[j],xsem.at[p,j]); wait(yb.at[k*2],ysem.at[p,k*2])
                if k:
                    A(r)[...]=add(A(r),xb.at[j],yb.at[k*2]).astype(bf)
                    start(A(r),zb.at[k],zsem.at[p,k],f"z{k}")
            yield
            for k in range(1,nz): wait(zb.at[k],zsem.at[p,k])
            outs[i][:,lo:hi]=add(A((0,0,0)),xb.at[0],yb.at[0],*[zb.at[k] for k in range(1,nz)])
        elif order=="yzx":
            for rx in (1,0):
                for k in range(nz-1,0,-1):
                    r=(k,rx,0); j=k*2+rx
                    wait(yb.at[j],ysem.at[p,j]); A(r)[...]=add(A(r),yb.at[j]).astype(bf)
                    start(A(r),zb.at[k*2+rx],zsem.at[p,k*2+rx],f"z{k}")
            yield
            r=(0,1,0)
            wait(yb.at[1],ysem.at[p,1])
            for k in range(1,nz): wait(zb.at[k*2+1],zsem.at[p,k*2+1])
            A(r)[...]=add(A(r),yb.at[1],*[zb.at[k*2+1] for k in range(1,nz)]).astype(bf)
            start(A(r),xb.at[0],xsem.at[p,0],"x")
            wait(yb.at[0],ysem.at[p,0])
            for k in range(1,nz): wait(zb.at[k*2],zsem.at[p,k*2])
            yield
            wait(xb.at[0],xsem.at[p,0])
            outs[i][:,lo:hi]=add(A((0,0,0)),yb.at[0],xb.at[0],*[zb.at[k*2] for k in range(1,nz)])
        else:
            for k in range(nz-1,-1,-1):
                r=(k,0,0); wait(xb.at[k*2],xsem.at[p,k*2]); A(r)[...]=add(A(r),xb.at[k*2]).astype(bf)
                start(A(r),yb.at[k],ysem.at[p,k],"y")
            yield
            for k in range(nz-1,0,-1):
                wait(yb.at[k],ysem.at[p,k]); zb[k]=add(A((k,0,0)),yb.at[k]).astype(bf)
                start(zb.at[k],zb.at[nz+k],zsem.at[p,k],f"z{k}")
            wait(yb.at[0],ysem.at[p,0])
            yield
            for k in range(1,nz): wait(zb.at[nz+k],zsem.at[p,k])
            outs[i][:,lo:hi]=add(A((0,0,0)),yb.at[0],*[zb.at[nz+k] for k in range(1,nz)])
    gens=[later(st) for st in state]
    live=list(gens)
    while live:
        nxt=[]
        for g in live:
            try: next(g); nxt.append(g)
            except StopIteration: pass
        live=nxt
    for cp in sent: cp.wait_send()

def scatter(parts,plan,dp,mp,cid):
    nz=dp//2; n=len(parts)
    outs=[jax.ShapeDtypeStruct(p.shape[-2:],f32) for p in parts]
    scr=[]; sends=0
    for i,lo,hi,order in plan:
        rows=parts[i].shape[-2]; w=hi-lo
        b=lambda k: pltpu.VMEM((k,rows,w),bf)
        nb=nz*4 if order!="xz" else nz*2
        scr+=[b(nb),b(nb)]
        if order=="xyz": scr+=[b(nz*2),b(nz*2),b(nz)]; sends+=nb+2*nz+nz+nz-1
        elif order=="yzx": scr+=[b(1),b(nz*2),b(nz*2)]; sends+=nb+2*nz+2*(nz-1)+1
        else: scr+=[b(nz*2),b(nz),b(2*nz)]; sends+=nb+nz+nz+nz-1
    np_=len(plan)
    return pl.pallas_call(functools.partial(scatter_kernel,nz,plan,n),
        in_specs=[pl.BlockSpec(memory_space=pltpu.VMEM)]*n,
        out_specs=[pl.BlockSpec(memory_space=pltpu.VMEM)]*n,
        out_shape=outs,
        scratch_shapes=scr+[pltpu.SemaphoreType.DMA((sends,)),pltpu.SemaphoreType.DMA((np_,4*nz)),pltpu.SemaphoreType.DMA((np_,2*nz)),pltpu.SemaphoreType.DMA((np_,2*nz)),pltpu.SemaphoreType.DMA((np_,2*nz))],
        compiler_params=pltpu.CompilerParams(collective_id=cid,has_side_effects=True,vmem_limit_bytes=60<<20),name="scatter_grads")(*parts)

NT=(((1,),(1,)),((),()))
NN=(((1,),(0,)),((),()))
def dg(a,b,dn): return lax.dot_general(a,b,dn,preferred_element_type=f32)
B=512
def attn_kernel(rb_ref,q_ref,do_ref,kv_ref,o_ref,dq_ref,dkv_ref,k2,v2,kvt,acck,accv,ps,mk):
    pair=pl.program_id(1)
    rb=rb_ref[0]
    nkb=kv_ref.shape[1]//B
    @pl.when(pair==0)
    def _():
        for kb in range(nkb):
            kv=kv_ref[0,kb*B:(kb+1)*B,:].astype(f32)
            rolled=pltpu.roll(kv,64,1)
            lane=lax.broadcasted_iota(jnp.int32,kv.shape,1)<64
            k2[kb]=jnp.where(lane,kv,rolled).astype(bf)
            v2[kb]=jnp.where(lane,rolled,kv).astype(bf)
            kvt[kb]=kv.T.astype(bf)
        acck[...]=jnp.zeros_like(acck); accv[...]=jnp.zeros_like(accv)
    q=q_ref[...]; do=do_ref[...]
    lane=lax.broadcasted_iota(jnp.int32,q.shape,1)<64
    zero=jnp.zeros_like(q)
    qm=(jnp.where(lane,q,zero),jnp.where(lane,zero,q))
    dom=(jnp.where(lane,do,zero),jnp.where(lane,zero,do))
    dot_=do.astype(f32).T
    def fwd(kb,carry,masked):
        new=[]
        for h in range(2):
            m,l,ot=carry[h]
            s=dg(k2[kb],qm[h],NT)
            if masked:
                ki=lax.broadcasted_iota(jnp.int32,s.shape,0); ri=lax.broadcasted_iota(jnp.int32,s.shape,1)
                s=jnp.where(ki<=ri,s,-1e30)
            mn=jnp.maximum(m,jnp.max(s,axis=0,keepdims=True))
            a=jnp.exp(m-mn)
            p=jnp.exp(s-mn)
            l=l*a+jnp.sum(p,axis=0,keepdims=True)
            pb=p.astype(bf)
            ps[h,kb]=pb
            mk[h,kb]=mn
            ot=ot*a+dg(kvt[kb,64:,:],pb,NN)
            new.append((mn,l,ot))
        return tuple(new)
    init=tuple((jnp.full((1,B),-1e30,f32),jnp.zeros((1,B),f32),jnp.zeros((64,B),f32)) for _ in range(2))
    carry=lax.fori_loop(0,rb,lambda kb,c: fwd(kb,c,False),init)
    carry=fwd(rb,carry,True)
    stats=[]
    ots=[]
    for h in range(2):
        m,l,ot=carry[h]
        inv=1.0/l
        ot=ot*inv
        ots.append(ot)
        delta=jnp.sum(ot*dot_[64*h:64*h+64,:],axis=0,keepdims=True)
        stats.append((m,inv,delta))
    o_ref[...]=jnp.concatenate(ots,axis=0).T.astype(bf)
    def bwd(kb,carry):
        new=[]; dsl=[]; pl_=[]
        for h in range(2):
            m,inv,delta=stats[h]
            alpha=jnp.exp(mk[h,kb]-m)*inv
            dp=dg(v2[kb],dom[h],NT)
            p=ps[h,kb].astype(f32)*alpha
            ds=(p*(dp-delta)).astype(bf)
            pn=p.astype(bf)
            acck[kb]+=dg(ds,qm[h],NN)
            accv[kb]+=dg(pn,dom[h],NN)
            new.append(carry[h]+dg(kvt[kb,:64,:],ds,NN))
        return tuple(new)
    c=lax.fori_loop(0,rb+1,bwd,(jnp.zeros((64,B),f32),jnp.zeros((64,B),f32)))
    dq_ref[...]=jnp.concatenate(c,axis=0).T
    @pl.when(pair==pl.num_programs(1)-1)
    def _():
        for kb in range(nkb):
            k=acck[kb]; v=accv[kb]
            lane=lax.broadcasted_iota(jnp.int32,k.shape,1)<64
            dkv_ref[0,kb*B:(kb+1)*B,:]=jnp.where(lane,k+pltpu.roll(k,64,1),v+pltpu.roll(v,64,1))
def attention(rb,q,do,kv,interpret=False):
    n=kv.shape[0]; S=kv.shape[1]; nkb=S//B
    blk=pl.BlockSpec((B,128),lambda b,p,r:(b,p))
    kvs=pl.BlockSpec((1,S,128),lambda b,p,r:(b,0,0))
    return pl.pallas_call(attn_kernel,
      grid_spec=pltpu.PrefetchScalarGridSpec(num_scalar_prefetch=1,grid=(n,6),in_specs=[blk,blk,kvs],out_specs=[blk,blk,kvs],
        scratch_shapes=[pltpu.VMEM((nkb,B,128),bf),pltpu.VMEM((nkb,B,128),bf),pltpu.VMEM((nkb,128,B),bf),pltpu.VMEM((nkb,B,128),f32),pltpu.VMEM((nkb,B,128),f32),
                        pltpu.VMEM((2,nkb,B,B),bf),pltpu.VMEM((2,nkb,1,B),f32)]),
      out_shape=[jax.ShapeDtypeStruct(q.shape,bf),jax.ShapeDtypeStruct(q.shape,f32),jax.ShapeDtypeStruct(kv.shape,f32)],
      compiler_params=pltpu.CompilerParams(vmem_limit_bytes=56<<20),name="attn")(rb,q,do,kv)


def kv_gather_kernel(nz, own_ref, full_ref, send, recv):
    pos = coords(nz)
    z, x, y, c = pos
    greet(pos, ["y", "c"], nz)
    nb = own_ref.shape[0]
    sent = []

    def go(b, m, src, kind):
        cp = pltpu.make_async_remote_copy(src, full_ref.at[b, m], send.at[len(sent)], recv.at[b, m],
                                          device_id=peer(pos, kind, nz), device_id_type=MESH)
        cp.start()
        sent.append(cp)

    def wait(b, m):
        pltpu.make_async_remote_copy(full_ref.at[b, m], full_ref.at[b, m], send.at[0], recv.at[b, m],
                                     device_id=peer(pos, "c", nz), device_id_type=MESH).wait_recv()

    for b in range(nb):
        go(b, y * 2 + c, own_ref.at[b], "y")
    for b in range(nb):
        go(b, y * 2 + c, own_ref.at[b], "c")
    for b in range(nb):
        full_ref[b, y * 2 + c] = own_ref[b]
    for b in range(nb):
        m = (1 - y) * 2 + c
        wait(b, m)
        go(b, m, full_ref.at[b, m], "c")
    for b in range(nb):
        wait(b, y * 2 + 1 - c)
        wait(b, (1 - y) * 2 + 1 - c)
    for cp in sent:
        cp.wait_send()


def kv_gather(own, dp, cid):
    nb, rows, w = own.shape
    return pl.pallas_call(
        functools.partial(kv_gather_kernel, dp // 2),
        in_specs=[pl.BlockSpec(memory_space=pltpu.VMEM)],
        out_specs=pl.BlockSpec(memory_space=pltpu.VMEM),
        out_shape=jax.ShapeDtypeStruct((nb, 4, rows, w), own.dtype),
        scratch_shapes=[pltpu.SemaphoreType.DMA((3 * nb,)), pltpu.SemaphoreType.DMA((nb, 4))],
        compiler_params=pltpu.CompilerParams(collective_id=cid, has_side_effects=True),
        name="gather_keyval",
    )(own)


def kv_reduce_kernel(nz, parts_ref, out_ref, low, cbuf, ybuf, ysend, send, crecv, yrecv):
    pos = coords(nz)
    z, x, y, c = pos
    greet(pos, ["y", "c"], nz)
    nb = parts_ref.shape[0]
    sent = []

    def go(src, dst, sem, kind):
        cp = pltpu.make_async_remote_copy(src, dst, send.at[len(sent)], sem, device_id=peer(pos, kind, nz), device_id_type=MESH)
        cp.start()
        sent.append(cp)

    def wait(dst, sem):
        pltpu.make_async_remote_copy(dst, dst, send.at[0], sem, device_id=peer(pos, "c", nz), device_id_type=MESH).wait_recv()

    for ry in (1, 0):
        yy = 1 - y if ry else y
        for b in range(nb):
            low[b, ry] = parts_ref[b, yy * 2 + 1 - c].astype(bf)
            go(low.at[b, ry], cbuf.at[b, ry], crecv.at[b, ry], "c")
    for b in range(nb):
        wait(cbuf.at[b, 1], crecv.at[b, 1])
        ysend[b] = (parts_ref[b, (1 - y) * 2 + c] + cbuf[b, 1].astype(f32)).astype(bf)
        go(ysend.at[b], ybuf.at[b], yrecv.at[b], "y")
    for b in range(nb):
        wait(cbuf.at[b, 0], crecv.at[b, 0])
        wait(ybuf.at[b], yrecv.at[b])
        out_ref[b] = parts_ref[b, y * 2 + c] + cbuf[b, 0].astype(f32) + ybuf[b].astype(f32)
    for cp in sent:
        cp.wait_send()


def kv_reduce(parts, dp, cid):
    nb, mp, rows, w = parts.shape
    return pl.pallas_call(
        functools.partial(kv_reduce_kernel, dp // 2),
        in_specs=[pl.BlockSpec(memory_space=pltpu.VMEM)],
        out_specs=pl.BlockSpec(memory_space=pltpu.VMEM),
        out_shape=jax.ShapeDtypeStruct((nb, rows, w), f32),
        scratch_shapes=[pltpu.VMEM((nb, 2, rows, w), bf), pltpu.VMEM((nb, 2, rows, w), bf), pltpu.VMEM((nb, rows, w), bf),
                        pltpu.VMEM((nb, rows, w), bf), pltpu.SemaphoreType.DMA((3 * nb,)), pltpu.SemaphoreType.DMA((nb, 2)), pltpu.SemaphoreType.DMA((nb,))],
        compiler_params=pltpu.CompilerParams(collective_id=cid, has_side_effects=True),
        name="reduce_keyval",
    )(parts)


def gather_all(qo, mlp, kvg, dp, mp):
    if dp == 8:
        plan = [(0, 0, 256, "zyx"), (0, 256, 384, "xzy"), (2, 0, 256, "zx"), (1, 0, 1024, "zyx"), (1, 1024, 1536, "xzy")]
        a, b, c = gather([qo, mlp, kvg], plan, dp, mp, 1)
    else:
        both = lambda s: lax.all_gather(s, ("dp", "mp")).reshape((dp, mp) + s.shape).transpose(1, 0, 2, 3)
        a, b, c = both(qo), both(mlp), lax.all_gather(kvg, "dp")
    return a.reshape(mp, -1, a.shape[-1]), b.reshape(mp, -1, b.shape[-1]), c.reshape(-1, c.shape[-1])


def scatter_all(qo, mlp, kvg, dp, mp):
    rows = kvg.shape[0] // dp
    cut = lambda p: p.reshape(p.shape[:-2] + (dp, rows, p.shape[-1]))
    if dp == 8:
        plan = [(0, 0, 256, "xyz"), (0, 256, 384, "yzx"), (2, 0, 256, "xz"), (1, 0, 1024, "xyz"), (1, 1024, 1536, "yzx")]
        return scatter([cut(qo), cut(mlp), cut(kvg)], plan, dp, mp, 2)
    both = lambda p: lax.psum_scatter(cut(p).transpose(1, 0, 2, 3).reshape((dp * mp, rows, p.shape[-1])).astype(f32), ("dp", "mp"), scatter_dimension=0)
    return both(qo), both(mlp), lax.psum(lax.psum_scatter(cut(kvg).astype(f32), "dp", scatter_dimension=0), "mp")


def rotary(position, width, heads):
    lane = jnp.arange(width, dtype=jnp.int32)
    inside = lane % HD
    frequency = 10000.0 ** (-2.0 * (inside % (ROT // 2)).astype(f32) / ROT)
    angle = position[:, None].astype(f32) * frequency[None, :]
    turned = ((inside < ROT) & (lane < heads * HD))[None, :]
    low = (inside < ROT // 2)[None, :]
    cosine = jnp.where(turned, jnp.cos(angle), 1.0)
    sine = jnp.where(turned, jnp.sin(angle), 0.0)
    return cosine, jnp.where(low, -sine, 0.0), jnp.where(low, 0.0, sine)


def rotate(v, tables, back=False):
    cosine, up, down = tables
    half = ROT // 2
    a = jnp.roll(v, -half, axis=1) * up
    b = jnp.roll(v, half, axis=1) * down
    return v * cosine - a - b if back else v * cosine + a + b


def shards(tokens, norm_gains, norm_biases, w_query, w_keyval, w_output, w_up, w_down, cotangent, subset_ids, subset_weights):
    dp, mp = lax.axis_size("dp"), lax.axis_size("mp")
    me = lax.axis_index("mp")
    nb, own, width = tokens.shape
    rows = nb * own
    heads = width // HD
    cols = w_query.shape[1]
    ff = w_up.shape[1]
    dot = functools.partial(jnp.dot, preferred_element_type=f32)
    nt = lambda a, b: lax.dot_general(a, b, (((1,), (1,)), ((), ())), preferred_element_type=f32)
    tn = lambda a, b: lax.dot_general(a, b, (((0,), (0,)), ((), ())), preferred_element_type=f32)
    qo = jnp.concatenate([w_query, w_output], axis=1)
    mlp = jnp.concatenate([w_up, w_down], axis=1)
    kvg = jnp.concatenate([w_keyval, norm_gains, norm_biases, jnp.zeros((w_keyval.shape[0], 124), bf)], axis=1)
    qo, mlp, kvg = gather_all(qo, mlp, kvg, dp, mp)
    wq = qo[:, :, :cols].transpose(1, 0, 2).reshape(width, width)
    wo = qo[:, :, cols:].transpose(1, 0, 2).reshape(width, width)
    wkv = kvg[:, : 2 * HD]
    small = kvg[:, 2 * HD : 2 * HD + 4].astype(f32).T
    gain_a, gain_m, bias_a, bias_m = small[0], small[1], small[2], small[3]

    ids = lax.dynamic_slice_in_dim(subset_ids.reshape(nb, mp * own), me * own, own, 1).reshape(rows)
    matches = ids[:, None] == jnp.arange(subset_weights.shape[0], dtype=jnp.int32)[None, :]
    scale = jnp.sum(jnp.where(matches, subset_weights[None, :], 0.0), axis=1, keepdims=True)
    grad_rows = cotangent.reshape(rows, width).astype(f32) * scale
    g = grad_rows.astype(bf)

    x = tokens.reshape(rows, width).astype(f32)
    centered = x - jnp.mean(x, axis=1, keepdims=True)
    inverse = lax.rsqrt(jnp.mean(centered * centered, axis=1, keepdims=True) + epsilon)
    normed = centered * inverse
    attn_in = (normed * gain_a + bias_a).astype(bf)
    mlp_in = (normed * gain_m + bias_m).astype(bf)
    position = jnp.tile(me * own + jnp.arange(own, dtype=jnp.int32), nb)
    tables = rotary(position, width, heads)
    kv_tables = rotary(position, 2 * HD, 1)
    q = (rotate(dot(attn_in, wq), tables) * HD ** (-0.5)).astype(bf)
    kv = rotate(dot(attn_in, wkv), kv_tables).astype(bf)
    kv_full = kv_gather(kv.reshape(nb, own, 2 * HD), dp, 3).reshape(nb, mp * own, 2 * HD)
    grad_heads = dot(g, wo).astype(bf)
    o, dq, dkv = attention(me.reshape(1), q, grad_heads, kv_full)
    dkv = kv_reduce(dkv.reshape(nb, mp, own, 2 * HD), dp, 4).reshape(rows, 2 * HD)

    out = x + nt(o, wo)
    dmlp = jnp.zeros((rows, width), f32)
    grads = []
    for m in range(mp):
        up, down = mlp[m, :, :ff], mlp[m, :, ff:]
        pre = dot(mlp_in, up)
        cdf = 0.5 * (1.0 + lax.erf(pre * sqrt_half))
        hidden = (pre * cdf).astype(bf)
        out = out + nt(hidden, down)
        slope = cdf + pre * (jnp.exp(-0.5 * pre * pre) * inv_sqrt_two_pi)
        dpre = (dot(g, down) * slope).astype(bf)
        dmlp = dmlp + nt(dpre, up)
        grads.append(jnp.concatenate([tn(mlp_in, dpre).astype(bf), tn(g, hidden).astype(bf)], axis=1))
    out = out.astype(bf)

    dqp = (rotate(dq, tables, True) * HD ** (-0.5)).astype(bf)
    dkvp = rotate(dkv, kv_tables, True).astype(bf)
    dattn = nt(dqp, wq) + nt(dkvp, wkv)
    dnormed = dattn * gain_a + dmlp * gain_m
    dx = (dnormed - jnp.mean(dnormed, axis=1, keepdims=True) - normed * jnp.mean(dnormed * normed, axis=1, keepdims=True)) * inverse
    input_grad = (grad_rows + dx).astype(bf)
    sums = jnp.stack([jnp.sum(dattn * normed, axis=0), jnp.sum(dmlp * normed, axis=0), jnp.sum(dattn, axis=0), jnp.sum(dmlp, axis=0)], axis=1)
    split = lambda a: a.astype(bf).reshape(width, mp, cols).transpose(1, 0, 2)
    gqo = jnp.concatenate([split(tn(attn_in, dqp)), split(tn(g, o))], axis=2)
    gkvg = jnp.concatenate([tn(attn_in, dkvp), sums, jnp.zeros((width, 124), f32)], axis=1).astype(bf)
    a, b, c = scatter_all(gqo, jnp.stack(grads), gkvg, dp, mp)
    k = 2 * HD
    return (
        out.reshape(tokens.shape),
        kv_full.reshape(-1, 2 * HD),
        input_grad.reshape(tokens.shape),
        c[:, k : k + 2],
        c[:, k + 2 : k + 4],
        a[:, :cols],
        c[:, :k],
        a[:, cols:],
        b[:, :ff],
        b[:, ff:],
    )


def solution(mesh):
    rows = P(None, ("dp", "mp"), None)
    d, dm = P("dp", None), P("dp", "mp")
    return jax.shard_map(
        shards,
        mesh=mesh,
        in_specs=(rows, d, d, dm, d, dm, dm, dm, rows, P("dp"), P()),
        out_specs=(rows, d, rows, d, d, dm, d, dm, dm, dm),
        check_vma=False,
    )
```

```python
import functools

import jax
import jax.numpy as jnp
from jax import lax
from jax.experimental import pallas as pl
from jax.experimental.pallas import tpu as pltpu
from jax.sharding import PartitionSpec as P

f32 = jnp.float32
bf = jnp.bfloat16
MESH = pl.DeviceIdType.MESH
HD = 64
ROT = 16
SEQ_LEN = 2048
epsilon = 1e-05
sqrt_half = 0.7071067811865476
inv_sqrt_two_pi = 0.3989422804014327


def coords(nz):
    d=lax.axis_index("dp"); m=lax.axis_index("mp")
    return d//2, d%2, m//2, m%2

def peer(pos,kind,nz):
    z,x,y,c=pos
    if kind[0]=="z": z=lax.rem(z+int(kind[1:]),nz)
    if kind=="x": x=1-x
    if kind=="y": y=1-y
    if kind=="c": c=1-c
    return (z*2+x, y*2+c)

def greet(pos,kinds,nz):
    bar=pltpu.get_barrier_semaphore()
    for k in kinds:
        pl.semaphore_signal(bar,inc=1,device_id=peer(pos,k,nz),device_id_type=MESH)
    pl.semaphore_wait(bar,len(kinds))

def gather_routes(order,nz):
    zs=[f"z{k}" for k in range(1,nz)]
    out=[]
    if order=="zyx":
        out.append(((0,0,0),zs+["y","x","c"]))
        out+=[((k,0,0),["y","x","c"]) for k in range(1,nz)]
        out+=[((k,0,1),["x","c"]) for k in range(nz)]
        out+=[((k,1,r),["c"]) for r in (0,1) for k in range(nz)]
    elif order=="xzy":
        out.append(((0,0,0),["x"]+zs+["y","c"]))
        out.append(((0,1,0),zs+["y","c"]))
        out+=[((k,r,0),["y","c"]) for k in range(1,nz) for r in (0,1)]
        out+=[((k,r,1),["c"]) for k in range(nz) for r in (0,1)]
    elif order=="zx":
        out.append(((0,0,0),zs+["x"]))
        out+=[((k,0,0),["x"]) for k in range(1,nz)]
        out+=[((k,1,0),[]) for k in range(nz)]
    return out

def columns(m,w,lo,hi):
    return pl.ds(pl.multiple_of(m*w+lo,128),hi-lo)

class Gather:
    def __init__(self,shards,plan,dp,mp):
        self.plan=plan; self.nz=dp//2; self.mp=mp; self.dp=dp
        inside={i for i,_,_,o in plan if o=="zx"}
        self.ins=[pl.BlockSpec(memory_space=pltpu.VMEM)]*len(shards)
        self.outs=[pl.BlockSpec(memory_space=pl.ANY)]*len(shards)
        self.shapes=[jax.ShapeDtypeStruct((dp,s.shape[0],s.shape[1]*(1 if i in inside else mp)),s.dtype) for i,s in enumerate(shards)]
        sends=sum(len(f) for _,_,_,o in plan for _,f in gather_routes(o,self.nz))
        self.scratch=[pltpu.SemaphoreType.DMA((sends,)),pltpu.SemaphoreType.DMA((len(plan),mp,dp)),pltpu.SemaphoreType.DMA((len(shards),))]
    def build(self,pos,shards,full,scr):
        send,recv,local=scr
        nz=self.nz; z,x,y,c=pos
        routes=[gather_routes(o,nz) for _,_,_,o in self.plan]
        sent=[]
        def where(p,rel,other):
            i,lo,hi,order=self.plan[p]; k,rx,ry=rel
            zz=lax.rem(z+nz-k,nz); xx=1-x if rx else x; yy=1-y if ry else y
            d=zz*2+xx; m=yy*2+(1-c if other else c)
            if order=="zx": return full[i].at[d,:,lo:hi],recv.at[p,0,d]
            return full[i].at[d,:,columns(m,shards[i].shape[1],lo,hi)],recv.at[p,m,d]
        def arrived(p,rel,other):
            dst,sem=where(p,rel,other)
            pltpu.make_async_remote_copy(dst,dst,send.at[0],sem,device_id=peer(pos,"c",nz),device_id_type=MESH).wait_recv()
        def copy(p,rel,f,own,n):
            i,lo,hi,_=self.plan[p]
            dst,sem=where(p,rel,False)
            src=shards[i].at[:,lo:hi] if own else dst
            return pltpu.make_async_remote_copy(src,dst,send.at[n],sem,device_id=peer(pos,f,nz),device_id_type=MESH)
        def step(p,s):
            rel,fw=routes[p][s]
            base=len(sent)
            cps=[functools.partial(copy,p,rel,f,s==0,base+j) for j,f in enumerate(fw)]
            sent.extend(cps)
            def go():
                if s: arrived(p,rel,False)
                for cp in cps: cp().start()
            return go
        def mine(i):
            order=[o for j,_,_,o in self.plan if j==i][0]
            d=z*2+x; w=shards[i].shape[1]
            dst=full[i].at[d] if order=="zx" else full[i].at[d,:,columns(y*2+c,w,0,w)]
            return pltpu.make_async_copy(shards[i],dst,local.at[i])
        first=[step(p,0) for p in range(len(self.plan))]
        steps=[]
        longest=max(len(r) for r in routes)
        for s in range(1,longest):
            for p,r in enumerate(routes):
                if s<len(r): steps.append(((s-1)/(longest-1),step(p,s)))
        def begin():
            for g in first: g()
            for i in range(len(shards)): mine(i).start()
        def end():
            for p,r in enumerate(routes):
                if self.plan[p][3]=="zx": continue
                for rel,_ in r: arrived(p,rel,True)
            for cp in sent: cp().wait_send()
            for i in range(len(shards)): mine(i).wait()
        return begin,steps,end

class Scatter:
    def __init__(self,parts,plan,dp,mp):
        self.plan=plan; nz=self.nz=dp//2; self.mp=mp
        self.width=[]
        for i,p in enumerate(parts):
            inside=[o for j,_,_,o in plan if j==i][0]=="xz"
            self.width.append(p.shape[-1]//(1 if inside else mp))
        self.ins=[pl.BlockSpec(memory_space=pltpu.VMEM)]*len(parts)
        self.outs=[pl.BlockSpec(memory_space=pltpu.VMEM)]*len(parts)
        self.shapes=[jax.ShapeDtypeStruct((p.shape[1],w),f32) for p,w in zip(parts,self.width)]
        scr=[]; sends=0
        for i,lo,hi,order in plan:
            rows=parts[i].shape[1]; w=hi-lo
            b=lambda k: pltpu.VMEM((k,rows,w),bf)
            nb=nz*4 if order!="xz" else nz*2
            scr+=[b(nb),b(nb)]
            if order=="xyz": scr+=[b(nz*2),b(nz),b(nz)]; sends+=nb+2*nz+nz+nz-1
            elif order=="yzx": scr+=[b(1),b(nz*2),b(nz*2)]; sends+=nb+2*nz+2*(nz-1)+1
            else: scr+=[b(nz*2),b(nz),b(2*nz)]; sends+=nb+nz+nz+nz-1
        n=len(plan)
        self.scratch=scr+[pltpu.SemaphoreType.DMA((sends,)),pltpu.SemaphoreType.DMA((n,4*nz)),pltpu.SemaphoreType.DMA((n,2*nz)),pltpu.SemaphoreType.DMA((n,2*nz)),pltpu.SemaphoreType.DMA((n,2*nz))]
    def build(self,pos,parts,outs,scr):
        plan=self.plan; nz=self.nz; z,x,y,c=pos; n=len(plan)
        per=scr[:5*n]; send,csem,xsem,ysem,zsem=scr[5*n:]
        sent=[]; begins=[]; steps=[]; ends=[]
        def sender(src,dst,rsem,kind):
            k=len(sent)
            cp=lambda: pltpu.make_async_remote_copy(src(),dst,send.at[k],rsem,device_id=peer(pos,kind,nz),device_id_type=MESH)
            sent.append(cp)
            return lambda: cp().start()
        def wait(dst,rsem):
            pltpu.make_async_remote_copy(dst,dst,send.at[0],rsem,device_id=peer(pos,"c",nz),device_id_type=MESH).wait_recv()
        def part(p,r,cc):
            i,lo,hi,order=plan[p]
            rz,rx,ry=r
            zz=lax.rem(z+rz,nz); xx=1-x if rx else x; yy=1-y if ry else y
            if order=="xz": return parts[i].at[zz*2+xx,:,lo:hi]
            return parts[i].at[zz*2+xx,:,columns(yy*2+cc,self.width[i],lo,hi)]
        def add(first,*others):
            v=first[...].astype(f32)
            for o in others: v=v+o[...].astype(f32)
            return v
        down=range(nz-1,-1,-1)
        for p,(i,lo,hi,order) in enumerate(plan):
            acc,cb,xb,yb,zb=per[5*p:5*p+5]
            if order=="xyz": seq=[(k,1,r) for r in (1,0) for k in down]+[(k,0,1) for k in down]+[(k,0,0) for k in down]
            elif order=="yzx": seq=[(k,r,1) for r in (1,0) for k in down]+[(k,1,0) for k in down]+[(k,0,0) for k in down]
            else: seq=[(k,1,0) for k in down]+[(k,0,0) for k in down]
            slot=(lambda r: (r[0]*2+r[1])*2+r[2]) if order!="xz" else (lambda r: r[0]*2+r[1])
            A=lambda r,acc=acc,slot=slot: acc.at[slot(r)]
            def plus(when,p=p):
                def note(f): steps.append((when,f))
                return note
            for t,r in enumerate(seq):
                s=slot(r); rz,rx,ry=r
                begins.append((t,sender(functools.partial(part,p,r,c if order=="xz" else 1-c),cb.at[s],csem.at[p,s],"c")))
                go=None
                if order in ("xyz","xz") and rx: go=sender(lambda v=A(r): v,xb.at[rz*2+ry],xsem.at[p,rz*2+ry],"x")
                if order=="yzx" and ry: go=sender(lambda v=A(r): v,yb.at[rz*2+rx],ysem.at[p,rz*2+rx],"y")
                @plus(0.22*t/len(seq))
                def _(p=p,r=r,s=s,acc=acc,cb=cb,go=go):
                    wait(cb.at[s],csem.at[p,s])
                    acc[s]=add(part(p,r,c),cb.at[s]).astype(bf)
                    if go: go()
            if order=="xyz":
                for n_,k in enumerate(down):
                    r=(k,0,1); j=k*2+1
                    go=sender(lambda v=A(r): v,yb.at[k],ysem.at[p,k],"y")
                    @plus(0.24+0.26*n_/nz)
                    def _(p=p,r=r,j=j,A=A,xb=xb,go=go):
                        wait(xb.at[j],xsem.at[p,j]); A(r)[...]=add(A(r),xb.at[j]).astype(bf)
                        go()
                for n_,k in enumerate(down):
                    r=(k,0,0); j=k*2
                    go=sender(lambda v=A(r): v,zb.at[k],zsem.at[p,k],f"z{k}") if k else None
                    @plus(0.52+0.26*n_/nz)
                    def _(p=p,r=r,j=j,k=k,A=A,xb=xb,yb=yb,go=go):
                        wait(xb.at[j],xsem.at[p,j]); wait(yb.at[k],ysem.at[p,k])
                        if go:
                            A(r)[...]=add(A(r),xb.at[j],yb.at[k]).astype(bf)
                            go()
                def fin(p=p,i=i,lo=lo,hi=hi,A=A,xb=xb,yb=yb,zb=zb):
                    for k in range(1,nz): wait(zb.at[k],zsem.at[p,k])
                    outs[i][:,lo:hi]=add(A((0,0,0)),xb.at[0],yb.at[0],*[zb.at[k] for k in range(1,nz)])
                ends.append(fin)
            elif order=="yzx":
                for n_,(rx,k) in enumerate([(rx,k) for rx in (1,0) for k in range(nz-1,0,-1)]):
                    r=(k,rx,0); j=k*2+rx
                    go=sender(lambda v=A(r): v,zb.at[k*2+rx],zsem.at[p,k*2+rx],f"z{k}")
                    @plus(0.24+0.3*n_/(2*nz-2))
                    def _(p=p,r=r,j=j,A=A,yb=yb,go=go):
                        wait(yb.at[j],ysem.at[p,j]); A(r)[...]=add(A(r),yb.at[j]).astype(bf)
                        go()
                r=(0,1,0)
                go=sender(lambda v=A(r): v,xb.at[0],xsem.at[p,0],"x")
                @plus(0.8)
                def _(p=p,r=r,A=A,yb=yb,zb=zb,go=go):
                    wait(yb.at[1],ysem.at[p,1])
                    for k in range(1,nz): wait(zb.at[k*2+1],zsem.at[p,k*2+1])
                    A(r)[...]=add(A(r),yb.at[1],*[zb.at[k*2+1] for k in range(1,nz)]).astype(bf)
                    go()
                def fin(p=p,i=i,lo=lo,hi=hi,A=A,xb=xb,yb=yb,zb=zb):
                    wait(yb.at[0],ysem.at[p,0])
                    for k in range(1,nz): wait(zb.at[k*2],zsem.at[p,k*2])
                    wait(xb.at[0],xsem.at[p,0])
                    outs[i][:,lo:hi]=add(A((0,0,0)),yb.at[0],xb.at[0],*[zb.at[k*2] for k in range(1,nz)])
                ends.append(fin)
            else:
                for n_,k in enumerate(down):
                    r=(k,0,0)
                    go=sender(lambda v=A(r): v,yb.at[k],ysem.at[p,k],"y")
                    @plus(0.24+0.26*n_/nz)
                    def _(p=p,r=r,k=k,A=A,xb=xb,go=go):
                        wait(xb.at[k*2],xsem.at[p,k*2]); A(r)[...]=add(A(r),xb.at[k*2]).astype(bf)
                        go()
                for n_,k in enumerate(range(nz-1,0,-1)):
                    go=sender(lambda v=zb.at[k]: v,zb.at[nz+k],zsem.at[p,k],f"z{k}")
                    @plus(0.52+0.26*n_/nz)
                    def _(p=p,k=k,A=A,yb=yb,zb=zb,go=go):
                        wait(yb.at[k],ysem.at[p,k]); zb[k]=add(A((k,0,0)),yb.at[k]).astype(bf)
                        go()
                def fin(p=p,i=i,lo=lo,hi=hi,A=A,yb=yb,zb=zb):
                    wait(yb.at[0],ysem.at[p,0])
                    for k in range(1,nz): wait(zb.at[nz+k],zsem.at[p,k])
                    outs[i][:,lo:hi]=add(A((0,0,0)),yb.at[0],*[zb.at[nz+k] for k in range(1,nz)])
                ends.append(fin)
        begins.sort(key=lambda e: e[0])
        steps.sort(key=lambda e: e[0])
        def begin():
            for _,g in begins: g()
        def end():
            for f in ends: f()
            for cp in sent: cp().wait_send()
        return begin,steps,end

def comm_kernel(nz,comm,n,*refs):
    pos=coords(nz)
    greet(pos,[f"z{k}" for k in range(1,nz)]+["x","y","c"],nz)
    begin,steps,end=comm.build(pos,refs[:n],refs[n:2*n],refs[2*n:])
    begin()
    for _,s in steps: s()
    end()

def communicate(comm,arrays,cid,name):
    return pl.pallas_call(functools.partial(comm_kernel,comm.nz,comm,len(arrays)),
        in_specs=comm.ins,out_specs=comm.outs,out_shape=comm.shapes,scratch_shapes=comm.scratch,
        compiler_params=pltpu.CompilerParams(collective_id=cid,has_side_effects=True,vmem_limit_bytes=60<<20),name=name)(*arrays)

NT=(((1,),(1,)),((),()))
NN=(((1,),(0,)),((),()))
def dg(a,b,dn): return lax.dot_general(a,b,dn,preferred_element_type=f32)
B=512
def turn(v,tab_ref,back):
    a=pltpu.roll(v,128-ROT//2,1)*tab_ref[1]
    b=pltpu.roll(v,ROT//2,1)*tab_ref[2]
    return v*tab_ref[0]-a-b if back else v*tab_ref[0]+a+b

def attn_kernel(nz,pairs,comm,nc,*refs):
    q_ref,do_ref,kv_ref,tab_ref=refs[:4]
    cin=refs[4:4+nc]
    o_ref,dq_ref,dkv_ref=refs[4+nc:7+nc]
    cout=refs[7+nc:7+2*nc]
    k2,v2,kvt,acck,accv,ps,mk,ms,ls,ots,dqs=refs[7+2*nc:18+2*nc]
    rb=lax.axis_index("mp")
    nkb=kv_ref.shape[1]//B
    slots=[[] for _ in range(pairs*2*nkb)]
    if comm:
        pos=coords(nz)
        greet(pos,[f"z{k}" for k in range(1,nz)]+["x","y","c"],nz)
        begin,steps,end=comm.build(pos,cin,cout,refs[18+2*nc:])
        begin()
        for when,s in steps: slots[int(when*len(slots))].append(s)
    def between(pair,kb,base):
        for p in range(pairs):
            todo=[k for k in range(nkb) if slots[(2*p+base)*nkb+k]]
            if not todo: continue
            @pl.when(pair==p)
            def _(p=p,todo=todo):
                for k in todo:
                    @pl.when(kb==k)
                    def _(k=k):
                        for s in slots[(2*p+base)*nkb+k]: s()
    for kb in range(nkb):
        kv=kv_ref[0,kb*B:(kb+1)*B,:].astype(f32)
        rolled=pltpu.roll(kv,64,1)
        lane=lax.broadcasted_iota(jnp.int32,kv.shape,1)<64
        k2[kb]=jnp.where(lane,kv,rolled).astype(bf)
        v2[kb]=jnp.where(lane,rolled,kv).astype(bf)
        kvt[kb]=kv.T.astype(bf)
    acck[...]=jnp.zeros_like(acck); accv[...]=jnp.zeros_like(accv)
    def one(pair,carry):
        cols=pl.ds(pl.multiple_of(pair*128,128),128)
        q=(turn(q_ref[:,cols],tab_ref,False)*HD**-0.5).astype(bf); do=do_ref[:,cols]
        lane=lax.broadcasted_iota(jnp.int32,q.shape,1)<64
        zero=jnp.zeros_like(q)
        qm=(jnp.where(lane,q,zero),jnp.where(lane,zero,q))
        dom=(jnp.where(lane,do,zero),jnp.where(lane,zero,do))
        ms[...]=jnp.full_like(ms,-1e30); ls[...]=jnp.zeros_like(ls)
        ots[...]=jnp.zeros_like(ots); dqs[...]=jnp.zeros_like(dqs)
        def fwd(kb,masked):
            for h in range(2):
                m=ms[h]
                s=dg(k2[kb],qm[h],NT)
                if masked:
                    ki=lax.broadcasted_iota(jnp.int32,s.shape,0); ri=lax.broadcasted_iota(jnp.int32,s.shape,1)
                    s=jnp.where(ki<=ri,s,-1e30)
                mn=jnp.maximum(m,jnp.max(s,axis=0,keepdims=True))
                a=jnp.exp(m-mn)
                p=jnp.exp(s-mn)
                ls[h]=ls[h]*a+jnp.sum(p,axis=0,keepdims=True)
                pb=p.astype(bf)
                ps[h,kb]=pb
                mk[h,kb]=mn
                ms[h]=mn
                ots[h]=ots[h]*a+dg(kvt[kb,64:,:],pb,NN)
        def fstep(kb,carry):
            @pl.when(kb<rb)
            def _(): fwd(kb,False)
            @pl.when(kb==rb)
            def _(): fwd(kb,True)
            between(pair,kb,0)
            return carry
        lax.fori_loop(0,nkb,fstep,0)
        dot_=do.astype(f32).T
        for h in range(2):
            inv=1.0/ls[h]
            ot=ots[h]*inv
            ots[h]=ot
            ls[h]=inv
        delta=[jnp.sum(ots[h]*dot_[64*h:64*h+64,:],axis=0,keepdims=True) for h in range(2)]
        o_ref[:,cols]=jnp.concatenate([ots[0],ots[1]],axis=0).T.astype(bf)
        def bwd(kb):
            for h in range(2):
                alpha=jnp.exp(mk[h,kb]-ms[h])*ls[h]
                dp=dg(v2[kb],dom[h],NT)
                p=ps[h,kb].astype(f32)*alpha
                ds=(p*(dp-delta[h])).astype(bf)
                pn=p.astype(bf)
                acck[kb]+=dg(ds,qm[h],NN)
                accv[kb]+=dg(pn,dom[h],NN)
                dqs[h]+=dg(kvt[kb,:64,:],ds,NN)
        def bstep(kb,carry):
            @pl.when(kb<=rb)
            def _(): bwd(kb)
            between(pair,kb,1)
            return carry
        lax.fori_loop(0,nkb,bstep,0)
        dq_ref[:,cols]=(turn(jnp.concatenate([dqs[0],dqs[1]],axis=0).T,tab_ref,True)*HD**-0.5).astype(bf)
        return carry
    lax.fori_loop(0,pairs,one,0)
    for kb in range(nkb):
        k=acck[kb]; v=accv[kb]
        lane=lax.broadcasted_iota(jnp.int32,k.shape,1)<64
        dkv_ref[0,kb*B:(kb+1)*B,:]=jnp.where(lane,k+pltpu.roll(k,64,1),v+pltpu.roll(v,64,1))
    if comm: end()

def attention(b,q,do,kv,tab,comm,arrays,dp,cid):
    S=kv.shape[1]; nkb=S//B; width=q.shape[1]
    blk=pl.BlockSpec((B,width),lambda *_: (b,0))
    own=pl.BlockSpec((B,width),lambda *_: (0,0))
    kvs=pl.BlockSpec((1,S,128),lambda *_: (b,0,0))
    dkvs=pl.BlockSpec((1,S,128),lambda *_: (0,0,0))
    tabs=pl.BlockSpec(tab.shape,lambda *_: (0,0,0))
    params=dict(vmem_limit_bytes=62<<20)
    if comm: params.update(collective_id=cid,has_side_effects=True)
    return pl.pallas_call(functools.partial(attn_kernel,dp//2,width//128,comm,len(arrays)),
      grid_spec=pltpu.PrefetchScalarGridSpec(num_scalar_prefetch=0,grid=(1,),in_specs=[blk,blk,kvs,tabs]+(comm.ins if comm else []),
        out_specs=[own,own,dkvs]+(comm.outs if comm else []),
        scratch_shapes=[pltpu.VMEM((nkb,B,128),bf),pltpu.VMEM((nkb,B,128),bf),pltpu.VMEM((nkb,128,B),bf),pltpu.VMEM((nkb,B,128),f32),pltpu.VMEM((nkb,B,128),f32),
                        pltpu.VMEM((2,nkb,B,B),bf),pltpu.VMEM((2,nkb,1,B),f32),pltpu.VMEM((2,1,B),f32),pltpu.VMEM((2,1,B),f32),pltpu.VMEM((2,64,B),f32),pltpu.VMEM((2,64,B),f32)]
                       +(comm.scratch if comm else [])),
      out_shape=[jax.ShapeDtypeStruct((B,width),bf),jax.ShapeDtypeStruct((B,width),bf),jax.ShapeDtypeStruct((1,S,128),f32)]+(comm.shapes if comm else []),
      compiler_params=pltpu.CompilerParams(**params),name="attn")(q,do,kv,tab,*arrays)


def kv_gather_kernel(nz, own_ref, full_ref, send, recv):
    pos = coords(nz)
    z, x, y, c = pos
    greet(pos, ["y", "c"], nz)
    nb = own_ref.shape[0]
    sent = []

    def go(b, m, src, kind):
        cp = pltpu.make_async_remote_copy(src, full_ref.at[b, m], send.at[len(sent)], recv.at[b, m],
                                          device_id=peer(pos, kind, nz), device_id_type=MESH)
        cp.start()
        sent.append(cp)

    def wait(b, m):
        pltpu.make_async_remote_copy(full_ref.at[b, m], full_ref.at[b, m], send.at[0], recv.at[b, m],
                                     device_id=peer(pos, "c", nz), device_id_type=MESH).wait_recv()

    for b in range(nb):
        go(b, y * 2 + c, own_ref.at[b], "y")
    for b in range(nb):
        go(b, y * 2 + c, own_ref.at[b], "c")
    for b in range(nb):
        full_ref[b, y * 2 + c] = own_ref[b]
    for b in range(nb):
        m = (1 - y) * 2 + c
        wait(b, m)
        go(b, m, full_ref.at[b, m], "c")
    for b in range(nb):
        wait(b, y * 2 + 1 - c)
        wait(b, (1 - y) * 2 + 1 - c)
    for cp in sent:
        cp.wait_send()


def kv_gather(own, dp, cid):
    nb, rows, w = own.shape
    return pl.pallas_call(
        functools.partial(kv_gather_kernel, dp // 2),
        in_specs=[pl.BlockSpec(memory_space=pltpu.VMEM)],
        out_specs=pl.BlockSpec(memory_space=pltpu.VMEM),
        out_shape=jax.ShapeDtypeStruct((nb, 4, rows, w), own.dtype),
        scratch_shapes=[pltpu.SemaphoreType.DMA((3 * nb,)), pltpu.SemaphoreType.DMA((nb, 4))],
        compiler_params=pltpu.CompilerParams(collective_id=cid, has_side_effects=True),
        name="gather_keyval",
    )(own)


def kv_reduce_kernel(nz, parts_ref, out_ref, low, cbuf, ybuf, ysend, send, crecv, yrecv):
    pos = coords(nz)
    z, x, y, c = pos
    greet(pos, ["y", "c"], nz)
    nb = parts_ref.shape[0]
    sent = []

    def go(src, dst, sem, kind):
        cp = pltpu.make_async_remote_copy(src, dst, send.at[len(sent)], sem, device_id=peer(pos, kind, nz), device_id_type=MESH)
        cp.start()
        sent.append(cp)

    def wait(dst, sem):
        pltpu.make_async_remote_copy(dst, dst, send.at[0], sem, device_id=peer(pos, "c", nz), device_id_type=MESH).wait_recv()

    for ry in (1, 0):
        yy = 1 - y if ry else y
        for b in range(nb):
            low[b, ry] = parts_ref[b, yy * 2 + 1 - c].astype(bf)
            go(low.at[b, ry], cbuf.at[b, ry], crecv.at[b, ry], "c")
    for b in range(nb):
        wait(cbuf.at[b, 1], crecv.at[b, 1])
        ysend[b] = (parts_ref[b, (1 - y) * 2 + c] + cbuf[b, 1].astype(f32)).astype(bf)
        go(ysend.at[b], ybuf.at[b], yrecv.at[b], "y")
    for b in range(nb):
        wait(cbuf.at[b, 0], crecv.at[b, 0])
        wait(ybuf.at[b], yrecv.at[b])
        out_ref[b] = parts_ref[b, y * 2 + c] + cbuf[b, 0].astype(f32) + ybuf[b].astype(f32)
    for cp in sent:
        cp.wait_send()


def kv_reduce(parts, dp, cid):
    nb, mp, rows, w = parts.shape
    return pl.pallas_call(
        functools.partial(kv_reduce_kernel, dp // 2),
        in_specs=[pl.BlockSpec(memory_space=pltpu.VMEM)],
        out_specs=pl.BlockSpec(memory_space=pltpu.VMEM),
        out_shape=jax.ShapeDtypeStruct((nb, rows, w), f32),
        scratch_shapes=[pltpu.VMEM((nb, 2, rows, w), bf), pltpu.VMEM((nb, 2, rows, w), bf), pltpu.VMEM((nb, rows, w), bf),
                        pltpu.VMEM((nb, rows, w), bf), pltpu.SemaphoreType.DMA((3 * nb,)), pltpu.SemaphoreType.DMA((nb, 2)), pltpu.SemaphoreType.DMA((nb,))],
        compiler_params=pltpu.CompilerParams(collective_id=cid, has_side_effects=True),
        name="reduce_keyval",
    )(parts)


def spread(arrays, inside, dp, mp):
    out = []
    for i, s in enumerate(arrays):
        if i in inside:
            out.append(lax.all_gather(s, "dp"))
        else:
            a = lax.all_gather(s, ("dp", "mp")).reshape((dp, mp) + s.shape)
            out.append(a.transpose(0, 2, 1, 3).reshape(dp, s.shape[0], -1))
    return out


def collect(parts, inside, dp, mp):
    out = []
    for i, p in enumerate(parts):
        p = p.astype(f32)
        if i in inside:
            out.append(lax.psum(lax.psum_scatter(p, "dp", scatter_dimension=0), "mp"))
        else:
            a = p.reshape(dp, p.shape[1], mp, -1).transpose(0, 2, 1, 3).reshape(dp * mp, p.shape[1], -1)
            out.append(lax.psum_scatter(a, ("dp", "mp"), scatter_dimension=0))
    return out


def rotary(position):
    lane = jnp.arange(2 * HD, dtype=jnp.int32)
    inside = lane % HD
    frequency = 10000.0 ** (-2.0 * (inside % (ROT // 2)).astype(f32) / ROT)
    angle = position[:, None].astype(f32) * frequency[None, :]
    turned = (inside < ROT)[None, :]
    low = (inside < ROT // 2)[None, :]
    cosine = jnp.where(turned, jnp.cos(angle), 1.0)
    sine = jnp.where(turned, jnp.sin(angle), 0.0)
    return jnp.stack([cosine, jnp.where(low, -sine, 0.0), jnp.where(low, 0.0, sine)])


def rotate(v, tables, back=False):
    cosine, up, down = tables
    half = ROT // 2
    a = jnp.roll(v, -half, axis=1) * up
    b = jnp.roll(v, half, axis=1) * down
    return v * cosine - a - b if back else v * cosine + a + b


def shards(tokens, norm_gains, norm_biases, w_query, w_keyval, w_output, w_up, w_down, cotangent, subset_ids, subset_weights):
    dp, mp = lax.axis_size("dp"), lax.axis_size("mp")
    me = lax.axis_index("mp")
    nb, own, width = tokens.shape
    rows = nb * own
    part = w_query.shape[0]
    cols = w_query.shape[1]
    ff = w_up.shape[1]
    mine = dp == 8
    dot = functools.partial(jnp.dot, preferred_element_type=f32)
    nt = lambda a, b: lax.dot_general(a, b, (((1,), (1,)), ((), ())), preferred_element_type=f32)
    tn = lambda a, b: lax.dot_general(a, b, (((0,), (0,)), ((), ())), preferred_element_type=f32)
    qo = jnp.concatenate([w_query, w_output], axis=1)
    kvg = jnp.concatenate([w_keyval, norm_gains, norm_biases, jnp.zeros((part, 124), bf)], axis=1)
    if mine:
        qo, kvg = communicate(Gather([qo, kvg], [(0, 0, 256, "zyx"), (0, 256, 384, "xzy"), (1, 0, 256, "zx")], dp, mp), [qo, kvg], 1, "gather_weights")
    else:
        qo, kvg = spread([qo, kvg], {1}, dp, mp)
    qo = qo.reshape(width, mp, 2 * cols)
    wq = qo[:, :, :cols].reshape(width, width)
    wo = qo[:, :, cols:].reshape(width, width)
    kvg = kvg.reshape(width, -1)
    wkv = kvg[:, : 2 * HD]
    small = kvg[:, 2 * HD : 2 * HD + 4].astype(f32).T
    gain_a, gain_m, bias_a, bias_m = small[0], small[1], small[2], small[3]

    ids = lax.dynamic_slice_in_dim(subset_ids.reshape(nb, mp * own), me * own, own, 1).reshape(rows)
    matches = ids[:, None] == jnp.arange(subset_weights.shape[0], dtype=jnp.int32)[None, :]
    scale = jnp.sum(jnp.where(matches, subset_weights[None, :], 0.0), axis=1, keepdims=True)
    grad_rows = cotangent.reshape(rows, width).astype(f32) * scale
    g = grad_rows.astype(bf)

    x = tokens.reshape(rows, width).astype(f32)
    centered = x - jnp.mean(x, axis=1, keepdims=True)
    inverse = lax.rsqrt(jnp.mean(centered * centered, axis=1, keepdims=True) + epsilon)
    normed = centered * inverse
    attn_in = (normed * gain_a + bias_a).astype(bf)
    mlp_in = (normed * gain_m + bias_m).astype(bf)
    tables = rotary(me * own + jnp.arange(own, dtype=jnp.int32))
    first = (jnp.arange(2 * HD) < HD)[None, :]
    kv_tables = [jnp.tile(jnp.where(first, t, e), (nb, 1)) for t, e in zip(tables, (1.0, 0.0, 0.0))]
    q = dot(attn_in, wq)
    kv = rotate(dot(attn_in, wkv), kv_tables).astype(bf)
    kv_full = kv_gather(kv.reshape(nb, own, 2 * HD), dp, 3).reshape(nb, mp * own, 2 * HD)
    grad_heads = dot(g, wo).astype(bf)
    mlp_plan = lambda a, b: [(0, 0, 768, a), (1, 0, 256, a), (1, 256, 768, b)]
    if mine:
        o0, dq0, dkv0, up, down = attention(0, q, grad_heads, kv_full, tables, Gather([w_up, w_down], mlp_plan("zyx", "xzy"), dp, mp), [w_up, w_down], dp, 5)
    else:
        o0, dq0, dkv0 = attention(0, q, grad_heads, kv_full, tables, None, [], dp, 5)
        up, down = spread([w_up, w_down], (), dp, mp)
    up = up.reshape(width, mp * ff)
    down = down.reshape(width, mp * ff)

    pre = dot(mlp_in, up)
    cdf = 0.5 * (1.0 + lax.erf(pre * sqrt_half))
    hidden = (pre * cdf).astype(bf)
    slope = cdf + pre * (jnp.exp(-0.5 * pre * pre) * inv_sqrt_two_pi)
    dpre = (dot(g, down) * slope).astype(bf)
    gup = tn(mlp_in, dpre).astype(bf).reshape(dp, part, mp * ff)
    gdown = tn(g, hidden).astype(bf).reshape(dp, part, mp * ff)
    if mine:
        o1, dq1, dkv1, grad_up, grad_down = attention(1, q, grad_heads, kv_full, tables, Scatter([gup, gdown], mlp_plan("xyz", "yzx"), dp, mp), [gup, gdown], dp, 6)
    else:
        o1, dq1, dkv1 = attention(1, q, grad_heads, kv_full, tables, None, [], dp, 6)
        grad_up, grad_down = collect([gup, gdown], (), dp, mp)
    dkv = kv_reduce(jnp.concatenate([dkv0, dkv1]).reshape(nb, mp, own, 2 * HD), dp, 4).reshape(rows, 2 * HD)
    o = jnp.concatenate([o0, o1])
    dqp = jnp.concatenate([dq0, dq1])

    out = (x + nt(o, wo) + nt(hidden, down)).astype(bf)
    dmlp = nt(dpre, up)
    dkvp = rotate(dkv, kv_tables, True).astype(bf)
    dattn = nt(dqp, wq) + nt(dkvp, wkv)
    dnormed = dattn * gain_a + dmlp * gain_m
    dx = (dnormed - jnp.mean(dnormed, axis=1, keepdims=True) - normed * jnp.mean(dnormed * normed, axis=1, keepdims=True)) * inverse
    input_grad = (grad_rows + dx).astype(bf)
    sums = jnp.stack([jnp.sum(dattn * normed, axis=0), jnp.sum(dmlp * normed, axis=0), jnp.sum(dattn, axis=0), jnp.sum(dmlp, axis=0)], axis=1)
    split = lambda a: a.astype(bf).reshape(width, mp, cols)
    gqo = jnp.concatenate([split(tn(attn_in, dqp)), split(tn(g, o))], axis=2).reshape(dp, part, -1)
    gkvg = jnp.concatenate([tn(attn_in, dkvp), sums, jnp.zeros((width, 124), f32)], axis=1).astype(bf).reshape(dp, part, -1)
    if mine:
        a, c = communicate(Scatter([gqo, gkvg], [(0, 0, 256, "xyz"), (0, 256, 384, "yzx"), (1, 0, 256, "xz")], dp, mp), [gqo, gkvg], 2, "scatter_grads")
    else:
        a, c = collect([gqo, gkvg], {1}, dp, mp)
    k = 2 * HD
    return (
        out.reshape(tokens.shape),
        kv_full.reshape(-1, 2 * HD),
        input_grad.reshape(tokens.shape),
        c[:, k : k + 2],
        c[:, k + 2 : k + 4],
        a[:, :cols],
        c[:, :k],
        a[:, cols:],
        grad_up,
        grad_down,
    )


def solution(mesh):
    rows = P(None, ("dp", "mp"), None)
    d, dm = P("dp", None), P("dp", "mp")
    return jax.shard_map(
        shards,
        mesh=mesh,
        in_specs=(rows, d, d, dm, d, dm, dm, dm, rows, P("dp"), P()),
        out_specs=(rows, d, rows, d, d, dm, d, dm, dm, dm),
        check_vma=False,
    )
```

```python
import functools

import jax
import jax.numpy as jnp
from jax import lax
from jax.experimental import pallas as pl
from jax.experimental.pallas import tpu as pltpu
from jax.sharding import PartitionSpec as P

f32 = jnp.float32
bf = jnp.bfloat16
MESH = pl.DeviceIdType.MESH
HD = 64
ROT = 16
SEQ_LEN = 2048
epsilon = 1e-05
sqrt_half = 0.7071067811865476
inv_sqrt_two_pi = 0.3989422804014327


def coords(nz):
    d=lax.axis_index("dp"); m=lax.axis_index("mp")
    return d//2, d%2, m//2, m%2

def peer(pos,kind,nz):
    z,x,y,c=pos
    if kind[0]=="z": z=lax.rem(z+int(kind[1:]),nz)
    if kind=="x": x=1-x
    if kind=="y": y=1-y
    if kind=="c": c=1-c
    return (z*2+x, y*2+c)

def greet(pos,kinds,nz):
    bar=pltpu.get_barrier_semaphore()
    for k in kinds:
        pl.semaphore_signal(bar,inc=1,device_id=peer(pos,k,nz),device_id_type=MESH)
    pl.semaphore_wait(bar,len(kinds))

def gather_routes(order,nz):
    zs=[f"z{k}" for k in range(1,nz)]
    out=[]
    if order=="zyx":
        out.append(((0,0,0),zs+["y","x","c"]))
        out+=[((k,0,0),["y","x","c"]) for k in range(1,nz)]
        out+=[((k,0,1),["x","c"]) for k in range(nz)]
        out+=[((k,1,r),["c"]) for r in (0,1) for k in range(nz)]
    elif order=="xzy":
        out.append(((0,0,0),["x"]+zs+["y","c"]))
        out.append(((0,1,0),zs+["y","c"]))
        out+=[((k,r,0),["y","c"]) for k in range(1,nz) for r in (0,1)]
        out+=[((k,r,1),["c"]) for k in range(nz) for r in (0,1)]
    elif order=="zx":
        out.append(((0,0,0),zs+["x"]))
        out+=[((k,0,0),["x"]) for k in range(1,nz)]
        out+=[((k,1,0),[]) for k in range(nz)]
    return out

def columns(m,w,lo,hi):
    return pl.ds(pl.multiple_of(m*w+lo,128),hi-lo)

class Gather:
    late=0.45
    def __init__(self,shards,plan,dp,mp):
        self.plan=plan; self.nz=dp//2; self.mp=mp; self.dp=dp
        inside={i for i,_,_,o in plan if o=="zx"}
        self.ins=[pl.BlockSpec(memory_space=pltpu.VMEM)]*len(shards)
        self.outs=[pl.BlockSpec(memory_space=pl.ANY)]*len(shards)
        self.shapes=[jax.ShapeDtypeStruct((dp,s.shape[0],s.shape[1]*(1 if i in inside else mp)),s.dtype) for i,s in enumerate(shards)]
        sends=sum(len(f) for _,_,_,o in plan for _,f in gather_routes(o,self.nz))
        self.scratch=[pltpu.SemaphoreType.DMA((sends,)),pltpu.SemaphoreType.DMA((len(plan),mp,dp)),pltpu.SemaphoreType.DMA((len(shards),))]
    def build(self,pos,shards,full,scr):
        send,recv,local=scr
        nz=self.nz; z,x,y,c=pos
        routes=[gather_routes(o,nz) for _,_,_,o in self.plan]
        sent=[]
        def where(p,rel,other):
            i,lo,hi,order=self.plan[p]; k,rx,ry=rel
            zz=lax.rem(z+nz-k,nz); xx=1-x if rx else x; yy=1-y if ry else y
            d=zz*2+xx; m=yy*2+(1-c if other else c)
            if order=="zx": return full[i].at[d,:,lo:hi],recv.at[p,0,d]
            return full[i].at[d,:,columns(m,shards[i].shape[1],lo,hi)],recv.at[p,m,d]
        def arrived(p,rel,other):
            dst,sem=where(p,rel,other)
            pltpu.make_async_remote_copy(dst,dst,send.at[0],sem,device_id=peer(pos,"c",nz),device_id_type=MESH).wait_recv()
        def copy(p,rel,f,own,n):
            i,lo,hi,_=self.plan[p]
            dst,sem=where(p,rel,False)
            src=shards[i].at[:,lo:hi] if own else dst
            return pltpu.make_async_remote_copy(src,dst,send.at[n],sem,device_id=peer(pos,f,nz),device_id_type=MESH)
        def step(p,s):
            rel,fw=routes[p][s]
            base=len(sent)
            cps=[functools.partial(copy,p,rel,f,s==0,base+j) for j,f in enumerate(fw)]
            sent.extend(cps)
            def go():
                if s: arrived(p,rel,False)
                for cp in cps: cp().start()
            return go
        def mine(i):
            order=[o for j,_,_,o in self.plan if j==i][0]
            d=z*2+x; w=shards[i].shape[1]
            dst=full[i].at[d] if order=="zx" else full[i].at[d,:,columns(y*2+c,w,0,w)]
            return pltpu.make_async_copy(shards[i],dst,local.at[i])
        first=[step(p,0) for p in range(len(self.plan))]
        steps=[]
        longest=max(len(r) for r in routes)
        for s in range(1,longest):
            for p,r in enumerate(routes):
                if s<len(r): steps.append(((s-1)/(longest-1),step(p,s)))
        def begin():
            for g in first: g()
            for i in range(len(shards)): mine(i).start()
        def end():
            for p,r in enumerate(routes):
                if self.plan[p][3]=="zx": continue
                for rel,_ in r: arrived(p,rel,True)
            for cp in sent: cp().wait_send()
            for i in range(len(shards)): mine(i).wait()
        return begin,steps,end

class Scatter:
    late=0.0
    def __init__(self,parts,plan,dp,mp):
        self.plan=plan; nz=self.nz=dp//2; self.mp=mp
        self.width=[]
        for i,p in enumerate(parts):
            inside=[o for j,_,_,o in plan if j==i][0]=="xz"
            self.width.append(p.shape[-1]//(1 if inside else mp))
        self.ins=[pl.BlockSpec(memory_space=pltpu.VMEM)]*len(parts)
        self.outs=[pl.BlockSpec(memory_space=pltpu.VMEM)]*len(parts)
        self.shapes=[jax.ShapeDtypeStruct((p.shape[1],w),f32) for p,w in zip(parts,self.width)]
        scr=[]; sends=0
        for i,lo,hi,order in plan:
            rows=parts[i].shape[1]; w=hi-lo
            b=lambda k: pltpu.VMEM((k,rows,w),bf)
            nb=nz*4 if order!="xz" else nz*2
            scr+=[b(nb),b(nb)]
            if order=="xyz": scr+=[b(nz*2),b(nz),b(nz)]; sends+=nb+2*nz+nz+nz-1
            elif order=="yzx": scr+=[b(1),b(nz*2),b(nz*2)]; sends+=nb+2*nz+2*(nz-1)+1
            else: scr+=[b(nz*2),b(nz),b(2*nz)]; sends+=nb+nz+nz+nz-1
        n=len(plan)
        self.scratch=scr+[pltpu.SemaphoreType.DMA((sends,)),pltpu.SemaphoreType.DMA((n,4*nz)),pltpu.SemaphoreType.DMA((n,2*nz)),pltpu.SemaphoreType.DMA((n,2*nz)),pltpu.SemaphoreType.DMA((n,2*nz))]
    def build(self,pos,parts,outs,scr):
        plan=self.plan; nz=self.nz; z,x,y,c=pos; n=len(plan)
        per=scr[:5*n]; send,csem,xsem,ysem,zsem=scr[5*n:]
        sent=[]; begins=[]; steps=[]; ends=[]
        def sender(src,dst,rsem,kind):
            k=len(sent)
            cp=lambda: pltpu.make_async_remote_copy(src(),dst,send.at[k],rsem,device_id=peer(pos,kind,nz),device_id_type=MESH)
            sent.append(cp)
            return lambda: cp().start()
        def wait(dst,rsem):
            pltpu.make_async_remote_copy(dst,dst,send.at[0],rsem,device_id=peer(pos,"c",nz),device_id_type=MESH).wait_recv()
        def part(p,r,cc):
            i,lo,hi,order=plan[p]
            rz,rx,ry=r
            zz=lax.rem(z+rz,nz); xx=1-x if rx else x; yy=1-y if ry else y
            if order=="xz": return parts[i].at[zz*2+xx,:,lo:hi]
            return parts[i].at[zz*2+xx,:,columns(yy*2+cc,self.width[i],lo,hi)]
        def add(first,*others):
            v=first[...].astype(f32)
            for o in others: v=v+o[...].astype(f32)
            return v
        down=range(nz-1,-1,-1)
        for p,(i,lo,hi,order) in enumerate(plan):
            acc,cb,xb,yb,zb=per[5*p:5*p+5]
            if order=="xyz": seq=[(k,1,r) for r in (1,0) for k in down]+[(k,0,1) for k in down]+[(k,0,0) for k in down]
            elif order=="yzx": seq=[(k,r,1) for r in (1,0) for k in down]+[(k,1,0) for k in down]+[(k,0,0) for k in down]
            else: seq=[(k,1,0) for k in down]+[(k,0,0) for k in down]
            slot=(lambda r: (r[0]*2+r[1])*2+r[2]) if order!="xz" else (lambda r: r[0]*2+r[1])
            A=lambda r,acc=acc,slot=slot: acc.at[slot(r)]
            def plus(when,p=p):
                def note(f): steps.append((when,f))
                return note
            for t,r in enumerate(seq):
                s=slot(r); rz,rx,ry=r
                begins.append((t,sender(functools.partial(part,p,r,c if order=="xz" else 1-c),cb.at[s],csem.at[p,s],"c")))
                go=None
                if order in ("xyz","xz") and rx: go=sender(lambda v=A(r): v,xb.at[rz*2+ry],xsem.at[p,rz*2+ry],"x")
                if order=="yzx" and ry: go=sender(lambda v=A(r): v,yb.at[rz*2+rx],ysem.at[p,rz*2+rx],"y")
                @plus(0.22*t/len(seq))
                def _(p=p,r=r,s=s,acc=acc,cb=cb,go=go):
                    wait(cb.at[s],csem.at[p,s])
                    acc[s]=add(part(p,r,c),cb.at[s]).astype(bf)
                    if go: go()
            if order=="xyz":
                for n_,k in enumerate(down):
                    r=(k,0,1); j=k*2+1
                    go=sender(lambda v=A(r): v,yb.at[k],ysem.at[p,k],"y")
                    @plus(0.24+0.26*n_/nz)
                    def _(p=p,r=r,j=j,A=A,xb=xb,go=go):
                        wait(xb.at[j],xsem.at[p,j]); A(r)[...]=add(A(r),xb.at[j]).astype(bf)
                        go()
                for n_,k in enumerate(down):
                    r=(k,0,0); j=k*2
                    go=sender(lambda v=A(r): v,zb.at[k],zsem.at[p,k],f"z{k}") if k else None
                    @plus(0.52+0.26*n_/nz)
                    def _(p=p,r=r,j=j,k=k,A=A,xb=xb,yb=yb,go=go):
                        wait(xb.at[j],xsem.at[p,j]); wait(yb.at[k],ysem.at[p,k])
                        if go:
                            A(r)[...]=add(A(r),xb.at[j],yb.at[k]).astype(bf)
                            go()
                def fin(p=p,i=i,lo=lo,hi=hi,A=A,xb=xb,yb=yb,zb=zb):
                    for k in range(1,nz): wait(zb.at[k],zsem.at[p,k])
                    outs[i][:,lo:hi]=add(A((0,0,0)),xb.at[0],yb.at[0],*[zb.at[k] for k in range(1,nz)])
                ends.append(fin)
            elif order=="yzx":
                for n_,(rx,k) in enumerate([(rx,k) for rx in (1,0) for k in range(nz-1,0,-1)]):
                    r=(k,rx,0); j=k*2+rx
                    go=sender(lambda v=A(r): v,zb.at[k*2+rx],zsem.at[p,k*2+rx],f"z{k}")
                    @plus(0.24+0.3*n_/(2*nz-2))
                    def _(p=p,r=r,j=j,A=A,yb=yb,go=go):
                        wait(yb.at[j],ysem.at[p,j]); A(r)[...]=add(A(r),yb.at[j]).astype(bf)
                        go()
                r=(0,1,0)
                go=sender(lambda v=A(r): v,xb.at[0],xsem.at[p,0],"x")
                @plus(0.8)
                def _(p=p,r=r,A=A,yb=yb,zb=zb,go=go):
                    wait(yb.at[1],ysem.at[p,1])
                    for k in range(1,nz): wait(zb.at[k*2+1],zsem.at[p,k*2+1])
                    A(r)[...]=add(A(r),yb.at[1],*[zb.at[k*2+1] for k in range(1,nz)]).astype(bf)
                    go()
                def fin(p=p,i=i,lo=lo,hi=hi,A=A,xb=xb,yb=yb,zb=zb):
                    wait(yb.at[0],ysem.at[p,0])
                    for k in range(1,nz): wait(zb.at[k*2],zsem.at[p,k*2])
                    wait(xb.at[0],xsem.at[p,0])
                    outs[i][:,lo:hi]=add(A((0,0,0)),yb.at[0],xb.at[0],*[zb.at[k*2] for k in range(1,nz)])
                ends.append(fin)
            else:
                for n_,k in enumerate(down):
                    r=(k,0,0)
                    go=sender(lambda v=A(r): v,yb.at[k],ysem.at[p,k],"y")
                    @plus(0.24+0.26*n_/nz)
                    def _(p=p,r=r,k=k,A=A,xb=xb,go=go):
                        wait(xb.at[k*2],xsem.at[p,k*2]); A(r)[...]=add(A(r),xb.at[k*2]).astype(bf)
                        go()
                for n_,k in enumerate(range(nz-1,0,-1)):
                    go=sender(lambda v=zb.at[k]: v,zb.at[nz+k],zsem.at[p,k],f"z{k}")
                    @plus(0.52+0.26*n_/nz)
                    def _(p=p,k=k,A=A,yb=yb,zb=zb,go=go):
                        wait(yb.at[k],ysem.at[p,k]); zb[k]=add(A((k,0,0)),yb.at[k]).astype(bf)
                        go()
                def fin(p=p,i=i,lo=lo,hi=hi,A=A,yb=yb,zb=zb):
                    wait(yb.at[0],ysem.at[p,0])
                    for k in range(1,nz): wait(zb.at[nz+k],zsem.at[p,k])
                    outs[i][:,lo:hi]=add(A((0,0,0)),yb.at[0],*[zb.at[nz+k] for k in range(1,nz)])
                ends.append(fin)
        begins.sort(key=lambda e: e[0])
        steps.sort(key=lambda e: e[0])
        def begin():
            for _,g in begins: g()
        def end():
            for f in ends: f()
            for cp in sent: cp().wait_send()
        return begin,steps,end

def scatter_kernel(nz,comm,*refs):
    gq_ref,go_ref,gkv_ref,sums_ref,a_ref,c_ref,qo,kvg=refs[:8]
    pos=coords(nz)
    greet(pos,[f"z{k}" for k in range(1,nz)]+["x","y","c"],nz)
    rows=gq_ref.shape[1]
    lane=lax.broadcasted_iota(jnp.int32,(rows,128),1)<64
    def tile(ref,d,h): return ref[d,:,128*(h//2):128*(h//2)+128].astype(f32)
    def pack(d,carry):
        for t in range(qo.shape[2]//128):
            m,k=t//3,t%3
            lo,hi=[((gq_ref,3*m),(gq_ref,3*m+1)),((gq_ref,3*m+2),(go_ref,3*m)),((go_ref,3*m+1),(go_ref,3*m+2))][k]
            qo[d,:,128*t:128*t+128]=halves(tile(lo[0],d,lo[1]),lo[1]%2,tile(hi[0],d,hi[1]),hi[1]%2,lane).astype(bf)
        return carry
    lax.fori_loop(0,qo.shape[0],pack,0)
    s=jnp.concatenate([sums_ref[...],jnp.zeros((120,sums_ref.shape[1]),f32)],axis=0).T
    for d in range(kvg.shape[0]):
        kvg[d,:,:128]=gkv_ref[d].astype(bf)
        kvg[d,:,128:]=s[rows*d:rows*d+rows].astype(bf)
    begin,steps,end=comm.build(pos,(qo,kvg),(a_ref,c_ref),refs[8:])
    begin()
    for _,s in steps: s()
    end()

def halves(lo,lo_at,hi,hi_at,lane):
    if lo_at: lo=pltpu.roll(lo,64,1)
    if not hi_at: hi=pltpu.roll(hi,64,1)
    return jnp.where(lane,lo,hi)

def scatter_small(gq,go,gkv,sums,dp,mp,cid):
    shape=lambda w: jax.ShapeDtypeStruct((dp,gq.shape[1],w),bf)
    qo,kvg=shape(2*gq.shape[2]),shape(256)
    comm=Scatter([qo,kvg],[(1,0,256,"xz"),(0,0,256,"xyz"),(0,256,384,"yzx")],dp,mp)
    vm=pl.BlockSpec(memory_space=pltpu.VMEM)
    return pl.pallas_call(functools.partial(scatter_kernel,comm.nz,comm),
        in_specs=[vm]*4,out_specs=comm.outs,out_shape=comm.shapes,scratch_shapes=[pltpu.VMEM(qo.shape,bf),pltpu.VMEM(kvg.shape,bf)]+comm.scratch,
        compiler_params=pltpu.CompilerParams(collective_id=cid,has_side_effects=True,vmem_limit_bytes=60<<20),name="scatter_grads")(gq,go,gkv,sums)

def prologue_kernel(nz,comms,*refs):
    tok_ref,cos_ref,sin_ref,wq_ref,wo_ref,wkv_ref,gain_ref,bias_ref=refs[:8]
    q_out,o_out,small_out,normed_out,ain_out,min_out,kv_out,wkv_out=refs[8:16]
    qo_own,kvg_own,qo_full,kvg_full,ksend,krecv=refs[16:22]
    pos=coords(nz); z,x,y,c=pos
    greet(pos,[f"z{k}" for k in range(1,nz)]+["x","y","c"],nz)
    rows=wq_ref.shape[0]
    kvg_own[:,:128]=wkv_ref[...]
    kvg_own[:,128:]=jnp.concatenate([gain_ref[...].astype(f32),bias_ref[...].astype(f32),jnp.zeros((rows,124),f32)],axis=1).astype(bf)
    g,b=comms
    ga=g.build(pos,(kvg_own,),(kvg_full,),refs[22:25])
    gb=b.build(pos,(qo_own,),(qo_full,),refs[25:28])
    ga[0]()
    wq=wq_ref[...].astype(f32); wo=wo_ref[...].astype(f32)
    qo_own[:,:128]=wq[:,:128].astype(bf)
    qo_own[:,128:256]=jnp.concatenate([wq[:,128:],wo[:,:64]],axis=1).astype(bf)
    qo_own[:,256:]=wo[:,64:].astype(bf)
    gb[0]()
    nb,own,width=tok_ref.shape
    def norm(k):
        s,r=k//4,(k%4)*(own//4)
        v=tok_ref[s,r:r+own//4,:].astype(f32)
        v=v-jnp.mean(v,axis=1,keepdims=True)
        normed_out[s*own+r:s*own+r+own//4,:]=v*lax.rsqrt(jnp.mean(v*v,axis=1,keepdims=True)+epsilon)
    sa=[s for _,s in ga[1]]; sb=[s for _,s in gb[1]]
    todo=[functools.partial(norm,k) for k in range(4*nb)]
    while sa:
        sa.pop(0)()
        if sb: sb.pop(0)()
        if todo: todo.pop(0)()
    for t in todo: t()
    ga[2]()
    kvg=kvg_full[...].reshape(width,256)
    small=kvg[:,128:].astype(f32).T
    small_out[...]=small[:8]
    wkv=kvg[:,:128]
    wkv_out[...]=wkv
    def copy(s,m,src,kind,n):
        return pltpu.make_async_remote_copy(src,kv_out.at[s,m],ksend.at[n],krecv.at[s,m],device_id=peer(pos,kind,nz),device_id_type=MESH)
    copies=[]
    me=y*2+c
    for s in range(nb):
        normed=normed_out[s*own:s*own+own,:]
        ain=(normed*small[0:1]+small[2:3]).astype(bf)
        ain_out[s*own:s*own+own,:]=ain
        kv=turn(dg(ain,wkv,NN),cos_ref[...],sin_ref[...],False,True)
        kv_out[s,me]=kv.astype(bf)
        for kind in ("y","c"):
            cp=copy(s,me,kv_out.at[s,me],kind,len(copies)); cp.start(); copies.append(cp)
        min_out[s*own:s*own+own,:]=(normed*small[1:2]+small[3:4]).astype(bf)
        for _ in range(6):
            if sb: sb.pop(0)()
    other=(1-y)*2+c
    for s in range(nb):
        copy(s,other,kv_out.at[s,other],"c",0).wait_recv()
        cp=copy(s,other,kv_out.at[s,other],"c",len(copies)); cp.start(); copies.append(cp)
    for s in sb: s()
    gb[2]()
    lane=lax.broadcasted_iota(jnp.int32,(rows,128),1)<64
    def unpack(d,carry):
        def tile(m,k): return qo_full[d,:,384*m+128*k:384*m+128*k+128].astype(f32)
        for ref,place in ((q_out,[(0,0),(0,1),(1,0)]),(o_out,[(1,1),(2,0),(2,1)])):
            for j in range(ref.shape[2]//128):
                (m0,(k0,h0)),(m1,(k1,h1))=[(h//3,place[h%3]) for h in (2*j,2*j+1)]
                ref[d,:,128*j:128*j+128]=halves(tile(m0,k0),h0,tile(m1,k1),h1,lane).astype(bf)
        return carry
    lax.fori_loop(0,q_out.shape[0],unpack,0)
    for s in range(nb):
        for m in (y*2+1-c,(1-y)*2+1-c): copy(s,m,kv_out.at[s,m],"c",0).wait_recv()
    for cp in copies: cp.wait_send()

def prologue(tokens,cos,sin,wq,wo,wkv,gains,biases,dp,mp,cid):
    nb,own,width=tokens.shape; part,cols=wq.shape
    kvg=jax.ShapeDtypeStruct((part,256),bf); qo=jax.ShapeDtypeStruct((part,2*cols),bf)
    comms=(Gather([kvg],[(0,0,256,"zx")],dp,mp),Gather([qo],[(0,0,256,"zyx"),(0,256,384,"xzy")],dp,mp))
    vm=pl.BlockSpec(memory_space=pltpu.VMEM)
    s=lambda *a: jax.ShapeDtypeStruct(a,bf)
    return pl.pallas_call(functools.partial(prologue_kernel,dp//2,comms),
        in_specs=[vm]*8,out_specs=[vm]*8,
        out_shape=[s(dp,part,width),s(dp,part,width),jax.ShapeDtypeStruct((8,width),f32),jax.ShapeDtypeStruct((nb*own,width),f32),s(nb*own,width),s(nb*own,width),s(nb,mp,own,128),s(width,128)],
        scratch_shapes=[pltpu.VMEM(qo.shape,bf),pltpu.VMEM(kvg.shape,bf),pltpu.VMEM((dp,part,mp*2*cols),bf),pltpu.VMEM((dp,part,256),bf),
                        pltpu.SemaphoreType.DMA((3*nb,)),pltpu.SemaphoreType.DMA((nb,mp))]+comms[0].scratch+comms[1].scratch,
        compiler_params=pltpu.CompilerParams(collective_id=cid,has_side_effects=True,vmem_limit_bytes=60<<20),name="gather_weights")(tokens,cos,sin,wq,wo,wkv,gains,biases)

NT=(((1,),(1,)),((),()))
NN=(((1,),(0,)),((),()))
def dg(a,b,dn): return lax.dot_general(a,b,dn,preferred_element_type=f32)
B=512
def turn(v,cos,sin,back,keys_only=False):
    lane=lax.broadcasted_iota(jnp.int32,v.shape,1)
    other=jnp.where(lane%HD<ROT//2,-pltpu.roll(v,128-ROT//2,1),pltpu.roll(v,ROT//2,1))*sin
    w=v*cos-other if back else v*cos+other
    return jnp.where(lane<HD,w,v) if keys_only else w

def attn_kernel(nz,pairs,comm,nc,*refs):
    q_ref,do_ref,kv_ref,cos_ref,sin_ref=refs[:5]
    cin=refs[5:5+nc]
    o_ref,dq_ref,dkv_ref=refs[5+nc:8+nc]
    cout=refs[8+nc:8+2*nc]
    k2,v2,kvt,acck,accv,ps,mk,ms,ls,ots,dqs=refs[8+2*nc:19+2*nc]
    rb=lax.axis_index("mp")
    nkb=kv_ref.shape[1]//B
    slots=[[] for _ in range(pairs*2*nkb)]
    if comm:
        pos=coords(nz)
        greet(pos,[f"z{k}" for k in range(1,nz)]+["x","y","c"],nz)
        begin,steps,end=comm.build(pos,cin,cout,refs[19+2*nc:])
        begin()
        for when,s in steps: slots[int((comm.late+(1-comm.late)*when)*len(slots))].append(s)
    def between(pair,kb,base):
        for p in range(pairs):
            todo=[k for k in range(nkb) if slots[(2*p+base)*nkb+k]]
            if not todo: continue
            @pl.when(pair==p)
            def _(p=p,todo=todo):
                for k in todo:
                    @pl.when(kb==k)
                    def _(k=k):
                        for s in slots[(2*p+base)*nkb+k]: s()
    for kb in range(nkb):
        kv=kv_ref[0,kb*B:(kb+1)*B,:].astype(f32)
        rolled=pltpu.roll(kv,64,1)
        lane=lax.broadcasted_iota(jnp.int32,kv.shape,1)<64
        k2[kb]=jnp.where(lane,kv,rolled).astype(bf)
        v2[kb]=jnp.where(lane,rolled,kv).astype(bf)
        kvt[kb]=kv.T.astype(bf)
    acck[...]=jnp.zeros_like(acck); accv[...]=jnp.zeros_like(accv)
    def one(pair,carry):
        cols=pl.ds(pl.multiple_of(pair*128,128),128)
        q=(turn(q_ref[:,cols],cos_ref[...],sin_ref[...],False)*HD**-0.5).astype(bf); do=do_ref[:,cols]
        lane=lax.broadcasted_iota(jnp.int32,q.shape,1)<64
        zero=jnp.zeros_like(q)
        qm=(jnp.where(lane,q,zero),jnp.where(lane,zero,q))
        dom=(jnp.where(lane,do,zero),jnp.where(lane,zero,do))
        ms[...]=jnp.full_like(ms,-1e30); ls[...]=jnp.zeros_like(ls)
        ots[...]=jnp.zeros_like(ots); dqs[...]=jnp.zeros_like(dqs)
        def fwd(kb,masked):
            for h in range(2):
                m=ms[h]
                s=dg(k2[kb],qm[h],NT)
                if masked:
                    ki=lax.broadcasted_iota(jnp.int32,s.shape,0); ri=lax.broadcasted_iota(jnp.int32,s.shape,1)
                    s=jnp.where(ki<=ri,s,-1e30)
                mn=jnp.maximum(m,jnp.max(s,axis=0,keepdims=True))
                a=jnp.exp(m-mn)
                p=jnp.exp(s-mn)
                ls[h]=ls[h]*a+jnp.sum(p,axis=0,keepdims=True)
                pb=p.astype(bf)
                ps[h,kb]=pb
                mk[h,kb]=mn
                ms[h]=mn
                ots[h]=ots[h]*a+dg(kvt[kb,64:,:],pb,NN)
        def fstep(kb,carry):
            @pl.when(kb<rb)
            def _(): fwd(kb,False)
            @pl.when(kb==rb)
            def _(): fwd(kb,True)
            between(pair,kb,0)
            return carry
        lax.fori_loop(0,nkb,fstep,0)
        dot_=do.astype(f32).T
        for h in range(2):
            inv=1.0/ls[h]
            ot=ots[h]*inv
            ots[h]=ot
            ls[h]=inv
        delta=[jnp.sum(ots[h]*dot_[64*h:64*h+64,:],axis=0,keepdims=True) for h in range(2)]
        o_ref[:,cols]=jnp.concatenate([ots[0],ots[1]],axis=0).T.astype(bf)
        def bwd(kb):
            for h in range(2):
                alpha=jnp.exp(mk[h,kb]-ms[h])*ls[h]
                dp=dg(v2[kb],dom[h],NT)
                p=ps[h,kb].astype(f32)*alpha
                ds=(p*(dp-delta[h])).astype(bf)
                pn=p.astype(bf)
                acck[kb]+=dg(ds,qm[h],NN)
                accv[kb]+=dg(pn,dom[h],NN)
                dqs[h]+=dg(kvt[kb,:64,:],ds,NN)
        def bstep(kb,carry):
            @pl.when(kb<=rb)
            def _(): bwd(kb)
            between(pair,kb,1)
            return carry
        lax.fori_loop(0,nkb,bstep,0)
        dq_ref[:,cols]=(turn(jnp.concatenate([dqs[0],dqs[1]],axis=0).T,cos_ref[...],sin_ref[...],True)*HD**-0.5).astype(bf)
        return carry
    lax.fori_loop(0,pairs,one,0)
    for kb in range(nkb):
        k=acck[kb]; v=accv[kb]
        lane=lax.broadcasted_iota(jnp.int32,k.shape,1)<64
        dkv_ref[0,kb*B:(kb+1)*B,:]=jnp.where(lane,k+pltpu.roll(k,64,1),v+pltpu.roll(v,64,1))
    if comm: end()

def attention(b,q,do,kv,cos,sin,comm,arrays,dp,cid):
    S=kv.shape[1]; nkb=S//B; width=q.shape[1]
    blk=pl.BlockSpec((B,width),lambda *_: (b,0))
    own=pl.BlockSpec((B,width),lambda *_: (0,0))
    kvs=pl.BlockSpec((1,S,128),lambda *_: (b,0,0))
    dkvs=pl.BlockSpec((1,S,128),lambda *_: (0,0,0))
    tabs=pl.BlockSpec(cos.shape,lambda *_: (0,0))
    params=dict(vmem_limit_bytes=62<<20)
    if comm: params.update(collective_id=cid,has_side_effects=True)
    return pl.pallas_call(functools.partial(attn_kernel,dp//2,width//128,comm,len(arrays)),
      grid_spec=pltpu.PrefetchScalarGridSpec(num_scalar_prefetch=0,grid=(1,),in_specs=[blk,blk,kvs,tabs,tabs]+(comm.ins if comm else []),
        out_specs=[own,own,dkvs]+(comm.outs if comm else []),
        scratch_shapes=[pltpu.VMEM((nkb,B,128),bf),pltpu.VMEM((nkb,B,128),bf),pltpu.VMEM((nkb,128,B),bf),pltpu.VMEM((nkb,B,128),f32),pltpu.VMEM((nkb,B,128),f32),
                        pltpu.VMEM((2,nkb,B,B),bf),pltpu.VMEM((2,nkb,1,B),f32),pltpu.VMEM((2,1,B),f32),pltpu.VMEM((2,1,B),f32),pltpu.VMEM((2,64,B),f32),pltpu.VMEM((2,64,B),f32)]
                       +(comm.scratch if comm else [])),
      out_shape=[jax.ShapeDtypeStruct((B,width),bf),jax.ShapeDtypeStruct((B,width),bf),jax.ShapeDtypeStruct((1,S,128),f32)]+(comm.shapes if comm else []),
      compiler_params=pltpu.CompilerParams(**params),name="attn")(q,do,kv,cos,sin,*arrays)


def kv_gather_kernel(nz, own_ref, full_ref, send, recv):
    pos = coords(nz)
    z, x, y, c = pos
    greet(pos, ["y", "c"], nz)
    nb = own_ref.shape[0]
    sent = []

    def go(b, m, src, kind):
        cp = pltpu.make_async_remote_copy(src, full_ref.at[b, m], send.at[len(sent)], recv.at[b, m],
                                          device_id=peer(pos, kind, nz), device_id_type=MESH)
        cp.start()
        sent.append(cp)

    def wait(b, m):
        pltpu.make_async_remote_copy(full_ref.at[b, m], full_ref.at[b, m], send.at[0], recv.at[b, m],
                                     device_id=peer(pos, "c", nz), device_id_type=MESH).wait_recv()

    for b in range(nb):
        go(b, y * 2 + c, own_ref.at[b], "y")
    for b in range(nb):
        go(b, y * 2 + c, own_ref.at[b], "c")
    for b in range(nb):
        full_ref[b, y * 2 + c] = own_ref[b]
    for b in range(nb):
        m = (1 - y) * 2 + c
        wait(b, m)
        go(b, m, full_ref.at[b, m], "c")
    for b in range(nb):
        wait(b, y * 2 + 1 - c)
        wait(b, (1 - y) * 2 + 1 - c)
    for cp in sent:
        cp.wait_send()


def kv_gather(own, dp, cid):
    nb, rows, w = own.shape
    return pl.pallas_call(
        functools.partial(kv_gather_kernel, dp // 2),
        in_specs=[pl.BlockSpec(memory_space=pltpu.VMEM)],
        out_specs=pl.BlockSpec(memory_space=pltpu.VMEM),
        out_shape=jax.ShapeDtypeStruct((nb, 4, rows, w), own.dtype),
        scratch_shapes=[pltpu.SemaphoreType.DMA((3 * nb,)), pltpu.SemaphoreType.DMA((nb, 4))],
        compiler_params=pltpu.CompilerParams(collective_id=cid, has_side_effects=True),
        name="gather_keyval",
    )(own)


def kv_reduce_kernel(nz, n, *refs):
    parts = refs[:n]
    cos_ref, sin_ref, out_ref, low, cbuf, ybuf, ysend, send, crecv, yrecv = refs[n:]
    pos = coords(nz)
    z, x, y, c = pos
    greet(pos, ["y", "c"], nz)
    sent = []

    def go(src, dst, sem, kind):
        cp = pltpu.make_async_remote_copy(src, dst, send.at[len(sent)], sem, device_id=peer(pos, kind, nz), device_id_type=MESH)
        cp.start()
        sent.append(cp)

    def wait(dst, sem):
        pltpu.make_async_remote_copy(dst, dst, send.at[0], sem, device_id=peer(pos, "c", nz), device_id_type=MESH).wait_recv()

    for ry in (1, 0):
        yy = 1 - y if ry else y
        for b in range(n):
            low[b, ry] = parts[b][yy * 2 + 1 - c].astype(bf)
            go(low.at[b, ry], cbuf.at[b, ry], crecv.at[b, ry], "c")
    for b in range(n):
        wait(cbuf.at[b, 1], crecv.at[b, 1])
        ysend[b] = (parts[b][(1 - y) * 2 + c] + cbuf[b, 1].astype(f32)).astype(bf)
        go(ysend.at[b], ybuf.at[b], yrecv.at[b], "y")
    for b in range(n):
        wait(cbuf.at[b, 0], crecv.at[b, 0])
        wait(ybuf.at[b], yrecv.at[b])
        v = parts[b][y * 2 + c] + cbuf[b, 0].astype(f32) + ybuf[b].astype(f32)
        out_ref[b] = turn(v, cos_ref[...], sin_ref[...], True, True).astype(bf)
    for cp in sent:
        cp.wait_send()


def kv_reduce(parts, cos, sin, dp, cid):
    nb = len(parts)
    mp, rows, w = parts[0].shape
    vm = pl.BlockSpec(memory_space=pltpu.VMEM)
    return pl.pallas_call(
        functools.partial(kv_reduce_kernel, dp // 2, nb),
        in_specs=[vm] * (nb + 2),
        out_specs=vm,
        out_shape=jax.ShapeDtypeStruct((nb, rows, w), bf),
        scratch_shapes=[pltpu.VMEM((nb, 2, rows, w), bf), pltpu.VMEM((nb, 2, rows, w), bf), pltpu.VMEM((nb, rows, w), bf),
                        pltpu.VMEM((nb, rows, w), bf), pltpu.SemaphoreType.DMA((3 * nb,)), pltpu.SemaphoreType.DMA((nb, 2)), pltpu.SemaphoreType.DMA((nb,))],
        compiler_params=pltpu.CompilerParams(collective_id=cid, has_side_effects=True),
        name="reduce_keyval",
    )(*parts, cos, sin)


def spread(arrays, inside, dp, mp):
    out = []
    for i, s in enumerate(arrays):
        if i in inside:
            out.append(lax.all_gather(s, "dp"))
        else:
            a = lax.all_gather(s, ("dp", "mp")).reshape((dp, mp) + s.shape)
            out.append(a.transpose(0, 2, 1, 3).reshape(dp, s.shape[0], -1))
    return out


def collect(parts, inside, dp, mp):
    out = []
    for i, p in enumerate(parts):
        p = p.astype(f32)
        if i in inside:
            out.append(lax.psum(lax.psum_scatter(p, "dp", scatter_dimension=0), "mp"))
        else:
            a = p.reshape(dp, p.shape[1], mp, -1).transpose(0, 2, 1, 3).reshape(dp * mp, p.shape[1], -1)
            out.append(lax.psum_scatter(a, ("dp", "mp"), scatter_dimension=0))
    return out


def rotary(position):
    lane = jnp.arange(2 * HD, dtype=jnp.int32)
    inside = lane % HD
    frequency = 10000.0 ** (-2.0 * (inside % (ROT // 2)).astype(f32) / ROT)
    angle = position[:, None].astype(f32) * frequency[None, :]
    turned = (inside < ROT)[None, :]
    return jnp.where(turned, jnp.cos(angle), 1.0), jnp.where(turned, jnp.sin(angle), 0.0)


def plain_prologue(tokens, cos, sin, wq, wo, wkv, gains, biases, dp, mp):
    nb, own, width = tokens.shape
    wq, wo, kvg = spread([wq, wo, jnp.concatenate([wkv, gains, biases], axis=1)], {2}, dp, mp)
    kvg = kvg.reshape(width, -1)
    small = kvg[:, 2 * HD :].astype(f32).T
    x = tokens.reshape(nb * own, width).astype(f32)
    centered = x - jnp.mean(x, axis=1, keepdims=True)
    normed = centered * lax.rsqrt(jnp.mean(centered * centered, axis=1, keepdims=True) + epsilon)
    ain = (normed * small[0] + small[2]).astype(bf)
    mlp_in = (normed * small[1] + small[3]).astype(bf)
    kv = jnp.dot(ain, kvg[:, : 2 * HD], preferred_element_type=f32).reshape(nb, own, 2 * HD)
    first, half = jnp.arange(2 * HD) < HD, ROT // 2
    other = jnp.where(jnp.arange(2 * HD) < half, -jnp.roll(kv, -half, axis=2), jnp.roll(kv, half, axis=2)) * sin
    kv = jnp.where(first, kv * cos + other, kv).astype(bf)
    return wq, wo, jnp.concatenate([small, small]), normed, ain, mlp_in, kv_gather(kv, dp, 3), kvg[:, : 2 * HD]


def shards(tokens, norm_gains, norm_biases, w_query, w_keyval, w_output, w_up, w_down, cotangent, subset_ids, subset_weights):
    dp, mp = lax.axis_size("dp"), lax.axis_size("mp")
    me = lax.axis_index("mp")
    nb, own, width = tokens.shape
    rows = nb * own
    part, cols = w_query.shape
    ff = w_up.shape[1]
    mine = dp == 8
    dot = functools.partial(jnp.dot, preferred_element_type=f32)
    nt = lambda a, b: lax.dot_general(a, b, (((1,), (1,)), ((), ())), preferred_element_type=f32)
    tn = lambda a, b: lax.dot_general(a, b, (((0,), (0,)), ((), ())), preferred_element_type=f32)
    cos, sin = rotary(me * own + jnp.arange(own, dtype=jnp.int32))
    small_weights = (w_query, w_output, w_keyval, norm_gains, norm_biases)
    if mine:
        wq, wo, small, normed, attn_in, mlp_in, kv, wkv = prologue(tokens, cos, sin, *small_weights, dp, mp, 1)
    else:
        wq, wo, small, normed, attn_in, mlp_in, kv, wkv = plain_prologue(tokens, cos, sin, *small_weights, dp, mp)
    wq, wo = wq.reshape(width, width), wo.reshape(width, width)
    kv_full = kv.reshape(nb, mp * own, 2 * HD)
    gain_a, gain_m = small[0], small[1]

    ids = lax.dynamic_slice_in_dim(subset_ids.reshape(nb, mp * own), me * own, own, 1).reshape(rows)
    matches = ids[:, None] == jnp.arange(subset_weights.shape[0], dtype=jnp.int32)[None, :]
    scale = jnp.sum(jnp.where(matches, subset_weights[None, :], 0.0), axis=1, keepdims=True)
    grad_rows = cotangent.reshape(rows, width).astype(f32) * scale
    g = grad_rows.astype(bf)

    q = dot(attn_in, wq)
    grad_heads = dot(g, wo).astype(bf)
    mlp_plan = lambda a, b: [(0, 0, 768, a), (1, 0, 256, a), (1, 256, 768, b)]
    if mine:
        o0, dq0, dkv0, up, down = attention(0, q, grad_heads, kv_full, cos, sin, Gather([w_up, w_down], mlp_plan("zyx", "xzy"), dp, mp), [w_up, w_down], dp, 5)
    else:
        o0, dq0, dkv0 = attention(0, q, grad_heads, kv_full, cos, sin, None, [], dp, 5)
        up, down = spread([w_up, w_down], (), dp, mp)
    up = up.reshape(width, mp * ff)
    down = down.reshape(width, mp * ff)

    pre = dot(mlp_in, up)
    cdf = 0.5 * (1.0 + lax.erf(pre * sqrt_half))
    hidden = (pre * cdf).astype(bf)
    slope = cdf + pre * (jnp.exp(-0.5 * pre * pre) * inv_sqrt_two_pi)
    dpre = (dot(g, down) * slope).astype(bf)
    gup = tn(mlp_in, dpre).astype(bf).reshape(dp, part, mp * ff)
    gdown = tn(g, hidden).astype(bf).reshape(dp, part, mp * ff)
    if mine:
        o1, dq1, dkv1, grad_up, grad_down = attention(1, q, grad_heads, kv_full, cos, sin, Scatter([gup, gdown], mlp_plan("xyz", "yzx"), dp, mp), [gup, gdown], dp, 6)
    else:
        o1, dq1, dkv1 = attention(1, q, grad_heads, kv_full, cos, sin, None, [], dp, 6)
        grad_up, grad_down = collect([gup, gdown], (), dp, mp)
    dkvp = kv_reduce([d.reshape(mp, own, 2 * HD) for d in (dkv0, dkv1)], cos, sin, dp, 4).reshape(rows, 2 * HD)
    o = jnp.concatenate([o0, o1])
    dqp = jnp.concatenate([dq0, dq1])

    x = tokens.reshape(rows, width).astype(f32)
    out = (x + nt(o, wo) + nt(hidden, down)).astype(bf)
    dmlp = nt(dpre, up)
    dattn = nt(dqp, wq) + nt(dkvp, wkv)
    dnormed = dattn * gain_a + dmlp * gain_m
    centered = x - jnp.mean(x, axis=1, keepdims=True)
    inverse = lax.rsqrt(jnp.mean(centered * centered, axis=1, keepdims=True) + epsilon)
    dx = (dnormed - jnp.mean(dnormed, axis=1, keepdims=True) - normed * jnp.mean(dnormed * normed, axis=1, keepdims=True)) * inverse
    input_grad = (grad_rows + dx).astype(bf)
    sums = [jnp.sum(dattn * normed, axis=0), jnp.sum(dmlp * normed, axis=0), jnp.sum(dattn, axis=0), jnp.sum(dmlp, axis=0)]
    gq = tn(attn_in, dqp).astype(bf).reshape(dp, part, width)
    go = tn(g, o).astype(bf).reshape(dp, part, width)
    gkv = tn(attn_in, dkvp).reshape(dp, part, 2 * HD)
    k = 2 * HD
    if mine:
        sums = jnp.concatenate([s[None] for s in sums] + [jnp.zeros((4, width), f32)])
        a, c = scatter_small(gq, go, gkv, sums, dp, mp, 2)
        grad_query, grad_output = a[:, :cols], a[:, cols:]
    else:
        gkvg = jnp.concatenate([gkv, jnp.stack(sums, axis=1).reshape(dp, part, 4)], axis=2)
        grad_query, grad_output, c = collect([gq, go, gkvg], {2}, dp, mp)
    return (
        out.reshape(tokens.shape),
        kv_full.reshape(-1, 2 * HD),
        input_grad.reshape(tokens.shape),
        c[:, k : k + 2],
        c[:, k + 2 : k + 4],
        grad_query,
        c[:, :k],
        grad_output,
        grad_up,
        grad_down,
    )


def solution(mesh):
    rows = P(None, ("dp", "mp"), None)
    d, dm = P("dp", None), P("dp", "mp")
    return jax.shard_map(
        shards,
        mesh=mesh,
        in_specs=(rows, d, d, dm, d, dm, dm, dm, rows, P("dp"), P()),
        out_specs=(rows, d, rows, d, d, dm, d, dm, dm, dm),
        check_vma=False,
    )
```

```python
import functools

import jax
import jax.numpy as jnp
from jax import lax
from jax.experimental import pallas as pl
from jax.experimental.pallas import tpu as pltpu
from jax.sharding import PartitionSpec as P

f32 = jnp.float32
bf = jnp.bfloat16
MESH = pl.DeviceIdType.MESH
HD = 64
ROT = 16
SEQ_LEN = 2048
epsilon = 1e-05
sqrt_half = 0.7071067811865476
inv_sqrt_two_pi = 0.3989422804014327


def coords(nz):
    d=lax.axis_index("dp"); m=lax.axis_index("mp")
    return d//2, d%2, m//2, m%2

def peer(pos,kind,nz):
    z,x,y,c=pos
    if kind[0]=="z": z=lax.rem(z+int(kind[1:]),nz)
    if kind=="x": x=1-x
    if kind=="y": y=1-y
    if kind=="c": c=1-c
    return (z*2+x, y*2+c)

def greet(pos,kinds,nz):
    bar=pltpu.get_barrier_semaphore()
    for k in kinds:
        pl.semaphore_signal(bar,inc=1,device_id=peer(pos,k,nz),device_id_type=MESH)
    pl.semaphore_wait(bar,len(kinds))

def gather_routes(order,nz):
    zs=[f"z{k}" for k in range(1,nz)]
    out=[]
    if order=="zyx":
        out.append(((0,0,0),zs+["y","x","c"]))
        out+=[((k,0,0),["y","x","c"]) for k in range(1,nz)]
        out+=[((k,0,1),["x","c"]) for k in range(nz)]
        out+=[((k,1,r),["c"]) for r in (0,1) for k in range(nz)]
    elif order=="xzy":
        out.append(((0,0,0),["x"]+zs+["y","c"]))
        out.append(((0,1,0),zs+["y","c"]))
        out+=[((k,r,0),["y","c"]) for k in range(1,nz) for r in (0,1)]
        out+=[((k,r,1),["c"]) for k in range(nz) for r in (0,1)]
    elif order=="zx":
        out.append(((0,0,0),zs+["x"]))
        out+=[((k,0,0),["x"]) for k in range(1,nz)]
        out+=[((k,1,0),[]) for k in range(nz)]
    return out

def columns(m,w,lo,hi):
    return pl.ds(pl.multiple_of(m*w+lo,128),hi-lo)

class Gather:
    late=0.45
    def __init__(self,shards,plan,dp,mp):
        self.plan=plan; self.nz=dp//2; self.mp=mp; self.dp=dp
        inside={i for i,_,_,o in plan if o=="zx"}
        self.ins=[pl.BlockSpec(memory_space=pltpu.VMEM)]*len(shards)
        self.outs=[pl.BlockSpec(memory_space=pl.ANY)]*len(shards)
        self.shapes=[jax.ShapeDtypeStruct((dp,s.shape[0],s.shape[1]*(1 if i in inside else mp)),s.dtype) for i,s in enumerate(shards)]
        sends=sum(len(f) for _,_,_,o in plan for _,f in gather_routes(o,self.nz))
        self.scratch=[pltpu.SemaphoreType.DMA((sends,)),pltpu.SemaphoreType.DMA((len(plan),mp,dp)),pltpu.SemaphoreType.DMA((len(shards),))]
    def build(self,pos,shards,full,scr):
        send,recv,local=scr
        nz=self.nz; z,x,y,c=pos
        routes=[gather_routes(o,nz) for _,_,_,o in self.plan]
        sent=[]
        def where(p,rel,other):
            i,lo,hi,order=self.plan[p]; k,rx,ry=rel
            zz=lax.rem(z+nz-k,nz); xx=1-x if rx else x; yy=1-y if ry else y
            d=zz*2+xx; m=yy*2+(1-c if other else c)
            if order=="zx": return full[i].at[d,:,lo:hi],recv.at[p,0,d]
            return full[i].at[d,:,columns(m,shards[i].shape[1],lo,hi)],recv.at[p,m,d]
        def arrived(p,rel,other):
            dst,sem=where(p,rel,other)
            pltpu.make_async_remote_copy(dst,dst,send.at[0],sem,device_id=peer(pos,"c",nz),device_id_type=MESH).wait_recv()
        def copy(p,rel,f,own,n):
            i,lo,hi,_=self.plan[p]
            dst,sem=where(p,rel,False)
            src=shards[i].at[:,lo:hi] if own else dst
            return pltpu.make_async_remote_copy(src,dst,send.at[n],sem,device_id=peer(pos,f,nz),device_id_type=MESH)
        def step(p,s):
            rel,fw=routes[p][s]
            base=len(sent)
            cps=[functools.partial(copy,p,rel,f,s==0,base+j) for j,f in enumerate(fw)]
            sent.extend(cps)
            def go():
                if s: arrived(p,rel,False)
                for cp in cps: cp().start()
            return go
        def mine(i):
            order=[o for j,_,_,o in self.plan if j==i][0]
            d=z*2+x; w=shards[i].shape[1]
            dst=full[i].at[d] if order=="zx" else full[i].at[d,:,columns(y*2+c,w,0,w)]
            return pltpu.make_async_copy(shards[i],dst,local.at[i])
        first=[step(p,0) for p in range(len(self.plan))]
        steps=[]
        longest=max(len(r) for r in routes)
        for s in range(1,longest):
            for p,r in enumerate(routes):
                if s<len(r): steps.append(((s-1)/(longest-1),step(p,s)))
        def begin():
            for g in first: g()
            for i in range(len(shards)): mine(i).start()
        def end():
            for p,r in enumerate(routes):
                if self.plan[p][3]=="zx": continue
                for rel,_ in r: arrived(p,rel,True)
            for cp in sent: cp().wait_send()
            for i in range(len(shards)): mine(i).wait()
        return begin,steps,end

class Scatter:
    late=0.0
    def __init__(self,parts,plan,dp,mp):
        self.plan=plan; nz=self.nz=dp//2; self.mp=mp
        self.width=[]
        for i,p in enumerate(parts):
            inside=[o for j,_,_,o in plan if j==i][0]=="xz"
            self.width.append(p.shape[-1]//(1 if inside else mp))
        self.ins=[pl.BlockSpec(memory_space=pltpu.VMEM)]*len(parts)
        self.outs=[pl.BlockSpec(memory_space=pltpu.VMEM)]*len(parts)
        self.shapes=[jax.ShapeDtypeStruct((p.shape[1],w),f32) for p,w in zip(parts,self.width)]
        scr=[]; sends=0
        for i,lo,hi,order in plan:
            rows=parts[i].shape[1]; w=hi-lo
            b=lambda k: pltpu.VMEM((k,rows,w),bf)
            nb=nz*4 if order!="xz" else nz*2
            scr+=[b(nb),b(nb)]
            if order=="xyz": scr+=[b(nz*2),b(nz),b(nz)]; sends+=nb+2*nz+nz+nz-1
            elif order=="yzx": scr+=[b(1),b(nz*2),b(nz*2)]; sends+=nb+2*nz+2*(nz-1)+1
            else: scr+=[b(nz*2),b(nz),b(2*nz)]; sends+=nb+nz+nz+nz-1
        n=len(plan)
        self.scratch=scr+[pltpu.SemaphoreType.DMA((sends,)),pltpu.SemaphoreType.DMA((n,4*nz)),pltpu.SemaphoreType.DMA((n,2*nz)),pltpu.SemaphoreType.DMA((n,2*nz)),pltpu.SemaphoreType.DMA((n,2*nz))]
    def build(self,pos,parts,outs,scr):
        plan=self.plan; nz=self.nz; z,x,y,c=pos; n=len(plan)
        per=scr[:5*n]; send,csem,xsem,ysem,zsem=scr[5*n:]
        sent=[]; begins=[]; steps=[]; ends=[]
        def sender(src,dst,rsem,kind):
            k=len(sent)
            cp=lambda: pltpu.make_async_remote_copy(src(),dst,send.at[k],rsem,device_id=peer(pos,kind,nz),device_id_type=MESH)
            sent.append(cp)
            return lambda: cp().start()
        def wait(dst,rsem):
            pltpu.make_async_remote_copy(dst,dst,send.at[0],rsem,device_id=peer(pos,"c",nz),device_id_type=MESH).wait_recv()
        def part(p,r,cc):
            i,lo,hi,order=plan[p]
            rz,rx,ry=r
            zz=lax.rem(z+rz,nz); xx=1-x if rx else x; yy=1-y if ry else y
            if order=="xz": return parts[i].at[zz*2+xx,:,lo:hi]
            return parts[i].at[zz*2+xx,:,columns(yy*2+cc,self.width[i],lo,hi)]
        def add(first,*others):
            v=first[...].astype(f32)
            for o in others: v=v+o[...].astype(f32)
            return v
        down=range(nz-1,-1,-1)
        for p,(i,lo,hi,order) in enumerate(plan):
            acc,cb,xb,yb,zb=per[5*p:5*p+5]
            if order=="xyz": seq=[(k,1,r) for r in (1,0) for k in down]+[(k,0,1) for k in down]+[(k,0,0) for k in down]
            elif order=="yzx": seq=[(k,r,1) for r in (1,0) for k in down]+[(k,1,0) for k in down]+[(k,0,0) for k in down]
            else: seq=[(k,1,0) for k in down]+[(k,0,0) for k in down]
            slot=(lambda r: (r[0]*2+r[1])*2+r[2]) if order!="xz" else (lambda r: r[0]*2+r[1])
            A=lambda r,acc=acc,slot=slot: acc.at[slot(r)]
            def plus(when,p=p):
                def note(f): steps.append((when,f))
                return note
            for t,r in enumerate(seq):
                s=slot(r); rz,rx,ry=r
                begins.append((t,sender(functools.partial(part,p,r,c if order=="xz" else 1-c),cb.at[s],csem.at[p,s],"c")))
                go=None
                if order in ("xyz","xz") and rx: go=sender(lambda v=A(r): v,xb.at[rz*2+ry],xsem.at[p,rz*2+ry],"x")
                if order=="yzx" and ry: go=sender(lambda v=A(r): v,yb.at[rz*2+rx],ysem.at[p,rz*2+rx],"y")
                @plus(0.22*t/len(seq))
                def _(p=p,r=r,s=s,acc=acc,cb=cb,go=go):
                    wait(cb.at[s],csem.at[p,s])
                    acc[s]=add(part(p,r,c),cb.at[s]).astype(bf)
                    if go: go()
            if order=="xyz":
                for n_,k in enumerate(down):
                    r=(k,0,1); j=k*2+1
                    go=sender(lambda v=A(r): v,yb.at[k],ysem.at[p,k],"y")
                    @plus(0.24+0.26*n_/nz)
                    def _(p=p,r=r,j=j,A=A,xb=xb,go=go):
                        wait(xb.at[j],xsem.at[p,j]); A(r)[...]=add(A(r),xb.at[j]).astype(bf)
                        go()
                for n_,k in enumerate(down):
                    r=(k,0,0); j=k*2
                    go=sender(lambda v=A(r): v,zb.at[k],zsem.at[p,k],f"z{k}") if k else None
                    @plus(0.52+0.26*n_/nz)
                    def _(p=p,r=r,j=j,k=k,A=A,xb=xb,yb=yb,go=go):
                        wait(xb.at[j],xsem.at[p,j]); wait(yb.at[k],ysem.at[p,k])
                        if go:
                            A(r)[...]=add(A(r),xb.at[j],yb.at[k]).astype(bf)
                            go()
                def fin(p=p,i=i,lo=lo,hi=hi,A=A,xb=xb,yb=yb,zb=zb):
                    for k in range(1,nz): wait(zb.at[k],zsem.at[p,k])
                    outs[i][:,lo:hi]=add(A((0,0,0)),xb.at[0],yb.at[0],*[zb.at[k] for k in range(1,nz)])
                ends.append(fin)
            elif order=="yzx":
                for n_,(rx,k) in enumerate([(rx,k) for rx in (1,0) for k in range(nz-1,0,-1)]):
                    r=(k,rx,0); j=k*2+rx
                    go=sender(lambda v=A(r): v,zb.at[k*2+rx],zsem.at[p,k*2+rx],f"z{k}")
                    @plus(0.24+0.3*n_/(2*nz-2))
                    def _(p=p,r=r,j=j,A=A,yb=yb,go=go):
                        wait(yb.at[j],ysem.at[p,j]); A(r)[...]=add(A(r),yb.at[j]).astype(bf)
                        go()
                r=(0,1,0)
                go=sender(lambda v=A(r): v,xb.at[0],xsem.at[p,0],"x")
                @plus(0.8)
                def _(p=p,r=r,A=A,yb=yb,zb=zb,go=go):
                    wait(yb.at[1],ysem.at[p,1])
                    for k in range(1,nz): wait(zb.at[k*2+1],zsem.at[p,k*2+1])
                    A(r)[...]=add(A(r),yb.at[1],*[zb.at[k*2+1] for k in range(1,nz)]).astype(bf)
                    go()
                def fin(p=p,i=i,lo=lo,hi=hi,A=A,xb=xb,yb=yb,zb=zb):
                    wait(yb.at[0],ysem.at[p,0])
                    for k in range(1,nz): wait(zb.at[k*2],zsem.at[p,k*2])
                    wait(xb.at[0],xsem.at[p,0])
                    outs[i][:,lo:hi]=add(A((0,0,0)),yb.at[0],xb.at[0],*[zb.at[k*2] for k in range(1,nz)])
                ends.append(fin)
            else:
                for n_,k in enumerate(down):
                    r=(k,0,0)
                    go=sender(lambda v=A(r): v,yb.at[k],ysem.at[p,k],"y")
                    @plus(0.24+0.26*n_/nz)
                    def _(p=p,r=r,k=k,A=A,xb=xb,go=go):
                        wait(xb.at[k*2],xsem.at[p,k*2]); A(r)[...]=add(A(r),xb.at[k*2]).astype(bf)
                        go()
                for n_,k in enumerate(range(nz-1,0,-1)):
                    go=sender(lambda v=zb.at[k]: v,zb.at[nz+k],zsem.at[p,k],f"z{k}")
                    @plus(0.52+0.26*n_/nz)
                    def _(p=p,k=k,A=A,yb=yb,zb=zb,go=go):
                        wait(yb.at[k],ysem.at[p,k]); zb[k]=add(A((k,0,0)),yb.at[k]).astype(bf)
                        go()
                def fin(p=p,i=i,lo=lo,hi=hi,A=A,yb=yb,zb=zb):
                    wait(yb.at[0],ysem.at[p,0])
                    for k in range(1,nz): wait(zb.at[nz+k],zsem.at[p,k])
                    outs[i][:,lo:hi]=add(A((0,0,0)),yb.at[0],*[zb.at[nz+k] for k in range(1,nz)])
                ends.append(fin)
        begins.sort(key=lambda e: e[0])
        steps.sort(key=lambda e: e[0])
        def begin():
            for _,g in begins: g()
        def end():
            for f in ends: f()
            for cp in sent: cp().wait_send()
        return begin,steps,end

def scatter_kernel(nz,comm,*refs):
    gq_ref,go_ref,gkv_ref,sums_ref,o_ref,wo_ref,hid_ref,down_ref,tok_ref,cot_ref,scale_ref,dn_ref=refs[:12]
    a_ref,c_ref,out_ref,ig_ref,qo,kvg=refs[12:18]
    pos=coords(nz)
    greet(pos,[f"z{k}" for k in range(1,nz)]+["x","y","c"],nz)
    rows=gq_ref.shape[1]
    lane=lax.broadcasted_iota(jnp.int32,(rows,128),1)<64
    def tile(ref,d,h): return ref[d,:,128*(h//2):128*(h//2)+128].astype(f32)
    def pack(d,carry):
        for t in range(qo.shape[2]//128):
            m,k=t//3,t%3
            lo,hi=[((gq_ref,3*m),(gq_ref,3*m+1)),((gq_ref,3*m+2),(go_ref,3*m)),((go_ref,3*m+1),(go_ref,3*m+2))][k]
            qo[d,:,128*t:128*t+128]=halves(tile(lo[0],d,lo[1]),lo[1]%2,tile(hi[0],d,hi[1]),hi[1]%2,lane).astype(bf)
        return carry
    lax.fori_loop(0,qo.shape[0],pack,0)
    s=jnp.concatenate([sums_ref[...],jnp.zeros((120,sums_ref.shape[1]),f32)],axis=0).T
    for d in range(kvg.shape[0]):
        kvg[d,:,:128]=gkv_ref[d].astype(bf)
        kvg[d,:,128:]=s[rows*d:rows*d+rows].astype(bf)
    begin,steps,end=comm.build(pos,(qo,kvg),(a_ref,c_ref),refs[18:])
    begin()
    T=256; across=out_ref.shape[1]//T; n=out_ref.shape[0]//T*across
    slots=[[] for _ in range(n)]
    for when,s in steps:
        if when<0.23: s()
        else: slots[min(n-1,int(n*(0.33+(when-0.24)*1.15)))].append(s)
    def chunk(it,carry):
        rows=pl.ds(pl.multiple_of(it//across*T,T),T); cols=pl.ds(pl.multiple_of(it%across*T,T),T)
        @pl.when(it%across==0)
        def _():
            v=tok_ref[rows,:].astype(f32)
            v=v-jnp.mean(v,axis=1,keepdims=True)
            inverse=lax.rsqrt(jnp.mean(v*v,axis=1,keepdims=True)+epsilon)
            v=v*inverse
            dn=dn_ref[rows,:]
            dx=(dn-jnp.mean(dn,axis=1,keepdims=True)-v*jnp.mean(dn*v,axis=1,keepdims=True))*inverse
            ig_ref[rows,:]=(cot_ref[rows,:].astype(f32)*scale_ref[rows,:]+dx).astype(bf)
        y=tok_ref[rows,cols].astype(f32)+dg(o_ref[rows,:],wo_ref[cols,:],NT)+dg(hid_ref[rows,:],down_ref[cols,:],NT)
        out_ref[rows,cols]=y.astype(bf)
        for k in range(n):
            if slots[k]:
                @pl.when(it==k)
                def _(k=k):
                    for s in slots[k]: s()
        return carry
    lax.fori_loop(0,n,chunk,0)
    end()

def halves(lo,lo_at,hi,hi_at,lane):
    if lo_at: lo=pltpu.roll(lo,64,1)
    if not hi_at: hi=pltpu.roll(hi,64,1)
    return jnp.where(lane,lo,hi)

def scatter_small(gq,go,gkv,sums,o,wo,hidden,down,tokens,cotangent,scale,dnormed,dp,mp,cid):
    shape=lambda w: jax.ShapeDtypeStruct((dp,gq.shape[1],w),bf)
    qo,kvg=shape(2*gq.shape[2]),shape(256)
    comm=Scatter([qo,kvg],[(1,0,256,"xz"),(0,0,256,"xyz"),(0,256,384,"yzx")],dp,mp)
    vm=pl.BlockSpec(memory_space=pltpu.VMEM)
    return pl.pallas_call(functools.partial(scatter_kernel,comm.nz,comm),
        in_specs=[vm]*12,out_specs=comm.outs+[vm]*2,out_shape=comm.shapes+[jax.ShapeDtypeStruct(o.shape,bf)]*2,
        scratch_shapes=[pltpu.VMEM(qo.shape,bf),pltpu.VMEM(kvg.shape,bf)]+comm.scratch,
        compiler_params=pltpu.CompilerParams(collective_id=cid,has_side_effects=True,vmem_limit_bytes=60<<20),name="scatter_grads")(gq,go,gkv,sums,o,wo,hidden,down,tokens,cotangent,scale,dnormed)

def prologue_kernel(nz,comms,*refs):
    tok_ref,cos_ref,sin_ref,wq_ref,wo_ref,wkv_ref,gain_ref,bias_ref=refs[:8]
    q_out,o_out,small_out,normed_out,ain_out,min_out,kv_out,wkv_out=refs[8:16]
    qo_own,kvg_own,qo_full,kvg_full,ksend,krecv=refs[16:22]
    pos=coords(nz); z,x,y,c=pos
    greet(pos,[f"z{k}" for k in range(1,nz)]+["x","y","c"],nz)
    rows=wq_ref.shape[0]
    kvg_own[:,:128]=wkv_ref[...]
    kvg_own[:,128:]=jnp.concatenate([gain_ref[...].astype(f32),bias_ref[...].astype(f32),jnp.zeros((rows,124),f32)],axis=1).astype(bf)
    g,b=comms
    ga=g.build(pos,(kvg_own,),(kvg_full,),refs[22:25])
    gb=b.build(pos,(qo_own,),(qo_full,),refs[25:28])
    ga[0]()
    wq=wq_ref[...].astype(f32); wo=wo_ref[...].astype(f32)
    qo_own[:,:128]=wq[:,:128].astype(bf)
    qo_own[:,128:256]=jnp.concatenate([wq[:,128:],wo[:,:64]],axis=1).astype(bf)
    qo_own[:,256:]=wo[:,64:].astype(bf)
    gb[0]()
    nb,own,width=tok_ref.shape
    def norm(k):
        s,r=k//4,(k%4)*(own//4)
        v=tok_ref[s,r:r+own//4,:].astype(f32)
        v=v-jnp.mean(v,axis=1,keepdims=True)
        normed_out[s*own+r:s*own+r+own//4,:]=v*lax.rsqrt(jnp.mean(v*v,axis=1,keepdims=True)+epsilon)
    sa=[s for _,s in ga[1]]; sb=[s for _,s in gb[1]]
    todo=[functools.partial(norm,k) for k in range(4*nb)]
    while sa:
        sa.pop(0)()
        if sb: sb.pop(0)()
        if todo: todo.pop(0)()
    for t in todo: t()
    ga[2]()
    kvg=kvg_full[...].reshape(width,256)
    small=kvg[:,128:].astype(f32).T
    small_out[...]=small[:8]
    wkv=kvg[:,:128]
    wkv_out[...]=wkv
    def copy(s,m,src,kind,n):
        return pltpu.make_async_remote_copy(src,kv_out.at[s,m],ksend.at[n],krecv.at[s,m],device_id=peer(pos,kind,nz),device_id_type=MESH)
    copies=[]
    me=y*2+c
    for s in range(nb):
        normed=normed_out[s*own:s*own+own,:]
        ain=(normed*small[0:1]+small[2:3]).astype(bf)
        ain_out[s*own:s*own+own,:]=ain
        kv=turn(dg(ain,wkv,NN),cos_ref[...],sin_ref[...],False,True)
        kv_out[s,me]=kv.astype(bf)
        for kind in ("y","c"):
            cp=copy(s,me,kv_out.at[s,me],kind,len(copies)); cp.start(); copies.append(cp)
        min_out[s*own:s*own+own,:]=(normed*small[1:2]+small[3:4]).astype(bf)
        for _ in range(6):
            if sb: sb.pop(0)()
    other=(1-y)*2+c
    for s in range(nb):
        copy(s,other,kv_out.at[s,other],"c",0).wait_recv()
        cp=copy(s,other,kv_out.at[s,other],"c",len(copies)); cp.start(); copies.append(cp)
    for s in sb: s()
    gb[2]()
    lane=lax.broadcasted_iota(jnp.int32,(rows,128),1)<64
    def unpack(d,carry):
        def tile(m,k): return qo_full[d,:,384*m+128*k:384*m+128*k+128].astype(f32)
        for ref,place in ((q_out,[(0,0),(0,1),(1,0)]),(o_out,[(1,1),(2,0),(2,1)])):
            for j in range(ref.shape[2]//128):
                (m0,(k0,h0)),(m1,(k1,h1))=[(h//3,place[h%3]) for h in (2*j,2*j+1)]
                ref[d,:,128*j:128*j+128]=halves(tile(m0,k0),h0,tile(m1,k1),h1,lane).astype(bf)
        return carry
    lax.fori_loop(0,q_out.shape[0],unpack,0)
    for s in range(nb):
        for m in (y*2+1-c,(1-y)*2+1-c): copy(s,m,kv_out.at[s,m],"c",0).wait_recv()
    for cp in copies: cp.wait_send()

def prologue(tokens,cos,sin,wq,wo,wkv,gains,biases,dp,mp,cid):
    nb,own,width=tokens.shape; part,cols=wq.shape
    kvg=jax.ShapeDtypeStruct((part,256),bf); qo=jax.ShapeDtypeStruct((part,2*cols),bf)
    comms=(Gather([kvg],[(0,0,256,"zx")],dp,mp),Gather([qo],[(0,0,256,"zyx"),(0,256,384,"xzy")],dp,mp))
    vm=pl.BlockSpec(memory_space=pltpu.VMEM)
    s=lambda *a: jax.ShapeDtypeStruct(a,bf)
    return pl.pallas_call(functools.partial(prologue_kernel,dp//2,comms),
        in_specs=[vm]*8,out_specs=[vm]*8,
        out_shape=[s(dp,part,width),s(dp,part,width),jax.ShapeDtypeStruct((8,width),f32),jax.ShapeDtypeStruct((nb*own,width),f32),s(nb*own,width),s(nb*own,width),s(nb,mp,own,128),s(width,128)],
        scratch_shapes=[pltpu.VMEM(qo.shape,bf),pltpu.VMEM(kvg.shape,bf),pltpu.VMEM((dp,part,mp*2*cols),bf),pltpu.VMEM((dp,part,256),bf),
                        pltpu.SemaphoreType.DMA((3*nb,)),pltpu.SemaphoreType.DMA((nb,mp))]+comms[0].scratch+comms[1].scratch,
        compiler_params=pltpu.CompilerParams(collective_id=cid,has_side_effects=True,vmem_limit_bytes=60<<20),name="gather_weights")(tokens,cos,sin,wq,wo,wkv,gains,biases)

NT=(((1,),(1,)),((),()))
NN=(((1,),(0,)),((),()))
def dg(a,b,dn): return lax.dot_general(a,b,dn,preferred_element_type=f32)
B=512
def turn(v,cos,sin,back,keys_only=False):
    lane=lax.broadcasted_iota(jnp.int32,v.shape,1)
    other=jnp.where(lane%HD<ROT//2,-pltpu.roll(v,128-ROT//2,1),pltpu.roll(v,ROT//2,1))*sin
    w=v*cos-other if back else v*cos+other
    return jnp.where(lane<HD,w,v) if keys_only else w

def attn_kernel(nz,pairs,comm,nc,*refs):
    q_ref,do_ref,kv_ref,cos_ref,sin_ref=refs[:5]
    cin=refs[5:5+nc]
    o_ref,dq_ref,dkv_ref=refs[5+nc:8+nc]
    cout=refs[8+nc:8+2*nc]
    k2,v2,kvt,acck,accv,ps,mk,ms,ls,ots,dqs=refs[8+2*nc:19+2*nc]
    rb=lax.axis_index("mp")
    nkb=kv_ref.shape[1]//B
    slots=[[] for _ in range(pairs*2*nkb)]
    if comm:
        pos=coords(nz)
        greet(pos,[f"z{k}" for k in range(1,nz)]+["x","y","c"],nz)
        begin,steps,end=comm.build(pos,cin,cout,refs[19+2*nc:])
        begin()
        for when,s in steps: slots[int((comm.late+(1-comm.late)*when)*len(slots))].append(s)
    def between(pair,kb,base):
        for p in range(pairs):
            todo=[k for k in range(nkb) if slots[(2*p+base)*nkb+k]]
            if not todo: continue
            @pl.when(pair==p)
            def _(p=p,todo=todo):
                for k in todo:
                    @pl.when(kb==k)
                    def _(k=k):
                        for s in slots[(2*p+base)*nkb+k]: s()
    for kb in range(nkb):
        kv=kv_ref[0,kb*B:(kb+1)*B,:].astype(f32)
        rolled=pltpu.roll(kv,64,1)
        lane=lax.broadcasted_iota(jnp.int32,kv.shape,1)<64
        k2[kb]=jnp.where(lane,kv,rolled).astype(bf)
        v2[kb]=jnp.where(lane,rolled,kv).astype(bf)
        kvt[kb]=kv.T.astype(bf)
    acck[...]=jnp.zeros_like(acck); accv[...]=jnp.zeros_like(accv)
    def one(pair,carry):
        cols=pl.ds(pl.multiple_of(pair*128,128),128)
        q=(turn(q_ref[:,cols],cos_ref[...],sin_ref[...],False)*HD**-0.5).astype(bf); do=do_ref[:,cols]
        lane=lax.broadcasted_iota(jnp.int32,q.shape,1)<64
        zero=jnp.zeros_like(q)
        qm=(jnp.where(lane,q,zero),jnp.where(lane,zero,q))
        dom=(jnp.where(lane,do,zero),jnp.where(lane,zero,do))
        ms[...]=jnp.full_like(ms,-1e30); ls[...]=jnp.zeros_like(ls)
        ots[...]=jnp.zeros_like(ots); dqs[...]=jnp.zeros_like(dqs)
        H=range(2)
        def fwd(kb,masked):
            ss=[dg(k2[kb],qm[h],NT) for h in H]
            if masked:
                ki=lax.broadcasted_iota(jnp.int32,(B,B),0); ri=lax.broadcasted_iota(jnp.int32,(B,B),1)
                ss=[jnp.where(ki<=ri,v,-1e30) for v in ss]
            mo=[ms[h] for h in H]
            mn=[jnp.maximum(mo[h],jnp.max(ss[h],axis=0,keepdims=True)) for h in H]
            al=[jnp.exp(mo[h]-mn[h]) for h in H]
            pp=[jnp.exp(ss[h]-mn[h]) for h in H]
            for h in H: ls[h]=ls[h]*al[h]+jnp.sum(pp[h],axis=0,keepdims=True)
            pb=[v.astype(bf) for v in pp]
            for h in H:
                ps[h,kb]=pb[h]
                mk[h,kb]=mn[h]
                ms[h]=mn[h]
            ob=[dg(kvt[kb,64:,:],pb[h],NN) for h in H]
            for h in H: ots[h]=ots[h]*al[h]+ob[h]
        def fstep(kb,carry):
            @pl.when(kb<rb)
            def _(): fwd(kb,False)
            @pl.when(kb==rb)
            def _(): fwd(kb,True)
            between(pair,kb,0)
            return carry
        lax.fori_loop(0,nkb,fstep,0)
        dot_=do.astype(f32).T
        for h in range(2):
            inv=1.0/ls[h]
            ot=ots[h]*inv
            ots[h]=ot
            ls[h]=inv
        delta=[jnp.sum(ots[h]*dot_[64*h:64*h+64,:],axis=0,keepdims=True) for h in range(2)]
        o_ref[:,cols]=jnp.concatenate([ots[0],ots[1]],axis=0).T.astype(bf)
        def bwd(kb):
            dps=[dg(v2[kb],dom[h],NT) for h in H]
            al=[jnp.exp(mk[h,kb]-ms[h])*ls[h] for h in H]
            pp=[ps[h,kb].astype(f32)*al[h] for h in H]
            ds=[(pp[h]*(dps[h]-delta[h])).astype(bf) for h in H]
            pn=[v.astype(bf) for v in pp]
            acck[kb]+=dg(ds[0],qm[0],NN)+dg(ds[1],qm[1],NN)
            accv[kb]+=dg(pn[0],dom[0],NN)+dg(pn[1],dom[1],NN)
            qb=[dg(kvt[kb,:64,:],ds[h],NN) for h in H]
            for h in H: dqs[h]+=qb[h]
        def bstep(kb,carry):
            @pl.when(kb<=rb)
            def _(): bwd(kb)
            between(pair,kb,1)
            return carry
        lax.fori_loop(0,nkb,bstep,0)
        dq_ref[:,cols]=(turn(jnp.concatenate([dqs[0],dqs[1]],axis=0).T,cos_ref[...],sin_ref[...],True)*HD**-0.5).astype(bf)
        return carry
    lax.fori_loop(0,pairs,one,0)
    for kb in range(nkb):
        k=acck[kb]; v=accv[kb]
        lane=lax.broadcasted_iota(jnp.int32,k.shape,1)<64
        dkv_ref[0,kb*B:(kb+1)*B,:]=jnp.where(lane,k+pltpu.roll(k,64,1),v+pltpu.roll(v,64,1))
    if comm: end()

def attention(b,q,do,kv,cos,sin,comm,arrays,dp,cid):
    S=kv.shape[1]; nkb=S//B; width=q.shape[1]
    blk=pl.BlockSpec((B,width),lambda *_: (b,0))
    own=pl.BlockSpec((B,width),lambda *_: (0,0))
    kvs=pl.BlockSpec((1,S,128),lambda *_: (b,0,0))
    dkvs=pl.BlockSpec((1,S,128),lambda *_: (0,0,0))
    tabs=pl.BlockSpec(cos.shape,lambda *_: (0,0))
    params=dict(vmem_limit_bytes=62<<20)
    if comm: params.update(collective_id=cid,has_side_effects=True)
    return pl.pallas_call(functools.partial(attn_kernel,dp//2,width//128,comm,len(arrays)),
      grid_spec=pltpu.PrefetchScalarGridSpec(num_scalar_prefetch=0,grid=(1,),in_specs=[blk,blk,kvs,tabs,tabs]+(comm.ins if comm else []),
        out_specs=[own,own,dkvs]+(comm.outs if comm else []),
        scratch_shapes=[pltpu.VMEM((nkb,B,128),bf),pltpu.VMEM((nkb,B,128),bf),pltpu.VMEM((nkb,128,B),bf),pltpu.VMEM((nkb,B,128),f32),pltpu.VMEM((nkb,B,128),f32),
                        pltpu.VMEM((2,nkb,B,B),bf),pltpu.VMEM((2,nkb,1,B),f32),pltpu.VMEM((2,1,B),f32),pltpu.VMEM((2,1,B),f32),pltpu.VMEM((2,64,B),f32),pltpu.VMEM((2,64,B),f32)]
                       +(comm.scratch if comm else [])),
      out_shape=[jax.ShapeDtypeStruct((B,width),bf),jax.ShapeDtypeStruct((B,width),bf),jax.ShapeDtypeStruct((1,S,128),f32)]+(comm.shapes if comm else []),
      compiler_params=pltpu.CompilerParams(**params),name="attn")(q,do,kv,cos,sin,*arrays)


def kv_gather_kernel(nz, own_ref, full_ref, send, recv):
    pos = coords(nz)
    z, x, y, c = pos
    greet(pos, ["y", "c"], nz)
    nb = own_ref.shape[0]
    sent = []

    def go(b, m, src, kind):
        cp = pltpu.make_async_remote_copy(src, full_ref.at[b, m], send.at[len(sent)], recv.at[b, m],
                                          device_id=peer(pos, kind, nz), device_id_type=MESH)
        cp.start()
        sent.append(cp)

    def wait(b, m):
        pltpu.make_async_remote_copy(full_ref.at[b, m], full_ref.at[b, m], send.at[0], recv.at[b, m],
                                     device_id=peer(pos, "c", nz), device_id_type=MESH).wait_recv()

    for b in range(nb):
        go(b, y * 2 + c, own_ref.at[b], "y")
    for b in range(nb):
        go(b, y * 2 + c, own_ref.at[b], "c")
    for b in range(nb):
        full_ref[b, y * 2 + c] = own_ref[b]
    for b in range(nb):
        m = (1 - y) * 2 + c
        wait(b, m)
        go(b, m, full_ref.at[b, m], "c")
    for b in range(nb):
        wait(b, y * 2 + 1 - c)
        wait(b, (1 - y) * 2 + 1 - c)
    for cp in sent:
        cp.wait_send()


def kv_gather(own, dp, cid):
    nb, rows, w = own.shape
    return pl.pallas_call(
        functools.partial(kv_gather_kernel, dp // 2),
        in_specs=[pl.BlockSpec(memory_space=pltpu.VMEM)],
        out_specs=pl.BlockSpec(memory_space=pltpu.VMEM),
        out_shape=jax.ShapeDtypeStruct((nb, 4, rows, w), own.dtype),
        scratch_shapes=[pltpu.SemaphoreType.DMA((3 * nb,)), pltpu.SemaphoreType.DMA((nb, 4))],
        compiler_params=pltpu.CompilerParams(collective_id=cid, has_side_effects=True),
        name="gather_keyval",
    )(own)


def kv_reduce_kernel(nz, n, *refs):
    parts = refs[:n]
    cos_ref, sin_ref, out_ref, low, cbuf, ybuf, ysend, send, crecv, yrecv = refs[n:]
    pos = coords(nz)
    z, x, y, c = pos
    greet(pos, ["y", "c"], nz)
    sent = []

    def go(src, dst, sem, kind):
        cp = pltpu.make_async_remote_copy(src, dst, send.at[len(sent)], sem, device_id=peer(pos, kind, nz), device_id_type=MESH)
        cp.start()
        sent.append(cp)

    def wait(dst, sem):
        pltpu.make_async_remote_copy(dst, dst, send.at[0], sem, device_id=peer(pos, "c", nz), device_id_type=MESH).wait_recv()

    for ry in (1, 0):
        yy = 1 - y if ry else y
        for b in range(n):
            low[b, ry] = parts[b][yy * 2 + 1 - c].astype(bf)
            go(low.at[b, ry], cbuf.at[b, ry], crecv.at[b, ry], "c")
    for b in range(n):
        wait(cbuf.at[b, 1], crecv.at[b, 1])
        ysend[b] = (parts[b][(1 - y) * 2 + c] + cbuf[b, 1].astype(f32)).astype(bf)
        go(ysend.at[b], ybuf.at[b], yrecv.at[b], "y")
    for b in range(n):
        wait(cbuf.at[b, 0], crecv.at[b, 0])
        wait(ybuf.at[b], yrecv.at[b])
        v = parts[b][y * 2 + c] + cbuf[b, 0].astype(f32) + ybuf[b].astype(f32)
        out_ref[b] = turn(v, cos_ref[...], sin_ref[...], True, True).astype(bf)
    for cp in sent:
        cp.wait_send()


def kv_reduce(parts, cos, sin, dp, cid):
    nb = len(parts)
    mp, rows, w = parts[0].shape
    vm = pl.BlockSpec(memory_space=pltpu.VMEM)
    return pl.pallas_call(
        functools.partial(kv_reduce_kernel, dp // 2, nb),
        in_specs=[vm] * (nb + 2),
        out_specs=vm,
        out_shape=jax.ShapeDtypeStruct((nb, rows, w), bf),
        scratch_shapes=[pltpu.VMEM((nb, 2, rows, w), bf), pltpu.VMEM((nb, 2, rows, w), bf), pltpu.VMEM((nb, rows, w), bf),
                        pltpu.VMEM((nb, rows, w), bf), pltpu.SemaphoreType.DMA((3 * nb,)), pltpu.SemaphoreType.DMA((nb, 2)), pltpu.SemaphoreType.DMA((nb,))],
        compiler_params=pltpu.CompilerParams(collective_id=cid, has_side_effects=True),
        name="reduce_keyval",
    )(*parts, cos, sin)


def spread(arrays, inside, dp, mp):
    out = []
    for i, s in enumerate(arrays):
        if i in inside:
            out.append(lax.all_gather(s, "dp"))
        else:
            a = lax.all_gather(s, ("dp", "mp")).reshape((dp, mp) + s.shape)
            out.append(a.transpose(0, 2, 1, 3).reshape(dp, s.shape[0], -1))
    return out


def collect(parts, inside, dp, mp):
    out = []
    for i, p in enumerate(parts):
        p = p.astype(f32)
        if i in inside:
            out.append(lax.psum(lax.psum_scatter(p, "dp", scatter_dimension=0), "mp"))
        else:
            a = p.reshape(dp, p.shape[1], mp, -1).transpose(0, 2, 1, 3).reshape(dp * mp, p.shape[1], -1)
            out.append(lax.psum_scatter(a, ("dp", "mp"), scatter_dimension=0))
    return out


def rotary(position):
    lane = jnp.arange(2 * HD, dtype=jnp.int32)
    inside = lane % HD
    frequency = 10000.0 ** (-2.0 * (inside % (ROT // 2)).astype(f32) / ROT)
    angle = position[:, None].astype(f32) * frequency[None, :]
    turned = (inside < ROT)[None, :]
    return jnp.where(turned, jnp.cos(angle), 1.0), jnp.where(turned, jnp.sin(angle), 0.0)


def plain_prologue(tokens, cos, sin, wq, wo, wkv, gains, biases, dp, mp):
    nb, own, width = tokens.shape
    wq, wo, kvg = spread([wq, wo, jnp.concatenate([wkv, gains, biases], axis=1)], {2}, dp, mp)
    kvg = kvg.reshape(width, -1)
    small = kvg[:, 2 * HD :].astype(f32).T
    x = tokens.reshape(nb * own, width).astype(f32)
    centered = x - jnp.mean(x, axis=1, keepdims=True)
    normed = centered * lax.rsqrt(jnp.mean(centered * centered, axis=1, keepdims=True) + epsilon)
    ain = (normed * small[0] + small[2]).astype(bf)
    mlp_in = (normed * small[1] + small[3]).astype(bf)
    kv = jnp.dot(ain, kvg[:, : 2 * HD], preferred_element_type=f32).reshape(nb, own, 2 * HD)
    first, half = jnp.arange(2 * HD) < HD, ROT // 2
    other = jnp.where(jnp.arange(2 * HD) < half, -jnp.roll(kv, -half, axis=2), jnp.roll(kv, half, axis=2)) * sin
    kv = jnp.where(first, kv * cos + other, kv).astype(bf)
    return wq, wo, jnp.concatenate([small, small]), normed, ain, mlp_in, kv_gather(kv, dp, 3), kvg[:, : 2 * HD]


def shards(tokens, norm_gains, norm_biases, w_query, w_keyval, w_output, w_up, w_down, cotangent, subset_ids, subset_weights):
    dp, mp = lax.axis_size("dp"), lax.axis_size("mp")
    me = lax.axis_index("mp")
    nb, own, width = tokens.shape
    rows = nb * own
    part, cols = w_query.shape
    ff = w_up.shape[1]
    mine = dp == 8
    dot = functools.partial(jnp.dot, preferred_element_type=f32)
    nt = lambda a, b: lax.dot_general(a, b, (((1,), (1,)), ((), ())), preferred_element_type=f32)
    tn = lambda a, b: lax.dot_general(a, b, (((0,), (0,)), ((), ())), preferred_element_type=f32)
    cos, sin = rotary(me * own + jnp.arange(own, dtype=jnp.int32))
    small_weights = (w_query, w_output, w_keyval, norm_gains, norm_biases)
    if mine:
        wq, wo, small, normed, attn_in, mlp_in, kv, wkv = prologue(tokens, cos, sin, *small_weights, dp, mp, 1)
    else:
        wq, wo, small, normed, attn_in, mlp_in, kv, wkv = plain_prologue(tokens, cos, sin, *small_weights, dp, mp)
    wq, wo = wq.reshape(width, width), wo.reshape(width, width)
    kv_full = kv.reshape(nb, mp * own, 2 * HD)
    gain_a, gain_m = small[0], small[1]

    ids = lax.dynamic_slice_in_dim(subset_ids.reshape(nb, mp * own), me * own, own, 1).reshape(rows)
    matches = ids[:, None] == jnp.arange(subset_weights.shape[0], dtype=jnp.int32)[None, :]
    scale = jnp.sum(jnp.where(matches, subset_weights[None, :], 0.0), axis=1, keepdims=True)
    g = (cotangent.reshape(rows, width).astype(f32) * scale).astype(bf)

    q = dot(attn_in, wq)
    grad_heads = dot(g, wo).astype(bf)
    mlp_plan = lambda a, b: [(0, 0, 768, a), (1, 0, 256, a), (1, 256, 768, b)]
    if mine:
        o0, dq0, dkv0, up, down = attention(0, q, grad_heads, kv_full, cos, sin, Gather([w_up, w_down], mlp_plan("zyx", "xzy"), dp, mp), [w_up, w_down], dp, 5)
    else:
        o0, dq0, dkv0 = attention(0, q, grad_heads, kv_full, cos, sin, None, [], dp, 5)
        up, down = spread([w_up, w_down], (), dp, mp)
    up = up.reshape(width, mp * ff)
    down = down.reshape(width, mp * ff)

    pre = dot(mlp_in, up)
    cdf = 0.5 * (1.0 + lax.erf(pre * sqrt_half))
    hidden = (pre * cdf).astype(bf)
    slope = cdf + pre * (jnp.exp(-0.5 * pre * pre) * inv_sqrt_two_pi)
    dpre = (dot(g, down) * slope).astype(bf)
    gup = tn(mlp_in, dpre).astype(bf).reshape(dp, part, mp * ff)
    gdown = tn(g, hidden).astype(bf).reshape(dp, part, mp * ff)
    if mine:
        o1, dq1, dkv1, grad_up, grad_down = attention(1, q, grad_heads, kv_full, cos, sin, Scatter([gup, gdown], mlp_plan("xyz", "yzx"), dp, mp), [gup, gdown], dp, 6)
    else:
        o1, dq1, dkv1 = attention(1, q, grad_heads, kv_full, cos, sin, None, [], dp, 6)
        grad_up, grad_down = collect([gup, gdown], (), dp, mp)
    dkvp = kv_reduce([d.reshape(mp, own, 2 * HD) for d in (dkv0, dkv1)], cos, sin, dp, 4).reshape(rows, 2 * HD)
    o = jnp.concatenate([o0, o1])
    dqp = jnp.concatenate([dq0, dq1])

    dmlp = nt(dpre, up)
    dattn = nt(dqp, wq) + nt(dkvp, wkv)
    dnormed = dattn * gain_a + dmlp * gain_m
    sums = [jnp.sum(dattn * normed, axis=0), jnp.sum(dmlp * normed, axis=0), jnp.sum(dattn, axis=0), jnp.sum(dmlp, axis=0)]
    gq = tn(attn_in, dqp).astype(bf).reshape(dp, part, width)
    go = tn(g, o).astype(bf).reshape(dp, part, width)
    gkv = tn(attn_in, dkvp).reshape(dp, part, 2 * HD)
    k = 2 * HD
    if mine:
        sums = jnp.concatenate([s[None] for s in sums] + [jnp.zeros((4, width), f32)])
        flat = lambda a: a.reshape(rows, width)
        a, c, out, input_grad = scatter_small(gq, go, gkv, sums, o, wo, hidden, down, flat(tokens), flat(cotangent), scale, dnormed, dp, mp, 2)
        grad_query, grad_output = a[:, :cols], a[:, cols:]
    else:
        x = tokens.reshape(rows, width).astype(f32)
        out = (x + nt(o, wo) + nt(hidden, down)).astype(bf)
        centered = x - jnp.mean(x, axis=1, keepdims=True)
        inverse = lax.rsqrt(jnp.mean(centered * centered, axis=1, keepdims=True) + epsilon)
        dx = (dnormed - jnp.mean(dnormed, axis=1, keepdims=True) - normed * jnp.mean(dnormed * normed, axis=1, keepdims=True)) * inverse
        input_grad = (cotangent.reshape(rows, width).astype(f32) * scale + dx).astype(bf)
        gkvg = jnp.concatenate([gkv, jnp.stack(sums, axis=1).reshape(dp, part, 4)], axis=2)
        grad_query, grad_output, c = collect([gq, go, gkvg], {2}, dp, mp)
    return (
        out.reshape(tokens.shape),
        kv_full.reshape(-1, 2 * HD),
        input_grad.reshape(tokens.shape),
        c[:, k : k + 2],
        c[:, k + 2 : k + 4],
        grad_query,
        c[:, :k],
        grad_output,
        grad_up,
        grad_down,
    )


def solution(mesh):
    rows = P(None, ("dp", "mp"), None)
    d, dm = P("dp", None), P("dp", "mp")
    return jax.shard_map(
        shards,
        mesh=mesh,
        in_specs=(rows, d, d, dm, d, dm, dm, dm, rows, P("dp"), P()),
        out_specs=(rows, d, rows, d, d, dm, d, dm, dm, dm),
        check_vma=False,
    )
```

```python
import functools

import jax
import jax.numpy as jnp
from jax import lax
from jax.experimental import pallas as pl
from jax.experimental.pallas import tpu as pltpu
from jax.sharding import PartitionSpec as P

f32 = jnp.float32
bf = jnp.bfloat16
MESH = pl.DeviceIdType.MESH
HD = 64
ROT = 16
B = 512
SEQ_LEN = 2048
epsilon = 1e-05
sqrt_half = 0.7071067811865476
inv_sqrt_two_pi = 0.3989422804014327


def coords(nz):
    d=lax.axis_index("dp"); m=lax.axis_index("mp")
    return d//2, d%2, m//2, m%2

def peer(pos,kind,nz):
    z,x,y,c=pos
    if kind[0]=="z": z=lax.rem(z+int(kind[1:]),nz)
    if kind=="x": x=1-x
    if kind=="y": y=1-y
    if kind=="c": c=1-c
    return (z*2+x, y*2+c)

def greet(pos,kinds,nz):
    bar=pltpu.get_barrier_semaphore()
    for k in kinds:
        pl.semaphore_signal(bar,inc=1,device_id=peer(pos,k,nz),device_id_type=MESH)
    pl.semaphore_wait(bar,len(kinds))

def gather_routes(order,nz):
    zs=[f"z{k}" for k in range(1,nz)]
    out=[]
    if order=="zyx":
        out.append(((0,0,0),zs+["y","x","c"]))
        out+=[((k,0,0),["y","x","c"]) for k in range(1,nz)]
        out+=[((k,0,1),["x","c"]) for k in range(nz)]
        out+=[((k,1,r),["c"]) for r in (0,1) for k in range(nz)]
    elif order=="xzy":
        out.append(((0,0,0),["x"]+zs+["y","c"]))
        out.append(((0,1,0),zs+["y","c"]))
        out+=[((k,r,0),["y","c"]) for k in range(1,nz) for r in (0,1)]
        out+=[((k,r,1),["c"]) for k in range(nz) for r in (0,1)]
    elif order=="zx":
        out.append(((0,0,0),zs+["x"]))
        out+=[((k,0,0),["x"]) for k in range(1,nz)]
        out+=[((k,1,0),[]) for k in range(nz)]
    return out

def columns(m,w,lo,hi):
    return pl.ds(pl.multiple_of(m*w+lo,128),hi-lo)

class Gather:
    late=0.45
    def __init__(self,shards,plan,dp,mp):
        self.plan=plan; self.nz=dp//2; self.mp=mp; self.dp=dp
        inside={i for i,_,_,o in plan if o=="zx"}
        self.ins=[pl.BlockSpec(memory_space=pltpu.VMEM)]*len(shards)
        self.outs=[pl.BlockSpec(memory_space=pl.ANY)]*len(shards)
        self.shapes=[jax.ShapeDtypeStruct((dp,s.shape[0],s.shape[1]*(1 if i in inside else mp)),s.dtype) for i,s in enumerate(shards)]
        sends=sum(len(f) for _,_,_,o in plan for _,f in gather_routes(o,self.nz))
        self.scratch=[pltpu.SemaphoreType.DMA((sends,)),pltpu.SemaphoreType.DMA((len(plan),mp,dp)),pltpu.SemaphoreType.DMA((len(shards),))]
    def build(self,pos,shards,full,scr):
        send,recv,local=scr
        nz=self.nz; z,x,y,c=pos
        routes=[gather_routes(o,nz) for _,_,_,o in self.plan]
        sent=[]
        def where(p,rel,other):
            i,lo,hi,order=self.plan[p]; k,rx,ry=rel
            zz=lax.rem(z+nz-k,nz); xx=1-x if rx else x; yy=1-y if ry else y
            d=zz*2+xx; m=yy*2+(1-c if other else c)
            if order=="zx": return full[i].at[d,:,lo:hi],recv.at[p,0,d]
            return full[i].at[d,:,columns(m,shards[i].shape[1],lo,hi)],recv.at[p,m,d]
        def arrived(p,rel,other):
            dst,sem=where(p,rel,other)
            pltpu.make_async_remote_copy(dst,dst,send.at[0],sem,device_id=peer(pos,"c",nz),device_id_type=MESH).wait_recv()
        def copy(p,rel,f,own,n):
            i,lo,hi,_=self.plan[p]
            dst,sem=where(p,rel,False)
            src=shards[i].at[:,lo:hi] if own else dst
            return pltpu.make_async_remote_copy(src,dst,send.at[n],sem,device_id=peer(pos,f,nz),device_id_type=MESH)
        def step(p,s):
            rel,fw=routes[p][s]
            base=len(sent)
            cps=[functools.partial(copy,p,rel,f,s==0,base+j) for j,f in enumerate(fw)]
            sent.extend(cps)
            def go():
                if s: arrived(p,rel,False)
                for cp in cps: cp().start()
            return go
        def mine(i):
            order=[o for j,_,_,o in self.plan if j==i][0]
            d=z*2+x; w=shards[i].shape[1]
            dst=full[i].at[d] if order=="zx" else full[i].at[d,:,columns(y*2+c,w,0,w)]
            return pltpu.make_async_copy(shards[i],dst,local.at[i])
        first=[step(p,0) for p in range(len(self.plan))]
        steps=[]
        longest=max(len(r) for r in routes)
        for s in range(1,longest):
            for p,r in enumerate(routes):
                if s<len(r): steps.append(((s-1)/(longest-1),step(p,s)))
        def begin():
            for g in first: g()
            for i in range(len(shards)): mine(i).start()
        def end():
            for p,r in enumerate(routes):
                if self.plan[p][3]=="zx": continue
                for rel,_ in r: arrived(p,rel,True)
            for cp in sent: cp().wait_send()
            for i in range(len(shards)): mine(i).wait()
        return begin,steps,end

class Scatter:
    late=0.0
    def __init__(self,parts,plan,dp,mp):
        self.plan=plan; nz=self.nz=dp//2; self.mp=mp
        self.width=[]
        for i,p in enumerate(parts):
            inside=[o for j,_,_,o in plan if j==i][0]=="xz"
            self.width.append(p.shape[-1]//(1 if inside else mp))
        self.ins=[pl.BlockSpec(memory_space=pltpu.VMEM)]*len(parts)
        self.outs=[pl.BlockSpec(memory_space=pltpu.VMEM)]*len(parts)
        self.shapes=[jax.ShapeDtypeStruct((p.shape[1],w),f32) for p,w in zip(parts,self.width)]
        scr=[]; sends=0
        for i,lo,hi,order in plan:
            rows=parts[i].shape[1]; w=hi-lo
            b=lambda k: pltpu.VMEM((k,rows,w),bf)
            nb=nz*4 if order!="xz" else nz*2
            scr+=[b(nb),b(nb)]
            if order=="xyz": scr+=[b(nz*2),b(nz),b(nz)]; sends+=nb+2*nz+nz+nz-1
            elif order=="yzx": scr+=[b(1),b(nz*2),b(nz*2)]; sends+=nb+2*nz+2*(nz-1)+1
            else: scr+=[b(nz*2),b(nz),b(2*nz)]; sends+=nb+nz+nz+nz-1
        n=len(plan)
        self.scratch=scr+[pltpu.SemaphoreType.DMA((sends,)),pltpu.SemaphoreType.DMA((n,4*nz)),pltpu.SemaphoreType.DMA((n,2*nz)),pltpu.SemaphoreType.DMA((n,2*nz)),pltpu.SemaphoreType.DMA((n,2*nz))]
    def build(self,pos,parts,outs,scr):
        plan=self.plan; nz=self.nz; z,x,y,c=pos; n=len(plan)
        per=scr[:5*n]; send,csem,xsem,ysem,zsem=scr[5*n:]
        sent=[]; begins=[]; steps=[]; ends=[]
        def sender(src,dst,rsem,kind):
            k=len(sent)
            cp=lambda: pltpu.make_async_remote_copy(src(),dst,send.at[k],rsem,device_id=peer(pos,kind,nz),device_id_type=MESH)
            sent.append(cp)
            return lambda: cp().start()
        def wait(dst,rsem):
            pltpu.make_async_remote_copy(dst,dst,send.at[0],rsem,device_id=peer(pos,"c",nz),device_id_type=MESH).wait_recv()
        def part(p,r,cc):
            i,lo,hi,order=plan[p]
            rz,rx,ry=r
            zz=lax.rem(z+rz,nz); xx=1-x if rx else x; yy=1-y if ry else y
            if order=="xz": return parts[i].at[zz*2+xx,:,lo:hi]
            return parts[i].at[zz*2+xx,:,columns(yy*2+cc,self.width[i],lo,hi)]
        def add(first,*others):
            v=first[...].astype(f32)
            for o in others: v=v+o[...].astype(f32)
            return v
        down=range(nz-1,-1,-1)
        for p,(i,lo,hi,order) in enumerate(plan):
            acc,cb,xb,yb,zb=per[5*p:5*p+5]
            if order=="xyz": seq=[(k,1,r) for r in (1,0) for k in down]+[(k,0,1) for k in down]+[(k,0,0) for k in down]
            elif order=="yzx": seq=[(k,r,1) for r in (1,0) for k in down]+[(k,1,0) for k in down]+[(k,0,0) for k in down]
            else: seq=[(k,1,0) for k in down]+[(k,0,0) for k in down]
            slot=(lambda r: (r[0]*2+r[1])*2+r[2]) if order!="xz" else (lambda r: r[0]*2+r[1])
            A=lambda r,acc=acc,slot=slot: acc.at[slot(r)]
            def plus(when,p=p):
                def note(f): steps.append((when,f))
                return note
            for t,r in enumerate(seq):
                s=slot(r); rz,rx,ry=r
                begins.append((t,sender(functools.partial(part,p,r,c if order=="xz" else 1-c),cb.at[s],csem.at[p,s],"c")))
                go=None
                if order in ("xyz","xz") and rx: go=sender(lambda v=A(r): v,xb.at[rz*2+ry],xsem.at[p,rz*2+ry],"x")
                if order=="yzx" and ry: go=sender(lambda v=A(r): v,yb.at[rz*2+rx],ysem.at[p,rz*2+rx],"y")
                @plus(0.22*t/len(seq))
                def _(p=p,r=r,s=s,acc=acc,cb=cb,go=go):
                    wait(cb.at[s],csem.at[p,s])
                    acc[s]=add(part(p,r,c),cb.at[s]).astype(bf)
                    if go: go()
            if order=="xyz":
                for n_,k in enumerate(down):
                    r=(k,0,1); j=k*2+1
                    go=sender(lambda v=A(r): v,yb.at[k],ysem.at[p,k],"y")
                    @plus(0.24+0.26*n_/nz)
                    def _(p=p,r=r,j=j,A=A,xb=xb,go=go):
                        wait(xb.at[j],xsem.at[p,j]); A(r)[...]=add(A(r),xb.at[j]).astype(bf)
                        go()
                for n_,k in enumerate(down):
                    r=(k,0,0); j=k*2
                    go=sender(lambda v=A(r): v,zb.at[k],zsem.at[p,k],f"z{k}") if k else None
                    @plus(0.52+0.26*n_/nz)
                    def _(p=p,r=r,j=j,k=k,A=A,xb=xb,yb=yb,go=go):
                        wait(xb.at[j],xsem.at[p,j]); wait(yb.at[k],ysem.at[p,k])
                        if go:
                            A(r)[...]=add(A(r),xb.at[j],yb.at[k]).astype(bf)
                            go()
                def fin(p=p,i=i,lo=lo,hi=hi,A=A,xb=xb,yb=yb,zb=zb):
                    for k in range(1,nz): wait(zb.at[k],zsem.at[p,k])
                    outs[i][:,lo:hi]=add(A((0,0,0)),xb.at[0],yb.at[0],*[zb.at[k] for k in range(1,nz)])
                ends.append(fin)
            elif order=="yzx":
                for n_,(rx,k) in enumerate([(rx,k) for rx in (1,0) for k in range(nz-1,0,-1)]):
                    r=(k,rx,0); j=k*2+rx
                    go=sender(lambda v=A(r): v,zb.at[k*2+rx],zsem.at[p,k*2+rx],f"z{k}")
                    @plus(0.24+0.3*n_/(2*nz-2))
                    def _(p=p,r=r,j=j,A=A,yb=yb,go=go):
                        wait(yb.at[j],ysem.at[p,j]); A(r)[...]=add(A(r),yb.at[j]).astype(bf)
                        go()
                r=(0,1,0)
                go=sender(lambda v=A(r): v,xb.at[0],xsem.at[p,0],"x")
                @plus(0.8)
                def _(p=p,r=r,A=A,yb=yb,zb=zb,go=go):
                    wait(yb.at[1],ysem.at[p,1])
                    for k in range(1,nz): wait(zb.at[k*2+1],zsem.at[p,k*2+1])
                    A(r)[...]=add(A(r),yb.at[1],*[zb.at[k*2+1] for k in range(1,nz)]).astype(bf)
                    go()
                def fin(p=p,i=i,lo=lo,hi=hi,A=A,xb=xb,yb=yb,zb=zb):
                    wait(yb.at[0],ysem.at[p,0])
                    for k in range(1,nz): wait(zb.at[k*2],zsem.at[p,k*2])
                    wait(xb.at[0],xsem.at[p,0])
                    outs[i][:,lo:hi]=add(A((0,0,0)),yb.at[0],xb.at[0],*[zb.at[k*2] for k in range(1,nz)])
                ends.append(fin)
            else:
                for n_,k in enumerate(down):
                    r=(k,0,0)
                    go=sender(lambda v=A(r): v,yb.at[k],ysem.at[p,k],"y")
                    @plus(0.24+0.26*n_/nz)
                    def _(p=p,r=r,k=k,A=A,xb=xb,go=go):
                        wait(xb.at[k*2],xsem.at[p,k*2]); A(r)[...]=add(A(r),xb.at[k*2]).astype(bf)
                        go()
                for n_,k in enumerate(range(nz-1,0,-1)):
                    go=sender(lambda v=zb.at[k]: v,zb.at[nz+k],zsem.at[p,k],f"z{k}")
                    @plus(0.52+0.26*n_/nz)
                    def _(p=p,k=k,A=A,yb=yb,zb=zb,go=go):
                        wait(yb.at[k],ysem.at[p,k]); zb[k]=add(A((k,0,0)),yb.at[k]).astype(bf)
                        go()
                def fin(p=p,i=i,lo=lo,hi=hi,A=A,yb=yb,zb=zb):
                    wait(yb.at[0],ysem.at[p,0])
                    for k in range(1,nz): wait(zb.at[nz+k],zsem.at[p,k])
                    outs[i][:,lo:hi]=add(A((0,0,0)),yb.at[0],*[zb.at[nz+k] for k in range(1,nz)])
                ends.append(fin)
        begins.sort(key=lambda e: e[0])
        steps.sort(key=lambda e: e[0])
        def begin():
            for _,g in begins: g()
        def end():
            for f in ends: f()
            for cp in sent: cp().wait_send()
        return begin,steps,end

def scatter_kernel(nz,comm,*refs):
    gq_ref,go_ref,gkv_ref,sums_ref,o_ref,wo_ref,hid_ref,down_ref,tok_ref,cot_ref,scale_ref,dn_ref=refs[:12]
    a_ref,c_ref,out_ref,ig_ref,qo,kvg=refs[12:18]
    pos=coords(nz)
    greet(pos,[f"z{k}" for k in range(1,nz)]+["x","y","c"],nz)
    rows=gq_ref.shape[1]
    lane=lax.broadcasted_iota(jnp.int32,(rows,128),1)<64
    def tile(ref,d,h): return ref[d,:,128*(h//2):128*(h//2)+128].astype(f32)
    def pack(d,carry):
        for t in range(qo.shape[2]//128):
            m,k=t//3,t%3
            lo,hi=[((gq_ref,3*m),(gq_ref,3*m+1)),((gq_ref,3*m+2),(go_ref,3*m)),((go_ref,3*m+1),(go_ref,3*m+2))][k]
            qo[d,:,128*t:128*t+128]=halves(tile(lo[0],d,lo[1]),lo[1]%2,tile(hi[0],d,hi[1]),hi[1]%2,lane).astype(bf)
        return carry
    lax.fori_loop(0,qo.shape[0],pack,0)
    s=jnp.concatenate([sums_ref[...],jnp.zeros((120,sums_ref.shape[1]),f32)],axis=0).T
    for d in range(kvg.shape[0]):
        kvg[d,:,:128]=gkv_ref[d].astype(bf)
        kvg[d,:,128:]=s[rows*d:rows*d+rows].astype(bf)
    begin,steps,end=comm.build(pos,(qo,kvg),(a_ref,c_ref),refs[18:])
    begin()
    T=256; across=out_ref.shape[1]//T; n=out_ref.shape[0]//T*across
    slots=[[] for _ in range(n)]
    for when,s in steps:
        if when<0.23: s()
        else: slots[min(n-1,int(n*(0.33+(when-0.24)*1.15)))].append(s)
    def chunk(it,carry):
        rows=pl.ds(pl.multiple_of(it//across*T,T),T); cols=pl.ds(pl.multiple_of(it%across*T,T),T)
        @pl.when(it%across==0)
        def _():
            v=tok_ref[rows,:].astype(f32)
            v=v-jnp.mean(v,axis=1,keepdims=True)
            inverse=lax.rsqrt(jnp.mean(v*v,axis=1,keepdims=True)+epsilon)
            v=v*inverse
            dn=dn_ref[rows,:]
            dx=(dn-jnp.mean(dn,axis=1,keepdims=True)-v*jnp.mean(dn*v,axis=1,keepdims=True))*inverse
            ig_ref[rows,:]=(cot_ref[rows,:].astype(f32)*scale_ref[rows,:]+dx).astype(bf)
        y=tok_ref[rows,cols].astype(f32)+dg(o_ref[rows,:],wo_ref[cols,:],NT)+dg(hid_ref[rows,:],down_ref[cols,:],NT)
        out_ref[rows,cols]=y.astype(bf)
        for k in range(n):
            if slots[k]:
                @pl.when(it==k)
                def _(k=k):
                    for s in slots[k]: s()
        return carry
    lax.fori_loop(0,n,chunk,0)
    end()

def halves(lo,lo_at,hi,hi_at,lane):
    if lo_at: lo=pltpu.roll(lo,64,1)
    if not hi_at: hi=pltpu.roll(hi,64,1)
    return jnp.where(lane,lo,hi)

def scatter_small(gq,go,gkv,sums,o,wo,hidden,down,tokens,cotangent,scale,dnormed,dp,mp,cid):
    shape=lambda w: jax.ShapeDtypeStruct((dp,gq.shape[1],w),bf)
    qo,kvg=shape(2*gq.shape[2]),shape(256)
    comm=Scatter([qo,kvg],[(1,0,256,"xz"),(0,0,256,"xyz"),(0,256,384,"yzx")],dp,mp)
    vm=pl.BlockSpec(memory_space=pltpu.VMEM)
    return pl.pallas_call(functools.partial(scatter_kernel,comm.nz,comm),
        in_specs=[vm]*12,out_specs=comm.outs+[vm]*2,out_shape=comm.shapes+[jax.ShapeDtypeStruct(o.shape,bf)]*2,
        scratch_shapes=[pltpu.VMEM(qo.shape,bf),pltpu.VMEM(kvg.shape,bf)]+comm.scratch,
        compiler_params=pltpu.CompilerParams(collective_id=cid,has_side_effects=True,vmem_limit_bytes=60<<20),name="scatter_grads")(gq,go,gkv,sums,o,wo,hidden,down,tokens,cotangent,scale,dnormed)

def prologue_kernel(nz,comms,*refs):
    tok_ref,cos_ref,sin_ref,wq_ref,wo_ref,wkv_ref,gain_ref,bias_ref=refs[:8]
    q_out,o_out,small_out,normed_out,ain_out,min_out,kv_out,wkv_out=refs[8:16]
    qo_own,kvg_own,qo_full,kvg_full,ksend,krecv=refs[16:22]
    pos=coords(nz); z,x,y,c=pos
    greet(pos,[f"z{k}" for k in range(1,nz)]+["x","y","c"],nz)
    rows=wq_ref.shape[0]
    kvg_own[:,:128]=wkv_ref[...]
    kvg_own[:,128:]=jnp.concatenate([gain_ref[...].astype(f32),bias_ref[...].astype(f32),jnp.zeros((124,rows),f32)],axis=0).T.astype(bf)
    g,b=comms
    ga=g.build(pos,(kvg_own,),(kvg_full,),refs[22:25])
    gb=b.build(pos,(qo_own,),(qo_full,),refs[25:28])
    ga[0]()
    wq=wq_ref[...].astype(f32); wo=wo_ref[...].astype(f32)
    qo_own[:,:128]=wq[:,:128].astype(bf)
    qo_own[:,128:256]=jnp.concatenate([wq[:,128:],wo[:,:64]],axis=1).astype(bf)
    qo_own[:,256:]=wo[:,64:].astype(bf)
    gb[0]()
    nb,own,width=tok_ref.shape
    part=own//4
    def norm(k,carry):
        v=tok_ref[k//4,pl.ds(pl.multiple_of(k%4*part,part),part),:].astype(f32)
        v=v-jnp.mean(v,axis=1,keepdims=True)
        normed_out[pl.ds(pl.multiple_of(k*part,part),part),:]=v*lax.rsqrt(jnp.mean(v*v,axis=1,keepdims=True)+epsilon)
        return carry
    lax.fori_loop(0,4*nb,norm,0)
    sa=[s for _,s in ga[1]]; sb=[s for _,s in gb[1]]
    while sa:
        sa.pop(0)()
        if sb: sb.pop(0)()
    ga[2]()
    kvg=kvg_full[...].reshape(width,256)
    small=kvg[:,128:].astype(f32).T
    small_out[...]=small[:8]
    wkv=kvg[:,:128]
    wkv_out[...]=wkv
    def copy(s,m,src,kind,n):
        return pltpu.make_async_remote_copy(src,kv_out.at[s,m],ksend.at[n],krecv.at[s,m],device_id=peer(pos,kind,nz),device_id_type=MESH)
    copies=[]
    me=y*2+c
    for s in range(nb):
        normed=normed_out[s*own:s*own+own,:]
        ain=(normed*small[0:1]+small[2:3]).astype(bf)
        ain_out[s*own:s*own+own,:]=ain
        kv=turn(dg(ain,wkv,NN),cos_ref[...],sin_ref[...],False,True)
        kv_out[s,me]=kv.astype(bf)
        for kind in ("y","c"):
            cp=copy(s,me,kv_out.at[s,me],kind,len(copies)); cp.start(); copies.append(cp)
        min_out[s*own:s*own+own,:]=(normed*small[1:2]+small[3:4]).astype(bf)
        for _ in range(6):
            if sb: sb.pop(0)()
    other=(1-y)*2+c
    for s in range(nb):
        copy(s,other,kv_out.at[s,other],"c",0).wait_recv()
        cp=copy(s,other,kv_out.at[s,other],"c",len(copies)); cp.start(); copies.append(cp)
    for s in sb: s()
    gb[2]()
    lane=lax.broadcasted_iota(jnp.int32,(rows,128),1)<64
    def unpack(d,carry):
        def tile(m,k): return qo_full[d,:,384*m+128*k:384*m+128*k+128].astype(f32)
        for ref,place in ((q_out,[(0,0),(0,1),(1,0)]),(o_out,[(1,1),(2,0),(2,1)])):
            for j in range(ref.shape[2]//128):
                (m0,(k0,h0)),(m1,(k1,h1))=[(h//3,place[h%3]) for h in (2*j,2*j+1)]
                ref[d,:,128*j:128*j+128]=halves(tile(m0,k0),h0,tile(m1,k1),h1,lane).astype(bf)
        return carry
    lax.fori_loop(0,q_out.shape[0],unpack,0)
    for s in range(nb):
        for m in (y*2+1-c,(1-y)*2+1-c): copy(s,m,kv_out.at[s,m],"c",0).wait_recv()
    for cp in copies: cp.wait_send()

def prologue(tokens,cos,sin,wq,wo,wkv,gains,biases,dp,mp,cid):
    nb,own,width=tokens.shape; part,cols=wq.shape
    kvg=jax.ShapeDtypeStruct((part,256),bf); qo=jax.ShapeDtypeStruct((part,2*cols),bf)
    comms=(Gather([kvg],[(0,0,256,"zx")],dp,mp),Gather([qo],[(0,0,256,"zyx"),(0,256,384,"xzy")],dp,mp))
    vm=pl.BlockSpec(memory_space=pltpu.VMEM)
    s=lambda *a: jax.ShapeDtypeStruct(a,bf)
    return pl.pallas_call(functools.partial(prologue_kernel,dp//2,comms),
        in_specs=[vm]*8,out_specs=[vm]*8,
        out_shape=[s(dp,part,width),s(dp,part,width),jax.ShapeDtypeStruct((8,width),f32),jax.ShapeDtypeStruct((nb*own,width),f32),s(nb*own,width),s(nb*own,width),s(nb,mp,own,128),s(width,128)],
        scratch_shapes=[pltpu.VMEM(qo.shape,bf),pltpu.VMEM(kvg.shape,bf),pltpu.VMEM((dp,part,mp*2*cols),bf),pltpu.VMEM((dp,part,256),bf),
                        pltpu.SemaphoreType.DMA((3*nb,)),pltpu.SemaphoreType.DMA((nb,mp))]+comms[0].scratch+comms[1].scratch,
        compiler_params=pltpu.CompilerParams(collective_id=cid,has_side_effects=True,vmem_limit_bytes=60<<20),name="gather_weights")(tokens,cos,sin,wq,wo,wkv,gains.T,biases.T)

NT=(((1,),(1,)),((),()))
NN=(((1,),(0,)),((),()))
def dg(a,b,dn): return lax.dot_general(a,b,dn,preferred_element_type=f32)
def turn(v,cos,sin,back,keys_only=False):
    lane=lax.broadcasted_iota(jnp.int32,v.shape,1)
    other=jnp.where(lane%HD<ROT//2,-pltpu.roll(v,128-ROT//2,1),pltpu.roll(v,ROT//2,1))*sin
    w=v*cos-other if back else v*cos+other
    return jnp.where(lane<HD,w,v) if keys_only else w

class Fold:
    scratch=[pltpu.VMEM((2,2,B,128),bf),pltpu.VMEM((2,2,B,128),bf),pltpu.VMEM((2,B,128),bf),pltpu.VMEM((2,B,128),bf),
             pltpu.SemaphoreType.DMA((6,)),pltpu.SemaphoreType.DMA((2,2)),pltpu.SemaphoreType.DMA((2,))]
    def __init__(self,pos,nz,out,cos,sin,scr):
        self.pos=pos; self.nz=nz; self.out=out; self.cos=cos; self.sin=sin; self.scr=scr
    def copy(self,b,n,src,dst,sem,kind):
        return pltpu.make_async_remote_copy(src,dst,self.scr[4].at[3*b+n],sem,device_id=peer(self.pos,kind,self.nz),device_id_type=MESH)
    def across(self,b,ry):
        low,cbuf=self.scr[:2]
        return self.copy(b,ry,low.at[b,ry],cbuf.at[b,ry],self.scr[5].at[b,ry],"c")
    def far(self,b):
        _,_,ybuf,ysend=self.scr[:4]
        return self.copy(b,2,ysend.at[b],ybuf.at[b],self.scr[6].at[b],"y")
    def one(self,b,part):
        _,_,y,c=self.pos
        for ry in (1,0):
            self.scr[0][b,ry]=part((1-y if ry else y)*2+1-c).astype(bf)
            self.across(b,ry).start()
    def two(self,b,part):
        _,_,y,c=self.pos
        self.across(b,1).wait_recv()
        self.scr[3][b]=(part((1-y)*2+c)+self.scr[1][b,1].astype(f32)).astype(bf)
        self.far(b).start()
    def three(self,b,part):
        _,_,y,c=self.pos
        self.across(b,0).wait_recv(); self.far(b).wait_recv()
        v=part(y*2+c)+self.scr[1][b,0].astype(f32)+self.scr[2][b].astype(f32)
        self.out[b]=turn(v,self.cos[...],self.sin[...],True,True).astype(bf)
        self.across(b,1).wait_send(); self.across(b,0).wait_send(); self.far(b).wait_send()

def attn_kernel(nz,pairs,comm,join,nc,*refs):
    q_ref,do_ref,kv_ref,cos_ref,sin_ref=refs[:5]
    refs=refs[5:]
    if join: prev,refs=refs[:3],refs[3:]
    cin=refs[:nc]
    o_ref,dq_ref,dkv_ref=refs[nc:3+nc]
    cout=refs[3+nc:3+2*nc]
    k2,v2,kvt,acck,accv,ps,mk,ms,ls,ots,dqs=refs[3+2*nc:14+2*nc]
    refs=refs[14+2*nc:]
    rb=lax.axis_index("mp")
    nkb=kv_ref.shape[1]//B
    at=0
    if join:
        dkvs,local,fold,refs=refs[0],refs[1],refs[2:9],refs[9:]
        at=B
        part0=lambda m: prev[2][0,pl.ds(pl.multiple_of(m*B,B),B),:]
        part1=lambda m: dkvs[m]
    own=slice(at,at+B)
    slots=[[] for _ in range(pairs*2*nkb)]
    if comm:
        pos=coords(nz)
        greet(pos,[f"z{k}" for k in range(1,nz)]+["x","y","c"],nz)
        begin,steps,end=comm.build(pos,cin,cout,refs)
        begin()
        for when,s in steps: slots[int((comm.late+(1-comm.late)*when)*len(slots))].append(s)
        if join:
            sums=Fold(pos,nz,dkv_ref,cos_ref,sin_ref,fold)
            sums.one(0,part0)
            slots[len(slots)//6].append(lambda: sums.two(0,part0))
            slots[len(slots)//2].append(lambda: sums.three(0,part0))
            before=[pltpu.make_async_copy(prev[k],r.at[:B],local.at[k]) for k,r in enumerate((o_ref,dq_ref))]
            for cp in before: cp.start()
    def between(pair,kb,base):
        for p in range(pairs):
            todo=[k for k in range(nkb) if slots[(2*p+base)*nkb+k]]
            if not todo: continue
            @pl.when(pair==p)
            def _(p=p,todo=todo):
                for k in todo:
                    @pl.when(kb==k)
                    def _(k=k):
                        for s in slots[(2*p+base)*nkb+k]: s()
    lane=lax.broadcasted_iota(jnp.int32,(B,128),1)<64
    def setup(kb,carry):
        kv=kv_ref[0,pl.ds(pl.multiple_of(kb*B,B),B),:].astype(f32)
        rolled=pltpu.roll(kv,64,1)
        k2[kb]=jnp.where(lane,kv,rolled).astype(bf)
        v2[kb]=jnp.where(lane,rolled,kv).astype(bf)
        kvt[kb]=kv.T.astype(bf)
        acck[kb]=jnp.zeros((B,128),f32); accv[kb]=jnp.zeros((B,128),f32)
        return carry
    lax.fori_loop(0,nkb,setup,0)
    def one(pair,carry):
        cols=pl.ds(pl.multiple_of(pair*128,128),128)
        q=(turn(q_ref[:,cols],cos_ref[...],sin_ref[...],False)*HD**-0.5).astype(bf); do=do_ref[:,cols]
        zero=jnp.zeros_like(q)
        qm=(jnp.where(lane,q,zero),jnp.where(lane,zero,q))
        dom=(jnp.where(lane,do,zero),jnp.where(lane,zero,do))
        ms[...]=jnp.full_like(ms,-1e30); ls[...]=jnp.zeros_like(ls)
        ots[...]=jnp.zeros_like(ots); dqs[...]=jnp.zeros_like(dqs)
        H=range(2)
        def fwd(kb,masked):
            ss=[dg(k2[kb],qm[h],NT) for h in H]
            if masked:
                ki=lax.broadcasted_iota(jnp.int32,(B,B),0); ri=lax.broadcasted_iota(jnp.int32,(B,B),1)
                ss=[jnp.where(ki<=ri,v,-1e30) for v in ss]
            mo=[ms[h] for h in H]
            mn=[jnp.maximum(mo[h],jnp.max(ss[h],axis=0,keepdims=True)) for h in H]
            al=[jnp.exp(mo[h]-mn[h]) for h in H]
            pp=[jnp.exp(ss[h]-mn[h]) for h in H]
            for h in H: ls[h]=ls[h]*al[h]+jnp.sum(pp[h],axis=0,keepdims=True)
            pb=[v.astype(bf) for v in pp]
            for h in H:
                ps[h,kb]=pb[h]
                mk[h,kb]=mn[h]
                ms[h]=mn[h]
            ob=[dg(kvt[kb,64:,:],pb[h],NN) for h in H]
            for h in H: ots[h]=ots[h]*al[h]+ob[h]
        def fstep(kb,carry):
            @pl.when(kb<rb)
            def _(): fwd(kb,False)
            @pl.when(kb==rb)
            def _(): fwd(kb,True)
            between(pair,kb,0)
            return carry
        lax.fori_loop(0,nkb,fstep,0)
        dot_=do.astype(f32).T
        for h in range(2):
            inv=1.0/ls[h]
            ot=ots[h]*inv
            ots[h]=ot
            ls[h]=inv
        delta=[jnp.sum(ots[h]*dot_[64*h:64*h+64,:],axis=0,keepdims=True) for h in range(2)]
        o_ref[own,cols]=jnp.concatenate([ots[0],ots[1]],axis=0).T.astype(bf)
        def bwd(kb):
            dps=[dg(v2[kb],dom[h],NT) for h in H]
            al=[jnp.exp(mk[h,kb]-ms[h])*ls[h] for h in H]
            pp=[ps[h,kb].astype(f32)*al[h] for h in H]
            ds=[(pp[h]*(dps[h]-delta[h])).astype(bf) for h in H]
            pn=[v.astype(bf) for v in pp]
            acck[kb]+=dg(ds[0],qm[0],NN)+dg(ds[1],qm[1],NN)
            accv[kb]+=dg(pn[0],dom[0],NN)+dg(pn[1],dom[1],NN)
            qb=[dg(kvt[kb,:64,:],ds[h],NN) for h in H]
            for h in H: dqs[h]+=qb[h]
        def bstep(kb,carry):
            @pl.when(kb<=rb)
            def _(): bwd(kb)
            between(pair,kb,1)
            return carry
        lax.fori_loop(0,nkb,bstep,0)
        dq_ref[own,cols]=(turn(jnp.concatenate([dqs[0],dqs[1]],axis=0).T,cos_ref[...],sin_ref[...],True)*HD**-0.5).astype(bf)
        return carry
    lax.fori_loop(0,pairs,one,0)
    def flush(kb,carry):
        k=acck[kb]; v=accv[kb]
        k=jnp.where(lane,k+pltpu.roll(k,64,1),v+pltpu.roll(v,64,1))
        if join: dkvs[kb]=k
        else: dkv_ref[0,pl.ds(pl.multiple_of(kb*B,B),B),:]=k
        return carry
    lax.fori_loop(0,nkb,flush,0)
    if join:
        sums.one(1,part1)
        sums.two(1,part1)
    if comm: end()
    if join:
        sums.three(1,part1)
        for cp in before: cp.wait()

def attention(b,q,do,kv,cos,sin,comm,arrays,dp,cid,prev=()):
    S=kv.shape[1]; nkb=S//B; width=q.shape[1]; join=len(prev)>0
    assert not join or (b==1 and nkb==4)
    whole=lambda *shape: pl.BlockSpec(shape,lambda *_: (0,)*len(shape))
    blk=pl.BlockSpec((B,width),lambda *_: (b,0))
    kvs=pl.BlockSpec((1,S,128),lambda *_: (b,0,0))
    hbm=pl.BlockSpec(memory_space=pl.ANY)
    rows=2*B if join else B
    kvout=jax.ShapeDtypeStruct((2,B,128),bf) if join else jax.ShapeDtypeStruct((1,S,128),f32)
    params=dict(vmem_limit_bytes=62<<20)
    if comm: params.update(collective_id=cid,has_side_effects=True)
    return pl.pallas_call(functools.partial(attn_kernel,dp//2,width//128,comm,join,len(arrays)),
      grid_spec=pltpu.PrefetchScalarGridSpec(num_scalar_prefetch=0,grid=(1,),
        in_specs=[blk,blk,kvs,whole(B,128),whole(B,128)]+([hbm,hbm,whole(1,S,128)] if join else [])+(comm.ins if comm else []),
        out_specs=[whole(rows,width),whole(rows,width),whole(*kvout.shape)]+(comm.outs if comm else []),
        scratch_shapes=[pltpu.VMEM((nkb,B,128),bf),pltpu.VMEM((nkb,B,128),bf),pltpu.VMEM((nkb,128,B),bf),pltpu.VMEM((nkb,B,128),f32),pltpu.VMEM((nkb,B,128),f32),
                        pltpu.VMEM((2,nkb,B,B),bf),pltpu.VMEM((2,nkb,1,B),f32),pltpu.VMEM((2,1,B),f32),pltpu.VMEM((2,1,B),f32),pltpu.VMEM((2,64,B),f32),pltpu.VMEM((2,64,B),f32)]
                       +([pltpu.VMEM((nkb,B,128),f32),pltpu.SemaphoreType.DMA((2,))]+Fold.scratch if join else [])
                       +(comm.scratch if comm else [])),
      out_shape=[jax.ShapeDtypeStruct((rows,width),bf),jax.ShapeDtypeStruct((rows,width),bf),kvout]+(comm.shapes if comm else []),
      compiler_params=pltpu.CompilerParams(**params),name="attn")(q,do,kv,cos,sin,*prev,*arrays)


def kv_gather_kernel(nz, own_ref, full_ref, send, recv):
    pos = coords(nz)
    z, x, y, c = pos
    greet(pos, ["y", "c"], nz)
    nb = own_ref.shape[0]
    sent = []

    def go(b, m, src, kind):
        cp = pltpu.make_async_remote_copy(src, full_ref.at[b, m], send.at[len(sent)], recv.at[b, m],
                                          device_id=peer(pos, kind, nz), device_id_type=MESH)
        cp.start()
        sent.append(cp)

    def wait(b, m):
        pltpu.make_async_remote_copy(full_ref.at[b, m], full_ref.at[b, m], send.at[0], recv.at[b, m],
                                     device_id=peer(pos, "c", nz), device_id_type=MESH).wait_recv()

    for b in range(nb):
        go(b, y * 2 + c, own_ref.at[b], "y")
    for b in range(nb):
        go(b, y * 2 + c, own_ref.at[b], "c")
    for b in range(nb):
        full_ref[b, y * 2 + c] = own_ref[b]
    for b in range(nb):
        m = (1 - y) * 2 + c
        wait(b, m)
        go(b, m, full_ref.at[b, m], "c")
    for b in range(nb):
        wait(b, y * 2 + 1 - c)
        wait(b, (1 - y) * 2 + 1 - c)
    for cp in sent:
        cp.wait_send()


def kv_gather(own, dp, cid):
    nb, rows, w = own.shape
    return pl.pallas_call(
        functools.partial(kv_gather_kernel, dp // 2),
        in_specs=[pl.BlockSpec(memory_space=pltpu.VMEM)],
        out_specs=pl.BlockSpec(memory_space=pltpu.VMEM),
        out_shape=jax.ShapeDtypeStruct((nb, 4, rows, w), own.dtype),
        scratch_shapes=[pltpu.SemaphoreType.DMA((3 * nb,)), pltpu.SemaphoreType.DMA((nb, 4))],
        compiler_params=pltpu.CompilerParams(collective_id=cid, has_side_effects=True),
        name="gather_keyval",
    )(own)


def kv_reduce_kernel(nz, n, *refs):
    parts = refs[:n]
    cos_ref, sin_ref, out_ref, low, cbuf, ybuf, ysend, send, crecv, yrecv = refs[n:]
    pos = coords(nz)
    z, x, y, c = pos
    greet(pos, ["y", "c"], nz)
    sent = []

    def go(src, dst, sem, kind):
        cp = pltpu.make_async_remote_copy(src, dst, send.at[len(sent)], sem, device_id=peer(pos, kind, nz), device_id_type=MESH)
        cp.start()
        sent.append(cp)

    def wait(dst, sem):
        pltpu.make_async_remote_copy(dst, dst, send.at[0], sem, device_id=peer(pos, "c", nz), device_id_type=MESH).wait_recv()

    for ry in (1, 0):
        yy = 1 - y if ry else y
        for b in range(n):
            low[b, ry] = parts[b][yy * 2 + 1 - c].astype(bf)
            go(low.at[b, ry], cbuf.at[b, ry], crecv.at[b, ry], "c")
    for b in range(n):
        wait(cbuf.at[b, 1], crecv.at[b, 1])
        ysend[b] = (parts[b][(1 - y) * 2 + c] + cbuf[b, 1].astype(f32)).astype(bf)
        go(ysend.at[b], ybuf.at[b], yrecv.at[b], "y")
    for b in range(n):
        wait(cbuf.at[b, 0], crecv.at[b, 0])
        wait(ybuf.at[b], yrecv.at[b])
        v = parts[b][y * 2 + c] + cbuf[b, 0].astype(f32) + ybuf[b].astype(f32)
        out_ref[b] = turn(v, cos_ref[...], sin_ref[...], True, True).astype(bf)
    for cp in sent:
        cp.wait_send()


def kv_reduce(parts, cos, sin, dp, cid):
    nb = len(parts)
    mp, rows, w = parts[0].shape
    vm = pl.BlockSpec(memory_space=pltpu.VMEM)
    return pl.pallas_call(
        functools.partial(kv_reduce_kernel, dp // 2, nb),
        in_specs=[vm] * (nb + 2),
        out_specs=vm,
        out_shape=jax.ShapeDtypeStruct((nb, rows, w), bf),
        scratch_shapes=[pltpu.VMEM((nb, 2, rows, w), bf), pltpu.VMEM((nb, 2, rows, w), bf), pltpu.VMEM((nb, rows, w), bf),
                        pltpu.VMEM((nb, rows, w), bf), pltpu.SemaphoreType.DMA((3 * nb,)), pltpu.SemaphoreType.DMA((nb, 2)), pltpu.SemaphoreType.DMA((nb,))],
        compiler_params=pltpu.CompilerParams(collective_id=cid, has_side_effects=True),
        name="reduce_keyval",
    )(*parts, cos, sin)


def spread(arrays, inside, dp, mp):
    out = []
    for i, s in enumerate(arrays):
        if i in inside:
            out.append(lax.all_gather(s, "dp"))
        else:
            a = lax.all_gather(s, ("dp", "mp")).reshape((dp, mp) + s.shape)
            out.append(a.transpose(0, 2, 1, 3).reshape(dp, s.shape[0], -1))
    return out


def collect(parts, inside, dp, mp):
    out = []
    for i, p in enumerate(parts):
        p = p.astype(f32)
        if i in inside:
            out.append(lax.psum(lax.psum_scatter(p, "dp", scatter_dimension=0), "mp"))
        else:
            a = p.reshape(dp, p.shape[1], mp, -1).transpose(0, 2, 1, 3).reshape(dp * mp, p.shape[1], -1)
            out.append(lax.psum_scatter(a, ("dp", "mp"), scatter_dimension=0))
    return out


def rotary(position):
    lane = jnp.arange(2 * HD, dtype=jnp.int32)
    inside = lane % HD
    frequency = 10000.0 ** (-2.0 * (inside % (ROT // 2)).astype(f32) / ROT)
    angle = position[:, None].astype(f32) * frequency[None, :]
    turned = (inside < ROT)[None, :]
    return jnp.where(turned, jnp.cos(angle), 1.0), jnp.where(turned, jnp.sin(angle), 0.0)


def plain_prologue(tokens, cos, sin, wq, wo, wkv, gains, biases, dp, mp):
    nb, own, width = tokens.shape
    wq, wo, kvg = spread([wq, wo, jnp.concatenate([wkv, gains, biases], axis=1)], {2}, dp, mp)
    kvg = kvg.reshape(width, -1)
    small = kvg[:, 2 * HD :].astype(f32).T
    x = tokens.reshape(nb * own, width).astype(f32)
    centered = x - jnp.mean(x, axis=1, keepdims=True)
    normed = centered * lax.rsqrt(jnp.mean(centered * centered, axis=1, keepdims=True) + epsilon)
    ain = (normed * small[0] + small[2]).astype(bf)
    mlp_in = (normed * small[1] + small[3]).astype(bf)
    kv = jnp.dot(ain, kvg[:, : 2 * HD], preferred_element_type=f32).reshape(nb, own, 2 * HD)
    first, half = jnp.arange(2 * HD) < HD, ROT // 2
    other = jnp.where(jnp.arange(2 * HD) < half, -jnp.roll(kv, -half, axis=2), jnp.roll(kv, half, axis=2)) * sin
    kv = jnp.where(first, kv * cos + other, kv).astype(bf)
    return wq, wo, jnp.concatenate([small, small]), normed, ain, mlp_in, kv_gather(kv, dp, 3), kvg[:, : 2 * HD]


def shards(tokens, norm_gains, norm_biases, w_query, w_keyval, w_output, w_up, w_down, cotangent, subset_ids, subset_weights):
    dp, mp = lax.axis_size("dp"), lax.axis_size("mp")
    me = lax.axis_index("mp")
    nb, own, width = tokens.shape
    rows = nb * own
    part, cols = w_query.shape
    ff = w_up.shape[1]
    mine = dp == 8
    dot = functools.partial(jnp.dot, preferred_element_type=f32)
    nt = lambda a, b: lax.dot_general(a, b, (((1,), (1,)), ((), ())), preferred_element_type=f32)
    tn = lambda a, b: lax.dot_general(a, b, (((0,), (0,)), ((), ())), preferred_element_type=f32)
    cos, sin = rotary(me * own + jnp.arange(own, dtype=jnp.int32))
    small_weights = (w_query, w_output, w_keyval, norm_gains, norm_biases)
    if mine:
        wq, wo, small, normed, attn_in, mlp_in, kv, wkv = prologue(tokens, cos, sin, *small_weights, dp, mp, 1)
    else:
        wq, wo, small, normed, attn_in, mlp_in, kv, wkv = plain_prologue(tokens, cos, sin, *small_weights, dp, mp)
    wq, wo = wq.reshape(width, width), wo.reshape(width, width)
    kv_full = kv.reshape(nb, mp * own, 2 * HD)
    gain_a, gain_m = small[0], small[1]

    ids = lax.dynamic_slice_in_dim(subset_ids.reshape(nb, mp * own), me * own, own, 1).reshape(rows)
    matches = ids[:, None] == jnp.arange(subset_weights.shape[0], dtype=jnp.int32)[None, :]
    scale = jnp.sum(jnp.where(matches, subset_weights[None, :], 0.0), axis=1, keepdims=True)
    g = (cotangent.reshape(rows, width).astype(f32) * scale).astype(bf)

    q = dot(attn_in, wq)
    grad_heads = dot(g, wo).astype(bf)
    mlp_plan = lambda a, b: [(0, 0, 768, a), (1, 0, 256, a), (1, 256, 768, b)]
    if mine:
        o0, dq0, dkv0, up, down = attention(0, q, grad_heads, kv_full, cos, sin, Gather([w_up, w_down], mlp_plan("zyx", "xzy"), dp, mp), [w_up, w_down], dp, 5)
    else:
        o0, dq0, dkv0 = attention(0, q, grad_heads, kv_full, cos, sin, None, [], dp, 5)
        up, down = spread([w_up, w_down], (), dp, mp)
    up = up.reshape(width, mp * ff)
    down = down.reshape(width, mp * ff)

    pre = dot(mlp_in, up)
    cdf = 0.5 * (1.0 + lax.erf(pre * sqrt_half))
    hidden = (pre * cdf).astype(bf)
    slope = cdf + pre * (jnp.exp(-0.5 * pre * pre) * inv_sqrt_two_pi)
    hidden, slope = lax.optimization_barrier((hidden, slope))
    dpre = (dot(g, down) * slope).astype(bf)
    gup = tn(mlp_in, dpre).astype(bf).reshape(dp, part, mp * ff)
    gdown = tn(g, hidden).astype(bf).reshape(dp, part, mp * ff)
    if mine:
        o, dqp, dkvp, grad_up, grad_down = attention(1, q, grad_heads, kv_full, cos, sin, Scatter([gup, gdown], mlp_plan("xyz", "yzx"), dp, mp), [gup, gdown], dp, 6, (o0, dq0, dkv0))
    else:
        o1, dq1, dkv1 = attention(1, q, grad_heads, kv_full, cos, sin, None, [], dp, 6)
        grad_up, grad_down = collect([gup, gdown], (), dp, mp)
        dkvp = kv_reduce([d.reshape(mp, own, 2 * HD) for d in (dkv0, dkv1)], cos, sin, dp, 4)
        o = jnp.concatenate([o0, o1])
        dqp = jnp.concatenate([dq0, dq1])
    dkvp = dkvp.reshape(rows, 2 * HD)

    dmlp = nt(dpre, up)
    dattn = nt(dqp, wq) + nt(dkvp, wkv)
    dnormed = dattn * gain_a + dmlp * gain_m
    sums = [jnp.sum(dattn * normed, axis=0), jnp.sum(dmlp * normed, axis=0), jnp.sum(dattn, axis=0), jnp.sum(dmlp, axis=0)]
    gq = tn(attn_in, dqp).astype(bf).reshape(dp, part, width)
    go = tn(g, o).astype(bf).reshape(dp, part, width)
    gkv = tn(attn_in, dkvp).reshape(dp, part, 2 * HD)
    k = 2 * HD
    if mine:
        sums = jnp.concatenate([s[None] for s in sums] + [jnp.zeros((4, width), f32)])
        flat = lambda a: a.reshape(rows, width)
        a, c, out, input_grad = scatter_small(gq, go, gkv, sums, o, wo, hidden, down, flat(tokens), flat(cotangent), scale, dnormed, dp, mp, 2)
        grad_query, grad_output = a[:, :cols], a[:, cols:]
    else:
        x = tokens.reshape(rows, width).astype(f32)
        out = (x + nt(o, wo) + nt(hidden, down)).astype(bf)
        centered = x - jnp.mean(x, axis=1, keepdims=True)
        inverse = lax.rsqrt(jnp.mean(centered * centered, axis=1, keepdims=True) + epsilon)
        dx = (dnormed - jnp.mean(dnormed, axis=1, keepdims=True) - normed * jnp.mean(dnormed * normed, axis=1, keepdims=True)) * inverse
        input_grad = (cotangent.reshape(rows, width).astype(f32) * scale + dx).astype(bf)
        gkvg = jnp.concatenate([gkv, jnp.stack(sums, axis=1).reshape(dp, part, 4)], axis=2)
        grad_query, grad_output, c = collect([gq, go, gkvg], {2}, dp, mp)
    return (
        out.reshape(tokens.shape),
        kv_full.reshape(-1, 2 * HD),
        input_grad.reshape(tokens.shape),
        c[:, k : k + 2],
        c[:, k + 2 : k + 4],
        grad_query,
        c[:, :k],
        grad_output,
        grad_up,
        grad_down,
    )


def solution(mesh):
    rows = P(None, ("dp", "mp"), None)
    d, dm = P("dp", None), P("dp", "mp")
    return jax.shard_map(
        shards,
        mesh=mesh,
        in_specs=(rows, d, d, dm, d, dm, dm, dm, rows, P("dp"), P()),
        out_specs=(rows, d, rows, d, d, dm, d, dm, dm, dm),
        check_vma=False,
    )
```

```python
import functools

import jax
import jax.numpy as jnp
from jax import lax
from jax.experimental import pallas as pl
from jax.experimental.pallas import tpu as pltpu
from jax.sharding import PartitionSpec as P

f32 = jnp.float32
bf = jnp.bfloat16
MESH = pl.DeviceIdType.MESH
HD = 64
ROT = 16
B = 512
SEQ_LEN = 2048
epsilon = 1e-05
sqrt_half = 0.7071067811865476
inv_sqrt_two_pi = 0.3989422804014327


def coords(nz):
    d=lax.axis_index("dp"); m=lax.axis_index("mp")
    return d//2, d%2, m//2, m%2

def peer(pos,kind,nz):
    z,x,y,c=pos
    if kind[0]=="z": z=lax.rem(z+int(kind[1:]),nz)
    if kind=="x": x=1-x
    if kind=="y": y=1-y
    if kind=="c": c=1-c
    return (z*2+x, y*2+c)

def greet(pos,kinds,nz):
    bar=pltpu.get_barrier_semaphore()
    for k in kinds:
        pl.semaphore_signal(bar,inc=1,device_id=peer(pos,k,nz),device_id_type=MESH)
    pl.semaphore_wait(bar,len(kinds))

def gather_routes(order,nz):
    zs=[f"z{k}" for k in range(1,nz)]
    out=[]
    if order=="zyx":
        out.append(((0,0,0),zs+["y","x","c"]))
        out+=[((k,0,0),["y","x","c"]) for k in range(1,nz)]
        out+=[((k,0,1),["x","c"]) for k in range(nz)]
        out+=[((k,1,r),["c"]) for r in (0,1) for k in range(nz)]
    elif order=="xzy":
        out.append(((0,0,0),["x"]+zs+["y","c"]))
        out.append(((0,1,0),zs+["y","c"]))
        out+=[((k,r,0),["y","c"]) for k in range(1,nz) for r in (0,1)]
        out+=[((k,r,1),["c"]) for k in range(nz) for r in (0,1)]
    elif order=="zx":
        out.append(((0,0,0),zs+["x"]))
        out+=[((k,0,0),["x"]) for k in range(1,nz)]
        out+=[((k,1,0),[]) for k in range(nz)]
    return out

def columns(m,w,lo,hi):
    return pl.ds(pl.multiple_of(m*w+lo,128),hi-lo)

class Gather:
    late=0.45
    def __init__(self,shards,plan,dp,mp):
        self.plan=plan; self.nz=dp//2; self.mp=mp; self.dp=dp
        inside={i for i,_,_,o in plan if o=="zx"}
        self.ins=[pl.BlockSpec(memory_space=pltpu.VMEM)]*len(shards)
        self.outs=[pl.BlockSpec(memory_space=pl.ANY)]*len(shards)
        self.shapes=[jax.ShapeDtypeStruct((dp,s.shape[0],s.shape[1]*(1 if i in inside else mp)),s.dtype) for i,s in enumerate(shards)]
        sends=sum(len(f) for _,_,_,o in plan for _,f in gather_routes(o,self.nz))
        self.scratch=[pltpu.SemaphoreType.DMA((sends,)),pltpu.SemaphoreType.DMA((len(plan),mp,dp)),pltpu.SemaphoreType.DMA((len(shards),))]
    def build(self,pos,shards,full,scr):
        send,recv,local=scr
        nz=self.nz; z,x,y,c=pos
        routes=[gather_routes(o,nz) for _,_,_,o in self.plan]
        sent=[]
        def where(p,rel,other):
            i,lo,hi,order=self.plan[p]; k,rx,ry=rel
            zz=lax.rem(z+nz-k,nz); xx=1-x if rx else x; yy=1-y if ry else y
            d=zz*2+xx; m=yy*2+(1-c if other else c)
            if order=="zx": return full[i].at[d,:,lo:hi],recv.at[p,0,d]
            return full[i].at[d,:,columns(m,shards[i].shape[1],lo,hi)],recv.at[p,m,d]
        def arrived(p,rel,other):
            dst,sem=where(p,rel,other)
            pltpu.make_async_remote_copy(dst,dst,send.at[0],sem,device_id=peer(pos,"c",nz),device_id_type=MESH).wait_recv()
        def copy(p,rel,f,own,n):
            i,lo,hi,_=self.plan[p]
            dst,sem=where(p,rel,False)
            src=shards[i].at[:,lo:hi] if own else dst
            return pltpu.make_async_remote_copy(src,dst,send.at[n],sem,device_id=peer(pos,f,nz),device_id_type=MESH)
        def step(p,s):
            rel,fw=routes[p][s]
            base=len(sent)
            cps=[functools.partial(copy,p,rel,f,s==0,base+j) for j,f in enumerate(fw)]
            sent.extend(cps)
            def go():
                if s: arrived(p,rel,False)
                for cp in cps: cp().start()
            return go
        def mine(i):
            order=[o for j,_,_,o in self.plan if j==i][0]
            d=z*2+x; w=shards[i].shape[1]
            dst=full[i].at[d] if order=="zx" else full[i].at[d,:,columns(y*2+c,w,0,w)]
            return pltpu.make_async_copy(shards[i],dst,local.at[i])
        first=[step(p,0) for p in range(len(self.plan))]
        steps=[]
        longest=max(len(r) for r in routes)
        for s in range(1,longest):
            for p,r in enumerate(routes):
                if s<len(r): steps.append(((s-1)/(longest-1),step(p,s)))
        def begin():
            for g in first: g()
            for i in range(len(shards)): mine(i).start()
        def end():
            for p,r in enumerate(routes):
                if self.plan[p][3]=="zx": continue
                for rel,_ in r: arrived(p,rel,True)
            for cp in sent: cp().wait_send()
            for i in range(len(shards)): mine(i).wait()
        return begin,steps,end

class Scatter:
    late=0.0
    def __init__(self,parts,plan,dp,mp):
        self.plan=plan; nz=self.nz=dp//2; self.mp=mp
        self.width=[]
        for i,p in enumerate(parts):
            inside=[o for j,_,_,o in plan if j==i][0]=="xz"
            self.width.append(p.shape[-1]//(1 if inside else mp))
        self.ins=[pl.BlockSpec(memory_space=pl.ANY)]*len(parts)
        self.outs=[pl.BlockSpec(memory_space=pltpu.VMEM)]*len(parts)
        self.shapes=[jax.ShapeDtypeStruct((p.shape[1],w),f32) for p,w in zip(parts,self.width)]
        scr=[]; sends=0
        for i,lo,hi,order in plan:
            rows=parts[i].shape[1]; w=hi-lo
            b=lambda k: pltpu.VMEM((k,rows,w),bf)
            nb=nz*4 if order!="xz" else nz*2
            scr+=[b(nb),b(nb)]
            if order=="xyz": scr+=[b(nz*2),b(nz),b(nz)]; sends+=nb+2*nz+nz+nz-1
            elif order=="yzx": scr+=[b(1),b(nz*2),b(nz*2)]; sends+=nb+2*nz+2*(nz-1)+1
            else: scr+=[b(nz*2),b(nz),b(2*nz)]; sends+=nb+nz+nz+nz-1
        n=len(plan)
        self.scratch=scr+[pltpu.SemaphoreType.DMA((n,4*nz)),pltpu.SemaphoreType.DMA((sends,)),pltpu.SemaphoreType.DMA((n,4*nz)),pltpu.SemaphoreType.DMA((n,2*nz)),pltpu.SemaphoreType.DMA((n,2*nz)),pltpu.SemaphoreType.DMA((n,2*nz))]
    def build(self,pos,parts,outs,scr):
        plan=self.plan; nz=self.nz; z,x,y,c=pos; n=len(plan)
        per=scr[:5*n]; own,send,csem,xsem,ysem,zsem=scr[5*n:]
        sent=[]; begins=[]; steps=[]; ends=[]
        def sender(src,dst,rsem,kind):
            k=len(sent)
            cp=lambda: pltpu.make_async_remote_copy(src(),dst,send.at[k],rsem,device_id=peer(pos,kind,nz),device_id_type=MESH)
            sent.append(cp)
            return lambda: cp().start()
        def wait(dst,rsem):
            pltpu.make_async_remote_copy(dst,dst,send.at[0],rsem,device_id=peer(pos,"c",nz),device_id_type=MESH).wait_recv()
        def part(p,r,cc):
            i,lo,hi,order=plan[p]
            rz,rx,ry=r
            zz=lax.rem(z+rz,nz); xx=1-x if rx else x; yy=1-y if ry else y
            if order=="xz": return parts[i].at[zz*2+xx,:,lo:hi]
            return parts[i].at[zz*2+xx,:,columns(yy*2+cc,self.width[i],lo,hi)]
        def add(first,*others):
            v=first[...].astype(f32)
            for o in others: v=v+o[...].astype(f32)
            return v
        down=range(nz-1,-1,-1)
        for p,(i,lo,hi,order) in enumerate(plan):
            acc,cb,xb,yb,zb=per[5*p:5*p+5]
            if order=="xyz": seq=[(k,1,r) for r in (1,0) for k in down]+[(k,0,1) for k in down]+[(k,0,0) for k in down]
            elif order=="yzx": seq=[(k,r,1) for r in (1,0) for k in down]+[(k,1,0) for k in down]+[(k,0,0) for k in down]
            else: seq=[(k,1,0) for k in down]+[(k,0,0) for k in down]
            slot=(lambda r: (r[0]*2+r[1])*2+r[2]) if order!="xz" else (lambda r: r[0]*2+r[1])
            A=lambda r,acc=acc,slot=slot: acc.at[slot(r)]
            def plus(when,p=p):
                def note(f): steps.append((when,f))
                return note
            for t,r in enumerate(seq):
                s=slot(r); rz,rx,ry=r
                begins.append((t,sender(functools.partial(part,p,r,c if order=="xz" else 1-c),cb.at[s],csem.at[p,s],"c")))
                mine=lambda p=p,r=r,s=s,acc=acc: pltpu.make_async_copy(part(p,r,c),acc.at[s],own.at[p,s])
                begins.append((t,lambda mine=mine: mine().start()))
                go=None
                if order in ("xyz","xz") and rx: go=sender(lambda v=A(r): v,xb.at[rz*2+ry],xsem.at[p,rz*2+ry],"x")
                if order=="yzx" and ry: go=sender(lambda v=A(r): v,yb.at[rz*2+rx],ysem.at[p,rz*2+rx],"y")
                @plus(0.22*t/len(seq))
                def _(p=p,s=s,acc=acc,cb=cb,go=go,mine=mine):
                    mine().wait()
                    wait(cb.at[s],csem.at[p,s])
                    acc[s]=add(acc.at[s],cb.at[s]).astype(bf)
                    if go: go()
            if order=="xyz":
                for n_,k in enumerate(down):
                    r=(k,0,1); j=k*2+1
                    go=sender(lambda v=A(r): v,yb.at[k],ysem.at[p,k],"y")
                    @plus(0.24+0.26*n_/nz)
                    def _(p=p,r=r,j=j,A=A,xb=xb,go=go):
                        wait(xb.at[j],xsem.at[p,j]); A(r)[...]=add(A(r),xb.at[j]).astype(bf)
                        go()
                for n_,k in enumerate(down):
                    r=(k,0,0); j=k*2
                    go=sender(lambda v=A(r): v,zb.at[k],zsem.at[p,k],f"z{k}") if k else None
                    @plus(0.52+0.26*n_/nz)
                    def _(p=p,r=r,j=j,k=k,A=A,xb=xb,yb=yb,go=go):
                        wait(xb.at[j],xsem.at[p,j]); wait(yb.at[k],ysem.at[p,k])
                        if go:
                            A(r)[...]=add(A(r),xb.at[j],yb.at[k]).astype(bf)
                            go()
                def fin(p=p,i=i,lo=lo,hi=hi,A=A,xb=xb,yb=yb,zb=zb):
                    for k in range(1,nz): wait(zb.at[k],zsem.at[p,k])
                    outs[i][:,lo:hi]=add(A((0,0,0)),xb.at[0],yb.at[0],*[zb.at[k] for k in range(1,nz)])
                ends.append(fin)
            elif order=="yzx":
                for n_,(rx,k) in enumerate([(rx,k) for rx in (1,0) for k in range(nz-1,0,-1)]):
                    r=(k,rx,0); j=k*2+rx
                    go=sender(lambda v=A(r): v,zb.at[k*2+rx],zsem.at[p,k*2+rx],f"z{k}")
                    @plus(0.24+0.3*n_/(2*nz-2))
                    def _(p=p,r=r,j=j,A=A,yb=yb,go=go):
                        wait(yb.at[j],ysem.at[p,j]); A(r)[...]=add(A(r),yb.at[j]).astype(bf)
                        go()
                r=(0,1,0)
                go=sender(lambda v=A(r): v,xb.at[0],xsem.at[p,0],"x")
                @plus(0.8)
                def _(p=p,r=r,A=A,yb=yb,zb=zb,go=go):
                    wait(yb.at[1],ysem.at[p,1])
                    for k in range(1,nz): wait(zb.at[k*2+1],zsem.at[p,k*2+1])
                    A(r)[...]=add(A(r),yb.at[1],*[zb.at[k*2+1] for k in range(1,nz)]).astype(bf)
                    go()
                def fin(p=p,i=i,lo=lo,hi=hi,A=A,xb=xb,yb=yb,zb=zb):
                    wait(yb.at[0],ysem.at[p,0])
                    for k in range(1,nz): wait(zb.at[k*2],zsem.at[p,k*2])
                    wait(xb.at[0],xsem.at[p,0])
                    outs[i][:,lo:hi]=add(A((0,0,0)),yb.at[0],xb.at[0],*[zb.at[k*2] for k in range(1,nz)])
                ends.append(fin)
            else:
                for n_,k in enumerate(down):
                    r=(k,0,0)
                    go=sender(lambda v=A(r): v,yb.at[k],ysem.at[p,k],"y")
                    @plus(0.24+0.26*n_/nz)
                    def _(p=p,r=r,k=k,A=A,xb=xb,go=go):
                        wait(xb.at[k*2],xsem.at[p,k*2]); A(r)[...]=add(A(r),xb.at[k*2]).astype(bf)
                        go()
                for n_,k in enumerate(range(nz-1,0,-1)):
                    go=sender(lambda v=zb.at[k]: v,zb.at[nz+k],zsem.at[p,k],f"z{k}")
                    @plus(0.52+0.26*n_/nz)
                    def _(p=p,k=k,A=A,yb=yb,zb=zb,go=go):
                        wait(yb.at[k],ysem.at[p,k]); zb[k]=add(A((k,0,0)),yb.at[k]).astype(bf)
                        go()
                def fin(p=p,i=i,lo=lo,hi=hi,A=A,yb=yb,zb=zb):
                    wait(yb.at[0],ysem.at[p,0])
                    for k in range(1,nz): wait(zb.at[nz+k],zsem.at[p,k])
                    outs[i][:,lo:hi]=add(A((0,0,0)),yb.at[0],*[zb.at[nz+k] for k in range(1,nz)])
                ends.append(fin)
        begins.sort(key=lambda e: e[0])
        steps.sort(key=lambda e: e[0])
        def begin():
            for _,g in begins: g()
        def end():
            for f in ends: f()
            for cp in sent: cp().wait_send()
        return begin,steps,end

def scatter_kernel(nz,comm,*refs):
    gq_ref,go_ref,gkv_ref,sums_ref,scale_ref=refs[:5]
    hosted=refs[5:12]
    a_ref,c_ref,out_ref,ig_ref,qo,kvg=refs[12:18]
    o_ref,wo_ref,hid_ref,down_ref,tok_ref,cot_ref,dn_ref=refs[18:25]
    fetch=[pltpu.make_async_copy(h,v,refs[25].at[k]) for k,(h,v) in enumerate(zip(hosted,refs[18:25]))]
    for f in fetch: f.start()
    pos=coords(nz)
    greet(pos,[f"z{k}" for k in range(1,nz)]+["x","y","c"],nz)
    rows=gq_ref.shape[1]
    lane=lax.broadcasted_iota(jnp.int32,(rows,128),1)<64
    def tile(ref,d,h): return ref[d,:,128*(h//2):128*(h//2)+128].astype(f32)
    def pack(d,carry):
        for t in range(qo.shape[2]//128):
            m,k=t//3,t%3
            lo,hi=[((gq_ref,3*m),(gq_ref,3*m+1)),((gq_ref,3*m+2),(go_ref,3*m)),((go_ref,3*m+1),(go_ref,3*m+2))][k]
            qo[d,:,128*t:128*t+128]=halves(tile(lo[0],d,lo[1]),lo[1]%2,tile(hi[0],d,hi[1]),hi[1]%2,lane).astype(bf)
        return carry
    lax.fori_loop(0,qo.shape[0],pack,0)
    s=jnp.concatenate([sums_ref[...],jnp.zeros((120,sums_ref.shape[1]),f32)],axis=0).T
    for d in range(kvg.shape[0]):
        kvg[d,:,:128]=gkv_ref[d].astype(bf)
        kvg[d,:,128:]=s[rows*d:rows*d+rows].astype(bf)
    begin,steps,end=comm.build(pos,(qo,kvg),(a_ref,c_ref),refs[26:])
    begin()
    T=256; across=out_ref.shape[1]//T; n=out_ref.shape[0]//T*across
    slots=[[] for _ in range(n)]
    for when,s in steps:
        if when<0.23: s()
        else: slots[min(n-1,int(n*(0.33+(when-0.24)*1.15)))].append(s)
    def chunk(it,carry):
        rows=pl.ds(pl.multiple_of(it//across*T,T),T); cols=pl.ds(pl.multiple_of(it%across*T,T),T)
        @pl.when(it%across==0)
        def _():
            v=tok_ref[rows,:].astype(f32)
            v=v-jnp.mean(v,axis=1,keepdims=True)
            inverse=lax.rsqrt(jnp.mean(v*v,axis=1,keepdims=True)+epsilon)
            v=v*inverse
            dn=dn_ref[rows,:]
            dx=(dn-jnp.mean(dn,axis=1,keepdims=True)-v*jnp.mean(dn*v,axis=1,keepdims=True))*inverse
            ig_ref[rows,:]=(cot_ref[rows,:].astype(f32)*scale_ref[rows,:]+dx).astype(bf)
        y=tok_ref[rows,cols].astype(f32)+dg(o_ref[rows,:],wo_ref[cols,:],NT)+dg(hid_ref[rows,:],down_ref[cols,:],NT)
        out_ref[rows,cols]=y.astype(bf)
        for k in range(n):
            if slots[k]:
                @pl.when(it==k)
                def _(k=k):
                    for s in slots[k]: s()
        return carry
    for f in fetch: f.wait()
    lax.fori_loop(0,n,chunk,0)
    end()

def halves(lo,lo_at,hi,hi_at,lane):
    if lo_at: lo=pltpu.roll(lo,64,1)
    if not hi_at: hi=pltpu.roll(hi,64,1)
    return jnp.where(lane,lo,hi)

def scatter_small(gq,go,gkv,sums,o,wo,hidden,down,tokens,cotangent,scale,dnormed,dp,mp,cid):
    hosted=(o,wo,hidden,down,tokens,cotangent,dnormed)
    shape=lambda w: jax.ShapeDtypeStruct((dp,gq.shape[1],w),bf)
    qo,kvg=shape(2*gq.shape[2]),shape(256)
    comm=Scatter([qo,kvg],[(1,0,256,"xz"),(0,0,256,"xyz"),(0,256,384,"yzx")],dp,mp)
    vm=pl.BlockSpec(memory_space=pltpu.VMEM)
    return pl.pallas_call(functools.partial(scatter_kernel,comm.nz,comm),
        in_specs=[vm]*5+[pl.BlockSpec(memory_space=pl.ANY)]*len(hosted),out_specs=comm.outs+[vm]*2,out_shape=comm.shapes+[jax.ShapeDtypeStruct(o.shape,bf)]*2,
        scratch_shapes=[pltpu.VMEM(qo.shape,bf),pltpu.VMEM(kvg.shape,bf)]+[pltpu.VMEM(h.shape,h.dtype) for h in hosted]+[pltpu.SemaphoreType.DMA((len(hosted),))]+comm.scratch,
        compiler_params=pltpu.CompilerParams(collective_id=cid,has_side_effects=True,vmem_limit_bytes=60<<20),name="scatter_grads")(gq,go,gkv,sums,scale,*hosted)

def prologue_kernel(nz,comms,*refs):
    tok_ref,cos_ref,sin_ref,wq_ref,wo_ref,wkv_ref,gain_ref,bias_ref=refs[:8]
    q_out,o_out,small_out,normed_out,ain_out,min_out,kv_out,wkv_out=refs[8:16]
    qo_own,kvg_own,qo_full,kvg_full,ksend,krecv=refs[16:22]
    pos=coords(nz); z,x,y,c=pos
    greet(pos,[f"z{k}" for k in range(1,nz)]+["x","y","c"],nz)
    rows=wq_ref.shape[0]
    kvg_own[:,:128]=wkv_ref[...]
    kvg_own[:,128:]=jnp.concatenate([gain_ref[...].astype(f32),bias_ref[...].astype(f32),jnp.zeros((124,rows),f32)],axis=0).T.astype(bf)
    g,b=comms
    ga=g.build(pos,(kvg_own,),(kvg_full,),refs[22:25])
    gb=b.build(pos,(qo_own,),(qo_full,),refs[25:28])
    ga[0]()
    wq=wq_ref[...].astype(f32); wo=wo_ref[...].astype(f32)
    qo_own[:,:128]=wq[:,:128].astype(bf)
    qo_own[:,128:256]=jnp.concatenate([wq[:,128:],wo[:,:64]],axis=1).astype(bf)
    qo_own[:,256:]=wo[:,64:].astype(bf)
    gb[0]()
    nb,own,width=tok_ref.shape
    part=own//4
    def norm(k,carry):
        v=tok_ref[k//4,pl.ds(pl.multiple_of(k%4*part,part),part),:].astype(f32)
        v=v-jnp.mean(v,axis=1,keepdims=True)
        normed_out[pl.ds(pl.multiple_of(k*part,part),part),:]=v*lax.rsqrt(jnp.mean(v*v,axis=1,keepdims=True)+epsilon)
        return carry
    lax.fori_loop(0,4*nb,norm,0)
    sa=[s for _,s in ga[1]]; sb=[s for _,s in gb[1]]
    while sa:
        sa.pop(0)()
        if sb: sb.pop(0)()
    ga[2]()
    kvg=kvg_full[...].reshape(width,256)
    small=kvg[:,128:].astype(f32).T
    small_out[...]=small[:8]
    wkv=kvg[:,:128]
    wkv_out[...]=wkv
    def copy(s,m,src,kind,n):
        return pltpu.make_async_remote_copy(src,kv_out.at[s,m],ksend.at[n],krecv.at[s,m],device_id=peer(pos,kind,nz),device_id_type=MESH)
    copies=[]
    me=y*2+c
    for s in range(nb):
        normed=normed_out[s*own:s*own+own,:]
        ain=(normed*small[0:1]+small[2:3]).astype(bf)
        ain_out[s*own:s*own+own,:]=ain
        kv=turn(dg(ain,wkv,NN),cos_ref[...],sin_ref[...],False,True)
        kv_out[s,me]=kv.astype(bf)
        for kind in ("y","c"):
            cp=copy(s,me,kv_out.at[s,me],kind,len(copies)); cp.start(); copies.append(cp)
        min_out[s*own:s*own+own,:]=(normed*small[1:2]+small[3:4]).astype(bf)
        for _ in range(6):
            if sb: sb.pop(0)()
    other=(1-y)*2+c
    for s in range(nb):
        copy(s,other,kv_out.at[s,other],"c",0).wait_recv()
        cp=copy(s,other,kv_out.at[s,other],"c",len(copies)); cp.start(); copies.append(cp)
    for s in sb: s()
    gb[2]()
    lane=lax.broadcasted_iota(jnp.int32,(rows,128),1)<64
    def unpack(d,carry):
        def tile(m,k): return qo_full[d,:,384*m+128*k:384*m+128*k+128].astype(f32)
        for ref,place in ((q_out,[(0,0),(0,1),(1,0)]),(o_out,[(1,1),(2,0),(2,1)])):
            for j in range(ref.shape[2]//128):
                (m0,(k0,h0)),(m1,(k1,h1))=[(h//3,place[h%3]) for h in (2*j,2*j+1)]
                ref[d,:,128*j:128*j+128]=halves(tile(m0,k0),h0,tile(m1,k1),h1,lane).astype(bf)
        return carry
    lax.fori_loop(0,q_out.shape[0],unpack,0)
    for s in range(nb):
        for m in (y*2+1-c,(1-y)*2+1-c): copy(s,m,kv_out.at[s,m],"c",0).wait_recv()
    for cp in copies: cp.wait_send()

def prologue(tokens,cos,sin,wq,wo,wkv,gains,biases,dp,mp,cid):
    nb,own,width=tokens.shape; part,cols=wq.shape
    kvg=jax.ShapeDtypeStruct((part,256),bf); qo=jax.ShapeDtypeStruct((part,2*cols),bf)
    comms=(Gather([kvg],[(0,0,256,"zx")],dp,mp),Gather([qo],[(0,0,256,"zyx"),(0,256,384,"xzy")],dp,mp))
    vm=pl.BlockSpec(memory_space=pltpu.VMEM)
    s=lambda *a: jax.ShapeDtypeStruct(a,bf)
    return pl.pallas_call(functools.partial(prologue_kernel,dp//2,comms),
        in_specs=[vm]*8,out_specs=[vm]*8,
        out_shape=[s(dp,part,width),s(dp,part,width),jax.ShapeDtypeStruct((8,width),f32),jax.ShapeDtypeStruct((nb*own,width),f32),s(nb*own,width),s(nb*own,width),s(nb,mp,own,128),s(width,128)],
        scratch_shapes=[pltpu.VMEM(qo.shape,bf),pltpu.VMEM(kvg.shape,bf),pltpu.VMEM((dp,part,mp*2*cols),bf),pltpu.VMEM((dp,part,256),bf),
                        pltpu.SemaphoreType.DMA((3*nb,)),pltpu.SemaphoreType.DMA((nb,mp))]+comms[0].scratch+comms[1].scratch,
        compiler_params=pltpu.CompilerParams(collective_id=cid,has_side_effects=True,vmem_limit_bytes=60<<20),name="gather_weights")(tokens,cos,sin,wq,wo,wkv,gains.T,biases.T)

NT=(((1,),(1,)),((),()))
NN=(((1,),(0,)),((),()))
def dg(a,b,dn): return lax.dot_general(a,b,dn,preferred_element_type=f32)
def turn(v,cos,sin,back,keys_only=False):
    lane=lax.broadcasted_iota(jnp.int32,v.shape,1)
    other=jnp.where(lane%HD<ROT//2,-pltpu.roll(v,128-ROT//2,1),pltpu.roll(v,ROT//2,1))*sin
    w=v*cos-other if back else v*cos+other
    return jnp.where(lane<HD,w,v) if keys_only else w

class Fold:
    scratch=[pltpu.VMEM((2,2,B,128),bf),pltpu.VMEM((2,2,B,128),bf),pltpu.VMEM((2,B,128),bf),pltpu.VMEM((2,B,128),bf),
             pltpu.SemaphoreType.DMA((6,)),pltpu.SemaphoreType.DMA((2,2)),pltpu.SemaphoreType.DMA((2,))]
    def __init__(self,pos,nz,out,cos,sin,scr):
        self.pos=pos; self.nz=nz; self.out=out; self.cos=cos; self.sin=sin; self.scr=scr
    def copy(self,b,n,src,dst,sem,kind):
        return pltpu.make_async_remote_copy(src,dst,self.scr[4].at[3*b+n],sem,device_id=peer(self.pos,kind,self.nz),device_id_type=MESH)
    def across(self,b,ry):
        low,cbuf=self.scr[:2]
        return self.copy(b,ry,low.at[b,ry],cbuf.at[b,ry],self.scr[5].at[b,ry],"c")
    def far(self,b):
        _,_,ybuf,ysend=self.scr[:4]
        return self.copy(b,2,ysend.at[b],ybuf.at[b],self.scr[6].at[b],"y")
    def one(self,b,part):
        _,_,y,c=self.pos
        for ry in (1,0):
            self.scr[0][b,ry]=part((1-y if ry else y)*2+1-c).astype(bf)
            self.across(b,ry).start()
    def two(self,b,part):
        _,_,y,c=self.pos
        self.across(b,1).wait_recv()
        self.scr[3][b]=(part((1-y)*2+c)+self.scr[1][b,1].astype(f32)).astype(bf)
        self.far(b).start()
    def three(self,b,part):
        _,_,y,c=self.pos
        self.across(b,0).wait_recv(); self.far(b).wait_recv()
        v=part(y*2+c)+self.scr[1][b,0].astype(f32)+self.scr[2][b].astype(f32)
        self.out[b]=turn(v,self.cos[...],self.sin[...],True,True).astype(bf)
        self.across(b,1).wait_send(); self.across(b,0).wait_send(); self.far(b).wait_send()

def attn_kernel(nz,pairs,comm,join,nc,*refs):
    q_ref,do_ref,kv_ref,cos_ref,sin_ref=refs[:5]
    refs=refs[5:]
    if join: prev,refs=refs[:3],refs[3:]
    cin=refs[:nc]
    o_ref,dq_ref,dkv_ref=refs[nc:3+nc]
    cout=refs[3+nc:3+2*nc]
    k2,v2,kvt,acck,accv,ps,mk,ms,ls,ots,dqs=refs[3+2*nc:14+2*nc]
    refs=refs[14+2*nc:]
    rb=lax.axis_index("mp")
    nkb=kv_ref.shape[1]//B
    at=0
    if join:
        dkvs,local,fold,refs=refs[0],refs[1],refs[2:9],refs[9:]
        at=B
        part0=lambda m: prev[2][0,pl.ds(pl.multiple_of(m*B,B),B),:]
        part1=lambda m: dkvs[m]
    own=slice(at,at+B)
    slots=[[] for _ in range(pairs*2*nkb)]
    if comm:
        pos=coords(nz)
        greet(pos,[f"z{k}" for k in range(1,nz)]+["x","y","c"],nz)
        begin,steps,end=comm.build(pos,cin,cout,refs)
        begin()
        for when,s in steps: slots[int((comm.late+(1-comm.late)*when)*len(slots))].append(s)
        if join:
            sums=Fold(pos,nz,dkv_ref,cos_ref,sin_ref,fold)
            sums.one(0,part0)
            slots[len(slots)//6].append(lambda: sums.two(0,part0))
            slots[len(slots)//2].append(lambda: sums.three(0,part0))
            before=[pltpu.make_async_copy(prev[k],r.at[:B],local.at[k]) for k,r in enumerate((o_ref,dq_ref))]
            for cp in before: cp.start()
    def between(pair,kb,base):
        for p in range(pairs):
            todo=[k for k in range(nkb) if slots[(2*p+base)*nkb+k]]
            if not todo: continue
            @pl.when(pair==p)
            def _(p=p,todo=todo):
                for k in todo:
                    @pl.when(kb==k)
                    def _(k=k):
                        for s in slots[(2*p+base)*nkb+k]: s()
    lane=lax.broadcasted_iota(jnp.int32,(B,128),1)<64
    def setup(kb,carry):
        kv=kv_ref[0,pl.ds(pl.multiple_of(kb*B,B),B),:].astype(f32)
        rolled=pltpu.roll(kv,64,1)
        k2[kb]=jnp.where(lane,kv,rolled).astype(bf)
        v2[kb]=jnp.where(lane,rolled,kv).astype(bf)
        kvt[kb]=kv.T.astype(bf)
        acck[kb]=jnp.zeros((B,128),f32); accv[kb]=jnp.zeros((B,128),f32)
        return carry
    lax.fori_loop(0,nkb,setup,0)
    def one(pair,carry):
        cols=pl.ds(pl.multiple_of(pair*128,128),128)
        q=(turn(q_ref[:,cols],cos_ref[...],sin_ref[...],False)*HD**-0.5).astype(bf); do=do_ref[:,cols]
        zero=jnp.zeros_like(q)
        qm=(jnp.where(lane,q,zero),jnp.where(lane,zero,q))
        dom=(jnp.where(lane,do,zero),jnp.where(lane,zero,do))
        ms[...]=jnp.full_like(ms,-1e30); ls[...]=jnp.zeros_like(ls)
        ots[...]=jnp.zeros_like(ots); dqs[...]=jnp.zeros_like(dqs)
        H=range(2)
        def fwd(kb,masked):
            ss=[dg(k2[kb],qm[h],NT) for h in H]
            if masked:
                ki=lax.broadcasted_iota(jnp.int32,(B,B),0); ri=lax.broadcasted_iota(jnp.int32,(B,B),1)
                ss=[jnp.where(ki<=ri,v,-1e30) for v in ss]
            mo=[ms[h] for h in H]
            mn=[jnp.maximum(mo[h],jnp.max(ss[h],axis=0,keepdims=True)) for h in H]
            al=[jnp.exp(mo[h]-mn[h]) for h in H]
            pp=[jnp.exp(ss[h]-mn[h]) for h in H]
            for h in H: ls[h]=ls[h]*al[h]+jnp.sum(pp[h],axis=0,keepdims=True)
            pb=[v.astype(bf) for v in pp]
            for h in H:
                ps[h,kb]=pb[h]
                mk[h,kb]=mn[h]
                ms[h]=mn[h]
            ob=[dg(kvt[kb,64:,:],pb[h],NN) for h in H]
            for h in H: ots[h]=ots[h]*al[h]+ob[h]
        def fstep(kb,carry):
            @pl.when(kb<rb)
            def _(): fwd(kb,False)
            @pl.when(kb==rb)
            def _(): fwd(kb,True)
            between(pair,kb,0)
            return carry
        lax.fori_loop(0,nkb,fstep,0)
        dot_=do.astype(f32).T
        for h in range(2):
            inv=1.0/ls[h]
            ot=ots[h]*inv
            ots[h]=ot
            ls[h]=inv
        delta=[jnp.sum(ots[h]*dot_[64*h:64*h+64,:],axis=0,keepdims=True) for h in range(2)]
        o_ref[own,cols]=jnp.concatenate([ots[0],ots[1]],axis=0).T.astype(bf)
        def bwd(kb):
            dps=[dg(v2[kb],dom[h],NT) for h in H]
            al=[jnp.exp(mk[h,kb]-ms[h])*ls[h] for h in H]
            pp=[ps[h,kb].astype(f32)*al[h] for h in H]
            ds=[(pp[h]*(dps[h]-delta[h])).astype(bf) for h in H]
            pn=[v.astype(bf) for v in pp]
            acck[kb]+=dg(ds[0],qm[0],NN)+dg(ds[1],qm[1],NN)
            accv[kb]+=dg(pn[0],dom[0],NN)+dg(pn[1],dom[1],NN)
            qb=[dg(kvt[kb,:64,:],ds[h],NN) for h in H]
            for h in H: dqs[h]+=qb[h]
        def bstep(kb,carry):
            @pl.when(kb<=rb)
            def _(): bwd(kb)
            between(pair,kb,1)
            return carry
        lax.fori_loop(0,nkb,bstep,0)
        dq_ref[own,cols]=(turn(jnp.concatenate([dqs[0],dqs[1]],axis=0).T,cos_ref[...],sin_ref[...],True)*HD**-0.5).astype(bf)
        return carry
    lax.fori_loop(0,pairs,one,0)
    def flush(kb,carry):
        k=acck[kb]; v=accv[kb]
        k=jnp.where(lane,k+pltpu.roll(k,64,1),v+pltpu.roll(v,64,1))
        if join: dkvs[kb]=k
        else: dkv_ref[0,pl.ds(pl.multiple_of(kb*B,B),B),:]=k
        return carry
    lax.fori_loop(0,nkb,flush,0)
    if join:
        sums.one(1,part1)
        sums.two(1,part1)
    if comm: end()
    if join:
        sums.three(1,part1)
        for cp in before: cp.wait()

def attention(b,q,do,kv,cos,sin,comm,arrays,dp,cid,prev=()):
    S=kv.shape[1]; nkb=S//B; width=q.shape[1]; join=len(prev)>0
    assert not join or (b==1 and nkb==4)
    whole=lambda *shape: pl.BlockSpec(shape,lambda *_: (0,)*len(shape))
    blk=pl.BlockSpec((B,width),lambda *_: (b,0))
    kvs=pl.BlockSpec((1,S,128),lambda *_: (b,0,0))
    hbm=pl.BlockSpec(memory_space=pl.ANY)
    rows=2*B if join else B
    kvout=jax.ShapeDtypeStruct((2,B,128),bf) if join else jax.ShapeDtypeStruct((1,S,128),f32)
    params=dict(vmem_limit_bytes=62<<20)
    if comm: params.update(collective_id=cid,has_side_effects=True)
    return pl.pallas_call(functools.partial(attn_kernel,dp//2,width//128,comm,join,len(arrays)),
      grid_spec=pltpu.PrefetchScalarGridSpec(num_scalar_prefetch=0,grid=(1,),
        in_specs=[blk,blk,kvs,whole(B,128),whole(B,128)]+([hbm,hbm,whole(1,S,128)] if join else [])+(comm.ins if comm else []),
        out_specs=[whole(rows,width),whole(rows,width),whole(*kvout.shape)]+(comm.outs if comm else []),
        scratch_shapes=[pltpu.VMEM((nkb,B,128),bf),pltpu.VMEM((nkb,B,128),bf),pltpu.VMEM((nkb,128,B),bf),pltpu.VMEM((nkb,B,128),f32),pltpu.VMEM((nkb,B,128),f32),
                        pltpu.VMEM((2,nkb,B,B),bf),pltpu.VMEM((2,nkb,1,B),f32),pltpu.VMEM((2,1,B),f32),pltpu.VMEM((2,1,B),f32),pltpu.VMEM((2,64,B),f32),pltpu.VMEM((2,64,B),f32)]
                       +([pltpu.VMEM((nkb,B,128),f32),pltpu.SemaphoreType.DMA((2,))]+Fold.scratch if join else [])
                       +(comm.scratch if comm else [])),
      out_shape=[jax.ShapeDtypeStruct((rows,width),bf),jax.ShapeDtypeStruct((rows,width),bf),kvout]+(comm.shapes if comm else []),
      compiler_params=pltpu.CompilerParams(**params),name="attn")(q,do,kv,cos,sin,*prev,*arrays)


def kv_gather_kernel(nz, own_ref, full_ref, send, recv):
    pos = coords(nz)
    z, x, y, c = pos
    greet(pos, ["y", "c"], nz)
    nb = own_ref.shape[0]
    sent = []

    def go(b, m, src, kind):
        cp = pltpu.make_async_remote_copy(src, full_ref.at[b, m], send.at[len(sent)], recv.at[b, m],
                                          device_id=peer(pos, kind, nz), device_id_type=MESH)
        cp.start()
        sent.append(cp)

    def wait(b, m):
        pltpu.make_async_remote_copy(full_ref.at[b, m], full_ref.at[b, m], send.at[0], recv.at[b, m],
                                     device_id=peer(pos, "c", nz), device_id_type=MESH).wait_recv()

    for b in range(nb):
        go(b, y * 2 + c, own_ref.at[b], "y")
    for b in range(nb):
        go(b, y * 2 + c, own_ref.at[b], "c")
    for b in range(nb):
        full_ref[b, y * 2 + c] = own_ref[b]
    for b in range(nb):
        m = (1 - y) * 2 + c
        wait(b, m)
        go(b, m, full_ref.at[b, m], "c")
    for b in range(nb):
        wait(b, y * 2 + 1 - c)
        wait(b, (1 - y) * 2 + 1 - c)
    for cp in sent:
        cp.wait_send()


def kv_gather(own, dp, cid):
    nb, rows, w = own.shape
    return pl.pallas_call(
        functools.partial(kv_gather_kernel, dp // 2),
        in_specs=[pl.BlockSpec(memory_space=pltpu.VMEM)],
        out_specs=pl.BlockSpec(memory_space=pltpu.VMEM),
        out_shape=jax.ShapeDtypeStruct((nb, 4, rows, w), own.dtype),
        scratch_shapes=[pltpu.SemaphoreType.DMA((3 * nb,)), pltpu.SemaphoreType.DMA((nb, 4))],
        compiler_params=pltpu.CompilerParams(collective_id=cid, has_side_effects=True),
        name="gather_keyval",
    )(own)


def kv_reduce_kernel(nz, n, *refs):
    parts = refs[:n]
    cos_ref, sin_ref, out_ref, low, cbuf, ybuf, ysend, send, crecv, yrecv = refs[n:]
    pos = coords(nz)
    z, x, y, c = pos
    greet(pos, ["y", "c"], nz)
    sent = []

    def go(src, dst, sem, kind):
        cp = pltpu.make_async_remote_copy(src, dst, send.at[len(sent)], sem, device_id=peer(pos, kind, nz), device_id_type=MESH)
        cp.start()
        sent.append(cp)

    def wait(dst, sem):
        pltpu.make_async_remote_copy(dst, dst, send.at[0], sem, device_id=peer(pos, "c", nz), device_id_type=MESH).wait_recv()

    for ry in (1, 0):
        yy = 1 - y if ry else y
        for b in range(n):
            low[b, ry] = parts[b][yy * 2 + 1 - c].astype(bf)
            go(low.at[b, ry], cbuf.at[b, ry], crecv.at[b, ry], "c")
    for b in range(n):
        wait(cbuf.at[b, 1], crecv.at[b, 1])
        ysend[b] = (parts[b][(1 - y) * 2 + c] + cbuf[b, 1].astype(f32)).astype(bf)
        go(ysend.at[b], ybuf.at[b], yrecv.at[b], "y")
    for b in range(n):
        wait(cbuf.at[b, 0], crecv.at[b, 0])
        wait(ybuf.at[b], yrecv.at[b])
        v = parts[b][y * 2 + c] + cbuf[b, 0].astype(f32) + ybuf[b].astype(f32)
        out_ref[b] = turn(v, cos_ref[...], sin_ref[...], True, True).astype(bf)
    for cp in sent:
        cp.wait_send()


def kv_reduce(parts, cos, sin, dp, cid):
    nb = len(parts)
    mp, rows, w = parts[0].shape
    vm = pl.BlockSpec(memory_space=pltpu.VMEM)
    return pl.pallas_call(
        functools.partial(kv_reduce_kernel, dp // 2, nb),
        in_specs=[vm] * (nb + 2),
        out_specs=vm,
        out_shape=jax.ShapeDtypeStruct((nb, rows, w), bf),
        scratch_shapes=[pltpu.VMEM((nb, 2, rows, w), bf), pltpu.VMEM((nb, 2, rows, w), bf), pltpu.VMEM((nb, rows, w), bf),
                        pltpu.VMEM((nb, rows, w), bf), pltpu.SemaphoreType.DMA((3 * nb,)), pltpu.SemaphoreType.DMA((nb, 2)), pltpu.SemaphoreType.DMA((nb,))],
        compiler_params=pltpu.CompilerParams(collective_id=cid, has_side_effects=True),
        name="reduce_keyval",
    )(*parts, cos, sin)


def spread(arrays, inside, dp, mp):
    out = []
    for i, s in enumerate(arrays):
        if i in inside:
            out.append(lax.all_gather(s, "dp"))
        else:
            a = lax.all_gather(s, ("dp", "mp")).reshape((dp, mp) + s.shape)
            out.append(a.transpose(0, 2, 1, 3).reshape(dp, s.shape[0], -1))
    return out


def collect(parts, inside, dp, mp):
    out = []
    for i, p in enumerate(parts):
        p = p.astype(f32)
        if i in inside:
            out.append(lax.psum(lax.psum_scatter(p, "dp", scatter_dimension=0), "mp"))
        else:
            a = p.reshape(dp, p.shape[1], mp, -1).transpose(0, 2, 1, 3).reshape(dp * mp, p.shape[1], -1)
            out.append(lax.psum_scatter(a, ("dp", "mp"), scatter_dimension=0))
    return out


def rotary(position):
    lane = jnp.arange(2 * HD, dtype=jnp.int32)
    inside = lane % HD
    frequency = 10000.0 ** (-2.0 * (inside % (ROT // 2)).astype(f32) / ROT)
    angle = position[:, None].astype(f32) * frequency[None, :]
    turned = (inside < ROT)[None, :]
    return jnp.where(turned, jnp.cos(angle), 1.0), jnp.where(turned, jnp.sin(angle), 0.0)


def plain_prologue(tokens, cos, sin, wq, wo, wkv, gains, biases, dp, mp):
    nb, own, width = tokens.shape
    wq, wo, kvg = spread([wq, wo, jnp.concatenate([wkv, gains, biases], axis=1)], {2}, dp, mp)
    kvg = kvg.reshape(width, -1)
    small = kvg[:, 2 * HD :].astype(f32).T
    x = tokens.reshape(nb * own, width).astype(f32)
    centered = x - jnp.mean(x, axis=1, keepdims=True)
    normed = centered * lax.rsqrt(jnp.mean(centered * centered, axis=1, keepdims=True) + epsilon)
    ain = (normed * small[0] + small[2]).astype(bf)
    mlp_in = (normed * small[1] + small[3]).astype(bf)
    kv = jnp.dot(ain, kvg[:, : 2 * HD], preferred_element_type=f32).reshape(nb, own, 2 * HD)
    first, half = jnp.arange(2 * HD) < HD, ROT // 2
    other = jnp.where(jnp.arange(2 * HD) < half, -jnp.roll(kv, -half, axis=2), jnp.roll(kv, half, axis=2)) * sin
    kv = jnp.where(first, kv * cos + other, kv).astype(bf)
    return wq, wo, jnp.concatenate([small, small]), normed, ain, mlp_in, kv_gather(kv, dp, 3), kvg[:, : 2 * HD]


def shards(tokens, norm_gains, norm_biases, w_query, w_keyval, w_output, w_up, w_down, cotangent, subset_ids, subset_weights):
    dp, mp = lax.axis_size("dp"), lax.axis_size("mp")
    me = lax.axis_index("mp")
    nb, own, width = tokens.shape
    rows = nb * own
    part, cols = w_query.shape
    ff = w_up.shape[1]
    mine = dp == 8
    dot = functools.partial(jnp.dot, preferred_element_type=f32)
    nt = lambda a, b: lax.dot_general(a, b, (((1,), (1,)), ((), ())), preferred_element_type=f32)
    tn = lambda a, b: lax.dot_general(a, b, (((0,), (0,)), ((), ())), preferred_element_type=f32)
    cos, sin = rotary(me * own + jnp.arange(own, dtype=jnp.int32))
    small_weights = (w_query, w_output, w_keyval, norm_gains, norm_biases)
    if mine:
        wq, wo, small, normed, attn_in, mlp_in, kv, wkv = prologue(tokens, cos, sin, *small_weights, dp, mp, 1)
    else:
        wq, wo, small, normed, attn_in, mlp_in, kv, wkv = plain_prologue(tokens, cos, sin, *small_weights, dp, mp)
    wq, wo = wq.reshape(width, width), wo.reshape(width, width)
    kv_full = kv.reshape(nb, mp * own, 2 * HD)
    gain_a, gain_m = small[0], small[1]

    ids = lax.dynamic_slice_in_dim(subset_ids.reshape(nb, mp * own), me * own, own, 1).reshape(rows)
    matches = ids[:, None] == jnp.arange(subset_weights.shape[0], dtype=jnp.int32)[None, :]
    scale = jnp.sum(jnp.where(matches, subset_weights[None, :], 0.0), axis=1, keepdims=True)
    g = (cotangent.reshape(rows, width).astype(f32) * scale).astype(bf)

    q = dot(attn_in, wq)
    grad_heads = dot(g, wo).astype(bf)
    mlp_plan = lambda a, b: [(0, 0, 768, a), (1, 0, 256, a), (1, 256, 768, b)]
    if mine:
        o0, dq0, dkv0, up, down = attention(0, q, grad_heads, kv_full, cos, sin, Gather([w_up, w_down], mlp_plan("zyx", "xzy"), dp, mp), [w_up, w_down], dp, 5)
    else:
        o0, dq0, dkv0 = attention(0, q, grad_heads, kv_full, cos, sin, None, [], dp, 5)
        up, down = spread([w_up, w_down], (), dp, mp)
    up = up.reshape(width, mp * ff)
    down = down.reshape(width, mp * ff)

    pre = dot(mlp_in, up)
    cdf = 0.5 * (1.0 + lax.erf(pre * sqrt_half))
    hidden = (pre * cdf).astype(bf)
    slope = cdf + pre * (jnp.exp(-0.5 * pre * pre) * inv_sqrt_two_pi)
    hidden, slope = lax.optimization_barrier((hidden, slope))
    dpre = (dot(g, down) * slope).astype(bf)
    gup = tn(mlp_in, dpre).astype(bf).reshape(dp, part, mp * ff)
    gdown = tn(g, hidden).astype(bf).reshape(dp, part, mp * ff)
    if mine:
        o, dqp, dkvp, grad_up, grad_down = attention(1, q, grad_heads, kv_full, cos, sin, Scatter([gup, gdown], mlp_plan("xyz", "yzx"), dp, mp), [gup, gdown], dp, 6, (o0, dq0, dkv0))
    else:
        o1, dq1, dkv1 = attention(1, q, grad_heads, kv_full, cos, sin, None, [], dp, 6)
        grad_up, grad_down = collect([gup, gdown], (), dp, mp)
        dkvp = kv_reduce([d.reshape(mp, own, 2 * HD) for d in (dkv0, dkv1)], cos, sin, dp, 4)
        o = jnp.concatenate([o0, o1])
        dqp = jnp.concatenate([dq0, dq1])
    dkvp = dkvp.reshape(rows, 2 * HD)

    dmlp = nt(dpre, up)
    dattn = nt(dqp, wq) + nt(dkvp, wkv)
    dnormed = dattn * gain_a + dmlp * gain_m
    sums = [jnp.sum(dattn * normed, axis=0), jnp.sum(dmlp * normed, axis=0), jnp.sum(dattn, axis=0), jnp.sum(dmlp, axis=0)]
    gq = tn(attn_in, dqp).astype(bf).reshape(dp, part, width)
    go = tn(g, o).astype(bf).reshape(dp, part, width)
    gkv = tn(attn_in, dkvp).reshape(dp, part, 2 * HD)
    k = 2 * HD
    if mine:
        sums = jnp.concatenate([s[None] for s in sums] + [jnp.zeros((4, width), f32)])
        flat = lambda a: a.reshape(rows, width)
        a, c, out, input_grad = scatter_small(gq, go, gkv, sums, o, wo, hidden, down, flat(tokens), flat(cotangent), scale, dnormed, dp, mp, 2)
        grad_query, grad_output = a[:, :cols], a[:, cols:]
    else:
        x = tokens.reshape(rows, width).astype(f32)
        out = (x + nt(o, wo) + nt(hidden, down)).astype(bf)
        centered = x - jnp.mean(x, axis=1, keepdims=True)
        inverse = lax.rsqrt(jnp.mean(centered * centered, axis=1, keepdims=True) + epsilon)
        dx = (dnormed - jnp.mean(dnormed, axis=1, keepdims=True) - normed * jnp.mean(dnormed * normed, axis=1, keepdims=True)) * inverse
        input_grad = (cotangent.reshape(rows, width).astype(f32) * scale + dx).astype(bf)
        gkvg = jnp.concatenate([gkv, jnp.stack(sums, axis=1).reshape(dp, part, 4)], axis=2)
        grad_query, grad_output, c = collect([gq, go, gkvg], {2}, dp, mp)
    return (
        out.reshape(tokens.shape),
        kv_full.reshape(-1, 2 * HD),
        input_grad.reshape(tokens.shape),
        c[:, k : k + 2],
        c[:, k + 2 : k + 4],
        grad_query,
        c[:, :k],
        grad_output,
        grad_up,
        grad_down,
    )


def solution(mesh):
    rows = P(None, ("dp", "mp"), None)
    d, dm = P("dp", None), P("dp", "mp")
    return jax.shard_map(
        shards,
        mesh=mesh,
        in_specs=(rows, d, d, dm, d, dm, dm, dm, rows, P("dp"), P()),
        out_specs=(rows, d, rows, d, d, dm, d, dm, dm, dm),
        check_vma=False,
    )
```

```python
import functools

import jax
import jax.numpy as jnp
from jax import lax
from jax.experimental import pallas as pl
from jax.experimental.pallas import tpu as pltpu
from jax.sharding import PartitionSpec as P

f32 = jnp.float32
bf = jnp.bfloat16
MESH = pl.DeviceIdType.MESH
HD = 64
ROT = 16
B = 512
SEQ_LEN = 2048
epsilon = 1e-05
sqrt_half = 0.7071067811865476
inv_sqrt_two_pi = 0.3989422804014327


def coords(nz):
    d=lax.axis_index("dp"); m=lax.axis_index("mp")
    return d//2, d%2, m//2, m%2

def peer(pos,kind,nz):
    z,x,y,c=pos
    if kind[0]=="z": z=lax.rem(z+int(kind[1:]),nz)
    if kind=="x": x=1-x
    if kind=="y": y=1-y
    if kind=="c": c=1-c
    return (z*2+x, y*2+c)

def greet(pos,kinds,nz):
    bar=pltpu.get_barrier_semaphore()
    for k in kinds:
        pl.semaphore_signal(bar,inc=1,device_id=peer(pos,k,nz),device_id_type=MESH)
    pl.semaphore_wait(bar,len(kinds))

def gather_routes(order,nz):
    zs=[f"z{k}" for k in range(1,nz)]
    out=[]
    if order=="zyx":
        out.append(((0,0,0),zs+["y","x","c"]))
        out+=[((k,0,0),["y","x","c"]) for k in range(1,nz)]
        out+=[((k,0,1),["x","c"]) for k in range(nz)]
        out+=[((k,1,r),["c"]) for r in (0,1) for k in range(nz)]
    elif order=="xzy":
        out.append(((0,0,0),["x"]+zs+["y","c"]))
        out.append(((0,1,0),zs+["y","c"]))
        out+=[((k,r,0),["y","c"]) for k in range(1,nz) for r in (0,1)]
        out+=[((k,r,1),["c"]) for k in range(nz) for r in (0,1)]
    elif order=="zx":
        out.append(((0,0,0),zs+["x"]))
        out+=[((k,0,0),["x"]) for k in range(1,nz)]
        out+=[((k,1,0),[]) for k in range(nz)]
    return out

def columns(m,w,lo,hi):
    return pl.ds(pl.multiple_of(m*w+lo,128),hi-lo)

class Gather:
    late=0.42
    def __init__(self,shards,plan,dp,mp):
        self.plan=plan; self.nz=dp//2; self.mp=mp; self.dp=dp
        inside={i for i,_,_,o in plan if o=="zx"}
        self.ins=[pl.BlockSpec(memory_space=pltpu.VMEM)]*len(shards)
        self.outs=[pl.BlockSpec(memory_space=pl.ANY)]*len(shards)
        self.shapes=[jax.ShapeDtypeStruct((dp,s.shape[0],s.shape[1]*(1 if i in inside else mp)),s.dtype) for i,s in enumerate(shards)]
        sends=sum(len(f) for _,_,_,o in plan for _,f in gather_routes(o,self.nz))
        self.scratch=[pltpu.SemaphoreType.DMA((sends,)),pltpu.SemaphoreType.DMA((len(plan),mp,dp)),pltpu.SemaphoreType.DMA((len(shards),))]
    def build(self,pos,shards,full,scr):
        send,recv,local=scr
        nz=self.nz; z,x,y,c=pos
        routes=[gather_routes(o,nz) for _,_,_,o in self.plan]
        sent=[]
        def where(p,rel,other):
            i,lo,hi,order=self.plan[p]; k,rx,ry=rel
            zz=lax.rem(z+nz-k,nz); xx=1-x if rx else x; yy=1-y if ry else y
            d=zz*2+xx; m=yy*2+(1-c if other else c)
            if order=="zx": return full[i].at[d,:,lo:hi],recv.at[p,0,d]
            return full[i].at[d,:,columns(m,shards[i].shape[1],lo,hi)],recv.at[p,m,d]
        def arrived(p,rel,other):
            dst,sem=where(p,rel,other)
            pltpu.make_async_remote_copy(dst,dst,send.at[0],sem,device_id=peer(pos,"c",nz),device_id_type=MESH).wait_recv()
        def copy(p,rel,f,own,n):
            i,lo,hi,_=self.plan[p]
            dst,sem=where(p,rel,False)
            src=shards[i].at[:,lo:hi] if own else dst
            return pltpu.make_async_remote_copy(src,dst,send.at[n],sem,device_id=peer(pos,f,nz),device_id_type=MESH)
        def step(p,s):
            rel,fw=routes[p][s]
            base=len(sent)
            cps=[functools.partial(copy,p,rel,f,s==0,base+j) for j,f in enumerate(fw)]
            sent.extend(cps)
            def go():
                if s: arrived(p,rel,False)
                for cp in cps: cp().start()
            return go
        def mine(i):
            order=[o for j,_,_,o in self.plan if j==i][0]
            d=z*2+x; w=shards[i].shape[1]
            dst=full[i].at[d] if order=="zx" else full[i].at[d,:,columns(y*2+c,w,0,w)]
            return pltpu.make_async_copy(shards[i],dst,local.at[i])
        first=[step(p,0) for p in range(len(self.plan))]
        steps=[]
        longest=max(len(r) for r in routes)
        for s in range(1,longest):
            for p,r in enumerate(routes):
                if s<len(r): steps.append(((s-1)/(longest-1),step(p,s)))
        def begin():
            for g in first: g()
            for i in range(len(shards)): mine(i).start()
        def end():
            for p,r in enumerate(routes):
                if self.plan[p][3]=="zx": continue
                for rel,_ in r: arrived(p,rel,True)
            for cp in sent: cp().wait_send()
            for i in range(len(shards)): mine(i).wait()
        return begin,steps,end

class Scatter:
    late=0.0
    def __init__(self,parts,plan,dp,mp):
        self.plan=plan; nz=self.nz=dp//2; self.mp=mp
        self.width=[]
        for i,p in enumerate(parts):
            inside=[o for j,_,_,o in plan if j==i][0]=="xz"
            self.width.append(p.shape[-1]//(1 if inside else mp))
        self.ins=[pl.BlockSpec(memory_space=pl.ANY)]*len(parts)
        self.outs=[pl.BlockSpec(memory_space=pltpu.VMEM)]*len(parts)
        self.shapes=[jax.ShapeDtypeStruct((p.shape[1],w),f32) for p,w in zip(parts,self.width)]
        scr=[]; sends=0
        for i,lo,hi,order in plan:
            rows=parts[i].shape[1]; w=hi-lo
            b=lambda k: pltpu.VMEM((k,rows,w),bf)
            nb=nz*4 if order!="xz" else nz*2
            scr+=[b(nb),b(nb)]
            if order=="xyz": scr+=[b(nz*2),b(nz),b(nz)]; sends+=nb+2*nz+nz+nz-1
            elif order=="yzx": scr+=[b(1),b(nz*2),b(nz*2)]; sends+=nb+2*nz+2*(nz-1)+1
            else: scr+=[b(nz*2),b(nz),b(2*nz)]; sends+=nb+nz+nz+nz-1
        n=len(plan)
        self.scratch=scr+[pltpu.SemaphoreType.DMA((n,4*nz)),pltpu.SemaphoreType.DMA((sends,)),pltpu.SemaphoreType.DMA((n,4*nz)),pltpu.SemaphoreType.DMA((n,2*nz)),pltpu.SemaphoreType.DMA((n,2*nz)),pltpu.SemaphoreType.DMA((n,2*nz))]
    def build(self,pos,parts,outs,scr):
        plan=self.plan; nz=self.nz; z,x,y,c=pos; n=len(plan)
        per=scr[:5*n]; own,send,csem,xsem,ysem,zsem=scr[5*n:]
        sent=[]; begins=[]; steps=[]; ends=[]
        def sender(src,dst,rsem,kind):
            k=len(sent)
            cp=lambda: pltpu.make_async_remote_copy(src(),dst,send.at[k],rsem,device_id=peer(pos,kind,nz),device_id_type=MESH)
            sent.append(cp)
            return lambda: cp().start()
        def wait(dst,rsem):
            pltpu.make_async_remote_copy(dst,dst,send.at[0],rsem,device_id=peer(pos,"c",nz),device_id_type=MESH).wait_recv()
        def part(p,r,cc):
            i,lo,hi,order=plan[p]
            rz,rx,ry=r
            zz=lax.rem(z+rz,nz); xx=1-x if rx else x; yy=1-y if ry else y
            if order=="xz": return parts[i].at[zz*2+xx,:,lo:hi]
            return parts[i].at[zz*2+xx,:,columns(yy*2+cc,self.width[i],lo,hi)]
        def total(dst,*refs):
            step=32 if dst.shape[0]%32==0 else dst.shape[0]
            def body(r,carry):
                w=pl.ds(pl.multiple_of(r*step,step),step)
                v=refs[0][w,:].astype(f32)
                for o in refs[1:]: v=v+o[w,:].astype(f32)
                dst[w,:]=v.astype(dst.dtype)
                return carry
            lax.fori_loop(0,dst.shape[0]//step,body,0)
        down=range(nz-1,-1,-1)
        for p,(i,lo,hi,order) in enumerate(plan):
            acc,cb,xb,yb,zb=per[5*p:5*p+5]
            if order=="xyz": seq=[(k,1,r) for r in (1,0) for k in down]+[(k,0,1) for k in down]+[(k,0,0) for k in down]
            elif order=="yzx": seq=[(k,r,1) for r in (1,0) for k in down]+[(k,1,0) for k in down]+[(k,0,0) for k in down]
            else: seq=[(k,1,0) for k in down]+[(k,0,0) for k in down]
            slot=(lambda r: (r[0]*2+r[1])*2+r[2]) if order!="xz" else (lambda r: r[0]*2+r[1])
            A=lambda r,acc=acc,slot=slot: acc.at[slot(r)]
            def plus(when,p=p):
                def note(f): steps.append((when,f))
                return note
            for t,r in enumerate(seq):
                s=slot(r); rz,rx,ry=r
                begins.append((t,sender(functools.partial(part,p,r,c if order=="xz" else 1-c),cb.at[s],csem.at[p,s],"c")))
                mine=lambda p=p,r=r,s=s,acc=acc: pltpu.make_async_copy(part(p,r,c),acc.at[s],own.at[p,s])
                begins.append((t,lambda mine=mine: mine().start()))
                go=None
                if order in ("xyz","xz") and rx: go=sender(lambda v=A(r): v,xb.at[rz*2+ry],xsem.at[p,rz*2+ry],"x")
                if order=="yzx" and ry: go=sender(lambda v=A(r): v,yb.at[rz*2+rx],ysem.at[p,rz*2+rx],"y")
                @plus(0.22*t/len(seq))
                def _(p=p,s=s,acc=acc,cb=cb,go=go,mine=mine):
                    mine().wait()
                    wait(cb.at[s],csem.at[p,s])
                    total(acc.at[s],acc.at[s],cb.at[s])
                    if go: go()
            if order=="xyz":
                for n_,k in enumerate(down):
                    r=(k,0,1); j=k*2+1
                    go=sender(lambda v=A(r): v,yb.at[k],ysem.at[p,k],"y")
                    @plus(0.24+0.26*n_/nz)
                    def _(p=p,r=r,j=j,A=A,xb=xb,go=go):
                        wait(xb.at[j],xsem.at[p,j]); total(A(r),A(r),xb.at[j])
                        go()
                for n_,k in enumerate(down):
                    r=(k,0,0); j=k*2
                    go=sender(lambda v=A(r): v,zb.at[k],zsem.at[p,k],f"z{k}") if k else None
                    @plus(0.52+0.26*n_/nz)
                    def _(p=p,r=r,j=j,k=k,A=A,xb=xb,yb=yb,go=go):
                        wait(xb.at[j],xsem.at[p,j]); wait(yb.at[k],ysem.at[p,k])
                        if go:
                            total(A(r),A(r),xb.at[j],yb.at[k])
                            go()
                def fin(p=p,i=i,lo=lo,hi=hi,A=A,xb=xb,yb=yb,zb=zb):
                    for k in range(1,nz): wait(zb.at[k],zsem.at[p,k])
                    total(outs[i].at[:,lo:hi],A((0,0,0)),xb.at[0],yb.at[0],*[zb.at[k] for k in range(1,nz)])
                ends.append(fin)
            elif order=="yzx":
                for n_,(rx,k) in enumerate([(rx,k) for rx in (1,0) for k in range(nz-1,0,-1)]):
                    r=(k,rx,0); j=k*2+rx
                    go=sender(lambda v=A(r): v,zb.at[k*2+rx],zsem.at[p,k*2+rx],f"z{k}")
                    @plus(0.24+0.3*n_/(2*nz-2))
                    def _(p=p,r=r,j=j,A=A,yb=yb,go=go):
                        wait(yb.at[j],ysem.at[p,j]); total(A(r),A(r),yb.at[j])
                        go()
                r=(0,1,0)
                go=sender(lambda v=A(r): v,xb.at[0],xsem.at[p,0],"x")
                @plus(0.8)
                def _(p=p,r=r,A=A,yb=yb,zb=zb,go=go):
                    wait(yb.at[1],ysem.at[p,1])
                    for k in range(1,nz): wait(zb.at[k*2+1],zsem.at[p,k*2+1])
                    total(A(r),A(r),yb.at[1],*[zb.at[k*2+1] for k in range(1,nz)])
                    go()
                def fin(p=p,i=i,lo=lo,hi=hi,A=A,xb=xb,yb=yb,zb=zb):
                    wait(yb.at[0],ysem.at[p,0])
                    for k in range(1,nz): wait(zb.at[k*2],zsem.at[p,k*2])
                    wait(xb.at[0],xsem.at[p,0])
                    total(outs[i].at[:,lo:hi],A((0,0,0)),yb.at[0],xb.at[0],*[zb.at[k*2] for k in range(1,nz)])
                ends.append(fin)
            else:
                for n_,k in enumerate(down):
                    r=(k,0,0)
                    go=sender(lambda v=A(r): v,yb.at[k],ysem.at[p,k],"y")
                    @plus(0.24+0.26*n_/nz)
                    def _(p=p,r=r,k=k,A=A,xb=xb,go=go):
                        wait(xb.at[k*2],xsem.at[p,k*2]); total(A(r),A(r),xb.at[k*2])
                        go()
                for n_,k in enumerate(range(nz-1,0,-1)):
                    go=sender(lambda v=zb.at[k]: v,zb.at[nz+k],zsem.at[p,k],f"z{k}")
                    @plus(0.52+0.26*n_/nz)
                    def _(p=p,k=k,A=A,yb=yb,zb=zb,go=go):
                        wait(yb.at[k],ysem.at[p,k]); total(zb.at[k],A((k,0,0)),yb.at[k])
                        go()
                def fin(p=p,i=i,lo=lo,hi=hi,A=A,yb=yb,zb=zb):
                    wait(yb.at[0],ysem.at[p,0])
                    for k in range(1,nz): wait(zb.at[nz+k],zsem.at[p,k])
                    total(outs[i].at[:,lo:hi],A((0,0,0)),yb.at[0],*[zb.at[nz+k] for k in range(1,nz)])
                ends.append(fin)
        begins.sort(key=lambda e: e[0])
        steps.sort(key=lambda e: e[0])
        def begin():
            for _,g in begins: g()
        def end():
            for f in ends: f()
            for cp in sent: cp().wait_send()
        return begin,steps,end

def scatter_kernel(nz,comm,*refs):
    gq_ref,go_ref,gkv_ref,sums_ref,scale_ref=refs[:5]
    hosted=refs[5:12]
    outq_ref,outo_ref,outkv_ref,outgb_ref,out_hbm,ig_hbm=refs[12:18]
    refs=refs[18:]
    qo,kvg,a_ref,c_ref,out_ref,ig_ref,osem=refs[:7]
    refs=refs[7:]
    o_ref,wo_ref,hid_ref,down_ref,tok_ref,cot_ref,dn_ref=refs[:7]
    fetch=[pltpu.make_async_copy(h,v,refs[7].at[k]) for k,(h,v) in enumerate(zip(hosted,refs[:7]))]
    for f in fetch: f.start()
    pos=coords(nz)
    greet(pos,[f"z{k}" for k in range(1,nz)]+["x","y","c"],nz)
    rows=gq_ref.shape[1]
    lane=lax.broadcasted_iota(jnp.int32,(rows,128),1)<64
    def tile(ref,d,h): return ref[d,:,128*(h//2):128*(h//2)+128].astype(f32)
    def pack(d,carry):
        for t in range(qo.shape[2]//128):
            m,k=t//3,t%3
            lo,hi=[((gq_ref,3*m),(gq_ref,3*m+1)),((gq_ref,3*m+2),(go_ref,3*m)),((go_ref,3*m+1),(go_ref,3*m+2))][k]
            qo[d,:,128*t:128*t+128]=halves(tile(lo[0],d,lo[1]),lo[1]%2,tile(hi[0],d,hi[1]),hi[1]%2,lane).astype(bf)
        return carry
    lax.fori_loop(0,qo.shape[0],pack,0)
    s=jnp.concatenate([sums_ref[...],jnp.zeros((120,sums_ref.shape[1]),f32)],axis=0).T
    for d in range(kvg.shape[0]):
        kvg[d,:,:128]=gkv_ref[d].astype(bf)
        kvg[d,:,128:]=s[rows*d:rows*d+rows].astype(bf)
    begin,steps,end=comm.build(pos,(qo,kvg),(a_ref,c_ref),refs[8:])
    begin()
    T=256
    def leave(k,r):
        rows=pl.ds(pl.multiple_of(r*T,T),T)
        src,dst=((out_ref,out_hbm),(ig_ref,ig_hbm))[k]
        return pltpu.make_async_copy(src.at[rows,:],dst.at[rows,:],osem.at[k,r])
    across=out_ref.shape[1]//T; n=out_ref.shape[0]//T*across
    slots=[[] for _ in range(n)]
    for when,s in steps:
        if when<0.23: s()
        else: slots[min(n-1,int(n*(0.33+(when-0.24)*1.15)))].append(s)
    def chunk(it,carry):
        rows=pl.ds(pl.multiple_of(it//across*T,T),T); cols=pl.ds(pl.multiple_of(it%across*T,T),T)
        @pl.when(it%across==0)
        def _():
            v=tok_ref[rows,:].astype(f32)
            v=v-jnp.mean(v,axis=1,keepdims=True)
            inverse=lax.rsqrt(jnp.mean(v*v,axis=1,keepdims=True)+epsilon)
            v=v*inverse
            dn=dn_ref[rows,:]
            dx=(dn-jnp.mean(dn,axis=1,keepdims=True)-v*jnp.mean(dn*v,axis=1,keepdims=True))*inverse
            ig_ref[rows,:]=(cot_ref[rows,:].astype(f32)*scale_ref[rows,:]+dx).astype(bf)
        y=tok_ref[rows,cols].astype(f32)+dg(o_ref[rows,:],wo_ref[cols,:],NT)+dg(hid_ref[rows,:],down_ref[cols,:],NT)
        out_ref[rows,cols]=y.astype(bf)
        @pl.when(it%across==across-1)
        def _():
            for k in range(2): leave(k,it//across).start()
        for k in range(n):
            if slots[k]:
                @pl.when(it==k)
                def _(k=k):
                    for s in slots[k]: s()
        return carry
    for f in fetch: f.wait()
    lax.fori_loop(0,n,chunk,0)
    end()
    a=a_ref[...]; half=a.shape[1]//2
    outq_ref[...]=a[:,:half]; outo_ref[...]=a[:,half:]
    outkv_ref[...]=c_ref[:,:128]
    outgb_ref[...]=c_ref[:,128:].T[:8]
    for r in range(n//across):
        for k in range(2): leave(k,r).wait()

def halves(lo,lo_at,hi,hi_at,lane):
    if lo_at: lo=pltpu.roll(lo,64,1)
    if not hi_at: hi=pltpu.roll(hi,64,1)
    return jnp.where(lane,lo,hi)

def scatter_small(gq,go,gkv,sums,o,wo,hidden,down,tokens,cotangent,scale,dnormed,dp,mp,cid):
    hosted=(o,wo,hidden,down,tokens,cotangent,dnormed)
    part=gq.shape[1]; cols=gq.shape[2]//mp
    shape=lambda w: jax.ShapeDtypeStruct((dp,gq.shape[1],w),bf)
    qo,kvg=shape(2*gq.shape[2]),shape(256)
    comm=Scatter([qo,kvg],[(1,0,256,"xz"),(0,0,256,"xyz"),(0,256,384,"yzx")],dp,mp)
    vm=pl.BlockSpec(memory_space=pltpu.VMEM)
    return pl.pallas_call(functools.partial(scatter_kernel,comm.nz,comm),
        in_specs=[vm]*5+[pl.BlockSpec(memory_space=pl.ANY)]*len(hosted),out_specs=[vm]*4+[pl.BlockSpec(memory_space=pl.ANY)]*2,
        out_shape=[jax.ShapeDtypeStruct(d,f32) for d in ((part,cols),(part,cols),(part,128),(8,part))]+[jax.ShapeDtypeStruct(o.shape,bf)]*2,
        scratch_shapes=[pltpu.VMEM(qo.shape,bf),pltpu.VMEM(kvg.shape,bf),pltpu.VMEM((part,2*cols),f32),pltpu.VMEM((part,256),f32),pltpu.VMEM(o.shape,bf),pltpu.VMEM(o.shape,bf),pltpu.SemaphoreType.DMA((2,o.shape[0]//256))]+[pltpu.VMEM(h.shape,h.dtype) for h in hosted]+[pltpu.SemaphoreType.DMA((len(hosted),))]+comm.scratch,
        compiler_params=pltpu.CompilerParams(collective_id=cid,has_side_effects=True,vmem_limit_bytes=60<<20),name="scatter_grads")(gq,go,gkv,sums,scale,*hosted)

def prologue_kernel(nz,comms,*refs):
    tok_ref,cos_ref,sin_ref,wq_ref,wo_ref,wkv_ref,gain_ref,bias_ref=refs[:8]
    q_out,o_out,small_out,normed_out,ain_out,min_out,kv_out,wkv_out=refs[8:16]
    qo_own,kvg_own,qo_full,kvg_full,ksend,krecv=refs[16:22]
    pos=coords(nz); z,x,y,c=pos
    greet(pos,[f"z{k}" for k in range(1,nz)]+["x","y","c"],nz)
    rows=wq_ref.shape[0]
    kvg_own[:,:128]=wkv_ref[...]
    kvg_own[:,128:]=jnp.concatenate([gain_ref[...].astype(f32),bias_ref[...].astype(f32),jnp.zeros((124,rows),f32)],axis=0).T.astype(bf)
    g,b=comms
    ga=g.build(pos,(kvg_own,),(kvg_full,),refs[22:25])
    gb=b.build(pos,(qo_own,),(qo_full,),refs[25:28])
    ga[0]()
    wq=wq_ref[...].astype(f32); wo=wo_ref[...].astype(f32)
    qo_own[:,:128]=wq[:,:128].astype(bf)
    qo_own[:,128:256]=jnp.concatenate([wq[:,128:],wo[:,:64]],axis=1).astype(bf)
    qo_own[:,256:]=wo[:,64:].astype(bf)
    gb[0]()
    nb,own,width=tok_ref.shape
    part=own//4
    def norm(k,carry):
        v=tok_ref[k//4,pl.ds(pl.multiple_of(k%4*part,part),part),:].astype(f32)
        v=v-jnp.mean(v,axis=1,keepdims=True)
        normed_out[pl.ds(pl.multiple_of(k*part,part),part),:]=v*lax.rsqrt(jnp.mean(v*v,axis=1,keepdims=True)+epsilon)
        return carry
    lax.fori_loop(0,4*nb,norm,0)
    sa=[s for _,s in ga[1]]; sb=[s for _,s in gb[1]]
    while sa:
        sa.pop(0)()
        if sb: sb.pop(0)()
    ga[2]()
    kvg=kvg_full[...].reshape(width,256)
    small=kvg[:,128:].astype(f32).T
    small_out[...]=small[:8]
    wkv_out[...]=kvg[:,:128]
    def copy(s,m,src,kind,n):
        return pltpu.make_async_remote_copy(src,kv_out.at[s,m],ksend.at[n],krecv.at[s,m],device_id=peer(pos,kind,nz),device_id_type=MESH)
    copies=[]
    me=y*2+c
    for s in range(nb):
        def project(k,carry):
            w=pl.ds(pl.multiple_of(k*part,part),part); rows=pl.ds(pl.multiple_of(s*own+k*part,part),part)
            ain=(normed_out[rows,:]*small[0:1]+small[2:3]).astype(bf)
            ain_out[rows,:]=ain
            kv_out[s,me,w,:]=turn(dg(ain,wkv_out[...],NN),cos_ref[w,:],sin_ref[w,:],False,True).astype(bf)
            return carry
        lax.fori_loop(0,4,project,0)
        for kind in ("y","c"):
            cp=copy(s,me,kv_out.at[s,me],kind,len(copies)); cp.start(); copies.append(cp)
        def feed(k,carry):
            rows=pl.ds(pl.multiple_of(s*own+k*part,part),part)
            min_out[rows,:]=(normed_out[rows,:]*small[1:2]+small[3:4]).astype(bf)
            return carry
        lax.fori_loop(0,4,feed,0)
        for _ in range(6):
            if sb: sb.pop(0)()
    other=(1-y)*2+c
    for s in range(nb):
        copy(s,other,kv_out.at[s,other],"c",0).wait_recv()
        cp=copy(s,other,kv_out.at[s,other],"c",len(copies)); cp.start(); copies.append(cp)
    for s in sb: s()
    gb[2]()
    lane=lax.broadcasted_iota(jnp.int32,(rows,128),1)<64
    def unpack(d,carry):
        def tile(m,k): return qo_full[d,:,384*m+128*k:384*m+128*k+128].astype(f32)
        for ref,place in ((q_out,[(0,0),(0,1),(1,0)]),(o_out,[(1,1),(2,0),(2,1)])):
            for j in range(ref.shape[2]//128):
                (m0,(k0,h0)),(m1,(k1,h1))=[(h//3,place[h%3]) for h in (2*j,2*j+1)]
                ref[d,:,128*j:128*j+128]=halves(tile(m0,k0),h0,tile(m1,k1),h1,lane).astype(bf)
        return carry
    lax.fori_loop(0,q_out.shape[0],unpack,0)
    for s in range(nb):
        for m in (y*2+1-c,(1-y)*2+1-c): copy(s,m,kv_out.at[s,m],"c",0).wait_recv()
    for cp in copies: cp.wait_send()

def prologue(tokens,cos,sin,wq,wo,wkv,gains,biases,dp,mp,cid):
    nb,own,width=tokens.shape; part,cols=wq.shape
    kvg=jax.ShapeDtypeStruct((part,256),bf); qo=jax.ShapeDtypeStruct((part,2*cols),bf)
    comms=(Gather([kvg],[(0,0,256,"zx")],dp,mp),Gather([qo],[(0,0,256,"zyx"),(0,256,384,"xzy")],dp,mp))
    vm=pl.BlockSpec(memory_space=pltpu.VMEM)
    s=lambda *a: jax.ShapeDtypeStruct(a,bf)
    return pl.pallas_call(functools.partial(prologue_kernel,dp//2,comms),
        in_specs=[vm]*8,out_specs=[vm]*8,
        out_shape=[s(dp,part,width),s(dp,part,width),jax.ShapeDtypeStruct((8,width),f32),jax.ShapeDtypeStruct((nb*own,width),f32),s(nb*own,width),s(nb*own,width),s(nb,mp,own,128),s(width,128)],
        scratch_shapes=[pltpu.VMEM(qo.shape,bf),pltpu.VMEM(kvg.shape,bf),pltpu.VMEM((dp,part,mp*2*cols),bf),pltpu.VMEM((dp,part,256),bf),
                        pltpu.SemaphoreType.DMA((3*nb,)),pltpu.SemaphoreType.DMA((nb,mp))]+comms[0].scratch+comms[1].scratch,
        compiler_params=pltpu.CompilerParams(collective_id=cid,has_side_effects=True,vmem_limit_bytes=60<<20),name="gather_weights")(tokens,cos,sin,wq,wo,wkv,gains.T,biases.T)

NT=(((1,),(1,)),((),()))
NN=(((1,),(0,)),((),()))
def dg(a,b,dn): return lax.dot_general(a,b,dn,preferred_element_type=f32)
def turn(v,cos,sin,back,keys_only=False):
    lane=lax.broadcasted_iota(jnp.int32,v.shape,1)
    other=jnp.where(lane%HD<ROT//2,-pltpu.roll(v,128-ROT//2,1),pltpu.roll(v,ROT//2,1))*sin
    w=v*cos-other if back else v*cos+other
    return jnp.where(lane<HD,w,v) if keys_only else w

class Fold:
    scratch=[pltpu.VMEM((2,2,B,128),bf),pltpu.VMEM((2,2,B,128),bf),pltpu.VMEM((2,B,128),bf),pltpu.VMEM((2,B,128),bf),
             pltpu.SemaphoreType.DMA((6,)),pltpu.SemaphoreType.DMA((2,2)),pltpu.SemaphoreType.DMA((2,))]
    def __init__(self,pos,nz,out,cos,sin,scr):
        self.pos=pos; self.nz=nz; self.out=out; self.cos=cos; self.sin=sin; self.scr=scr
    def copy(self,b,n,src,dst,sem,kind):
        return pltpu.make_async_remote_copy(src,dst,self.scr[4].at[3*b+n],sem,device_id=peer(self.pos,kind,self.nz),device_id_type=MESH)
    def across(self,b,ry):
        low,cbuf=self.scr[:2]
        return self.copy(b,ry,low.at[b,ry],cbuf.at[b,ry],self.scr[5].at[b,ry],"c")
    def far(self,b):
        _,_,ybuf,ysend=self.scr[:4]
        return self.copy(b,2,ysend.at[b],ybuf.at[b],self.scr[6].at[b],"y")
    def one(self,b,part):
        _,_,y,c=self.pos
        for ry in (1,0):
            self.scr[0][b,ry]=part((1-y if ry else y)*2+1-c).astype(bf)
            self.across(b,ry).start()
    def two(self,b,part):
        _,_,y,c=self.pos
        self.across(b,1).wait_recv()
        self.scr[3][b]=(part((1-y)*2+c)+self.scr[1][b,1].astype(f32)).astype(bf)
        self.far(b).start()
    def three(self,b,part):
        _,_,y,c=self.pos
        self.across(b,0).wait_recv(); self.far(b).wait_recv()
        v=part(y*2+c)+self.scr[1][b,0].astype(f32)+self.scr[2][b].astype(f32)
        self.out[b]=turn(v,self.cos[...],self.sin[...],True,True).astype(bf)
        self.across(b,1).wait_send(); self.across(b,0).wait_send(); self.far(b).wait_send()

def attn_kernel(nz,pairs,comm,join,nc,*refs):
    q_ref,do_ref,kv_ref,cos_ref,sin_ref=refs[:5]
    refs=refs[5:]
    if join: prev,refs=refs[:3],refs[3:]
    cin=refs[:nc]
    o_ref,dq_ref,dkv_ref=refs[nc:3+nc]
    cout=refs[3+nc:3+2*nc]
    k2,v2,kvt,acck,accv,ps,mk,ms,ls,ots,dqs=refs[3+2*nc:14+2*nc]
    refs=refs[14+2*nc:]
    rb=lax.axis_index("mp")
    nkb=kv_ref.shape[1]//B
    at=0
    if join:
        dkvs,local,fold,refs=refs[0],refs[1],refs[2:9],refs[9:]
        at=B
        part0=lambda m: prev[2][0,pl.ds(pl.multiple_of(m*B,B),B),:]
        part1=lambda m: dkvs[m]
    own=slice(at,at+B)
    slots=[[] for _ in range(pairs*2*nkb)]
    if comm:
        pos=coords(nz)
        greet(pos,[f"z{k}" for k in range(1,nz)]+["x","y","c"],nz)
        begin,steps,end=comm.build(pos,cin,cout,refs)
        begin()
        for when,s in steps: slots[int((comm.late+(1-comm.late)*when)*len(slots))].append(s)
        if join:
            sums=Fold(pos,nz,dkv_ref,cos_ref,sin_ref,fold)
            sums.one(0,part0)
            slots[len(slots)//6].append(lambda: sums.two(0,part0))
            slots[len(slots)//2].append(lambda: sums.three(0,part0))
            before=[pltpu.make_async_copy(prev[k],r.at[:B],local.at[k]) for k,r in enumerate((o_ref,dq_ref))]
            for cp in before: cp.start()
    def between(pair,kb,base):
        for p in range(pairs):
            todo=[k for k in range(nkb) if slots[(2*p+base)*nkb+k]]
            if not todo: continue
            @pl.when(pair==p)
            def _(p=p,todo=todo):
                for k in todo:
                    @pl.when(kb==k)
                    def _(k=k):
                        for s in slots[(2*p+base)*nkb+k]: s()
    lane=lax.broadcasted_iota(jnp.int32,(B,128),1)<64
    def setup(kb,carry):
        kv=kv_ref[0,pl.ds(pl.multiple_of(kb*B,B),B),:].astype(f32)
        rolled=pltpu.roll(kv,64,1)
        k2[kb]=jnp.where(lane,kv,rolled).astype(bf)
        v2[kb]=jnp.where(lane,rolled,kv).astype(bf)
        kvt[kb]=kv.T.astype(bf)
        acck[kb]=jnp.zeros((B,128),f32); accv[kb]=jnp.zeros((B,128),f32)
        return carry
    lax.fori_loop(0,nkb,setup,0)
    def one(pair,carry):
        cols=pl.ds(pl.multiple_of(pair*128,128),128)
        q=(turn(q_ref[:,cols],cos_ref[...],sin_ref[...],False)*HD**-0.5).astype(bf); do=do_ref[:,cols]
        zero=jnp.zeros_like(q)
        qm=(jnp.where(lane,q,zero),jnp.where(lane,zero,q))
        dom=(jnp.where(lane,do,zero),jnp.where(lane,zero,do))
        ms[...]=jnp.full_like(ms,-1e30); ls[...]=jnp.zeros_like(ls)
        ots[...]=jnp.zeros_like(ots); dqs[...]=jnp.zeros_like(dqs)
        H=range(2)
        def fwd(kb,masked):
            ss=[dg(k2[kb],qm[h],NT) for h in H]
            if masked:
                ki=lax.broadcasted_iota(jnp.int32,(B,B),0); ri=lax.broadcasted_iota(jnp.int32,(B,B),1)
                ss=[jnp.where(ki<=ri,v,-1e30) for v in ss]
            mo=[ms[h] for h in H]
            mn=[jnp.maximum(mo[h],jnp.max(ss[h],axis=0,keepdims=True)) for h in H]
            al=[jnp.exp(mo[h]-mn[h]) for h in H]
            pp=[jnp.exp(ss[h]-mn[h]) for h in H]
            for h in H: ls[h]=ls[h]*al[h]+jnp.sum(pp[h],axis=0,keepdims=True)
            pb=[v.astype(bf) for v in pp]
            for h in H:
                ps[h,kb]=pb[h]
                mk[h,kb]=mn[h]
                ms[h]=mn[h]
            ob=[dg(kvt[kb,64:,:],pb[h],NN) for h in H]
            for h in H: ots[h]=ots[h]*al[h]+ob[h]
        def fstep(kb,carry):
            @pl.when(kb<rb)
            def _(): fwd(kb,False)
            @pl.when(kb==rb)
            def _(): fwd(kb,True)
            between(pair,kb,0)
            return carry
        lax.fori_loop(0,nkb,fstep,0)
        dot_=do.astype(f32).T
        for h in range(2):
            inv=1.0/ls[h]
            ot=ots[h]*inv
            ots[h]=ot
            ls[h]=inv
        delta=[jnp.sum(ots[h]*dot_[64*h:64*h+64,:],axis=0,keepdims=True) for h in range(2)]
        o_ref[own,cols]=jnp.concatenate([ots[0],ots[1]],axis=0).T.astype(bf)
        def bwd(kb):
            dps=[dg(v2[kb],dom[h],NT) for h in H]
            al=[jnp.exp(mk[h,kb]-ms[h])*ls[h] for h in H]
            pp=[ps[h,kb].astype(f32)*al[h] for h in H]
            ds=[(pp[h]*(dps[h]-delta[h])).astype(bf) for h in H]
            pn=[v.astype(bf) for v in pp]
            acck[kb]+=dg(ds[0],qm[0],NN)+dg(ds[1],qm[1],NN)
            accv[kb]+=dg(pn[0],dom[0],NN)+dg(pn[1],dom[1],NN)
            qb=[dg(kvt[kb,:64,:],ds[h],NN) for h in H]
            for h in H: dqs[h]+=qb[h]
        def bstep(kb,carry):
            @pl.when(kb<=rb)
            def _(): bwd(kb)
            between(pair,kb,1)
            return carry
        lax.fori_loop(0,nkb,bstep,0)
        dq_ref[own,cols]=(turn(jnp.concatenate([dqs[0],dqs[1]],axis=0).T,cos_ref[...],sin_ref[...],True)*HD**-0.5).astype(bf)
        return carry
    lax.fori_loop(0,pairs,one,0)
    def flush(kb,carry):
        k=acck[kb]; v=accv[kb]
        k=jnp.where(lane,k+pltpu.roll(k,64,1),v+pltpu.roll(v,64,1))
        if join: dkvs[kb]=k
        else: dkv_ref[0,pl.ds(pl.multiple_of(kb*B,B),B),:]=k
        return carry
    lax.fori_loop(0,nkb,flush,0)
    if join:
        sums.one(1,part1)
        sums.two(1,part1)
    if comm: end()
    if join:
        sums.three(1,part1)
        for cp in before: cp.wait()

def attention(b,q,do,kv,cos,sin,comm,arrays,dp,cid,prev=()):
    S=kv.shape[1]; nkb=S//B; width=q.shape[1]; join=len(prev)>0
    assert not join or (b==1 and nkb==4)
    whole=lambda *shape: pl.BlockSpec(shape,lambda *_: (0,)*len(shape))
    blk=pl.BlockSpec((B,width),lambda *_: (b,0))
    kvs=pl.BlockSpec((1,S,128),lambda *_: (b,0,0))
    hbm=pl.BlockSpec(memory_space=pl.ANY)
    rows=2*B if join else B
    kvout=jax.ShapeDtypeStruct((2,B,128),bf) if join else jax.ShapeDtypeStruct((1,S,128),f32)
    params=dict(vmem_limit_bytes=62<<20)
    if comm: params.update(collective_id=cid,has_side_effects=True)
    return pl.pallas_call(functools.partial(attn_kernel,dp//2,width//128,comm,join,len(arrays)),
      grid_spec=pltpu.PrefetchScalarGridSpec(num_scalar_prefetch=0,grid=(1,),
        in_specs=[blk,blk,kvs,whole(B,128),whole(B,128)]+([hbm,hbm,whole(1,S,128)] if join else [])+(comm.ins if comm else []),
        out_specs=[whole(rows,width),whole(rows,width),whole(*kvout.shape)]+(comm.outs if comm else []),
        scratch_shapes=[pltpu.VMEM((nkb,B,128),bf),pltpu.VMEM((nkb,B,128),bf),pltpu.VMEM((nkb,128,B),bf),pltpu.VMEM((nkb,B,128),f32),pltpu.VMEM((nkb,B,128),f32),
                        pltpu.VMEM((2,nkb,B,B),bf),pltpu.VMEM((2,nkb,1,B),f32),pltpu.VMEM((2,1,B),f32),pltpu.VMEM((2,1,B),f32),pltpu.VMEM((2,64,B),f32),pltpu.VMEM((2,64,B),f32)]
                       +([pltpu.VMEM((nkb,B,128),f32),pltpu.SemaphoreType.DMA((2,))]+Fold.scratch if join else [])
                       +(comm.scratch if comm else [])),
      out_shape=[jax.ShapeDtypeStruct((rows,width),bf),jax.ShapeDtypeStruct((rows,width),bf),kvout]+(comm.shapes if comm else []),
      compiler_params=pltpu.CompilerParams(**params),name="attn")(q,do,kv,cos,sin,*prev,*arrays)


def kv_gather_kernel(nz, own_ref, full_ref, send, recv):
    pos = coords(nz)
    z, x, y, c = pos
    greet(pos, ["y", "c"], nz)
    nb = own_ref.shape[0]
    sent = []

    def go(b, m, src, kind):
        cp = pltpu.make_async_remote_copy(src, full_ref.at[b, m], send.at[len(sent)], recv.at[b, m],
                                          device_id=peer(pos, kind, nz), device_id_type=MESH)
        cp.start()
        sent.append(cp)

    def wait(b, m):
        pltpu.make_async_remote_copy(full_ref.at[b, m], full_ref.at[b, m], send.at[0], recv.at[b, m],
                                     device_id=peer(pos, "c", nz), device_id_type=MESH).wait_recv()

    for b in range(nb):
        go(b, y * 2 + c, own_ref.at[b], "y")
    for b in range(nb):
        go(b, y * 2 + c, own_ref.at[b], "c")
    for b in range(nb):
        full_ref[b, y * 2 + c] = own_ref[b]
    for b in range(nb):
        m = (1 - y) * 2 + c
        wait(b, m)
        go(b, m, full_ref.at[b, m], "c")
    for b in range(nb):
        wait(b, y * 2 + 1 - c)
        wait(b, (1 - y) * 2 + 1 - c)
    for cp in sent:
        cp.wait_send()


def kv_gather(own, dp, cid):
    nb, rows, w = own.shape
    return pl.pallas_call(
        functools.partial(kv_gather_kernel, dp // 2),
        in_specs=[pl.BlockSpec(memory_space=pltpu.VMEM)],
        out_specs=pl.BlockSpec(memory_space=pltpu.VMEM),
        out_shape=jax.ShapeDtypeStruct((nb, 4, rows, w), own.dtype),
        scratch_shapes=[pltpu.SemaphoreType.DMA((3 * nb,)), pltpu.SemaphoreType.DMA((nb, 4))],
        compiler_params=pltpu.CompilerParams(collective_id=cid, has_side_effects=True),
        name="gather_keyval",
    )(own)


def kv_reduce_kernel(nz, n, *refs):
    parts = refs[:n]
    cos_ref, sin_ref, out_ref, low, cbuf, ybuf, ysend, send, crecv, yrecv = refs[n:]
    pos = coords(nz)
    z, x, y, c = pos
    greet(pos, ["y", "c"], nz)
    sent = []

    def go(src, dst, sem, kind):
        cp = pltpu.make_async_remote_copy(src, dst, send.at[len(sent)], sem, device_id=peer(pos, kind, nz), device_id_type=MESH)
        cp.start()
        sent.append(cp)

    def wait(dst, sem):
        pltpu.make_async_remote_copy(dst, dst, send.at[0], sem, device_id=peer(pos, "c", nz), device_id_type=MESH).wait_recv()

    for ry in (1, 0):
        yy = 1 - y if ry else y
        for b in range(n):
            low[b, ry] = parts[b][yy * 2 + 1 - c].astype(bf)
            go(low.at[b, ry], cbuf.at[b, ry], crecv.at[b, ry], "c")
    for b in range(n):
        wait(cbuf.at[b, 1], crecv.at[b, 1])
        ysend[b] = (parts[b][(1 - y) * 2 + c] + cbuf[b, 1].astype(f32)).astype(bf)
        go(ysend.at[b], ybuf.at[b], yrecv.at[b], "y")
    for b in range(n):
        wait(cbuf.at[b, 0], crecv.at[b, 0])
        wait(ybuf.at[b], yrecv.at[b])
        v = parts[b][y * 2 + c] + cbuf[b, 0].astype(f32) + ybuf[b].astype(f32)
        out_ref[b] = turn(v, cos_ref[...], sin_ref[...], True, True).astype(bf)
    for cp in sent:
        cp.wait_send()


def kv_reduce(parts, cos, sin, dp, cid):
    nb = len(parts)
    mp, rows, w = parts[0].shape
    vm = pl.BlockSpec(memory_space=pltpu.VMEM)
    return pl.pallas_call(
        functools.partial(kv_reduce_kernel, dp // 2, nb),
        in_specs=[vm] * (nb + 2),
        out_specs=vm,
        out_shape=jax.ShapeDtypeStruct((nb, rows, w), bf),
        scratch_shapes=[pltpu.VMEM((nb, 2, rows, w), bf), pltpu.VMEM((nb, 2, rows, w), bf), pltpu.VMEM((nb, rows, w), bf),
                        pltpu.VMEM((nb, rows, w), bf), pltpu.SemaphoreType.DMA((3 * nb,)), pltpu.SemaphoreType.DMA((nb, 2)), pltpu.SemaphoreType.DMA((nb,))],
        compiler_params=pltpu.CompilerParams(collective_id=cid, has_side_effects=True),
        name="reduce_keyval",
    )(*parts, cos, sin)


def spread(arrays, inside, dp, mp):
    out = []
    for i, s in enumerate(arrays):
        if i in inside:
            out.append(lax.all_gather(s, "dp"))
        else:
            a = lax.all_gather(s, ("dp", "mp")).reshape((dp, mp) + s.shape)
            out.append(a.transpose(0, 2, 1, 3).reshape(dp, s.shape[0], -1))
    return out


def collect(parts, inside, dp, mp):
    out = []
    for i, p in enumerate(parts):
        p = p.astype(f32)
        if i in inside:
            out.append(lax.psum(lax.psum_scatter(p, "dp", scatter_dimension=0), "mp"))
        else:
            a = p.reshape(dp, p.shape[1], mp, -1).transpose(0, 2, 1, 3).reshape(dp * mp, p.shape[1], -1)
            out.append(lax.psum_scatter(a, ("dp", "mp"), scatter_dimension=0))
    return out


def rotary(position):
    lane = jnp.arange(2 * HD, dtype=jnp.int32)
    inside = lane % HD
    frequency = 10000.0 ** (-2.0 * (inside % (ROT // 2)).astype(f32) / ROT)
    angle = position[:, None].astype(f32) * frequency[None, :]
    turned = (inside < ROT)[None, :]
    return jnp.where(turned, jnp.cos(angle), 1.0), jnp.where(turned, jnp.sin(angle), 0.0)


def plain_prologue(tokens, cos, sin, wq, wo, wkv, gains, biases, dp, mp):
    nb, own, width = tokens.shape
    wq, wo, kvg = spread([wq, wo, jnp.concatenate([wkv, gains, biases], axis=1)], {2}, dp, mp)
    kvg = kvg.reshape(width, -1)
    small = kvg[:, 2 * HD :].astype(f32).T
    x = tokens.reshape(nb * own, width).astype(f32)
    centered = x - jnp.mean(x, axis=1, keepdims=True)
    normed = centered * lax.rsqrt(jnp.mean(centered * centered, axis=1, keepdims=True) + epsilon)
    ain = (normed * small[0] + small[2]).astype(bf)
    mlp_in = (normed * small[1] + small[3]).astype(bf)
    kv = jnp.dot(ain, kvg[:, : 2 * HD], preferred_element_type=f32).reshape(nb, own, 2 * HD)
    first, half = jnp.arange(2 * HD) < HD, ROT // 2
    other = jnp.where(jnp.arange(2 * HD) < half, -jnp.roll(kv, -half, axis=2), jnp.roll(kv, half, axis=2)) * sin
    kv = jnp.where(first, kv * cos + other, kv).astype(bf)
    return wq, wo, jnp.concatenate([small, small]), normed, ain, mlp_in, kv_gather(kv, dp, 3), kvg[:, : 2 * HD]


def shards(tokens, norm_gains, norm_biases, w_query, w_keyval, w_output, w_up, w_down, cotangent, subset_ids, subset_weights):
    dp, mp = lax.axis_size("dp"), lax.axis_size("mp")
    me = lax.axis_index("mp")
    nb, own, width = tokens.shape
    rows = nb * own
    part, cols = w_query.shape
    ff = w_up.shape[1]
    mine = dp == 8
    dot = functools.partial(jnp.dot, preferred_element_type=f32)
    nt = lambda a, b: lax.dot_general(a, b, (((1,), (1,)), ((), ())), preferred_element_type=f32)
    tn = lambda a, b: lax.dot_general(a, b, (((0,), (0,)), ((), ())), preferred_element_type=f32)
    cos, sin = rotary(me * own + jnp.arange(own, dtype=jnp.int32))
    small_weights = (w_query, w_output, w_keyval, norm_gains, norm_biases)
    if mine:
        wq, wo, small, normed, attn_in, mlp_in, kv, wkv = prologue(tokens, cos, sin, *small_weights, dp, mp, 1)
    else:
        wq, wo, small, normed, attn_in, mlp_in, kv, wkv = plain_prologue(tokens, cos, sin, *small_weights, dp, mp)
    wq, wo = wq.reshape(width, width), wo.reshape(width, width)
    kv_full = kv.reshape(nb, mp * own, 2 * HD)
    gain_a, gain_m = small[0], small[1]

    ids = lax.dynamic_slice_in_dim(subset_ids.reshape(nb, mp * own), me * own, own, 1).reshape(rows)
    matches = ids[:, None] == jnp.arange(subset_weights.shape[0], dtype=jnp.int32)[None, :]
    scale = jnp.sum(jnp.where(matches, subset_weights[None, :], 0.0), axis=1, keepdims=True)
    g = (cotangent.reshape(rows, width).astype(f32) * scale).astype(bf)

    q = dot(attn_in, wq)
    grad_heads = dot(g, wo).astype(bf)
    mlp_plan = lambda a, b: [(0, 0, 768, a), (1, 0, 256, a), (1, 256, 768, b)]
    if mine:
        o0, dq0, dkv0, up, down = attention(0, q, grad_heads, kv_full, cos, sin, Gather([w_up, w_down], mlp_plan("zyx", "xzy"), dp, mp), [w_up, w_down], dp, 5)
    else:
        o0, dq0, dkv0 = attention(0, q, grad_heads, kv_full, cos, sin, None, [], dp, 5)
        up, down = spread([w_up, w_down], (), dp, mp)
    up = up.reshape(width, mp * ff)
    down = down.reshape(width, mp * ff)

    pre = dot(mlp_in, up)
    cdf = 0.5 * (1.0 + lax.erf(pre * sqrt_half))
    hidden = (pre * cdf).astype(bf)
    slope = (cdf + pre * (jnp.exp(-0.5 * pre * pre) * inv_sqrt_two_pi)).astype(bf)
    hidden, slope = lax.optimization_barrier((hidden, slope))
    dpre = (dot(g, down) * slope).astype(bf)
    gup = tn(mlp_in, dpre).astype(bf).reshape(dp, part, mp * ff)
    gdown = tn(g, hidden).astype(bf).reshape(dp, part, mp * ff)
    if mine:
        o, dqp, dkvp, grad_up, grad_down = attention(1, q, grad_heads, kv_full, cos, sin, Scatter([gup, gdown], mlp_plan("xyz", "yzx"), dp, mp), [gup, gdown], dp, 6, (o0, dq0, dkv0))
    else:
        o1, dq1, dkv1 = attention(1, q, grad_heads, kv_full, cos, sin, None, [], dp, 6)
        grad_up, grad_down = collect([gup, gdown], (), dp, mp)
        dkvp = kv_reduce([d.reshape(mp, own, 2 * HD) for d in (dkv0, dkv1)], cos, sin, dp, 4)
        o = jnp.concatenate([o0, o1])
        dqp = jnp.concatenate([dq0, dq1])
    dkvp = dkvp.reshape(rows, 2 * HD)

    dmlp = nt(dpre, up)
    dattn = nt(dqp, wq) + nt(dkvp, wkv)
    dnormed = dattn * gain_a + dmlp * gain_m
    sums = [jnp.sum(dattn * normed, axis=0), jnp.sum(dmlp * normed, axis=0), jnp.sum(dattn, axis=0), jnp.sum(dmlp, axis=0)]
    gq = tn(attn_in, dqp).astype(bf).reshape(dp, part, width)
    go = tn(g, o).astype(bf).reshape(dp, part, width)
    gkv = tn(attn_in, dkvp).reshape(dp, part, 2 * HD)
    k = 2 * HD
    if mine:
        sums = jnp.concatenate([s[None] for s in sums] + [jnp.zeros((4, width), f32)])
        flat = lambda a: a.reshape(rows, width)
        grad_query, grad_output, grad_keyval, gb, out, input_grad = scatter_small(gq, go, gkv, sums, o, wo, hidden, down, flat(tokens), flat(cotangent), scale, dnormed, dp, mp, 2)
        grad_gains, grad_biases = gb[:2].T, gb[2:4].T
    else:
        x = tokens.reshape(rows, width).astype(f32)
        out = (x + nt(o, wo) + nt(hidden, down)).astype(bf)
        centered = x - jnp.mean(x, axis=1, keepdims=True)
        inverse = lax.rsqrt(jnp.mean(centered * centered, axis=1, keepdims=True) + epsilon)
        dx = (dnormed - jnp.mean(dnormed, axis=1, keepdims=True) - normed * jnp.mean(dnormed * normed, axis=1, keepdims=True)) * inverse
        input_grad = (cotangent.reshape(rows, width).astype(f32) * scale + dx).astype(bf)
        gkvg = jnp.concatenate([gkv, jnp.stack(sums, axis=1).reshape(dp, part, 4)], axis=2)
        grad_query, grad_output, c = collect([gq, go, gkvg], {2}, dp, mp)
        grad_keyval, grad_gains, grad_biases = c[:, :k], c[:, k : k + 2], c[:, k + 2 : k + 4]
    return (
        out.reshape(tokens.shape),
        kv_full.reshape(-1, 2 * HD),
        input_grad.reshape(tokens.shape),
        grad_gains,
        grad_biases,
        grad_query,
        grad_keyval,
        grad_output,
        grad_up,
        grad_down,
    )


def solution(mesh):
    rows = P(None, ("dp", "mp"), None)
    d, dm = P("dp", None), P("dp", "mp")
    return jax.shard_map(
        shards,
        mesh=mesh,
        in_specs=(rows, d, d, dm, d, dm, dm, dm, rows, P("dp"), P()),
        out_specs=(rows, d, rows, d, d, dm, d, dm, dm, dm),
        check_vma=False,
    )
```

```python
import functools

import jax
import jax.numpy as jnp
from jax import lax
from jax.experimental import pallas as pl
from jax.experimental.pallas import tpu as pltpu
from jax.sharding import PartitionSpec as P

f32 = jnp.float32
bf = jnp.bfloat16
MESH = pl.DeviceIdType.MESH
HD = 64
ROT = 16
B = 512
SEQ_LEN = 2048
epsilon = 1e-05
sqrt_half = 0.7071067811865476
inv_sqrt_two_pi = 0.3989422804014327


def coords(nz):
    d=lax.axis_index("dp"); m=lax.axis_index("mp")
    return d//2, d%2, m//2, m%2

def peer(pos,kind,nz):
    z,x,y,c=pos
    if kind[0]=="z": z=lax.rem(z+int(kind[1:]),nz)
    if kind=="x": x=1-x
    if kind=="y": y=1-y
    if kind=="c": c=1-c
    return (z*2+x, y*2+c)

def greet(pos,kinds,nz):
    bar=pltpu.get_barrier_semaphore()
    for k in kinds:
        pl.semaphore_signal(bar,inc=1,device_id=peer(pos,k,nz),device_id_type=MESH)
    pl.semaphore_wait(bar,len(kinds))

def gather_routes(order,nz):
    zs=[f"z{k}" for k in range(1,nz)]
    out=[]
    if order=="zyx":
        out.append(((0,0,0),zs+["y","x","c"]))
        out+=[((k,0,0),["y","x","c"]) for k in range(1,nz)]
        out+=[((k,0,1),["x","c"]) for k in range(nz)]
        out+=[((k,1,r),["c"]) for r in (0,1) for k in range(nz)]
    elif order=="xzy":
        out.append(((0,0,0),["x"]+zs+["y","c"]))
        out.append(((0,1,0),zs+["y","c"]))
        out+=[((k,r,0),["y","c"]) for k in range(1,nz) for r in (0,1)]
        out+=[((k,r,1),["c"]) for k in range(nz) for r in (0,1)]
    elif order=="zx":
        out.append(((0,0,0),zs+["x"]))
        out+=[((k,0,0),["x"]) for k in range(1,nz)]
        out+=[((k,1,0),[]) for k in range(nz)]
    return out

def columns(m,w,lo,hi):
    return pl.ds(pl.multiple_of(m*w+lo,128),hi-lo)

class Gather:
    late=0.42
    def __init__(self,shards,plan,dp,mp):
        self.plan=plan; self.nz=dp//2; self.mp=mp; self.dp=dp
        inside={i for i,_,_,o in plan if o=="zx"}
        self.ins=[pl.BlockSpec(memory_space=pltpu.VMEM)]*len(shards)
        self.outs=[pl.BlockSpec(memory_space=pl.ANY)]*len(shards)
        self.shapes=[jax.ShapeDtypeStruct((dp,s.shape[0],s.shape[1]*(1 if i in inside else mp)),s.dtype) for i,s in enumerate(shards)]
        sends=sum(len(f) for _,_,_,o in plan for _,f in gather_routes(o,self.nz))
        self.scratch=[pltpu.SemaphoreType.DMA((sends,)),pltpu.SemaphoreType.DMA((len(plan),mp,dp)),pltpu.SemaphoreType.DMA((len(shards),))]
    def build(self,pos,shards,full,scr):
        send,recv,local=scr
        nz=self.nz; z,x,y,c=pos
        routes=[gather_routes(o,nz) for _,_,_,o in self.plan]
        sent=[]
        def where(p,rel,other):
            i,lo,hi,order=self.plan[p]; k,rx,ry=rel
            zz=lax.rem(z+nz-k,nz); xx=1-x if rx else x; yy=1-y if ry else y
            d=zz*2+xx; m=yy*2+(1-c if other else c)
            if order=="zx": return full[i].at[d,:,lo:hi],recv.at[p,0,d]
            return full[i].at[d,:,columns(m,shards[i].shape[1],lo,hi)],recv.at[p,m,d]
        def arrived(p,rel,other):
            dst,sem=where(p,rel,other)
            pltpu.make_async_remote_copy(dst,dst,send.at[0],sem,device_id=peer(pos,"c",nz),device_id_type=MESH).wait_recv()
        def copy(p,rel,f,own,n):
            i,lo,hi,_=self.plan[p]
            dst,sem=where(p,rel,False)
            src=shards[i].at[:,lo:hi] if own else dst
            return pltpu.make_async_remote_copy(src,dst,send.at[n],sem,device_id=peer(pos,f,nz),device_id_type=MESH)
        def step(p,s):
            rel,fw=routes[p][s]
            base=len(sent)
            cps=[functools.partial(copy,p,rel,f,s==0,base+j) for j,f in enumerate(fw)]
            sent.extend(cps)
            def go():
                if s: arrived(p,rel,False)
                for cp in cps: cp().start()
            return go
        def mine(i):
            order=[o for j,_,_,o in self.plan if j==i][0]
            d=z*2+x; w=shards[i].shape[1]
            dst=full[i].at[d] if order=="zx" else full[i].at[d,:,columns(y*2+c,w,0,w)]
            return pltpu.make_async_copy(shards[i],dst,local.at[i])
        first=[step(p,0) for p in range(len(self.plan))]
        steps=[]
        longest=max(len(r) for r in routes)
        for s in range(1,longest):
            for p,r in enumerate(routes):
                if s<len(r): steps.append(((s-1)/(longest-1),step(p,s)))
        def begin():
            for g in first: g()
            for i in range(len(shards)): mine(i).start()
        def end():
            for p,r in enumerate(routes):
                if self.plan[p][3]=="zx": continue
                for rel,_ in r: arrived(p,rel,True)
            for cp in sent: cp().wait_send()
            for i in range(len(shards)): mine(i).wait()
        return begin,steps,end

class Scatter:
    loop=False
    late=0.0
    def __init__(self,parts,plan,dp,mp):
        self.plan=plan; nz=self.nz=dp//2; self.mp=mp
        self.width=[]
        for i,p in enumerate(parts):
            inside=[o for j,_,_,o in plan if j==i][0]=="xz"
            self.width.append(p.shape[-1]//(1 if inside else mp))
        self.ins=[pl.BlockSpec(memory_space=pl.ANY)]*len(parts)
        self.outs=[pl.BlockSpec(memory_space=pltpu.VMEM)]*len(parts)
        self.shapes=[jax.ShapeDtypeStruct((p.shape[1],w),f32) for p,w in zip(parts,self.width)]
        scr=[]; sends=0
        for i,lo,hi,order in plan:
            rows=parts[i].shape[1]; w=hi-lo
            b=lambda k: pltpu.VMEM((k,rows,w),bf)
            nb=nz*4 if order!="xz" else nz*2
            scr+=[b(nb),b(nb)]
            if order=="xyz": scr+=[b(nz*2),b(nz),b(nz)]; sends+=nb+2*nz+nz+nz-1
            elif order=="yzx": scr+=[b(1),b(nz*2),b(nz*2)]; sends+=nb+2*nz+2*(nz-1)+1
            else: scr+=[b(nz*2),b(nz),b(2*nz)]; sends+=nb+nz+nz+nz-1
        n=len(plan)
        self.scratch=scr+[pltpu.SemaphoreType.DMA((n,4*nz)),pltpu.SemaphoreType.DMA((sends,)),pltpu.SemaphoreType.DMA((n,4*nz)),pltpu.SemaphoreType.DMA((n,2*nz)),pltpu.SemaphoreType.DMA((n,2*nz)),pltpu.SemaphoreType.DMA((n,2*nz))]
    def build(self,pos,parts,outs,scr):
        plan=self.plan; nz=self.nz; z,x,y,c=pos; n=len(plan)
        per=scr[:5*n]; own,send,csem,xsem,ysem,zsem=scr[5*n:]
        sent=[]; begins=[]; steps=[]; ends=[]
        def sender(src,dst,rsem,kind):
            k=len(sent)
            cp=lambda: pltpu.make_async_remote_copy(src(),dst,send.at[k],rsem,device_id=peer(pos,kind,nz),device_id_type=MESH)
            sent.append(cp)
            return lambda: cp().start()
        def wait(dst,rsem):
            pltpu.make_async_remote_copy(dst,dst,send.at[0],rsem,device_id=peer(pos,"c",nz),device_id_type=MESH).wait_recv()
        def part(p,r,cc):
            i,lo,hi,order=plan[p]
            rz,rx,ry=r
            zz=lax.rem(z+rz,nz); xx=1-x if rx else x; yy=1-y if ry else y
            if order=="xz": return parts[i].at[zz*2+xx,:,lo:hi]
            return parts[i].at[zz*2+xx,:,columns(yy*2+cc,self.width[i],lo,hi)]
        def total(dst,*refs):
            step=32 if self.loop and dst.shape[0]%32==0 else dst.shape[0]
            def body(r,carry):
                w=pl.ds(pl.multiple_of(r*step,step),step)
                v=refs[0][w,:].astype(f32)
                for o in refs[1:]: v=v+o[w,:].astype(f32)
                dst[w,:]=v.astype(dst.dtype)
                return carry
            if step==dst.shape[0]: body(0,0)
            else: lax.fori_loop(0,dst.shape[0]//step,body,0)
        down=range(nz-1,-1,-1)
        for p,(i,lo,hi,order) in enumerate(plan):
            acc,cb,xb,yb,zb=per[5*p:5*p+5]
            if order=="xyz": seq=[(k,1,r) for r in (1,0) for k in down]+[(k,0,1) for k in down]+[(k,0,0) for k in down]
            elif order=="yzx": seq=[(k,r,1) for r in (1,0) for k in down]+[(k,1,0) for k in down]+[(k,0,0) for k in down]
            else: seq=[(k,1,0) for k in down]+[(k,0,0) for k in down]
            slot=(lambda r: (r[0]*2+r[1])*2+r[2]) if order!="xz" else (lambda r: r[0]*2+r[1])
            A=lambda r,acc=acc,slot=slot: acc.at[slot(r)]
            def plus(when,p=p):
                def note(f): steps.append((when,f))
                return note
            for t,r in enumerate(seq):
                s=slot(r); rz,rx,ry=r
                begins.append((t,sender(functools.partial(part,p,r,c if order=="xz" else 1-c),cb.at[s],csem.at[p,s],"c")))
                mine=lambda p=p,r=r,s=s,acc=acc: pltpu.make_async_copy(part(p,r,c),acc.at[s],own.at[p,s])
                begins.append((t,lambda mine=mine: mine().start()))
                go=None
                if order in ("xyz","xz") and rx: go=sender(lambda v=A(r): v,xb.at[rz*2+ry],xsem.at[p,rz*2+ry],"x")
                if order=="yzx" and ry: go=sender(lambda v=A(r): v,yb.at[rz*2+rx],ysem.at[p,rz*2+rx],"y")
                @plus(0.22*t/len(seq))
                def _(p=p,s=s,acc=acc,cb=cb,go=go,mine=mine):
                    mine().wait()
                    wait(cb.at[s],csem.at[p,s])
                    total(acc.at[s],acc.at[s],cb.at[s])
                    if go: go()
            if order=="xyz":
                for n_,k in enumerate(down):
                    r=(k,0,1); j=k*2+1
                    go=sender(lambda v=A(r): v,yb.at[k],ysem.at[p,k],"y")
                    @plus(0.24+0.26*n_/nz)
                    def _(p=p,r=r,j=j,A=A,xb=xb,go=go):
                        wait(xb.at[j],xsem.at[p,j]); total(A(r),A(r),xb.at[j])
                        go()
                for n_,k in enumerate(down):
                    r=(k,0,0); j=k*2
                    go=sender(lambda v=A(r): v,zb.at[k],zsem.at[p,k],f"z{k}") if k else None
                    @plus(0.52+0.26*n_/nz)
                    def _(p=p,r=r,j=j,k=k,A=A,xb=xb,yb=yb,go=go):
                        wait(xb.at[j],xsem.at[p,j]); wait(yb.at[k],ysem.at[p,k])
                        if go:
                            total(A(r),A(r),xb.at[j],yb.at[k])
                            go()
                def fin(p=p,i=i,lo=lo,hi=hi,A=A,xb=xb,yb=yb,zb=zb):
                    for k in range(1,nz): wait(zb.at[k],zsem.at[p,k])
                    total(outs[i].at[:,lo:hi],A((0,0,0)),xb.at[0],yb.at[0],*[zb.at[k] for k in range(1,nz)])
                ends.append(fin)
            elif order=="yzx":
                for n_,(rx,k) in enumerate([(rx,k) for rx in (1,0) for k in range(nz-1,0,-1)]):
                    r=(k,rx,0); j=k*2+rx
                    go=sender(lambda v=A(r): v,zb.at[k*2+rx],zsem.at[p,k*2+rx],f"z{k}")
                    @plus(0.24+0.3*n_/(2*nz-2))
                    def _(p=p,r=r,j=j,A=A,yb=yb,go=go):
                        wait(yb.at[j],ysem.at[p,j]); total(A(r),A(r),yb.at[j])
                        go()
                r=(0,1,0)
                go=sender(lambda v=A(r): v,xb.at[0],xsem.at[p,0],"x")
                @plus(0.8)
                def _(p=p,r=r,A=A,yb=yb,zb=zb,go=go):
                    wait(yb.at[1],ysem.at[p,1])
                    for k in range(1,nz): wait(zb.at[k*2+1],zsem.at[p,k*2+1])
                    total(A(r),A(r),yb.at[1],*[zb.at[k*2+1] for k in range(1,nz)])
                    go()
                def fin(p=p,i=i,lo=lo,hi=hi,A=A,xb=xb,yb=yb,zb=zb):
                    wait(yb.at[0],ysem.at[p,0])
                    for k in range(1,nz): wait(zb.at[k*2],zsem.at[p,k*2])
                    wait(xb.at[0],xsem.at[p,0])
                    total(outs[i].at[:,lo:hi],A((0,0,0)),yb.at[0],xb.at[0],*[zb.at[k*2] for k in range(1,nz)])
                ends.append(fin)
            else:
                for n_,k in enumerate(down):
                    r=(k,0,0)
                    go=sender(lambda v=A(r): v,yb.at[k],ysem.at[p,k],"y")
                    @plus(0.24+0.26*n_/nz)
                    def _(p=p,r=r,k=k,A=A,xb=xb,go=go):
                        wait(xb.at[k*2],xsem.at[p,k*2]); total(A(r),A(r),xb.at[k*2])
                        go()
                for n_,k in enumerate(range(nz-1,0,-1)):
                    go=sender(lambda v=zb.at[k]: v,zb.at[nz+k],zsem.at[p,k],f"z{k}")
                    @plus(0.52+0.26*n_/nz)
                    def _(p=p,k=k,A=A,yb=yb,zb=zb,go=go):
                        wait(yb.at[k],ysem.at[p,k]); total(zb.at[k],A((k,0,0)),yb.at[k])
                        go()
                def fin(p=p,i=i,lo=lo,hi=hi,A=A,yb=yb,zb=zb):
                    wait(yb.at[0],ysem.at[p,0])
                    for k in range(1,nz): wait(zb.at[nz+k],zsem.at[p,k])
                    total(outs[i].at[:,lo:hi],A((0,0,0)),yb.at[0],*[zb.at[nz+k] for k in range(1,nz)])
                ends.append(fin)
        begins.sort(key=lambda e: e[0])
        steps.sort(key=lambda e: e[0])
        def begin():
            for _,g in begins: g()
        def end():
            for f in ends: f()
            for cp in sent: cp().wait_send()
        return begin,steps,end

def scatter_kernel(nz,comm,*refs):
    gq_ref,go_ref,sums_ref,scale_ref=refs[:4]
    hosted=refs[4:11]
    outq_ref,outo_ref,outkv_ref,outgb_ref,out_hbm,ig_hbm=refs[11:17]
    refs=refs[17:]
    qo,kvg,a_ref,c_ref,out_ref,ig_ref,osem=refs[:7]
    refs=refs[7:]
    o_ref,wo_ref,hid_ref,down_ref,tok_ref,cot_ref,dn_ref=refs[:7]
    fetch=[pltpu.make_async_copy(h,v,refs[7].at[k]) for k,(h,v) in enumerate(zip(hosted,refs[:7]))]
    for f in fetch: f.start()
    pos=coords(nz)
    greet(pos,[f"z{k}" for k in range(1,nz)]+["x","y","c"],nz)
    rows=gq_ref.shape[1]
    lane=lax.broadcasted_iota(jnp.int32,(rows,128),1)<64
    def tile(ref,d,h): return ref[d,:,128*(h//2):128*(h//2)+128].astype(f32)
    def pack(d,carry):
        for t in range(qo.shape[2]//128):
            m,k=t//3,t%3
            lo,hi=[((gq_ref,3*m),(gq_ref,3*m+1)),((gq_ref,3*m+2),(go_ref,3*m)),((go_ref,3*m+1),(go_ref,3*m+2))][k]
            qo[d,:,128*t:128*t+128]=halves(tile(lo[0],d,lo[1]),lo[1]%2,tile(hi[0],d,hi[1]),hi[1]%2,lane).astype(bf)
        return carry
    lax.fori_loop(0,qo.shape[0],pack,0)
    s=jnp.concatenate([sums_ref[...],jnp.zeros((120,sums_ref.shape[1]),f32)],axis=0).T
    for d in range(kvg.shape[0]):
        kvg[d,:,:128]=gq_ref[d,:,gq_ref.shape[2]-128:]
        kvg[d,:,128:]=s[rows*d:rows*d+rows].astype(bf)
    begin,steps,end=comm.build(pos,(qo,kvg),(a_ref,c_ref),refs[8:])
    begin()
    T=256
    def leave(k,r):
        rows=pl.ds(pl.multiple_of(r*T,T),T)
        src,dst=((out_ref,out_hbm),(ig_ref,ig_hbm))[k]
        return pltpu.make_async_copy(src.at[rows,:],dst.at[rows,:],osem.at[k,r])
    across=out_ref.shape[1]//T; n=out_ref.shape[0]//T*across
    slots=[[] for _ in range(n)]
    for when,s in steps:
        if when<0.23: s()
        else: slots[min(n-1,int(n*(0.33+(when-0.24)*1.15)))].append(s)
    def chunk(it,carry):
        rows=pl.ds(pl.multiple_of(it//across*T,T),T); cols=pl.ds(pl.multiple_of(it%across*T,T),T)
        @pl.when(it%across==0)
        def _():
            v=tok_ref[rows,:].astype(f32)
            v=v-jnp.mean(v,axis=1,keepdims=True)
            inverse=lax.rsqrt(jnp.mean(v*v,axis=1,keepdims=True)+epsilon)
            v=v*inverse
            dn=dn_ref[rows,:]
            dx=(dn-jnp.mean(dn,axis=1,keepdims=True)-v*jnp.mean(dn*v,axis=1,keepdims=True))*inverse
            ig_ref[rows,:]=(cot_ref[rows,:].astype(f32)*scale_ref[rows,:]+dx).astype(bf)
        y=tok_ref[rows,cols].astype(f32)+dg(o_ref[rows,:],wo_ref[cols,:],NT)+dg(hid_ref[rows,:],down_ref[cols,:],NT)
        out_ref[rows,cols]=y.astype(bf)
        @pl.when(it%across==across-1)
        def _():
            for k in range(2): leave(k,it//across).start()
        for k in range(n):
            if slots[k]:
                @pl.when(it==k)
                def _(k=k):
                    for s in slots[k]: s()
        return carry
    for f in fetch: f.wait()
    lax.fori_loop(0,n,chunk,0)
    end()
    a=a_ref[...]; half=a.shape[1]//2
    outq_ref[...]=a[:,:half]; outo_ref[...]=a[:,half:]
    outkv_ref[...]=c_ref[:,:128]
    outgb_ref[...]=c_ref[:,128:].T[:8]
    for r in range(n//across):
        for k in range(2): leave(k,r).wait()

def halves(lo,lo_at,hi,hi_at,lane):
    if lo_at: lo=pltpu.roll(lo,64,1)
    if not hi_at: hi=pltpu.roll(hi,64,1)
    return jnp.where(lane,lo,hi)

def scatter_small(gq,go,sums,o,wo,hidden,down,tokens,cotangent,scale,dnormed,dp,mp,cid):
    hosted=(o,wo,hidden,down,tokens,cotangent,dnormed)
    part=gq.shape[1]; cols=go.shape[2]//mp
    shape=lambda w: jax.ShapeDtypeStruct((dp,gq.shape[1],w),bf)
    qo,kvg=shape(2*go.shape[2]),shape(256)
    comm=Scatter([qo,kvg],[(1,0,256,"xz"),(0,0,256,"xyz"),(0,256,384,"yzx")],dp,mp)
    comm.loop=True
    vm=pl.BlockSpec(memory_space=pltpu.VMEM)
    return pl.pallas_call(functools.partial(scatter_kernel,comm.nz,comm),
        in_specs=[vm]*4+[pl.BlockSpec(memory_space=pl.ANY)]*len(hosted),out_specs=[vm]*4+[pl.BlockSpec(memory_space=pl.ANY)]*2,
        out_shape=[jax.ShapeDtypeStruct(d,f32) for d in ((part,cols),(part,cols),(part,128),(8,part))]+[jax.ShapeDtypeStruct(o.shape,bf)]*2,
        scratch_shapes=[pltpu.VMEM(qo.shape,bf),pltpu.VMEM(kvg.shape,bf),pltpu.VMEM((part,2*cols),f32),pltpu.VMEM((part,256),f32),pltpu.VMEM(o.shape,bf),pltpu.VMEM(o.shape,bf),pltpu.SemaphoreType.DMA((2,o.shape[0]//256))]+[pltpu.VMEM(h.shape,h.dtype) for h in hosted]+[pltpu.SemaphoreType.DMA((len(hosted),))]+comm.scratch,
        compiler_params=pltpu.CompilerParams(collective_id=cid,has_side_effects=True,vmem_limit_bytes=60<<20),name="scatter_grads")(gq,go,sums,scale,*hosted)

def prologue_kernel(nz,comms,*refs):
    tok_ref,cos_ref,sin_ref,wq_ref,wo_ref,wkv_ref,gain_ref,bias_ref=refs[:8]
    q_out,o_out,small_out,normed_out,ain_out,min_out,kv_out,all_out=refs[8:16]
    qo_own,kvg_own,qo_full,kvg_full,wkv_scr,ksend,krecv=refs[16:23]
    pos=coords(nz); z,x,y,c=pos
    greet(pos,[f"z{k}" for k in range(1,nz)]+["x","y","c"],nz)
    rows=wq_ref.shape[0]
    kvg_own[:,:128]=wkv_ref[...]
    kvg_own[:,128:]=jnp.concatenate([gain_ref[...].astype(f32),bias_ref[...].astype(f32),jnp.zeros((124,rows),f32)],axis=0).T.astype(bf)
    g,b=comms
    ga=g.build(pos,(kvg_own,),(kvg_full,),refs[23:26])
    gb=b.build(pos,(qo_own,),(qo_full,),refs[26:29])
    ga[0]()
    wq=wq_ref[...].astype(f32); wo=wo_ref[...].astype(f32)
    qo_own[:,:128]=wq[:,:128].astype(bf)
    qo_own[:,128:256]=jnp.concatenate([wq[:,128:],wo[:,:64]],axis=1).astype(bf)
    qo_own[:,256:]=wo[:,64:].astype(bf)
    gb[0]()
    nb,own,width=tok_ref.shape
    part=own//4
    def norm(k,carry):
        v=tok_ref[k//4,pl.ds(pl.multiple_of(k%4*part,part),part),:].astype(f32)
        v=v-jnp.mean(v,axis=1,keepdims=True)
        normed_out[pl.ds(pl.multiple_of(k*part,part),part),:]=v*lax.rsqrt(jnp.mean(v*v,axis=1,keepdims=True)+epsilon)
        return carry
    lax.fori_loop(0,4*nb,norm,0)
    sa=[s for _,s in ga[1]]; sb=[s for _,s in gb[1]]
    while sa:
        sa.pop(0)()
        if sb: sb.pop(0)()
    ga[2]()
    kvg=kvg_full[...].reshape(width,256)
    small=kvg[:,128:].astype(f32).T
    small_out[...]=small[:8]
    wkv=kvg[:,:128]
    for d in range(q_out.shape[0]): all_out[d,:,width:]=kvg_full[d,:,:128]
    wkv_scr[...]=wkv
    def copy(s,m,src,kind,n):
        return pltpu.make_async_remote_copy(src,kv_out.at[s,m],ksend.at[n],krecv.at[s,m],device_id=peer(pos,kind,nz),device_id_type=MESH)
    copies=[]
    me=y*2+c
    for s in range(nb):
        def project(k,carry):
            w=pl.ds(pl.multiple_of(k*part,part),part); rows=pl.ds(pl.multiple_of(s*own+k*part,part),part)
            ain=(normed_out[rows,:]*small[0:1]+small[2:3]).astype(bf)
            ain_out[rows,:]=ain
            kv_out[s,me,w,:]=turn(dg(ain,wkv_scr[...],NN),cos_ref[w,:],sin_ref[w,:],False,True).astype(bf)
            return carry
        lax.fori_loop(0,4,project,0)
        for kind in ("y","c"):
            cp=copy(s,me,kv_out.at[s,me],kind,len(copies)); cp.start(); copies.append(cp)
        def feed(k,carry):
            rows=pl.ds(pl.multiple_of(s*own+k*part,part),part)
            min_out[rows,:]=(normed_out[rows,:]*small[1:2]+small[3:4]).astype(bf)
            return carry
        lax.fori_loop(0,4,feed,0)
        for _ in range(6):
            if sb: sb.pop(0)()
    other=(1-y)*2+c
    for s in range(nb):
        copy(s,other,kv_out.at[s,other],"c",0).wait_recv()
        cp=copy(s,other,kv_out.at[s,other],"c",len(copies)); cp.start(); copies.append(cp)
    for s in sb: s()
    gb[2]()
    lane=lax.broadcasted_iota(jnp.int32,(rows,128),1)<64
    def unpack(d,carry):
        def tile(m,k): return qo_full[d,:,384*m+128*k:384*m+128*k+128].astype(f32)
        for ref,place in ((q_out,[(0,0),(0,1),(1,0)]),(o_out,[(1,1),(2,0),(2,1)])):
            for j in range(ref.shape[2]//128):
                (m0,(k0,h0)),(m1,(k1,h1))=[(h//3,place[h%3]) for h in (2*j,2*j+1)]
                t=halves(tile(m0,k0),h0,tile(m1,k1),h1,lane).astype(bf)
                ref[d,:,128*j:128*j+128]=t
                if ref is q_out: all_out[d,:,128*j:128*j+128]=t
        return carry
    lax.fori_loop(0,q_out.shape[0],unpack,0)
    for s in range(nb):
        for m in (y*2+1-c,(1-y)*2+1-c): copy(s,m,kv_out.at[s,m],"c",0).wait_recv()
    for cp in copies: cp.wait_send()

def prologue(tokens,cos,sin,wq,wo,wkv,gains,biases,dp,mp,cid):
    nb,own,width=tokens.shape; part,cols=wq.shape
    kvg=jax.ShapeDtypeStruct((part,256),bf); qo=jax.ShapeDtypeStruct((part,2*cols),bf)
    comms=(Gather([kvg],[(0,0,256,"zx")],dp,mp),Gather([qo],[(0,0,256,"zyx"),(0,256,384,"xzy")],dp,mp))
    vm=pl.BlockSpec(memory_space=pltpu.VMEM)
    s=lambda *a: jax.ShapeDtypeStruct(a,bf)
    return pl.pallas_call(functools.partial(prologue_kernel,dp//2,comms),
        in_specs=[vm]*8,out_specs=[vm]*8,
        out_shape=[s(dp,part,width),s(dp,part,width),jax.ShapeDtypeStruct((8,width),f32),jax.ShapeDtypeStruct((nb*own,width),f32),s(nb*own,width),s(nb*own,width),s(nb,mp,own,128),s(dp,part,width+128)],
        scratch_shapes=[pltpu.VMEM(qo.shape,bf),pltpu.VMEM(kvg.shape,bf),pltpu.VMEM((dp,part,mp*2*cols),bf),pltpu.VMEM((dp,part,256),bf),pltpu.VMEM((width,128),bf),
                        pltpu.SemaphoreType.DMA((3*nb,)),pltpu.SemaphoreType.DMA((nb,mp))]+comms[0].scratch+comms[1].scratch,
        compiler_params=pltpu.CompilerParams(collective_id=cid,has_side_effects=True,vmem_limit_bytes=60<<20),name="gather_weights")(tokens,cos,sin,wq,wo,wkv,gains.T,biases.T)

NT=(((1,),(1,)),((),()))
NN=(((1,),(0,)),((),()))
def dg(a,b,dn): return lax.dot_general(a,b,dn,preferred_element_type=f32)
def turn(v,cos,sin,back,keys_only=False):
    lane=lax.broadcasted_iota(jnp.int32,v.shape,1)
    other=jnp.where(lane%HD<ROT//2,-pltpu.roll(v,128-ROT//2,1),pltpu.roll(v,ROT//2,1))*sin
    w=v*cos-other if back else v*cos+other
    return jnp.where(lane<HD,w,v) if keys_only else w

class Fold:
    scratch=[pltpu.VMEM((2,2,B,128),bf),pltpu.VMEM((2,2,B,128),bf),pltpu.VMEM((2,B,128),bf),pltpu.VMEM((2,B,128),bf),
             pltpu.SemaphoreType.DMA((6,)),pltpu.SemaphoreType.DMA((2,2)),pltpu.SemaphoreType.DMA((2,))]
    def __init__(self,pos,nz,out,cos,sin,scr):
        self.pos=pos; self.nz=nz; self.out=out; self.cos=cos; self.sin=sin; self.scr=scr
    def copy(self,b,n,src,dst,sem,kind):
        return pltpu.make_async_remote_copy(src,dst,self.scr[4].at[3*b+n],sem,device_id=peer(self.pos,kind,self.nz),device_id_type=MESH)
    def across(self,b,ry):
        low,cbuf=self.scr[:2]
        return self.copy(b,ry,low.at[b,ry],cbuf.at[b,ry],self.scr[5].at[b,ry],"c")
    def far(self,b):
        _,_,ybuf,ysend=self.scr[:4]
        return self.copy(b,2,ysend.at[b],ybuf.at[b],self.scr[6].at[b],"y")
    def one(self,b,part):
        _,_,y,c=self.pos
        for ry in (1,0):
            self.scr[0][b,ry]=part((1-y if ry else y)*2+1-c).astype(bf)
            self.across(b,ry).start()
    def two(self,b,part):
        _,_,y,c=self.pos
        self.across(b,1).wait_recv()
        self.scr[3][b]=(part((1-y)*2+c)+self.scr[1][b,1].astype(f32)).astype(bf)
        self.far(b).start()
    def three(self,b,part):
        _,_,y,c=self.pos
        self.across(b,0).wait_recv(); self.far(b).wait_recv()
        v=part(y*2+c)+self.scr[1][b,0].astype(f32)+self.scr[2][b].astype(f32)
        self.out[b*B:b*B+B,self.out.shape[1]-128:]=turn(v,self.cos[...],self.sin[...],True,True).astype(bf)
        self.across(b,1).wait_send(); self.across(b,0).wait_send(); self.far(b).wait_send()

def attn_kernel(nz,pairs,comm,join,nc,*refs):
    q_ref,do_ref,kv_ref,cos_ref,sin_ref=refs[:5]
    refs=refs[5:]
    if join: prev,refs=refs[:3],refs[3:]
    cin=refs[:nc]
    o_ref,dq_ref=refs[nc:2+nc]
    refs=refs[2+nc:]
    if not join: dkv_ref,refs=refs[0],refs[1:]
    cout=refs[:nc]
    k2,v2,kvt,acck,accv,ps,mk,ms,ls,ots,dqs=refs[nc:11+nc]
    refs=refs[11+nc:]
    rb=lax.axis_index("mp")
    nkb=kv_ref.shape[1]//B
    at=0
    if join:
        dkvs,local,fold,refs=refs[0],refs[1],refs[2:9],refs[9:]
        at=B
        part0=lambda m: prev[2][0,pl.ds(pl.multiple_of(m*B,B),B),:]
        part1=lambda m: dkvs[m]
    own=slice(at,at+B)
    slots=[[] for _ in range(pairs*2*nkb)]
    if comm:
        pos=coords(nz)
        greet(pos,[f"z{k}" for k in range(1,nz)]+["x","y","c"],nz)
        begin,steps,end=comm.build(pos,cin,cout,refs)
        begin()
        for when,s in steps: slots[int((comm.late+(1-comm.late)*when)*len(slots))].append(s)
        if join:
            sums=Fold(pos,nz,dq_ref,cos_ref,sin_ref,fold)
            sums.one(0,part0)
            slots[len(slots)//6].append(lambda: sums.two(0,part0))
            slots[len(slots)//2].append(lambda: sums.three(0,part0))
            before=[pltpu.make_async_copy(prev[k],r.at[:B,:prev[k].shape[1]],local.at[k]) for k,r in enumerate((o_ref,dq_ref))]
            for cp in before: cp.start()
    def between(pair,kb,base):
        for p in range(pairs):
            todo=[k for k in range(nkb) if slots[(2*p+base)*nkb+k]]
            if not todo: continue
            @pl.when(pair==p)
            def _(p=p,todo=todo):
                for k in todo:
                    @pl.when(kb==k)
                    def _(k=k):
                        for s in slots[(2*p+base)*nkb+k]: s()
    lane=lax.broadcasted_iota(jnp.int32,(B,128),1)<64
    def setup(kb,carry):
        kv=kv_ref[0,pl.ds(pl.multiple_of(kb*B,B),B),:].astype(f32)
        rolled=pltpu.roll(kv,64,1)
        k2[kb]=jnp.where(lane,kv,rolled).astype(bf)
        v2[kb]=jnp.where(lane,rolled,kv).astype(bf)
        kvt[kb]=kv.T.astype(bf)
        acck[kb]=jnp.zeros((B,128),f32); accv[kb]=jnp.zeros((B,128),f32)
        return carry
    lax.fori_loop(0,nkb,setup,0)
    def one(pair,carry):
        cols=pl.ds(pl.multiple_of(pair*128,128),128)
        q=(turn(q_ref[:,cols],cos_ref[...],sin_ref[...],False)*HD**-0.5).astype(bf); do=do_ref[:,cols]
        zero=jnp.zeros_like(q)
        qm=(jnp.where(lane,q,zero),jnp.where(lane,zero,q))
        dom=(jnp.where(lane,do,zero),jnp.where(lane,zero,do))
        ms[...]=jnp.full_like(ms,-1e30); ls[...]=jnp.zeros_like(ls)
        ots[...]=jnp.zeros_like(ots); dqs[...]=jnp.zeros_like(dqs)
        H=range(2)
        def fwd(kb,masked):
            ss=[dg(k2[kb],qm[h],NT) for h in H]
            if masked:
                ki=lax.broadcasted_iota(jnp.int32,(B,B),0); ri=lax.broadcasted_iota(jnp.int32,(B,B),1)
                ss=[jnp.where(ki<=ri,v,-1e30) for v in ss]
            mo=[ms[h] for h in H]
            mn=[jnp.maximum(mo[h],jnp.max(ss[h],axis=0,keepdims=True)) for h in H]
            al=[jnp.exp(mo[h]-mn[h]) for h in H]
            pp=[jnp.exp(ss[h]-mn[h]) for h in H]
            for h in H: ls[h]=ls[h]*al[h]+jnp.sum(pp[h],axis=0,keepdims=True)
            pb=[v.astype(bf) for v in pp]
            for h in H:
                ps[h,kb]=pb[h]
                mk[h,kb]=mn[h]
                ms[h]=mn[h]
            ob=[dg(kvt[kb,64:,:],pb[h],NN) for h in H]
            for h in H: ots[h]=ots[h]*al[h]+ob[h]
        def fstep(kb,carry):
            @pl.when(kb<rb)
            def _(): fwd(kb,False)
            @pl.when(kb==rb)
            def _(): fwd(kb,True)
            between(pair,kb,0)
            return carry
        lax.fori_loop(0,nkb,fstep,0)
        dot_=do.astype(f32).T
        for h in range(2):
            inv=1.0/ls[h]
            ot=ots[h]*inv
            ots[h]=ot
            ls[h]=inv
        delta=[jnp.sum(ots[h]*dot_[64*h:64*h+64,:],axis=0,keepdims=True) for h in range(2)]
        o_ref[own,cols]=jnp.concatenate([ots[0],ots[1]],axis=0).T.astype(bf)
        def bwd(kb):
            dps=[dg(v2[kb],dom[h],NT) for h in H]
            al=[jnp.exp(mk[h,kb]-ms[h])*ls[h] for h in H]
            pp=[ps[h,kb].astype(f32)*al[h] for h in H]
            ds=[(pp[h]*(dps[h]-delta[h])).astype(bf) for h in H]
            pn=[v.astype(bf) for v in pp]
            acck[kb]+=dg(ds[0],qm[0],NN)+dg(ds[1],qm[1],NN)
            accv[kb]+=dg(pn[0],dom[0],NN)+dg(pn[1],dom[1],NN)
            qb=[dg(kvt[kb,:64,:],ds[h],NN) for h in H]
            for h in H: dqs[h]+=qb[h]
        def bstep(kb,carry):
            @pl.when(kb<=rb)
            def _(): bwd(kb)
            between(pair,kb,1)
            return carry
        lax.fori_loop(0,nkb,bstep,0)
        dq_ref[own,cols]=(turn(jnp.concatenate([dqs[0],dqs[1]],axis=0).T,cos_ref[...],sin_ref[...],True)*HD**-0.5).astype(bf)
        return carry
    lax.fori_loop(0,pairs,one,0)
    def flush(kb,carry):
        k=acck[kb]; v=accv[kb]
        k=jnp.where(lane,k+pltpu.roll(k,64,1),v+pltpu.roll(v,64,1))
        if join: dkvs[kb]=k
        else: dkv_ref[0,pl.ds(pl.multiple_of(kb*B,B),B),:]=k
        return carry
    lax.fori_loop(0,nkb,flush,0)
    if join:
        sums.one(1,part1)
        sums.two(1,part1)
    if comm: end()
    if join:
        sums.three(1,part1)
        for cp in before: cp.wait()

def attention(b,q,do,kv,cos,sin,comm,arrays,dp,cid,prev=()):
    S=kv.shape[1]; nkb=S//B; width=q.shape[1]; join=len(prev)>0
    assert not join or (b==1 and nkb==4)
    whole=lambda *shape: pl.BlockSpec(shape,lambda *_: (0,)*len(shape))
    blk=pl.BlockSpec((B,width),lambda *_: (b,0))
    kvs=pl.BlockSpec((1,S,128),lambda *_: (b,0,0))
    hbm=pl.BlockSpec(memory_space=pl.ANY)
    rows=2*B if join else B
    outs=[jax.ShapeDtypeStruct((rows,width),bf),jax.ShapeDtypeStruct((rows,width+128*join),bf)]+([] if join else [jax.ShapeDtypeStruct((1,S,128),f32)])
    params=dict(vmem_limit_bytes=62<<20)
    if comm: params.update(collective_id=cid,has_side_effects=True)
    return pl.pallas_call(functools.partial(attn_kernel,dp//2,width//128,comm,join,len(arrays)),
      grid_spec=pltpu.PrefetchScalarGridSpec(num_scalar_prefetch=0,grid=(1,),
        in_specs=[blk,blk,kvs,whole(B,128),whole(B,128)]+([hbm,hbm,whole(1,S,128)] if join else [])+(comm.ins if comm else []),
        out_specs=[whole(*t.shape) for t in outs]+(comm.outs if comm else []),
        scratch_shapes=[pltpu.VMEM((nkb,B,128),bf),pltpu.VMEM((nkb,B,128),bf),pltpu.VMEM((nkb,128,B),bf),pltpu.VMEM((nkb,B,128),f32),pltpu.VMEM((nkb,B,128),f32),
                        pltpu.VMEM((2,nkb,B,B),bf),pltpu.VMEM((2,nkb,1,B),f32),pltpu.VMEM((2,1,B),f32),pltpu.VMEM((2,1,B),f32),pltpu.VMEM((2,64,B),f32),pltpu.VMEM((2,64,B),f32)]
                       +([pltpu.VMEM((nkb,B,128),f32),pltpu.SemaphoreType.DMA((2,))]+Fold.scratch if join else [])
                       +(comm.scratch if comm else [])),
      out_shape=outs+(comm.shapes if comm else []),
      compiler_params=pltpu.CompilerParams(**params),name="attn")(q,do,kv,cos,sin,*prev,*arrays)


def kv_gather_kernel(nz, own_ref, full_ref, send, recv):
    pos = coords(nz)
    z, x, y, c = pos
    greet(pos, ["y", "c"], nz)
    nb = own_ref.shape[0]
    sent = []

    def go(b, m, src, kind):
        cp = pltpu.make_async_remote_copy(src, full_ref.at[b, m], send.at[len(sent)], recv.at[b, m],
                                          device_id=peer(pos, kind, nz), device_id_type=MESH)
        cp.start()
        sent.append(cp)

    def wait(b, m):
        pltpu.make_async_remote_copy(full_ref.at[b, m], full_ref.at[b, m], send.at[0], recv.at[b, m],
                                     device_id=peer(pos, "c", nz), device_id_type=MESH).wait_recv()

    for b in range(nb):
        go(b, y * 2 + c, own_ref.at[b], "y")
    for b in range(nb):
        go(b, y * 2 + c, own_ref.at[b], "c")
    for b in range(nb):
        full_ref[b, y * 2 + c] = own_ref[b]
    for b in range(nb):
        m = (1 - y) * 2 + c
        wait(b, m)
        go(b, m, full_ref.at[b, m], "c")
    for b in range(nb):
        wait(b, y * 2 + 1 - c)
        wait(b, (1 - y) * 2 + 1 - c)
    for cp in sent:
        cp.wait_send()


def kv_gather(own, dp, cid):
    nb, rows, w = own.shape
    return pl.pallas_call(
        functools.partial(kv_gather_kernel, dp // 2),
        in_specs=[pl.BlockSpec(memory_space=pltpu.VMEM)],
        out_specs=pl.BlockSpec(memory_space=pltpu.VMEM),
        out_shape=jax.ShapeDtypeStruct((nb, 4, rows, w), own.dtype),
        scratch_shapes=[pltpu.SemaphoreType.DMA((3 * nb,)), pltpu.SemaphoreType.DMA((nb, 4))],
        compiler_params=pltpu.CompilerParams(collective_id=cid, has_side_effects=True),
        name="gather_keyval",
    )(own)


def kv_reduce_kernel(nz, n, *refs):
    parts = refs[:n]
    cos_ref, sin_ref, out_ref, low, cbuf, ybuf, ysend, send, crecv, yrecv = refs[n:]
    pos = coords(nz)
    z, x, y, c = pos
    greet(pos, ["y", "c"], nz)
    sent = []

    def go(src, dst, sem, kind):
        cp = pltpu.make_async_remote_copy(src, dst, send.at[len(sent)], sem, device_id=peer(pos, kind, nz), device_id_type=MESH)
        cp.start()
        sent.append(cp)

    def wait(dst, sem):
        pltpu.make_async_remote_copy(dst, dst, send.at[0], sem, device_id=peer(pos, "c", nz), device_id_type=MESH).wait_recv()

    for ry in (1, 0):
        yy = 1 - y if ry else y
        for b in range(n):
            low[b, ry] = parts[b][yy * 2 + 1 - c].astype(bf)
            go(low.at[b, ry], cbuf.at[b, ry], crecv.at[b, ry], "c")
    for b in range(n):
        wait(cbuf.at[b, 1], crecv.at[b, 1])
        ysend[b] = (parts[b][(1 - y) * 2 + c] + cbuf[b, 1].astype(f32)).astype(bf)
        go(ysend.at[b], ybuf.at[b], yrecv.at[b], "y")
    for b in range(n):
        wait(cbuf.at[b, 0], crecv.at[b, 0])
        wait(ybuf.at[b], yrecv.at[b])
        v = parts[b][y * 2 + c] + cbuf[b, 0].astype(f32) + ybuf[b].astype(f32)
        out_ref[b] = turn(v, cos_ref[...], sin_ref[...], True, True).astype(bf)
    for cp in sent:
        cp.wait_send()


def kv_reduce(parts, cos, sin, dp, cid):
    nb = len(parts)
    mp, rows, w = parts[0].shape
    vm = pl.BlockSpec(memory_space=pltpu.VMEM)
    return pl.pallas_call(
        functools.partial(kv_reduce_kernel, dp // 2, nb),
        in_specs=[vm] * (nb + 2),
        out_specs=vm,
        out_shape=jax.ShapeDtypeStruct((nb, rows, w), bf),
        scratch_shapes=[pltpu.VMEM((nb, 2, rows, w), bf), pltpu.VMEM((nb, 2, rows, w), bf), pltpu.VMEM((nb, rows, w), bf),
                        pltpu.VMEM((nb, rows, w), bf), pltpu.SemaphoreType.DMA((3 * nb,)), pltpu.SemaphoreType.DMA((nb, 2)), pltpu.SemaphoreType.DMA((nb,))],
        compiler_params=pltpu.CompilerParams(collective_id=cid, has_side_effects=True),
        name="reduce_keyval",
    )(*parts, cos, sin)


def spread(arrays, inside, dp, mp):
    out = []
    for i, s in enumerate(arrays):
        if i in inside:
            out.append(lax.all_gather(s, "dp"))
        else:
            a = lax.all_gather(s, ("dp", "mp")).reshape((dp, mp) + s.shape)
            out.append(a.transpose(0, 2, 1, 3).reshape(dp, s.shape[0], -1))
    return out


def collect(parts, inside, dp, mp):
    out = []
    for i, p in enumerate(parts):
        p = p.astype(f32)
        if i in inside:
            out.append(lax.psum(lax.psum_scatter(p, "dp", scatter_dimension=0), "mp"))
        else:
            a = p.reshape(dp, p.shape[1], mp, -1).transpose(0, 2, 1, 3).reshape(dp * mp, p.shape[1], -1)
            out.append(lax.psum_scatter(a, ("dp", "mp"), scatter_dimension=0))
    return out


def rotary(position):
    lane = jnp.arange(2 * HD, dtype=jnp.int32)
    inside = lane % HD
    frequency = 10000.0 ** (-2.0 * (inside % (ROT // 2)).astype(f32) / ROT)
    angle = position[:, None].astype(f32) * frequency[None, :]
    turned = (inside < ROT)[None, :]
    return jnp.where(turned, jnp.cos(angle), 1.0), jnp.where(turned, jnp.sin(angle), 0.0)


def plain_prologue(tokens, cos, sin, wq, wo, wkv, gains, biases, dp, mp):
    nb, own, width = tokens.shape
    wq, wo, kvg = spread([wq, wo, jnp.concatenate([wkv, gains, biases], axis=1)], {2}, dp, mp)
    kvg = kvg.reshape(width, -1)
    small = kvg[:, 2 * HD :].astype(f32).T
    x = tokens.reshape(nb * own, width).astype(f32)
    centered = x - jnp.mean(x, axis=1, keepdims=True)
    normed = centered * lax.rsqrt(jnp.mean(centered * centered, axis=1, keepdims=True) + epsilon)
    ain = (normed * small[0] + small[2]).astype(bf)
    mlp_in = (normed * small[1] + small[3]).astype(bf)
    kv = jnp.dot(ain, kvg[:, : 2 * HD], preferred_element_type=f32).reshape(nb, own, 2 * HD)
    first, half = jnp.arange(2 * HD) < HD, ROT // 2
    other = jnp.where(jnp.arange(2 * HD) < half, -jnp.roll(kv, -half, axis=2), jnp.roll(kv, half, axis=2)) * sin
    kv = jnp.where(first, kv * cos + other, kv).astype(bf)
    return wq, wo, jnp.concatenate([small, small]), normed, ain, mlp_in, kv_gather(kv, dp, 3), jnp.concatenate([wq.reshape(width, width), kvg[:, : 2 * HD]], axis=1)


def shards(tokens, norm_gains, norm_biases, w_query, w_keyval, w_output, w_up, w_down, cotangent, subset_ids, subset_weights):
    dp, mp = lax.axis_size("dp"), lax.axis_size("mp")
    me = lax.axis_index("mp")
    nb, own, width = tokens.shape
    rows = nb * own
    part, cols = w_query.shape
    ff = w_up.shape[1]
    mine = dp == 8
    dot = functools.partial(jnp.dot, preferred_element_type=f32)
    nt = lambda a, b: lax.dot_general(a, b, (((1,), (1,)), ((), ())), preferred_element_type=f32)
    tn = lambda a, b: lax.dot_general(a, b, (((0,), (0,)), ((), ())), preferred_element_type=f32)
    cos, sin = rotary(me * own + jnp.arange(own, dtype=jnp.int32))
    small_weights = (w_query, w_output, w_keyval, norm_gains, norm_biases)
    if mine:
        wq, wo, small, normed, attn_in, mlp_in, kv, wqkv = prologue(tokens, cos, sin, *small_weights, dp, mp, 1)
    else:
        wq, wo, small, normed, attn_in, mlp_in, kv, wqkv = plain_prologue(tokens, cos, sin, *small_weights, dp, mp)
    wq, wo, wqkv = wq.reshape(width, width), wo.reshape(width, width), wqkv.reshape(width, -1)
    kv_full = kv.reshape(nb, mp * own, 2 * HD)
    gain_a, gain_m = small[0], small[1]

    ids = lax.dynamic_slice_in_dim(subset_ids.reshape(nb, mp * own), me * own, own, 1).reshape(rows)
    matches = ids[:, None] == jnp.arange(subset_weights.shape[0], dtype=jnp.int32)[None, :]
    scale = jnp.sum(jnp.where(matches, subset_weights[None, :], 0.0), axis=1, keepdims=True)
    g = (cotangent.reshape(rows, width).astype(f32) * scale).astype(bf)

    q = dot(attn_in, wq)
    grad_heads = dot(g, wo).astype(bf)
    mlp_plan = lambda a, b: [(0, 0, 768, a), (1, 0, 256, a), (1, 256, 768, b)]
    if mine:
        o0, dq0, dkv0, up, down = attention(0, q, grad_heads, kv_full, cos, sin, Gather([w_up, w_down], mlp_plan("zyx", "xzy"), dp, mp), [w_up, w_down], dp, 5)
    else:
        o0, dq0, dkv0 = attention(0, q, grad_heads, kv_full, cos, sin, None, [], dp, 5)
        up, down = spread([w_up, w_down], (), dp, mp)
    up = up.reshape(width, mp * ff)
    down = down.reshape(width, mp * ff)

    pre = dot(mlp_in, up)
    cdf = 0.5 * (1.0 + lax.erf(pre * sqrt_half))
    hidden = (pre * cdf).astype(bf)
    slope = (cdf + pre * (jnp.exp(-0.5 * pre * pre) * inv_sqrt_two_pi)).astype(bf)
    hidden, slope = lax.optimization_barrier((hidden, slope))
    dpre = (dot(g, down) * slope).astype(bf)
    gup = tn(mlp_in, dpre).astype(bf).reshape(dp, part, mp * ff)
    gdown = tn(g, hidden).astype(bf).reshape(dp, part, mp * ff)
    if mine:
        o, dqkv, grad_up, grad_down = attention(1, q, grad_heads, kv_full, cos, sin, Scatter([gup, gdown], mlp_plan("xyz", "yzx"), dp, mp), [gup, gdown], dp, 6, (o0, dq0, dkv0))
    else:
        o1, dq1, dkv1 = attention(1, q, grad_heads, kv_full, cos, sin, None, [], dp, 6)
        grad_up, grad_down = collect([gup, gdown], (), dp, mp)
        dkvp = kv_reduce([d.reshape(mp, own, 2 * HD) for d in (dkv0, dkv1)], cos, sin, dp, 4)
        o = jnp.concatenate([o0, o1])
        dqkv = jnp.concatenate([jnp.concatenate([dq0, dq1]), dkvp.reshape(rows, 2 * HD)], axis=1)

    dmlp = nt(dpre, up)
    dattn = nt(dqkv, wqkv)
    dnormed = dattn * gain_a + dmlp * gain_m
    sums = [jnp.sum(dattn * normed, axis=0), jnp.sum(dmlp * normed, axis=0), jnp.sum(dattn, axis=0), jnp.sum(dmlp, axis=0)]
    gq = tn(attn_in, dqkv).astype(bf).reshape(dp, part, -1)
    go = tn(g, o).astype(bf).reshape(dp, part, width)
    k = 2 * HD
    if mine:
        sums = jnp.concatenate([s[None] for s in sums] + [jnp.zeros((4, width), f32)])
        flat = lambda a: a.reshape(rows, width)
        grad_query, grad_output, grad_keyval, gb, out, input_grad = scatter_small(gq, go, sums, o, wo, hidden, down, flat(tokens), flat(cotangent), scale, dnormed, dp, mp, 2)
        grad_gains, grad_biases = gb[:2].T, gb[2:4].T
    else:
        x = tokens.reshape(rows, width).astype(f32)
        out = (x + nt(o, wo) + nt(hidden, down)).astype(bf)
        centered = x - jnp.mean(x, axis=1, keepdims=True)
        inverse = lax.rsqrt(jnp.mean(centered * centered, axis=1, keepdims=True) + epsilon)
        dx = (dnormed - jnp.mean(dnormed, axis=1, keepdims=True) - normed * jnp.mean(dnormed * normed, axis=1, keepdims=True)) * inverse
        input_grad = (cotangent.reshape(rows, width).astype(f32) * scale + dx).astype(bf)
        gq, gkv = gq[:, :, :width], gq[:, :, width:].astype(f32)
        gkvg = jnp.concatenate([gkv, jnp.stack(sums, axis=1).reshape(dp, part, 4)], axis=2)
        grad_query, grad_output, c = collect([gq, go, gkvg], {2}, dp, mp)
        grad_keyval, grad_gains, grad_biases = c[:, :k], c[:, k : k + 2], c[:, k + 2 : k + 4]
    return (
        out.reshape(tokens.shape),
        kv_full.reshape(-1, 2 * HD),
        input_grad.reshape(tokens.shape),
        grad_gains,
        grad_biases,
        grad_query,
        grad_keyval,
        grad_output,
        grad_up,
        grad_down,
    )


def solution(mesh):
    rows = P(None, ("dp", "mp"), None)
    d, dm = P("dp", None), P("dp", "mp")
    return jax.shard_map(
        shards,
        mesh=mesh,
        in_specs=(rows, d, d, dm, d, dm, dm, dm, rows, P("dp"), P()),
        out_specs=(rows, d, rows, d, d, dm, d, dm, dm, dm),
        check_vma=False,
    )
```

```python
import functools

import jax
import jax.numpy as jnp
from jax import lax
from jax.experimental import pallas as pl
from jax.experimental.pallas import tpu as pltpu
from jax.sharding import PartitionSpec as P

f32 = jnp.float32
bf = jnp.bfloat16
MESH = pl.DeviceIdType.MESH
HD = 64
ROT = 16
B = 512
SEQ_LEN = 2048
epsilon = 1e-05
sqrt_half = 0.7071067811865476
inv_sqrt_two_pi = 0.3989422804014327


def coords(nz):
    d=lax.axis_index("dp"); m=lax.axis_index("mp")
    return d//2, d%2, m//2, m%2

def peer(pos,kind,nz):
    z,x,y,c=pos
    if kind[0]=="z": z=lax.rem(z+int(kind[1:]),nz)
    if kind=="x": x=1-x
    if kind=="y": y=1-y
    if kind=="c": c=1-c
    return (z*2+x, y*2+c)

def greet(pos,kinds,nz):
    bar=pltpu.get_barrier_semaphore()
    for k in kinds:
        pl.semaphore_signal(bar,inc=1,device_id=peer(pos,k,nz),device_id_type=MESH)
    pl.semaphore_wait(bar,len(kinds))

def gather_routes(order,nz):
    zs=[f"z{k}" for k in range(1,nz)]
    out=[]
    if order=="zyx":
        out.append(((0,0,0),zs+["y","x","c"]))
        out+=[((k,0,0),["y","x","c"]) for k in range(1,nz)]
        out+=[((k,0,1),["x","c"]) for k in range(nz)]
        out+=[((k,1,r),["c"]) for r in (0,1) for k in range(nz)]
    elif order=="xzy":
        out.append(((0,0,0),["x"]+zs+["y","c"]))
        out.append(((0,1,0),zs+["y","c"]))
        out+=[((k,r,0),["y","c"]) for k in range(1,nz) for r in (0,1)]
        out+=[((k,r,1),["c"]) for k in range(nz) for r in (0,1)]
    elif order=="zx":
        out.append(((0,0,0),zs+["x"]))
        out+=[((k,0,0),["x"]) for k in range(1,nz)]
        out+=[((k,1,0),[]) for k in range(nz)]
    return out

def columns(m,w,lo,hi):
    return pl.ds(pl.multiple_of(m*w+lo,128),hi-lo)

class Gather:
    late=0.42
    def __init__(self,shards,plan,dp,mp):
        self.plan=plan; self.nz=dp//2; self.mp=mp; self.dp=dp
        inside={i for i,_,_,o in plan if o=="zx"}
        self.ins=[pl.BlockSpec(memory_space=pltpu.VMEM)]*len(shards)
        self.outs=[pl.BlockSpec(memory_space=pl.ANY)]*len(shards)
        self.shapes=[jax.ShapeDtypeStruct((dp,s.shape[0],s.shape[1]*(1 if i in inside else mp)),s.dtype) for i,s in enumerate(shards)]
        sends=sum(len(f) for _,_,_,o in plan for _,f in gather_routes(o,self.nz))
        self.scratch=[pltpu.SemaphoreType.DMA((sends,)),pltpu.SemaphoreType.DMA((len(plan),mp,dp)),pltpu.SemaphoreType.DMA((len(shards),))]
    def build(self,pos,shards,full,scr):
        send,recv,local=scr
        nz=self.nz; z,x,y,c=pos
        routes=[gather_routes(o,nz) for _,_,_,o in self.plan]
        sent=[]
        def where(p,rel,other):
            i,lo,hi,order=self.plan[p]; k,rx,ry=rel
            zz=lax.rem(z+nz-k,nz); xx=1-x if rx else x; yy=1-y if ry else y
            d=zz*2+xx; m=yy*2+(1-c if other else c)
            if order=="zx": return full[i].at[d,:,lo:hi],recv.at[p,0,d]
            return full[i].at[d,:,columns(m,shards[i].shape[1],lo,hi)],recv.at[p,m,d]
        def arrived(p,rel,other):
            dst,sem=where(p,rel,other)
            pltpu.make_async_remote_copy(dst,dst,send.at[0],sem,device_id=peer(pos,"c",nz),device_id_type=MESH).wait_recv()
        def copy(p,rel,f,own,n):
            i,lo,hi,_=self.plan[p]
            dst,sem=where(p,rel,False)
            src=shards[i].at[:,lo:hi] if own else dst
            return pltpu.make_async_remote_copy(src,dst,send.at[n],sem,device_id=peer(pos,f,nz),device_id_type=MESH)
        def step(p,s):
            rel,fw=routes[p][s]
            base=len(sent)
            cps=[functools.partial(copy,p,rel,f,s==0,base+j) for j,f in enumerate(fw)]
            sent.extend(cps)
            def go():
                if s: arrived(p,rel,False)
                for cp in cps: cp().start()
            return go
        def mine(i):
            order=[o for j,_,_,o in self.plan if j==i][0]
            d=z*2+x; w=shards[i].shape[1]
            dst=full[i].at[d] if order=="zx" else full[i].at[d,:,columns(y*2+c,w,0,w)]
            return pltpu.make_async_copy(shards[i],dst,local.at[i])
        first=[step(p,0) for p in range(len(self.plan))]
        steps=[]
        longest=max(len(r) for r in routes)
        for s in range(1,longest):
            for p,r in enumerate(routes):
                if s<len(r): steps.append(((s-1)/(longest-1),step(p,s)))
        def begin():
            for g in first: g()
            for i in range(len(shards)): mine(i).start()
        def end():
            for p,r in enumerate(routes):
                if self.plan[p][3]=="zx": continue
                for rel,_ in r: arrived(p,rel,True)
            for cp in sent: cp().wait_send()
            for i in range(len(shards)): mine(i).wait()
        return begin,steps,end

class Scatter:
    loop=False
    late=0.0
    def __init__(self,parts,plan,dp,mp):
        self.plan=plan; nz=self.nz=dp//2; self.mp=mp
        self.width=[]
        for i,p in enumerate(parts):
            inside=[o for j,_,_,o in plan if j==i][0]=="xz"
            self.width.append(p.shape[-1]//(1 if inside else mp))
        self.ins=[pl.BlockSpec(memory_space=pl.ANY)]*len(parts)
        self.outs=[pl.BlockSpec(memory_space=pltpu.VMEM)]*len(parts)
        self.shapes=[jax.ShapeDtypeStruct((p.shape[1],w),f32) for p,w in zip(parts,self.width)]
        scr=[]; sends=0
        for i,lo,hi,order in plan:
            rows=parts[i].shape[1]; w=hi-lo
            b=lambda k: pltpu.VMEM((k,rows,w),bf)
            nb=nz*4 if order!="xz" else nz*2
            scr+=[b(nb),b(nb)]
            if order=="xyz": scr+=[b(nz*2),b(nz),b(nz)]; sends+=nb+2*nz+nz+nz-1
            elif order=="yzx": scr+=[b(1),b(nz*2),b(nz*2)]; sends+=nb+2*nz+2*(nz-1)+1
            else: scr+=[b(nz*2),b(nz),b(2*nz)]; sends+=nb+nz+nz+nz-1
        n=len(plan)
        self.scratch=scr+[pltpu.SemaphoreType.DMA((n,4*nz)),pltpu.SemaphoreType.DMA((sends,)),pltpu.SemaphoreType.DMA((n,4*nz)),pltpu.SemaphoreType.DMA((n,2*nz)),pltpu.SemaphoreType.DMA((n,2*nz)),pltpu.SemaphoreType.DMA((n,2*nz))]
    def build(self,pos,parts,outs,scr):
        plan=self.plan; nz=self.nz; z,x,y,c=pos; n=len(plan)
        per=scr[:5*n]; own,send,csem,xsem,ysem,zsem=scr[5*n:]
        sent=[]; begins=[]; steps=[]; ends=[]
        def sender(src,dst,rsem,kind):
            k=len(sent)
            cp=lambda: pltpu.make_async_remote_copy(src(),dst,send.at[k],rsem,device_id=peer(pos,kind,nz),device_id_type=MESH)
            sent.append(cp)
            return lambda: cp().start()
        def wait(dst,rsem):
            pltpu.make_async_remote_copy(dst,dst,send.at[0],rsem,device_id=peer(pos,"c",nz),device_id_type=MESH).wait_recv()
        def part(p,r,cc):
            i,lo,hi,order=plan[p]
            rz,rx,ry=r
            zz=lax.rem(z+rz,nz); xx=1-x if rx else x; yy=1-y if ry else y
            if order=="xz": return parts[i].at[zz*2+xx,:,lo:hi]
            return parts[i].at[zz*2+xx,:,columns(yy*2+cc,self.width[i],lo,hi)]
        def total(dst,*refs):
            step=32 if self.loop and dst.shape[0]%32==0 else dst.shape[0]
            def body(r,carry):
                w=pl.ds(pl.multiple_of(r*step,step),step)
                v=refs[0][w,:].astype(f32)
                for o in refs[1:]: v=v+o[w,:].astype(f32)
                dst[w,:]=v.astype(dst.dtype)
                return carry
            if step==dst.shape[0]: body(0,0)
            else: lax.fori_loop(0,dst.shape[0]//step,body,0)
        down=range(nz-1,-1,-1)
        for p,(i,lo,hi,order) in enumerate(plan):
            acc,cb,xb,yb,zb=per[5*p:5*p+5]
            if order=="xyz": seq=[(k,1,r) for r in (1,0) for k in down]+[(k,0,1) for k in down]+[(k,0,0) for k in down]
            elif order=="yzx": seq=[(k,r,1) for r in (1,0) for k in down]+[(k,1,0) for k in down]+[(k,0,0) for k in down]
            else: seq=[(k,1,0) for k in down]+[(k,0,0) for k in down]
            slot=(lambda r: (r[0]*2+r[1])*2+r[2]) if order!="xz" else (lambda r: r[0]*2+r[1])
            A=lambda r,acc=acc,slot=slot: acc.at[slot(r)]
            def plus(when,p=p):
                def note(f): steps.append((when,f))
                return note
            for t,r in enumerate(seq):
                s=slot(r); rz,rx,ry=r
                begins.append((t,sender(functools.partial(part,p,r,c if order=="xz" else 1-c),cb.at[s],csem.at[p,s],"c")))
                mine=lambda p=p,r=r,s=s,acc=acc: pltpu.make_async_copy(part(p,r,c),acc.at[s],own.at[p,s])
                begins.append((t,lambda mine=mine: mine().start()))
                go=None
                if order in ("xyz","xz") and rx: go=sender(lambda v=A(r): v,xb.at[rz*2+ry],xsem.at[p,rz*2+ry],"x")
                if order=="yzx" and ry: go=sender(lambda v=A(r): v,yb.at[rz*2+rx],ysem.at[p,rz*2+rx],"y")
                @plus(0.22*t/len(seq))
                def _(p=p,s=s,acc=acc,cb=cb,go=go,mine=mine):
                    mine().wait()
                    wait(cb.at[s],csem.at[p,s])
                    total(acc.at[s],acc.at[s],cb.at[s])
                    if go: go()
            if order=="xyz":
                for n_,k in enumerate(down):
                    r=(k,0,1); j=k*2+1
                    go=sender(lambda v=A(r): v,yb.at[k],ysem.at[p,k],"y")
                    @plus(0.24+0.26*n_/nz)
                    def _(p=p,r=r,j=j,A=A,xb=xb,go=go):
                        wait(xb.at[j],xsem.at[p,j]); total(A(r),A(r),xb.at[j])
                        go()
                for n_,k in enumerate(down):
                    r=(k,0,0); j=k*2
                    go=sender(lambda v=A(r): v,zb.at[k],zsem.at[p,k],f"z{k}") if k else None
                    @plus(0.52+0.26*n_/nz)
                    def _(p=p,r=r,j=j,k=k,A=A,xb=xb,yb=yb,go=go):
                        wait(xb.at[j],xsem.at[p,j]); wait(yb.at[k],ysem.at[p,k])
                        if go:
                            total(A(r),A(r),xb.at[j],yb.at[k])
                            go()
                def fin(p=p,i=i,lo=lo,hi=hi,A=A,xb=xb,yb=yb,zb=zb):
                    for k in range(1,nz): wait(zb.at[k],zsem.at[p,k])
                    total(outs[i].at[:,lo:hi],A((0,0,0)),xb.at[0],yb.at[0],*[zb.at[k] for k in range(1,nz)])
                ends.append(fin)
            elif order=="yzx":
                for n_,(rx,k) in enumerate([(rx,k) for rx in (1,0) for k in range(nz-1,0,-1)]):
                    r=(k,rx,0); j=k*2+rx
                    go=sender(lambda v=A(r): v,zb.at[k*2+rx],zsem.at[p,k*2+rx],f"z{k}")
                    @plus(0.24+0.3*n_/(2*nz-2))
                    def _(p=p,r=r,j=j,A=A,yb=yb,go=go):
                        wait(yb.at[j],ysem.at[p,j]); total(A(r),A(r),yb.at[j])
                        go()
                r=(0,1,0)
                go=sender(lambda v=A(r): v,xb.at[0],xsem.at[p,0],"x")
                @plus(0.8)
                def _(p=p,r=r,A=A,yb=yb,zb=zb,go=go):
                    wait(yb.at[1],ysem.at[p,1])
                    for k in range(1,nz): wait(zb.at[k*2+1],zsem.at[p,k*2+1])
                    total(A(r),A(r),yb.at[1],*[zb.at[k*2+1] for k in range(1,nz)])
                    go()
                def fin(p=p,i=i,lo=lo,hi=hi,A=A,xb=xb,yb=yb,zb=zb):
                    wait(yb.at[0],ysem.at[p,0])
                    for k in range(1,nz): wait(zb.at[k*2],zsem.at[p,k*2])
                    wait(xb.at[0],xsem.at[p,0])
                    total(outs[i].at[:,lo:hi],A((0,0,0)),yb.at[0],xb.at[0],*[zb.at[k*2] for k in range(1,nz)])
                ends.append(fin)
            else:
                for n_,k in enumerate(down):
                    r=(k,0,0)
                    go=sender(lambda v=A(r): v,yb.at[k],ysem.at[p,k],"y")
                    @plus(0.24+0.26*n_/nz)
                    def _(p=p,r=r,k=k,A=A,xb=xb,go=go):
                        wait(xb.at[k*2],xsem.at[p,k*2]); total(A(r),A(r),xb.at[k*2])
                        go()
                for n_,k in enumerate(range(nz-1,0,-1)):
                    go=sender(lambda v=zb.at[k]: v,zb.at[nz+k],zsem.at[p,k],f"z{k}")
                    @plus(0.52+0.26*n_/nz)
                    def _(p=p,k=k,A=A,yb=yb,zb=zb,go=go):
                        wait(yb.at[k],ysem.at[p,k]); total(zb.at[k],A((k,0,0)),yb.at[k])
                        go()
                def fin(p=p,i=i,lo=lo,hi=hi,A=A,yb=yb,zb=zb):
                    wait(yb.at[0],ysem.at[p,0])
                    for k in range(1,nz): wait(zb.at[nz+k],zsem.at[p,k])
                    total(outs[i].at[:,lo:hi],A((0,0,0)),yb.at[0],*[zb.at[nz+k] for k in range(1,nz)])
                ends.append(fin)
        begins.sort(key=lambda e: e[0])
        steps.sort(key=lambda e: e[0])
        def begin():
            for _,g in begins: g()
        def end():
            for f in ends: f()
            for cp in sent: cp().wait_send()
        return begin,steps,end

def scatter_kernel(nz,comm,*refs):
    gq_ref,go_ref,sums_ref,scale_ref=refs[:4]
    hosted=refs[4:11]
    outq_ref,outo_ref,outkv_ref,outgb_ref,out_hbm,ig_hbm=refs[11:17]
    refs=refs[17:]
    qo,kvg,a_ref,c_ref,out_ref,ig_ref,osem=refs[:7]
    refs=refs[7:]
    o_ref,wo_ref,hid_ref,down_ref,tok_ref,cot_ref,dn_ref=refs[:7]
    fetch=[pltpu.make_async_copy(h,v,refs[7].at[k]) for k,(h,v) in enumerate(zip(hosted,refs[:7]))]
    for f in fetch: f.start()
    pos=coords(nz)
    greet(pos,[f"z{k}" for k in range(1,nz)]+["x","y","c"],nz)
    rows=gq_ref.shape[1]
    lane=lax.broadcasted_iota(jnp.int32,(rows,128),1)<64
    def tile(ref,d,h): return ref[d,:,128*(h//2):128*(h//2)+128].astype(f32)
    def pack(d,carry):
        for t in range(qo.shape[2]//128):
            m,k=t//3,t%3
            lo,hi=[((gq_ref,3*m),(gq_ref,3*m+1)),((gq_ref,3*m+2),(go_ref,3*m)),((go_ref,3*m+1),(go_ref,3*m+2))][k]
            qo[d,:,128*t:128*t+128]=halves(tile(lo[0],d,lo[1]),lo[1]%2,tile(hi[0],d,hi[1]),hi[1]%2,lane).astype(bf)
        return carry
    lax.fori_loop(0,qo.shape[0],pack,0)
    s=jnp.concatenate([sums_ref[...],jnp.zeros((120,sums_ref.shape[1]),f32)],axis=0).T
    for d in range(kvg.shape[0]):
        kvg[d,:,:128]=gq_ref[d,:,gq_ref.shape[2]-128:]
        kvg[d,:,128:]=s[rows*d:rows*d+rows].astype(bf)
    begin,steps,end=comm.build(pos,(qo,kvg),(a_ref,c_ref),refs[8:])
    begin()
    T=256
    def leave(k,r):
        rows=pl.ds(pl.multiple_of(r*T,T),T)
        src,dst=((out_ref,out_hbm),(ig_ref,ig_hbm))[k]
        return pltpu.make_async_copy(src.at[rows,:],dst.at[rows,:],osem.at[k,r])
    across=out_ref.shape[1]//T; n=out_ref.shape[0]//T*across
    slots=[[] for _ in range(n)]
    for when,s in steps:
        if when<0.23: s()
        else: slots[min(n-1,int(n*(0.33+(when-0.24)*1.15)))].append(s)
    def chunk(it,carry):
        rows=pl.ds(pl.multiple_of(it//across*T,T),T); cols=pl.ds(pl.multiple_of(it%across*T,T),T)
        @pl.when(it%across==0)
        def _():
            v=tok_ref[rows,:].astype(f32)
            v=v-jnp.mean(v,axis=1,keepdims=True)
            inverse=lax.rsqrt(jnp.mean(v*v,axis=1,keepdims=True)+epsilon)
            v=v*inverse
            dn=dn_ref[rows,:]
            dx=(dn-jnp.mean(dn,axis=1,keepdims=True)-v*jnp.mean(dn*v,axis=1,keepdims=True))*inverse
            ig_ref[rows,:]=(cot_ref[rows,:].astype(f32)*scale_ref[rows,:]+dx).astype(bf)
        y=tok_ref[rows,cols].astype(f32)+dg(o_ref[rows,:],wo_ref[cols,:],NT)+dg(hid_ref[rows,:],down_ref[cols,:],NT)
        out_ref[rows,cols]=y.astype(bf)
        @pl.when(it%across==across-1)
        def _():
            for k in range(2): leave(k,it//across).start()
        for k in range(n):
            if slots[k]:
                @pl.when(it==k)
                def _(k=k):
                    for s in slots[k]: s()
        return carry
    for f in fetch: f.wait()
    lax.fori_loop(0,n,chunk,0)
    end()
    a=a_ref[...]; half=a.shape[1]//2
    outq_ref[...]=a[:,:half]; outo_ref[...]=a[:,half:]
    outkv_ref[...]=c_ref[:,:128]
    outgb_ref[...]=c_ref[:,128:].T[:8]
    for r in range(n//across):
        for k in range(2): leave(k,r).wait()

def halves(lo,lo_at,hi,hi_at,lane):
    if lo_at: lo=pltpu.roll(lo,64,1)
    if not hi_at: hi=pltpu.roll(hi,64,1)
    return jnp.where(lane,lo,hi)

def scatter_small(gq,go,sums,o,wo,hidden,down,tokens,cotangent,scale,dnormed,dp,mp,cid):
    hosted=(o,wo,hidden,down,tokens,cotangent,dnormed)
    part=gq.shape[1]; cols=go.shape[2]//mp
    shape=lambda w: jax.ShapeDtypeStruct((dp,gq.shape[1],w),bf)
    qo,kvg=shape(2*go.shape[2]),shape(256)
    comm=Scatter([qo,kvg],[(1,0,256,"xz"),(0,0,256,"xyz"),(0,256,384,"yzx")],dp,mp)
    comm.loop=True
    vm=pl.BlockSpec(memory_space=pltpu.VMEM)
    return pl.pallas_call(functools.partial(scatter_kernel,comm.nz,comm),
        in_specs=[vm]*4+[pl.BlockSpec(memory_space=pl.ANY)]*len(hosted),out_specs=[vm]*4+[pl.BlockSpec(memory_space=pl.ANY)]*2,
        out_shape=[jax.ShapeDtypeStruct(d,f32) for d in ((part,cols),(part,cols),(part,128),(8,part))]+[jax.ShapeDtypeStruct(o.shape,bf)]*2,
        scratch_shapes=[pltpu.VMEM(qo.shape,bf),pltpu.VMEM(kvg.shape,bf),pltpu.VMEM((part,2*cols),f32),pltpu.VMEM((part,256),f32),pltpu.VMEM(o.shape,bf),pltpu.VMEM(o.shape,bf),pltpu.SemaphoreType.DMA((2,o.shape[0]//256))]+[pltpu.VMEM(h.shape,h.dtype) for h in hosted]+[pltpu.SemaphoreType.DMA((len(hosted),))]+comm.scratch,
        compiler_params=pltpu.CompilerParams(collective_id=cid,has_side_effects=True,vmem_limit_bytes=60<<20),name="scatter_grads")(gq,go,sums,scale,*hosted)

def prologue_kernel(nz,comms,*refs):
    tok_ref,cos_ref,sin_ref,wq_ref,wo_ref,wkv_ref,gain_ref,bias_ref=refs[:8]
    q_out,o_out,small_out,normed_out,aint_out,min_out,kv_out,all_out=refs[8:16]
    qo_own,kvg_own,qo_full,kvg_full,wkv_scr,ain_out,ksend,krecv=refs[16:24]
    pos=coords(nz); z,x,y,c=pos
    greet(pos,[f"z{k}" for k in range(1,nz)]+["x","y","c"],nz)
    rows=wq_ref.shape[0]
    kvg_own[:,:128]=wkv_ref[...]
    kvg_own[:,128:]=jnp.concatenate([gain_ref[...].astype(f32),bias_ref[...].astype(f32),jnp.zeros((124,rows),f32)],axis=0).T.astype(bf)
    g,b=comms
    ga=g.build(pos,(kvg_own,),(kvg_full,),refs[24:27])
    gb=b.build(pos,(qo_own,),(qo_full,),refs[27:30])
    ga[0]()
    wq=wq_ref[...].astype(f32); wo=wo_ref[...].astype(f32)
    qo_own[:,:128]=wq[:,:128].astype(bf)
    qo_own[:,128:256]=jnp.concatenate([wq[:,128:],wo[:,:64]],axis=1).astype(bf)
    qo_own[:,256:]=wo[:,64:].astype(bf)
    gb[0]()
    nb,own,width=tok_ref.shape
    part=own//4
    def norm(k,carry):
        v=tok_ref[k//4,pl.ds(pl.multiple_of(k%4*part,part),part),:].astype(f32)
        v=v-jnp.mean(v,axis=1,keepdims=True)
        normed_out[pl.ds(pl.multiple_of(k*part,part),part),:]=v*lax.rsqrt(jnp.mean(v*v,axis=1,keepdims=True)+epsilon)
        return carry
    lax.fori_loop(0,4*nb,norm,0)
    sa=[s for _,s in ga[1]]; sb=[s for _,s in gb[1]]
    while sa:
        sa.pop(0)()
        if sb: sb.pop(0)()
    ga[2]()
    kvg=kvg_full[...].reshape(width,256)
    small=kvg[:,128:].astype(f32).T
    small_out[...]=small[:8]
    wkv=kvg[:,:128]
    for d in range(all_out.shape[0]): all_out[d,:,width:]=kvg_full[d,:,:128]
    wkv_scr[...]=wkv
    def copy(s,m,src,kind,n):
        return pltpu.make_async_remote_copy(src,kv_out.at[s,m],ksend.at[n],krecv.at[s,m],device_id=peer(pos,kind,nz),device_id_type=MESH)
    copies=[]
    me=y*2+c
    for s in range(nb):
        def project(k,carry):
            w=pl.ds(pl.multiple_of(k*part,part),part); rows=pl.ds(pl.multiple_of(s*own+k*part,part),part)
            ain=normed_out[rows,:]*small[0:1]+small[2:3]
            aint_out[:,rows]=ain.T.astype(bf)
            ain=ain.astype(bf)
            ain_out[rows,:]=ain
            kv_out[s,me,w,:]=turn(dg(ain,wkv_scr[...],NN),cos_ref[w,:],sin_ref[w,:],False,True).astype(bf)
            return carry
        lax.fori_loop(0,4,project,0)
        for kind in ("y","c"):
            cp=copy(s,me,kv_out.at[s,me],kind,len(copies)); cp.start(); copies.append(cp)
        def feed(k,carry):
            rows=pl.ds(pl.multiple_of(s*own+k*part,part),part)
            min_out[rows,:]=(normed_out[rows,:]*small[1:2]+small[3:4]).astype(bf)
            return carry
        lax.fori_loop(0,4,feed,0)
        for _ in range(6):
            if sb: sb.pop(0)()
    other=(1-y)*2+c
    for s in range(nb):
        copy(s,other,kv_out.at[s,other],"c",0).wait_recv()
        cp=copy(s,other,kv_out.at[s,other],"c",len(copies)); cp.start(); copies.append(cp)
    for s in sb: s()
    gb[2]()
    lane=lax.broadcasted_iota(jnp.int32,(rows,128),1)<64
    def unpack(d,carry):
        def tile(m,k): return qo_full[d,:,384*m+128*k:384*m+128*k+128].astype(f32)
        for ref,place in ((all_out,[(0,0),(0,1),(1,0)]),(o_out,[(1,1),(2,0),(2,1)])):
            for j in range(width//128):
                (m0,(k0,h0)),(m1,(k1,h1))=[(h//3,place[h%3]) for h in (2*j,2*j+1)]
                t=halves(tile(m0,k0),h0,tile(m1,k1),h1,lane).astype(bf)
                ref[d,:,128*j:128*j+128]=t
        return carry
    lax.fori_loop(0,all_out.shape[0],unpack,0)
    def queries(k,carry):
        T=own//2
        rows=pl.ds(pl.multiple_of(k*T,T),T); w=pl.ds(pl.multiple_of(k%2*T,T),T)
        v=dg(ain_out[rows,:],all_out[:,:,:width].reshape(width,width),NN)
        for j in range(width//128):
            q_out[rows,128*j:128*j+128]=(turn(v[:,128*j:128*j+128],cos_ref[w,:],sin_ref[w,:],False)*HD**-0.5).astype(bf)
        return carry
    lax.fori_loop(0,2*nb,queries,0)
    for s in range(nb):
        for m in (y*2+1-c,(1-y)*2+1-c): copy(s,m,kv_out.at[s,m],"c",0).wait_recv()
    for cp in copies: cp.wait_send()

def prologue(tokens,cos,sin,wq,wo,wkv,gains,biases,dp,mp,cid):
    nb,own,width=tokens.shape; part,cols=wq.shape
    kvg=jax.ShapeDtypeStruct((part,256),bf); qo=jax.ShapeDtypeStruct((part,2*cols),bf)
    comms=(Gather([kvg],[(0,0,256,"zx")],dp,mp),Gather([qo],[(0,0,256,"zyx"),(0,256,384,"xzy")],dp,mp))
    vm=pl.BlockSpec(memory_space=pltpu.VMEM)
    s=lambda *a: jax.ShapeDtypeStruct(a,bf)
    return pl.pallas_call(functools.partial(prologue_kernel,dp//2,comms),
        in_specs=[vm]*8,out_specs=[vm]*8,
        out_shape=[s(nb*own,width),s(dp,part,width),jax.ShapeDtypeStruct((8,width),f32),jax.ShapeDtypeStruct((nb*own,width),f32),s(width,nb*own),s(nb*own,width),s(nb,mp,own,128),s(dp,part,width+128)],
        scratch_shapes=[pltpu.VMEM(qo.shape,bf),pltpu.VMEM(kvg.shape,bf),pltpu.VMEM((dp,part,mp*2*cols),bf),pltpu.VMEM((dp,part,256),bf),pltpu.VMEM((width,128),bf),pltpu.VMEM((nb*own,width),bf),
                        pltpu.SemaphoreType.DMA((3*nb,)),pltpu.SemaphoreType.DMA((nb,mp))]+comms[0].scratch+comms[1].scratch,
        compiler_params=pltpu.CompilerParams(collective_id=cid,has_side_effects=True,vmem_limit_bytes=60<<20),name="gather_weights")(tokens,cos,sin,wq,wo,wkv,gains.T,biases.T)

NT=(((1,),(1,)),((),()))
NN=(((1,),(0,)),((),()))
def dg(a,b,dn): return lax.dot_general(a,b,dn,preferred_element_type=f32)
def turn(v,cos,sin,back,keys_only=False):
    lane=lax.broadcasted_iota(jnp.int32,v.shape,1)
    other=jnp.where(lane%HD<ROT//2,-pltpu.roll(v,128-ROT//2,1),pltpu.roll(v,ROT//2,1))*sin
    w=v*cos-other if back else v*cos+other
    return jnp.where(lane<HD,w,v) if keys_only else w

class Fold:
    scratch=[pltpu.VMEM((2,2,B,128),bf),pltpu.VMEM((2,2,B,128),bf),pltpu.VMEM((2,B,128),bf),pltpu.VMEM((2,B,128),bf),
             pltpu.SemaphoreType.DMA((6,)),pltpu.SemaphoreType.DMA((2,2)),pltpu.SemaphoreType.DMA((2,))]
    def __init__(self,pos,nz,out,cos,sin,scr):
        self.pos=pos; self.nz=nz; self.out=out; self.cos=cos; self.sin=sin; self.scr=scr
    def copy(self,b,n,src,dst,sem,kind):
        return pltpu.make_async_remote_copy(src,dst,self.scr[4].at[3*b+n],sem,device_id=peer(self.pos,kind,self.nz),device_id_type=MESH)
    def across(self,b,ry):
        low,cbuf=self.scr[:2]
        return self.copy(b,ry,low.at[b,ry],cbuf.at[b,ry],self.scr[5].at[b,ry],"c")
    def far(self,b):
        _,_,ybuf,ysend=self.scr[:4]
        return self.copy(b,2,ysend.at[b],ybuf.at[b],self.scr[6].at[b],"y")
    def one(self,b,part):
        _,_,y,c=self.pos
        for ry in (1,0):
            self.scr[0][b,ry]=part((1-y if ry else y)*2+1-c).astype(bf)
            self.across(b,ry).start()
    def two(self,b,part):
        _,_,y,c=self.pos
        self.across(b,1).wait_recv()
        self.scr[3][b]=(part((1-y)*2+c)+self.scr[1][b,1].astype(f32)).astype(bf)
        self.far(b).start()
    def three(self,b,part):
        _,_,y,c=self.pos
        self.across(b,0).wait_recv(); self.far(b).wait_recv()
        v=part(y*2+c)+self.scr[1][b,0].astype(f32)+self.scr[2][b].astype(f32)
        self.out[b*B:b*B+B,self.out.shape[1]-128:]=turn(v,self.cos[...],self.sin[...],True,True).astype(bf)
        self.across(b,1).wait_send(); self.across(b,0).wait_send(); self.far(b).wait_send()

def attn_kernel(nz,pairs,comm,join,nc,*refs):
    q_ref,do_ref,kv_ref,cos_ref,sin_ref=refs[:5]
    refs=refs[5:]
    if join: prev,refs=refs[:3],refs[3:]
    cin=refs[:nc]
    o_ref,dq_ref=refs[nc:2+nc]
    refs=refs[2+nc:]
    if not join: dkv_ref,refs=refs[0],refs[1:]
    cout=refs[:nc]
    k2,v2,kvt,acck,accv,ps,mk,ms,ls,ots,dqs=refs[nc:11+nc]
    refs=refs[11+nc:]
    rb=lax.axis_index("mp")
    nkb=kv_ref.shape[1]//B
    at=0
    if join:
        dkvs,local,fold,refs=refs[0],refs[1],refs[2:9],refs[9:]
        at=B
        part0=lambda m: prev[2][0,pl.ds(pl.multiple_of(m*B,B),B),:]
        part1=lambda m: dkvs[m]
    own=slice(at,at+B)
    slots=[[] for _ in range(pairs*2*nkb)]
    if comm:
        pos=coords(nz)
        greet(pos,[f"z{k}" for k in range(1,nz)]+["x","y","c"],nz)
        begin,steps,end=comm.build(pos,cin,cout,refs)
        begin()
        for when,s in steps: slots[int((comm.late+(1-comm.late)*when)*len(slots))].append(s)
        if join:
            sums=Fold(pos,nz,dq_ref,cos_ref,sin_ref,fold)
            sums.one(0,part0)
            slots[len(slots)//6].append(lambda: sums.two(0,part0))
            slots[len(slots)//2].append(lambda: sums.three(0,part0))
            before=[pltpu.make_async_copy(prev[k],r.at[:B,:prev[k].shape[1]],local.at[k]) for k,r in enumerate((o_ref,dq_ref))]
            for cp in before: cp.start()
    def between(pair,kb,base):
        for p in range(pairs):
            todo=[k for k in range(nkb) if slots[(2*p+base)*nkb+k]]
            if not todo: continue
            @pl.when(pair==p)
            def _(p=p,todo=todo):
                for k in todo:
                    @pl.when(kb==k)
                    def _(k=k):
                        for s in slots[(2*p+base)*nkb+k]: s()
    lane=lax.broadcasted_iota(jnp.int32,(B,128),1)<64
    def setup(kb,carry):
        kv=kv_ref[0,pl.ds(pl.multiple_of(kb*B,B),B),:].astype(f32)
        rolled=pltpu.roll(kv,64,1)
        k2[kb]=jnp.where(lane,kv,rolled).astype(bf)
        v2[kb]=jnp.where(lane,rolled,kv).astype(bf)
        kvt[kb]=kv.T.astype(bf)
        acck[kb]=jnp.zeros((B,128),f32); accv[kb]=jnp.zeros((B,128),f32)
        return carry
    lax.fori_loop(0,nkb,setup,0)
    def one(pair,carry):
        cols=pl.ds(pl.multiple_of(pair*128,128),128)
        q=q_ref[:,cols]; do=do_ref[:,cols]
        zero=jnp.zeros_like(q)
        qm=(jnp.where(lane,q,zero),jnp.where(lane,zero,q))
        dom=(jnp.where(lane,do,zero),jnp.where(lane,zero,do))
        ms[...]=jnp.full_like(ms,-1e30); ls[...]=jnp.zeros_like(ls)
        ots[...]=jnp.zeros_like(ots); dqs[...]=jnp.zeros_like(dqs)
        H=range(2)
        def fwd(kb,masked):
            ss=[dg(k2[kb],qm[h],NT) for h in H]
            if masked:
                ki=lax.broadcasted_iota(jnp.int32,(B,B),0); ri=lax.broadcasted_iota(jnp.int32,(B,B),1)
                ss=[jnp.where(ki<=ri,v,-1e30) for v in ss]
            mo=[ms[h] for h in H]
            mn=[jnp.maximum(mo[h],jnp.max(ss[h],axis=0,keepdims=True)) for h in H]
            al=[jnp.exp(mo[h]-mn[h]) for h in H]
            pp=[jnp.exp(ss[h]-mn[h]) for h in H]
            for h in H: ls[h]=ls[h]*al[h]+jnp.sum(pp[h],axis=0,keepdims=True)
            pb=[v.astype(bf) for v in pp]
            for h in H:
                ps[h,kb]=pb[h]
                mk[h,kb]=mn[h]
                ms[h]=mn[h]
            ob=[dg(kvt[kb,64:,:],pb[h],NN) for h in H]
            for h in H: ots[h]=ots[h]*al[h]+ob[h]
        def fstep(kb,carry):
            @pl.when(kb<rb)
            def _(): fwd(kb,False)
            @pl.when(kb==rb)
            def _(): fwd(kb,True)
            between(pair,kb,0)
            return carry
        lax.fori_loop(0,nkb,fstep,0)
        dot_=do.astype(f32).T
        for h in range(2):
            inv=1.0/ls[h]
            ot=ots[h]*inv
            ots[h]=ot
            ls[h]=inv
        delta=[jnp.sum(ots[h]*dot_[64*h:64*h+64,:],axis=0,keepdims=True) for h in range(2)]
        o_ref[own,cols]=jnp.concatenate([ots[0],ots[1]],axis=0).T.astype(bf)
        def bwd(kb):
            dps=[dg(v2[kb],dom[h],NT) for h in H]
            al=[jnp.exp(mk[h,kb]-ms[h])*ls[h] for h in H]
            pp=[ps[h,kb].astype(f32)*al[h] for h in H]
            ds=[(pp[h]*(dps[h]-delta[h])).astype(bf) for h in H]
            pn=[v.astype(bf) for v in pp]
            acck[kb]+=dg(ds[0],qm[0],NN)+dg(ds[1],qm[1],NN)
            accv[kb]+=dg(pn[0],dom[0],NN)+dg(pn[1],dom[1],NN)
            qb=[dg(kvt[kb,:64,:],ds[h],NN) for h in H]
            for h in H: dqs[h]+=qb[h]
        def bstep(kb,carry):
            @pl.when(kb<=rb)
            def _(): bwd(kb)
            between(pair,kb,1)
            return carry
        lax.fori_loop(0,nkb,bstep,0)
        dq_ref[own,cols]=(turn(jnp.concatenate([dqs[0],dqs[1]],axis=0).T,cos_ref[...],sin_ref[...],True)*HD**-0.5).astype(bf)
        return carry
    lax.fori_loop(0,pairs,one,0)
    def flush(kb,carry):
        k=acck[kb]; v=accv[kb]
        k=jnp.where(lane,k+pltpu.roll(k,64,1),v+pltpu.roll(v,64,1))
        if join: dkvs[kb]=k
        else: dkv_ref[0,pl.ds(pl.multiple_of(kb*B,B),B),:]=k
        return carry
    lax.fori_loop(0,nkb,flush,0)
    if join:
        sums.one(1,part1)
        sums.two(1,part1)
    if comm: end()
    if join:
        sums.three(1,part1)
        for cp in before: cp.wait()

def attention(b,q,do,kv,cos,sin,comm,arrays,dp,cid,prev=()):
    S=kv.shape[1]; nkb=S//B; width=q.shape[1]; join=len(prev)>0
    assert not join or (b==1 and nkb==4)
    whole=lambda *shape: pl.BlockSpec(shape,lambda *_: (0,)*len(shape))
    blk=pl.BlockSpec((B,width),lambda *_: (b,0))
    kvs=pl.BlockSpec((1,S,128),lambda *_: (b,0,0))
    hbm=pl.BlockSpec(memory_space=pl.ANY)
    rows=2*B if join else B
    outs=[jax.ShapeDtypeStruct((rows,width),bf),jax.ShapeDtypeStruct((rows,width+128*join),bf)]+([] if join else [jax.ShapeDtypeStruct((1,S,128),f32)])
    params=dict(vmem_limit_bytes=62<<20)
    if comm: params.update(collective_id=cid,has_side_effects=True)
    return pl.pallas_call(functools.partial(attn_kernel,dp//2,width//128,comm,join,len(arrays)),
      grid_spec=pltpu.PrefetchScalarGridSpec(num_scalar_prefetch=0,grid=(1,),
        in_specs=[blk,blk,kvs,whole(B,128),whole(B,128)]+([hbm,hbm,whole(1,S,128)] if join else [])+(comm.ins if comm else []),
        out_specs=[whole(*t.shape) for t in outs]+(comm.outs if comm else []),
        scratch_shapes=[pltpu.VMEM((nkb,B,128),bf),pltpu.VMEM((nkb,B,128),bf),pltpu.VMEM((nkb,128,B),bf),pltpu.VMEM((nkb,B,128),f32),pltpu.VMEM((nkb,B,128),f32),
                        pltpu.VMEM((2,nkb,B,B),bf),pltpu.VMEM((2,nkb,1,B),f32),pltpu.VMEM((2,1,B),f32),pltpu.VMEM((2,1,B),f32),pltpu.VMEM((2,64,B),f32),pltpu.VMEM((2,64,B),f32)]
                       +([pltpu.VMEM((nkb,B,128),f32),pltpu.SemaphoreType.DMA((2,))]+Fold.scratch if join else [])
                       +(comm.scratch if comm else [])),
      out_shape=outs+(comm.shapes if comm else []),
      compiler_params=pltpu.CompilerParams(**params),name="attn")(q,do,kv,cos,sin,*prev,*arrays)


def kv_gather_kernel(nz, own_ref, full_ref, send, recv):
    pos = coords(nz)
    z, x, y, c = pos
    greet(pos, ["y", "c"], nz)
    nb = own_ref.shape[0]
    sent = []

    def go(b, m, src, kind):
        cp = pltpu.make_async_remote_copy(src, full_ref.at[b, m], send.at[len(sent)], recv.at[b, m],
                                          device_id=peer(pos, kind, nz), device_id_type=MESH)
        cp.start()
        sent.append(cp)

    def wait(b, m):
        pltpu.make_async_remote_copy(full_ref.at[b, m], full_ref.at[b, m], send.at[0], recv.at[b, m],
                                     device_id=peer(pos, "c", nz), device_id_type=MESH).wait_recv()

    for b in range(nb):
        go(b, y * 2 + c, own_ref.at[b], "y")
    for b in range(nb):
        go(b, y * 2 + c, own_ref.at[b], "c")
    for b in range(nb):
        full_ref[b, y * 2 + c] = own_ref[b]
    for b in range(nb):
        m = (1 - y) * 2 + c
        wait(b, m)
        go(b, m, full_ref.at[b, m], "c")
    for b in range(nb):
        wait(b, y * 2 + 1 - c)
        wait(b, (1 - y) * 2 + 1 - c)
    for cp in sent:
        cp.wait_send()


def kv_gather(own, dp, cid):
    nb, rows, w = own.shape
    return pl.pallas_call(
        functools.partial(kv_gather_kernel, dp // 2),
        in_specs=[pl.BlockSpec(memory_space=pltpu.VMEM)],
        out_specs=pl.BlockSpec(memory_space=pltpu.VMEM),
        out_shape=jax.ShapeDtypeStruct((nb, 4, rows, w), own.dtype),
        scratch_shapes=[pltpu.SemaphoreType.DMA((3 * nb,)), pltpu.SemaphoreType.DMA((nb, 4))],
        compiler_params=pltpu.CompilerParams(collective_id=cid, has_side_effects=True),
        name="gather_keyval",
    )(own)


def kv_reduce_kernel(nz, n, *refs):
    parts = refs[:n]
    cos_ref, sin_ref, out_ref, low, cbuf, ybuf, ysend, send, crecv, yrecv = refs[n:]
    pos = coords(nz)
    z, x, y, c = pos
    greet(pos, ["y", "c"], nz)
    sent = []

    def go(src, dst, sem, kind):
        cp = pltpu.make_async_remote_copy(src, dst, send.at[len(sent)], sem, device_id=peer(pos, kind, nz), device_id_type=MESH)
        cp.start()
        sent.append(cp)

    def wait(dst, sem):
        pltpu.make_async_remote_copy(dst, dst, send.at[0], sem, device_id=peer(pos, "c", nz), device_id_type=MESH).wait_recv()

    for ry in (1, 0):
        yy = 1 - y if ry else y
        for b in range(n):
            low[b, ry] = parts[b][yy * 2 + 1 - c].astype(bf)
            go(low.at[b, ry], cbuf.at[b, ry], crecv.at[b, ry], "c")
    for b in range(n):
        wait(cbuf.at[b, 1], crecv.at[b, 1])
        ysend[b] = (parts[b][(1 - y) * 2 + c] + cbuf[b, 1].astype(f32)).astype(bf)
        go(ysend.at[b], ybuf.at[b], yrecv.at[b], "y")
    for b in range(n):
        wait(cbuf.at[b, 0], crecv.at[b, 0])
        wait(ybuf.at[b], yrecv.at[b])
        v = parts[b][y * 2 + c] + cbuf[b, 0].astype(f32) + ybuf[b].astype(f32)
        out_ref[b] = turn(v, cos_ref[...], sin_ref[...], True, True).astype(bf)
    for cp in sent:
        cp.wait_send()


def kv_reduce(parts, cos, sin, dp, cid):
    nb = len(parts)
    mp, rows, w = parts[0].shape
    vm = pl.BlockSpec(memory_space=pltpu.VMEM)
    return pl.pallas_call(
        functools.partial(kv_reduce_kernel, dp // 2, nb),
        in_specs=[vm] * (nb + 2),
        out_specs=vm,
        out_shape=jax.ShapeDtypeStruct((nb, rows, w), bf),
        scratch_shapes=[pltpu.VMEM((nb, 2, rows, w), bf), pltpu.VMEM((nb, 2, rows, w), bf), pltpu.VMEM((nb, rows, w), bf),
                        pltpu.VMEM((nb, rows, w), bf), pltpu.SemaphoreType.DMA((3 * nb,)), pltpu.SemaphoreType.DMA((nb, 2)), pltpu.SemaphoreType.DMA((nb,))],
        compiler_params=pltpu.CompilerParams(collective_id=cid, has_side_effects=True),
        name="reduce_keyval",
    )(*parts, cos, sin)


def spread(arrays, inside, dp, mp):
    out = []
    for i, s in enumerate(arrays):
        if i in inside:
            out.append(lax.all_gather(s, "dp"))
        else:
            a = lax.all_gather(s, ("dp", "mp")).reshape((dp, mp) + s.shape)
            out.append(a.transpose(0, 2, 1, 3).reshape(dp, s.shape[0], -1))
    return out


def collect(parts, inside, dp, mp):
    out = []
    for i, p in enumerate(parts):
        p = p.astype(f32)
        if i in inside:
            out.append(lax.psum(lax.psum_scatter(p, "dp", scatter_dimension=0), "mp"))
        else:
            a = p.reshape(dp, p.shape[1], mp, -1).transpose(0, 2, 1, 3).reshape(dp * mp, p.shape[1], -1)
            out.append(lax.psum_scatter(a, ("dp", "mp"), scatter_dimension=0))
    return out


def rotary(position):
    lane = jnp.arange(2 * HD, dtype=jnp.int32)
    inside = lane % HD
    frequency = 10000.0 ** (-2.0 * (inside % (ROT // 2)).astype(f32) / ROT)
    angle = position[:, None].astype(f32) * frequency[None, :]
    turned = (inside < ROT)[None, :]
    return jnp.where(turned, jnp.cos(angle), 1.0), jnp.where(turned, jnp.sin(angle), 0.0)


def plain_prologue(tokens, cos, sin, wq, wo, wkv, gains, biases, dp, mp):
    nb, own, width = tokens.shape
    wq, wo, kvg = spread([wq, wo, jnp.concatenate([wkv, gains, biases], axis=1)], {2}, dp, mp)
    kvg = kvg.reshape(width, -1)
    small = kvg[:, 2 * HD :].astype(f32).T
    x = tokens.reshape(nb * own, width).astype(f32)
    centered = x - jnp.mean(x, axis=1, keepdims=True)
    normed = centered * lax.rsqrt(jnp.mean(centered * centered, axis=1, keepdims=True) + epsilon)
    ain = (normed * small[0] + small[2]).astype(bf)
    mlp_in = (normed * small[1] + small[3]).astype(bf)
    kv = jnp.dot(ain, kvg[:, : 2 * HD], preferred_element_type=f32).reshape(nb, own, 2 * HD)
    first, half = jnp.arange(2 * HD) < HD, ROT // 2
    other = jnp.where(jnp.arange(2 * HD) < half, -jnp.roll(kv, -half, axis=2), jnp.roll(kv, half, axis=2)) * sin
    kv = jnp.where(first, kv * cos + other, kv).astype(bf)
    wq = wq.reshape(width, width)
    q = jnp.dot(ain, wq, preferred_element_type=f32).reshape(nb, own, width // 128, 128)
    low = jnp.arange(128) % HD < half
    other = jnp.where(low, -jnp.roll(q, -half, axis=3), jnp.roll(q, half, axis=3)) * sin[:, None, :]
    q = ((q * cos[:, None, :] + other) * HD**-0.5).astype(bf).reshape(nb * own, width)
    return q, wo, jnp.concatenate([small, small]), normed, ain.T, mlp_in, kv_gather(kv, dp, 3), jnp.concatenate([wq, kvg[:, : 2 * HD]], axis=1)


def shards(tokens, norm_gains, norm_biases, w_query, w_keyval, w_output, w_up, w_down, cotangent, subset_ids, subset_weights):
    dp, mp = lax.axis_size("dp"), lax.axis_size("mp")
    me = lax.axis_index("mp")
    nb, own, width = tokens.shape
    rows = nb * own
    part, cols = w_query.shape
    ff = w_up.shape[1]
    mine = dp == 8
    dot = functools.partial(jnp.dot, preferred_element_type=f32)
    nt = lambda a, b: lax.dot_general(a, b, (((1,), (1,)), ((), ())), preferred_element_type=f32)
    tn = lambda a, b: lax.dot_general(a, b, (((0,), (0,)), ((), ())), preferred_element_type=f32)
    cos, sin = rotary(me * own + jnp.arange(own, dtype=jnp.int32))
    small_weights = (w_query, w_output, w_keyval, norm_gains, norm_biases)
    if mine:
        q, wo, small, normed, attn_in_t, mlp_in, kv, wqkv = prologue(tokens, cos, sin, *small_weights, dp, mp, 1)
    else:
        q, wo, small, normed, attn_in_t, mlp_in, kv, wqkv = plain_prologue(tokens, cos, sin, *small_weights, dp, mp)
    wo, wqkv = wo.reshape(width, width), wqkv.reshape(width, -1)
    kv_full = kv.reshape(nb, mp * own, 2 * HD)
    gain_a, gain_m = small[0], small[1]

    ids = lax.dynamic_slice_in_dim(subset_ids.reshape(nb, mp * own), me * own, own, 1).reshape(rows)
    matches = ids[:, None] == jnp.arange(subset_weights.shape[0], dtype=jnp.int32)[None, :]
    scale = jnp.sum(jnp.where(matches, subset_weights[None, :], 0.0), axis=1, keepdims=True)
    g = (cotangent.reshape(rows, width).astype(f32) * scale).astype(bf)

    grad_heads = dot(g, wo).astype(bf)
    mlp_plan = lambda a, b: [(0, 0, 768, a), (1, 0, 256, a), (1, 256, 768, b)]
    if mine:
        o0, dq0, dkv0, up, down = attention(0, q, grad_heads, kv_full, cos, sin, Gather([w_up, w_down], mlp_plan("zyx", "xzy"), dp, mp), [w_up, w_down], dp, 5)
    else:
        o0, dq0, dkv0 = attention(0, q, grad_heads, kv_full, cos, sin, None, [], dp, 5)
        up, down = spread([w_up, w_down], (), dp, mp)
    up = up.reshape(width, mp * ff)
    down = down.reshape(width, mp * ff)

    pre = dot(mlp_in, up)
    cdf = 0.5 * (1.0 + lax.erf(pre * sqrt_half))
    hidden = (pre * cdf).astype(bf)
    slope = (cdf + pre * (jnp.exp(-0.5 * pre * pre) * inv_sqrt_two_pi)).astype(bf)
    hidden, slope = lax.optimization_barrier((hidden, slope))
    dpre = (dot(g, down) * slope).astype(bf)
    gup = tn(mlp_in, dpre).astype(bf).reshape(dp, part, mp * ff)
    gdown = tn(g, hidden).astype(bf).reshape(dp, part, mp * ff)
    if mine:
        o, dqkv, grad_up, grad_down = attention(1, q, grad_heads, kv_full, cos, sin, Scatter([gup, gdown], mlp_plan("xyz", "yzx"), dp, mp), [gup, gdown], dp, 6, (o0, dq0, dkv0))
    else:
        o1, dq1, dkv1 = attention(1, q, grad_heads, kv_full, cos, sin, None, [], dp, 6)
        grad_up, grad_down = collect([gup, gdown], (), dp, mp)
        dkvp = kv_reduce([d.reshape(mp, own, 2 * HD) for d in (dkv0, dkv1)], cos, sin, dp, 4)
        o = jnp.concatenate([o0, o1])
        dqkv = jnp.concatenate([jnp.concatenate([dq0, dq1]), dkvp.reshape(rows, 2 * HD)], axis=1)

    dmlp = nt(dpre, up)
    dattn = nt(dqkv, wqkv)
    dnormed = dattn * gain_a + dmlp * gain_m
    sums = [jnp.sum(dattn * normed, axis=0), jnp.sum(dmlp * normed, axis=0), jnp.sum(dattn, axis=0), jnp.sum(dmlp, axis=0)]
    gq = dot(attn_in_t, dqkv).astype(bf).reshape(dp, part, -1)
    go = tn(g, o).astype(bf).reshape(dp, part, width)
    k = 2 * HD
    if mine:
        sums = jnp.concatenate([s[None] for s in sums] + [jnp.zeros((4, width), f32)])
        flat = lambda a: a.reshape(rows, width)
        grad_query, grad_output, grad_keyval, gb, out, input_grad = scatter_small(gq, go, sums, o, wo, hidden, down, flat(tokens), flat(cotangent), scale, dnormed, dp, mp, 2)
        grad_gains, grad_biases = gb[:2].T, gb[2:4].T
    else:
        x = tokens.reshape(rows, width).astype(f32)
        out = (x + nt(o, wo) + nt(hidden, down)).astype(bf)
        centered = x - jnp.mean(x, axis=1, keepdims=True)
        inverse = lax.rsqrt(jnp.mean(centered * centered, axis=1, keepdims=True) + epsilon)
        dx = (dnormed - jnp.mean(dnormed, axis=1, keepdims=True) - normed * jnp.mean(dnormed * normed, axis=1, keepdims=True)) * inverse
        input_grad = (cotangent.reshape(rows, width).astype(f32) * scale + dx).astype(bf)
        gq, gkv = gq[:, :, :width], gq[:, :, width:].astype(f32)
        gkvg = jnp.concatenate([gkv, jnp.stack(sums, axis=1).reshape(dp, part, 4)], axis=2)
        grad_query, grad_output, c = collect([gq, go, gkvg], {2}, dp, mp)
        grad_keyval, grad_gains, grad_biases = c[:, :k], c[:, k : k + 2], c[:, k + 2 : k + 4]
    return (
        out.reshape(tokens.shape),
        kv_full.reshape(-1, 2 * HD),
        input_grad.reshape(tokens.shape),
        grad_gains,
        grad_biases,
        grad_query,
        grad_keyval,
        grad_output,
        grad_up,
        grad_down,
    )


def solution(mesh):
    rows = P(None, ("dp", "mp"), None)
    d, dm = P("dp", None), P("dp", "mp")
    return jax.shard_map(
        shards,
        mesh=mesh,
        in_specs=(rows, d, d, dm, d, dm, dm, dm, rows, P("dp"), P()),
        out_specs=(rows, d, rows, d, d, dm, d, dm, dm, dm),
        check_vma=False,
    )
```

```python
import functools

import jax
import jax.numpy as jnp
from jax import lax
from jax.experimental import pallas as pl
from jax.experimental.pallas import tpu as pltpu
from jax.sharding import PartitionSpec as P

f32 = jnp.float32
bf = jnp.bfloat16
MESH = pl.DeviceIdType.MESH
HD = 64
ROT = 16
B = 512
SEQ_LEN = 2048
epsilon = 1e-05
sqrt_half = 0.7071067811865476
inv_sqrt_two_pi = 0.3989422804014327


def coords(nz):
    d=lax.axis_index("dp"); m=lax.axis_index("mp")
    return d//2, d%2, m//2, m%2

def peer(pos,kind,nz):
    z,x,y,c=pos
    if kind[0]=="z": z=lax.rem(z+int(kind[1:]),nz)
    if kind=="x": x=1-x
    if kind=="y": y=1-y
    if kind=="c": c=1-c
    return (z*2+x, y*2+c)

def greet(pos,kinds,nz):
    bar=pltpu.get_barrier_semaphore()
    for k in kinds:
        pl.semaphore_signal(bar,inc=1,device_id=peer(pos,k,nz),device_id_type=MESH)
    pl.semaphore_wait(bar,len(kinds))

def gather_routes(order,nz):
    zs=[f"z{k}" for k in range(1,nz)]
    out=[]
    if order=="zyx":
        out.append(((0,0,0),zs+["y","x","c"]))
        out+=[((k,0,0),["y","x","c"]) for k in range(1,nz)]
        out+=[((k,0,1),["x","c"]) for k in range(nz)]
        out+=[((k,1,r),["c"]) for r in (0,1) for k in range(nz)]
    elif order=="xzy":
        out.append(((0,0,0),["x"]+zs+["y","c"]))
        out.append(((0,1,0),zs+["y","c"]))
        out+=[((k,r,0),["y","c"]) for k in range(1,nz) for r in (0,1)]
        out+=[((k,r,1),["c"]) for k in range(nz) for r in (0,1)]
    elif order=="zx":
        out.append(((0,0,0),zs+["x"]))
        out+=[((k,0,0),["x"]) for k in range(1,nz)]
        out+=[((k,1,0),[]) for k in range(nz)]
    return out

def columns(m,w,lo,hi):
    return pl.ds(pl.multiple_of(m*w+lo,128),hi-lo)

class Gather:
    late=0.42
    def __init__(self,shards,plan,dp,mp):
        self.plan=plan; self.nz=dp//2; self.mp=mp; self.dp=dp
        inside={i for i,_,_,o in plan if o=="zx"}
        self.ins=[pl.BlockSpec(memory_space=pltpu.VMEM)]*len(shards)
        self.outs=[pl.BlockSpec(memory_space=pl.ANY)]*len(shards)
        self.shapes=[jax.ShapeDtypeStruct((dp,s.shape[0],s.shape[1]*(1 if i in inside else mp)),s.dtype) for i,s in enumerate(shards)]
        sends=sum(len(f) for _,_,_,o in plan for _,f in gather_routes(o,self.nz))
        self.scratch=[pltpu.SemaphoreType.DMA((sends,)),pltpu.SemaphoreType.DMA((len(plan),mp,dp)),pltpu.SemaphoreType.DMA((len(shards),))]
    def build(self,pos,shards,full,scr):
        send,recv,local=scr
        nz=self.nz; z,x,y,c=pos
        routes=[gather_routes(o,nz) for _,_,_,o in self.plan]
        sent=[]
        def where(p,rel,other):
            i,lo,hi,order=self.plan[p]; k,rx,ry=rel
            zz=lax.rem(z+nz-k,nz); xx=1-x if rx else x; yy=1-y if ry else y
            d=zz*2+xx; m=yy*2+(1-c if other else c)
            if order=="zx": return full[i].at[d,:,lo:hi],recv.at[p,0,d]
            return full[i].at[d,:,columns(m,shards[i].shape[1],lo,hi)],recv.at[p,m,d]
        def arrived(p,rel,other):
            dst,sem=where(p,rel,other)
            pltpu.make_async_remote_copy(dst,dst,send.at[0],sem,device_id=peer(pos,"c",nz),device_id_type=MESH).wait_recv()
        def copy(p,rel,f,own,n):
            i,lo,hi,_=self.plan[p]
            dst,sem=where(p,rel,False)
            src=shards[i].at[:,lo:hi] if own else dst
            return pltpu.make_async_remote_copy(src,dst,send.at[n],sem,device_id=peer(pos,f,nz),device_id_type=MESH)
        def step(p,s):
            rel,fw=routes[p][s]
            base=len(sent)
            cps=[functools.partial(copy,p,rel,f,s==0,base+j) for j,f in enumerate(fw)]
            sent.extend(cps)
            def go():
                if s: arrived(p,rel,False)
                for cp in cps: cp().start()
            return go
        def mine(i):
            order=[o for j,_,_,o in self.plan if j==i][0]
            d=z*2+x; w=shards[i].shape[1]
            dst=full[i].at[d] if order=="zx" else full[i].at[d,:,columns(y*2+c,w,0,w)]
            return pltpu.make_async_copy(shards[i],dst,local.at[i])
        first=[step(p,0) for p in range(len(self.plan))]
        steps=[]
        longest=max(len(r) for r in routes)
        for s in range(1,longest):
            for p,r in enumerate(routes):
                if s<len(r): steps.append(((s-1)/(longest-1),step(p,s)))
        def begin():
            for g in first: g()
            for i in range(len(shards)): mine(i).start()
        def end():
            for p,r in enumerate(routes):
                if self.plan[p][3]=="zx": continue
                for rel,_ in r: arrived(p,rel,True)
            for cp in sent: cp().wait_send()
            for i in range(len(shards)): mine(i).wait()
        return begin,steps,end

class Scatter:
    loop=False
    late=0.0
    def __init__(self,parts,plan,dp,mp):
        self.plan=plan; nz=self.nz=dp//2; self.mp=mp
        self.width=[]
        for i,p in enumerate(parts):
            inside=[o for j,_,_,o in plan if j==i][0]=="xz"
            self.width.append(p.shape[-1]//(1 if inside else mp))
        self.ins=[pl.BlockSpec(memory_space=pl.ANY)]*len(parts)
        self.outs=[pl.BlockSpec(memory_space=pltpu.VMEM)]*len(parts)
        self.shapes=[jax.ShapeDtypeStruct((p.shape[1],w),f32) for p,w in zip(parts,self.width)]
        scr=[]; sends=0
        for i,lo,hi,order in plan:
            rows=parts[i].shape[1]; w=hi-lo
            b=lambda k: pltpu.VMEM((k,rows,w),bf)
            nb=nz*4 if order!="xz" else nz*2
            scr+=[b(nb),b(nb)]
            if order=="xyz": scr+=[b(nz*2),b(nz),b(nz)]; sends+=nb+2*nz+nz+nz-1
            elif order=="yzx": scr+=[b(1),b(nz*2),b(nz*2)]; sends+=nb+2*nz+2*(nz-1)+1
            else: scr+=[b(nz*2),b(nz),b(2*nz)]; sends+=nb+nz+nz+nz-1
        n=len(plan)
        self.scratch=scr+[pltpu.SemaphoreType.DMA((n,4*nz)),pltpu.SemaphoreType.DMA((sends,)),pltpu.SemaphoreType.DMA((n,4*nz)),pltpu.SemaphoreType.DMA((n,2*nz)),pltpu.SemaphoreType.DMA((n,2*nz)),pltpu.SemaphoreType.DMA((n,2*nz))]
    def build(self,pos,parts,outs,scr):
        plan=self.plan; nz=self.nz; z,x,y,c=pos; n=len(plan)
        per=scr[:5*n]; own,send,csem,xsem,ysem,zsem=scr[5*n:]
        sent=[]; begins=[]; steps=[]; ends=[]
        def sender(src,dst,rsem,kind):
            k=len(sent)
            cp=lambda: pltpu.make_async_remote_copy(src(),dst,send.at[k],rsem,device_id=peer(pos,kind,nz),device_id_type=MESH)
            sent.append(cp)
            return lambda: cp().start()
        def wait(dst,rsem):
            pltpu.make_async_remote_copy(dst,dst,send.at[0],rsem,device_id=peer(pos,"c",nz),device_id_type=MESH).wait_recv()
        def part(p,r,cc):
            i,lo,hi,order=plan[p]
            rz,rx,ry=r
            zz=lax.rem(z+rz,nz); xx=1-x if rx else x; yy=1-y if ry else y
            if order=="xz": return parts[i].at[zz*2+xx,:,lo:hi]
            return parts[i].at[zz*2+xx,:,columns(yy*2+cc,self.width[i],lo,hi)]
        def total(dst,*refs):
            step=32 if self.loop and dst.shape[0]%32==0 else dst.shape[0]
            def body(r,carry):
                w=pl.ds(pl.multiple_of(r*step,step),step)
                v=refs[0][w,:].astype(f32)
                for o in refs[1:]: v=v+o[w,:].astype(f32)
                dst[w,:]=v.astype(dst.dtype)
                return carry
            if step==dst.shape[0]: body(0,0)
            else: lax.fori_loop(0,dst.shape[0]//step,body,0)
        down=range(nz-1,-1,-1)
        for p,(i,lo,hi,order) in enumerate(plan):
            acc,cb,xb,yb,zb=per[5*p:5*p+5]
            if order=="xyz": seq=[(k,1,r) for r in (1,0) for k in down]+[(k,0,1) for k in down]+[(k,0,0) for k in down]
            elif order=="yzx": seq=[(k,r,1) for r in (1,0) for k in down]+[(k,1,0) for k in down]+[(k,0,0) for k in down]
            else: seq=[(k,1,0) for k in down]+[(k,0,0) for k in down]
            slot=(lambda r: (r[0]*2+r[1])*2+r[2]) if order!="xz" else (lambda r: r[0]*2+r[1])
            A=lambda r,acc=acc,slot=slot: acc.at[slot(r)]
            def plus(when,p=p):
                def note(f): steps.append((when,f))
                return note
            for t,r in enumerate(seq):
                s=slot(r); rz,rx,ry=r
                begins.append((t,sender(functools.partial(part,p,r,c if order=="xz" else 1-c),cb.at[s],csem.at[p,s],"c")))
                mine=lambda p=p,r=r,s=s,acc=acc: pltpu.make_async_copy(part(p,r,c),acc.at[s],own.at[p,s])
                begins.append((t,lambda mine=mine: mine().start()))
                go=None
                if order in ("xyz","xz") and rx: go=sender(lambda v=A(r): v,xb.at[rz*2+ry],xsem.at[p,rz*2+ry],"x")
                if order=="yzx" and ry: go=sender(lambda v=A(r): v,yb.at[rz*2+rx],ysem.at[p,rz*2+rx],"y")
                @plus(0.22*t/len(seq))
                def _(p=p,s=s,acc=acc,cb=cb,go=go,mine=mine):
                    mine().wait()
                    wait(cb.at[s],csem.at[p,s])
                    total(acc.at[s],acc.at[s],cb.at[s])
                    if go: go()
            if order=="xyz":
                for n_,k in enumerate(down):
                    r=(k,0,1); j=k*2+1
                    go=sender(lambda v=A(r): v,yb.at[k],ysem.at[p,k],"y")
                    @plus(0.24+0.26*n_/nz)
                    def _(p=p,r=r,j=j,A=A,xb=xb,go=go):
                        wait(xb.at[j],xsem.at[p,j]); total(A(r),A(r),xb.at[j])
                        go()
                for n_,k in enumerate(down):
                    r=(k,0,0); j=k*2
                    go=sender(lambda v=A(r): v,zb.at[k],zsem.at[p,k],f"z{k}") if k else None
                    @plus(0.52+0.26*n_/nz)
                    def _(p=p,r=r,j=j,k=k,A=A,xb=xb,yb=yb,go=go):
                        wait(xb.at[j],xsem.at[p,j]); wait(yb.at[k],ysem.at[p,k])
                        if go:
                            total(A(r),A(r),xb.at[j],yb.at[k])
                            go()
                def fin(p=p,i=i,lo=lo,hi=hi,A=A,xb=xb,yb=yb,zb=zb):
                    for k in range(1,nz): wait(zb.at[k],zsem.at[p,k])
                    total(outs[i].at[:,lo:hi],A((0,0,0)),xb.at[0],yb.at[0],*[zb.at[k] for k in range(1,nz)])
                ends.append(fin)
            elif order=="yzx":
                for n_,(rx,k) in enumerate([(rx,k) for rx in (1,0) for k in range(nz-1,0,-1)]):
                    r=(k,rx,0); j=k*2+rx
                    go=sender(lambda v=A(r): v,zb.at[k*2+rx],zsem.at[p,k*2+rx],f"z{k}")
                    @plus(0.24+0.3*n_/(2*nz-2))
                    def _(p=p,r=r,j=j,A=A,yb=yb,go=go):
                        wait(yb.at[j],ysem.at[p,j]); total(A(r),A(r),yb.at[j])
                        go()
                r=(0,1,0)
                go=sender(lambda v=A(r): v,xb.at[0],xsem.at[p,0],"x")
                @plus(0.8)
                def _(p=p,r=r,A=A,yb=yb,zb=zb,go=go):
                    wait(yb.at[1],ysem.at[p,1])
                    for k in range(1,nz): wait(zb.at[k*2+1],zsem.at[p,k*2+1])
                    total(A(r),A(r),yb.at[1],*[zb.at[k*2+1] for k in range(1,nz)])
                    go()
                def fin(p=p,i=i,lo=lo,hi=hi,A=A,xb=xb,yb=yb,zb=zb):
                    wait(yb.at[0],ysem.at[p,0])
                    for k in range(1,nz): wait(zb.at[k*2],zsem.at[p,k*2])
                    wait(xb.at[0],xsem.at[p,0])
                    total(outs[i].at[:,lo:hi],A((0,0,0)),yb.at[0],xb.at[0],*[zb.at[k*2] for k in range(1,nz)])
                ends.append(fin)
            else:
                for n_,k in enumerate(down):
                    r=(k,0,0)
                    go=sender(lambda v=A(r): v,yb.at[k],ysem.at[p,k],"y")
                    @plus(0.24+0.26*n_/nz)
                    def _(p=p,r=r,k=k,A=A,xb=xb,go=go):
                        wait(xb.at[k*2],xsem.at[p,k*2]); total(A(r),A(r),xb.at[k*2])
                        go()
                for n_,k in enumerate(range(nz-1,0,-1)):
                    go=sender(lambda v=zb.at[k]: v,zb.at[nz+k],zsem.at[p,k],f"z{k}")
                    @plus(0.52+0.26*n_/nz)
                    def _(p=p,k=k,A=A,yb=yb,zb=zb,go=go):
                        wait(yb.at[k],ysem.at[p,k]); total(zb.at[k],A((k,0,0)),yb.at[k])
                        go()
                def fin(p=p,i=i,lo=lo,hi=hi,A=A,yb=yb,zb=zb):
                    wait(yb.at[0],ysem.at[p,0])
                    for k in range(1,nz): wait(zb.at[nz+k],zsem.at[p,k])
                    total(outs[i].at[:,lo:hi],A((0,0,0)),yb.at[0],*[zb.at[nz+k] for k in range(1,nz)])
                ends.append(fin)
        begins.sort(key=lambda e: e[0])
        steps.sort(key=lambda e: e[0])
        def begin():
            for _,g in begins: g()
        def end():
            for f in ends: f()
            for cp in sent: cp().wait_send()
        return begin,steps,end

def scatter_kernel(nz,comm,*refs):
    gq_ref,go_ref,sums_ref,scale_ref=refs[:4]
    hosted=refs[4:11]
    outq_ref,outo_ref,outkv_ref,outgb_ref,out_hbm,ig_hbm=refs[11:17]
    refs=refs[17:]
    qo,kvg,a_ref,c_ref,out_ref,ig_ref,osem=refs[:7]
    refs=refs[7:]
    o_ref,wo_ref,hid_ref,down_ref,tok_ref,cot_ref,dn_ref=refs[:7]
    fetch=[pltpu.make_async_copy(h,v,refs[7].at[k]) for k,(h,v) in enumerate(zip(hosted,refs[:7]))]
    for f in fetch: f.start()
    pos=coords(nz)
    greet(pos,[f"z{k}" for k in range(1,nz)]+["x","y","c"],nz)
    rows=gq_ref.shape[1]
    lane=lax.broadcasted_iota(jnp.int32,(rows,128),1)<64
    def tile(ref,d,h): return ref[d,:,128*(h//2):128*(h//2)+128].astype(f32)
    def pack(d,carry):
        for t in range(qo.shape[2]//128):
            m,k=t//3,t%3
            lo,hi=[((gq_ref,3*m),(gq_ref,3*m+1)),((gq_ref,3*m+2),(go_ref,3*m)),((go_ref,3*m+1),(go_ref,3*m+2))][k]
            qo[d,:,128*t:128*t+128]=halves(tile(lo[0],d,lo[1]),lo[1]%2,tile(hi[0],d,hi[1]),hi[1]%2,lane).astype(bf)
        return carry
    lax.fori_loop(0,qo.shape[0],pack,0)
    s=jnp.concatenate([sums_ref[...],jnp.zeros((120,sums_ref.shape[1]),f32)],axis=0).T
    for d in range(kvg.shape[0]):
        kvg[d,:,:128]=gq_ref[d,:,gq_ref.shape[2]-128:]
        kvg[d,:,128:]=s[rows*d:rows*d+rows].astype(bf)
    begin,steps,end=comm.build(pos,(qo,kvg),(a_ref,c_ref),refs[8:])
    begin()
    T=256
    def leave(k,r):
        rows=pl.ds(pl.multiple_of(r*T,T),T)
        src,dst=((out_ref,out_hbm),(ig_ref,ig_hbm))[k]
        return pltpu.make_async_copy(src.at[rows,:],dst.at[rows,:],osem.at[k,r])
    across=out_ref.shape[1]//T; n=out_ref.shape[0]//T*across
    slots=[[] for _ in range(n)]
    for when,s in steps:
        if when<0.23: s()
        else: slots[min(n-1,int(n*(0.33+(when-0.24)*1.15)))].append(s)
    def chunk(it,carry):
        rows=pl.ds(pl.multiple_of(it//across*T,T),T); cols=pl.ds(pl.multiple_of(it%across*T,T),T)
        @pl.when(it%across==0)
        def _():
            v=tok_ref[rows,:].astype(f32)
            v=v-jnp.mean(v,axis=1,keepdims=True)
            inverse=lax.rsqrt(jnp.mean(v*v,axis=1,keepdims=True)+epsilon)
            v=v*inverse
            dn=dn_ref[rows,:]
            dx=(dn-jnp.mean(dn,axis=1,keepdims=True)-v*jnp.mean(dn*v,axis=1,keepdims=True))*inverse
            ig_ref[rows,:]=(cot_ref[rows,:].astype(f32)*scale_ref[rows,:]+dx).astype(bf)
        y=tok_ref[rows,cols].astype(f32)+dg(o_ref[rows,:],wo_ref[cols,:],NT)+dg(hid_ref[rows,:],down_ref[cols,:],NT)
        out_ref[rows,cols]=y.astype(bf)
        @pl.when(it%across==across-1)
        def _():
            for k in range(2): leave(k,it//across).start()
        for k in range(n):
            if slots[k]:
                @pl.when(it==k)
                def _(k=k):
                    for s in slots[k]: s()
        return carry
    for f in fetch: f.wait()
    lax.fori_loop(0,n,chunk,0)
    end()
    a=a_ref[...]; half=a.shape[1]//2
    outq_ref[...]=a[:,:half]; outo_ref[...]=a[:,half:]
    outkv_ref[...]=c_ref[:,:128]
    outgb_ref[...]=c_ref[:,128:].T[:8]
    for r in range(n//across):
        for k in range(2): leave(k,r).wait()

def halves(lo,lo_at,hi,hi_at,lane):
    if lo_at: lo=pltpu.roll(lo,64,1)
    if not hi_at: hi=pltpu.roll(hi,64,1)
    return jnp.where(lane,lo,hi)

def scatter_small(gq,go,sums,o,wo,hidden,down,tokens,cotangent,scale,dnormed,dp,mp,cid):
    hosted=(o,wo,hidden,down,tokens,cotangent,dnormed)
    part=gq.shape[1]; cols=go.shape[2]//mp
    shape=lambda w: jax.ShapeDtypeStruct((dp,gq.shape[1],w),bf)
    qo,kvg=shape(2*go.shape[2]),shape(256)
    comm=Scatter([qo,kvg],[(1,0,256,"xz"),(0,0,256,"xyz"),(0,256,384,"yzx")],dp,mp)
    comm.loop=True
    vm=pl.BlockSpec(memory_space=pltpu.VMEM)
    return pl.pallas_call(functools.partial(scatter_kernel,comm.nz,comm),
        in_specs=[vm]*4+[pl.BlockSpec(memory_space=pl.ANY)]*len(hosted),out_specs=[vm]*4+[pl.BlockSpec(memory_space=pl.ANY)]*2,
        out_shape=[jax.ShapeDtypeStruct(d,f32) for d in ((part,cols),(part,cols),(part,128),(8,part))]+[jax.ShapeDtypeStruct(o.shape,bf)]*2,
        scratch_shapes=[pltpu.VMEM(qo.shape,bf),pltpu.VMEM(kvg.shape,bf),pltpu.VMEM((part,2*cols),f32),pltpu.VMEM((part,256),f32),pltpu.VMEM(o.shape,bf),pltpu.VMEM(o.shape,bf),pltpu.SemaphoreType.DMA((2,o.shape[0]//256))]+[pltpu.VMEM(h.shape,h.dtype) for h in hosted]+[pltpu.SemaphoreType.DMA((len(hosted),))]+comm.scratch,
        compiler_params=pltpu.CompilerParams(collective_id=cid,has_side_effects=True,vmem_limit_bytes=60<<20),name="scatter_grads")(gq,go,sums,scale,*hosted)

def prologue_kernel(nz,comms,*refs):
    tok_ref,wq_ref,wo_ref,wkv_ref,gain_ref,bias_ref,cos_ref,sin_ref=refs[:6]+refs[14:16]
    refs=refs[:2]+refs[:14]+refs[16:]
    q_out,o_out,small_out,normed_out,aint_out,min_out,kv_out,all_out=refs[8:16]
    qo_own,kvg_own,qo_full,kvg_full,wkv_scr,ain_out,ksend,krecv=refs[16:24]
    pos=coords(nz); z,x,y,c=pos
    greet(pos,[f"z{k}" for k in range(1,nz)]+["x","y","c"],nz)
    rows=wq_ref.shape[0]
    kvg_own[:,:128]=wkv_ref[...]
    kvg_own[:,128:]=jnp.concatenate([gain_ref[...].astype(f32),bias_ref[...].astype(f32),jnp.zeros((124,rows),f32)],axis=0).T.astype(bf)
    g,b=comms
    ga=g.build(pos,(kvg_own,),(kvg_full,),refs[24:27])
    gb=b.build(pos,(qo_own,),(qo_full,),refs[27:30])
    ga[0]()
    wq=wq_ref[...].astype(f32); wo=wo_ref[...].astype(f32)
    qo_own[:,:128]=wq[:,:128].astype(bf)
    qo_own[:,128:256]=jnp.concatenate([wq[:,128:],wo[:,:64]],axis=1).astype(bf)
    qo_own[:,256:]=wo[:,64:].astype(bf)
    gb[0]()
    nb,own,width=tok_ref.shape
    part=own//4
    half=ROT//2
    row=lax.broadcasted_iota(jnp.int32,(half,own),0)
    frequency=jnp.ones((half,own),f32)
    for i in range(1,half): frequency=jnp.where(row==i,10000.0**(-2.0*i/ROT),frequency)
    angle=((y*2+c)*own+lax.broadcasted_iota(jnp.int32,(half,own),1)).astype(f32)*frequency
    for ref,f,rest in ((cos_ref,jnp.cos,jnp.ones),(sin_ref,jnp.sin,jnp.zeros)):
        t=f(angle); head=[t,t,rest((HD-ROT,own),f32)]
        ref[...]=jnp.concatenate(head+head,axis=0).T
    def norm(k,carry):
        v=tok_ref[k//4,pl.ds(pl.multiple_of(k%4*part,part),part),:].astype(f32)
        v=v-jnp.mean(v,axis=1,keepdims=True)
        normed_out[pl.ds(pl.multiple_of(k*part,part),part),:]=v*lax.rsqrt(jnp.mean(v*v,axis=1,keepdims=True)+epsilon)
        return carry
    lax.fori_loop(0,4*nb,norm,0)
    sa=[s for _,s in ga[1]]; sb=[s for _,s in gb[1]]
    while sa:
        sa.pop(0)()
        if sb: sb.pop(0)()
    ga[2]()
    kvg=kvg_full[...].reshape(width,256)
    small=kvg[:,128:].astype(f32).T
    small_out[...]=small[:8]
    wkv=kvg[:,:128]
    for d in range(all_out.shape[0]): all_out[d,:,width:]=kvg_full[d,:,:128]
    wkv_scr[...]=wkv
    def copy(s,m,src,kind,n):
        return pltpu.make_async_remote_copy(src,kv_out.at[s,m],ksend.at[n],krecv.at[s,m],device_id=peer(pos,kind,nz),device_id_type=MESH)
    copies=[]
    me=y*2+c
    for s in range(nb):
        def project(k,carry):
            w=pl.ds(pl.multiple_of(k*part,part),part); rows=pl.ds(pl.multiple_of(s*own+k*part,part),part)
            ain=normed_out[rows,:]*small[0:1]+small[2:3]
            aint_out[:,rows]=ain.T.astype(bf)
            ain=ain.astype(bf)
            ain_out[rows,:]=ain
            kv_out[s,me,w,:]=turn(dg(ain,wkv_scr[...],NN),cos_ref[w,:],sin_ref[w,:],False,True).astype(bf)
            return carry
        lax.fori_loop(0,4,project,0)
        for kind in ("y","c"):
            cp=copy(s,me,kv_out.at[s,me],kind,len(copies)); cp.start(); copies.append(cp)
        def feed(k,carry):
            rows=pl.ds(pl.multiple_of(s*own+k*part,part),part)
            min_out[rows,:]=(normed_out[rows,:]*small[1:2]+small[3:4]).astype(bf)
            return carry
        lax.fori_loop(0,4,feed,0)
        for _ in range(6):
            if sb: sb.pop(0)()
    other=(1-y)*2+c
    for s in range(nb):
        copy(s,other,kv_out.at[s,other],"c",0).wait_recv()
        cp=copy(s,other,kv_out.at[s,other],"c",len(copies)); cp.start(); copies.append(cp)
    for s in sb: s()
    gb[2]()
    lane=lax.broadcasted_iota(jnp.int32,(rows,128),1)<64
    def unpack(d,carry):
        def tile(m,k): return qo_full[d,:,384*m+128*k:384*m+128*k+128].astype(f32)
        for ref,place in ((all_out,[(0,0),(0,1),(1,0)]),(o_out,[(1,1),(2,0),(2,1)])):
            for j in range(width//128):
                (m0,(k0,h0)),(m1,(k1,h1))=[(h//3,place[h%3]) for h in (2*j,2*j+1)]
                t=halves(tile(m0,k0),h0,tile(m1,k1),h1,lane).astype(bf)
                ref[d,:,128*j:128*j+128]=t
        return carry
    lax.fori_loop(0,all_out.shape[0],unpack,0)
    def queries(k,carry):
        T=own//2
        rows=pl.ds(pl.multiple_of(k*T,T),T); w=pl.ds(pl.multiple_of(k%2*T,T),T)
        v=dg(ain_out[rows,:],all_out[:,:,:width].reshape(width,width),NN)
        for j in range(width//128):
            q_out[rows,128*j:128*j+128]=(turn(v[:,128*j:128*j+128],cos_ref[w,:],sin_ref[w,:],False)*HD**-0.5).astype(bf)
        return carry
    lax.fori_loop(0,2*nb,queries,0)
    for s in range(nb):
        for m in (y*2+1-c,(1-y)*2+1-c): copy(s,m,kv_out.at[s,m],"c",0).wait_recv()
    for cp in copies: cp.wait_send()

def prologue(tokens,wq,wo,wkv,gains,biases,dp,mp,cid):
    nb,own,width=tokens.shape; part,cols=wq.shape
    kvg=jax.ShapeDtypeStruct((part,256),bf); qo=jax.ShapeDtypeStruct((part,2*cols),bf)
    comms=(Gather([kvg],[(0,0,256,"zx")],dp,mp),Gather([qo],[(0,0,256,"zyx"),(0,256,384,"xzy")],dp,mp))
    vm=pl.BlockSpec(memory_space=pltpu.VMEM)
    s=lambda *a: jax.ShapeDtypeStruct(a,bf)
    return pl.pallas_call(functools.partial(prologue_kernel,dp//2,comms),
        in_specs=[vm]*6,out_specs=[vm]*10,
        out_shape=[s(nb*own,width),s(dp,part,width),jax.ShapeDtypeStruct((8,width),f32),jax.ShapeDtypeStruct((nb*own,width),f32),s(width,nb*own),s(nb*own,width),s(nb,mp,own,128),s(dp,part,width+128)]+[jax.ShapeDtypeStruct((own,128),f32)]*2,
        scratch_shapes=[pltpu.VMEM(qo.shape,bf),pltpu.VMEM(kvg.shape,bf),pltpu.VMEM((dp,part,mp*2*cols),bf),pltpu.VMEM((dp,part,256),bf),pltpu.VMEM((width,128),bf),pltpu.VMEM((nb*own,width),bf),
                        pltpu.SemaphoreType.DMA((3*nb,)),pltpu.SemaphoreType.DMA((nb,mp))]+comms[0].scratch+comms[1].scratch,
        compiler_params=pltpu.CompilerParams(collective_id=cid,has_side_effects=True,vmem_limit_bytes=60<<20),name="gather_weights")(tokens,wq,wo,wkv,gains.T,biases.T)

NT=(((1,),(1,)),((),()))
NN=(((1,),(0,)),((),()))
def dg(a,b,dn): return lax.dot_general(a,b,dn,preferred_element_type=f32)
def turn(v,cos,sin,back,keys_only=False):
    lane=lax.broadcasted_iota(jnp.int32,v.shape,1)
    other=jnp.where(lane%HD<ROT//2,-pltpu.roll(v,128-ROT//2,1),pltpu.roll(v,ROT//2,1))*sin
    w=v*cos-other if back else v*cos+other
    return jnp.where(lane<HD,w,v) if keys_only else w

class Fold:
    scratch=[pltpu.VMEM((2,2,B,128),bf),pltpu.VMEM((2,2,B,128),bf),pltpu.VMEM((2,B,128),bf),pltpu.VMEM((2,B,128),bf),
             pltpu.SemaphoreType.DMA((6,)),pltpu.SemaphoreType.DMA((2,2)),pltpu.SemaphoreType.DMA((2,))]
    def __init__(self,pos,nz,out,cos,sin,scr):
        self.pos=pos; self.nz=nz; self.out=out; self.cos=cos; self.sin=sin; self.scr=scr
    def copy(self,b,n,src,dst,sem,kind):
        return pltpu.make_async_remote_copy(src,dst,self.scr[4].at[3*b+n],sem,device_id=peer(self.pos,kind,self.nz),device_id_type=MESH)
    def across(self,b,ry):
        low,cbuf=self.scr[:2]
        return self.copy(b,ry,low.at[b,ry],cbuf.at[b,ry],self.scr[5].at[b,ry],"c")
    def far(self,b):
        _,_,ybuf,ysend=self.scr[:4]
        return self.copy(b,2,ysend.at[b],ybuf.at[b],self.scr[6].at[b],"y")
    def one(self,b,part):
        _,_,y,c=self.pos
        for ry in (1,0):
            self.scr[0][b,ry]=part((1-y if ry else y)*2+1-c).astype(bf)
            self.across(b,ry).start()
    def two(self,b,part):
        _,_,y,c=self.pos
        self.across(b,1).wait_recv()
        self.scr[3][b]=(part((1-y)*2+c)+self.scr[1][b,1].astype(f32)).astype(bf)
        self.far(b).start()
    def three(self,b,part):
        _,_,y,c=self.pos
        self.across(b,0).wait_recv(); self.far(b).wait_recv()
        v=part(y*2+c)+self.scr[1][b,0].astype(f32)+self.scr[2][b].astype(f32)
        self.out[b*B:b*B+B,self.out.shape[1]-128:]=turn(v,self.cos[...],self.sin[...],True,True).astype(bf)
        self.across(b,1).wait_send(); self.across(b,0).wait_send(); self.far(b).wait_send()

def attn_kernel(nz,pairs,comm,join,nc,*refs):
    q_ref,do_ref,kv_ref,cos_ref,sin_ref=refs[:5]
    refs=refs[5:]
    if join: prev,refs=refs[:3],refs[3:]
    cin=refs[:nc]
    o_ref,dq_ref=refs[nc:2+nc]
    refs=refs[2+nc:]
    if not join: dkv_ref,refs=refs[0],refs[1:]
    cout=refs[:nc]
    k2,v2,kvt,acck,accv,ps,mk,ms,ls,ots,dqs=refs[nc:11+nc]
    refs=refs[11+nc:]
    rb=lax.axis_index("mp")
    nkb=kv_ref.shape[1]//B
    at=0
    if join:
        dkvs,local,fold,refs=refs[0],refs[1],refs[2:9],refs[9:]
        at=B
        part0=lambda m: prev[2][0,pl.ds(pl.multiple_of(m*B,B),B),:]
        part1=lambda m: dkvs[m]
    own=slice(at,at+B)
    slots=[[] for _ in range(pairs*2*nkb)]
    if comm:
        pos=coords(nz)
        greet(pos,[f"z{k}" for k in range(1,nz)]+["x","y","c"],nz)
        begin,steps,end=comm.build(pos,cin,cout,refs)
        begin()
        for when,s in steps: slots[int((comm.late+(1-comm.late)*when)*len(slots))].append(s)
        if join:
            sums=Fold(pos,nz,dq_ref,cos_ref,sin_ref,fold)
            sums.one(0,part0)
            slots[len(slots)//6].append(lambda: sums.two(0,part0))
            slots[len(slots)//2].append(lambda: sums.three(0,part0))
            before=[pltpu.make_async_copy(prev[k],r.at[:B,:prev[k].shape[1]],local.at[k]) for k,r in enumerate((o_ref,dq_ref))]
            for cp in before: cp.start()
    def between(pair,kb,base):
        for p in range(pairs):
            todo=[k for k in range(nkb) if slots[(2*p+base)*nkb+k]]
            if not todo: continue
            @pl.when(pair==p)
            def _(p=p,todo=todo):
                for k in todo:
                    @pl.when(kb==k)
                    def _(k=k):
                        for s in slots[(2*p+base)*nkb+k]: s()
    lane=lax.broadcasted_iota(jnp.int32,(B,128),1)<64
    def setup(kb,carry):
        kv=kv_ref[0,pl.ds(pl.multiple_of(kb*B,B),B),:].astype(f32)
        rolled=pltpu.roll(kv,64,1)
        k2[kb]=jnp.where(lane,kv,rolled).astype(bf)
        v2[kb]=jnp.where(lane,rolled,kv).astype(bf)
        kvt[kb]=kv.T.astype(bf)
        acck[kb]=jnp.zeros((B,128),f32); accv[kb]=jnp.zeros((B,128),f32)
        return carry
    lax.fori_loop(0,nkb,setup,0)
    def one(pair,carry):
        cols=pl.ds(pl.multiple_of(pair*128,128),128)
        q=q_ref[:,cols]; do=do_ref[:,cols]
        zero=jnp.zeros_like(q)
        qm=(jnp.where(lane,q,zero),jnp.where(lane,zero,q))
        dom=(jnp.where(lane,do,zero),jnp.where(lane,zero,do))
        ms[...]=jnp.full_like(ms,-1e30); ls[...]=jnp.zeros_like(ls)
        ots[...]=jnp.zeros_like(ots); dqs[...]=jnp.zeros_like(dqs)
        H=range(2)
        def fwd(kb,masked):
            ss=[dg(k2[kb],qm[h],NT) for h in H]
            if masked:
                ki=lax.broadcasted_iota(jnp.int32,(B,B),0); ri=lax.broadcasted_iota(jnp.int32,(B,B),1)
                ss=[jnp.where(ki<=ri,v,-1e30) for v in ss]
            mo=[ms[h] for h in H]
            mn=[jnp.maximum(mo[h],jnp.max(ss[h],axis=0,keepdims=True)) for h in H]
            al=[jnp.exp(mo[h]-mn[h]) for h in H]
            pp=[jnp.exp(ss[h]-mn[h]) for h in H]
            for h in H: ls[h]=ls[h]*al[h]+jnp.sum(pp[h],axis=0,keepdims=True)
            pb=[v.astype(bf) for v in pp]
            for h in H:
                ps[h,kb]=pb[h]
                mk[h,kb]=mn[h]
                ms[h]=mn[h]
            ob=[dg(kvt[kb,64:,:],pb[h],NN) for h in H]
            for h in H: ots[h]=ots[h]*al[h]+ob[h]
        def fstep(kb,carry):
            @pl.when(kb<rb)
            def _(): fwd(kb,False)
            @pl.when(kb==rb)
            def _(): fwd(kb,True)
            between(pair,kb,0)
            return carry
        lax.fori_loop(0,nkb,fstep,0)
        dot_=do.astype(f32).T
        for h in range(2):
            inv=1.0/ls[h]
            ot=ots[h]*inv
            ots[h]=ot
            ls[h]=inv
        delta=[jnp.sum(ots[h]*dot_[64*h:64*h+64,:],axis=0,keepdims=True) for h in range(2)]
        o_ref[own,cols]=jnp.concatenate([ots[0],ots[1]],axis=0).T.astype(bf)
        def bwd(kb):
            dps=[dg(v2[kb],dom[h],NT) for h in H]
            al=[jnp.exp(mk[h,kb]-ms[h])*ls[h] for h in H]
            pp=[ps[h,kb].astype(f32)*al[h] for h in H]
            ds=[(pp[h]*(dps[h]-delta[h])).astype(bf) for h in H]
            pn=[v.astype(bf) for v in pp]
            acck[kb]+=dg(ds[0],qm[0],NN)+dg(ds[1],qm[1],NN)
            accv[kb]+=dg(pn[0],dom[0],NN)+dg(pn[1],dom[1],NN)
            qb=[dg(kvt[kb,:64,:],ds[h],NN) for h in H]
            for h in H: dqs[h]+=qb[h]
        def bstep(kb,carry):
            @pl.when(kb<=rb)
            def _(): bwd(kb)
            between(pair,kb,1)
            return carry
        lax.fori_loop(0,nkb,bstep,0)
        dq_ref[own,cols]=(turn(jnp.concatenate([dqs[0],dqs[1]],axis=0).T,cos_ref[...],sin_ref[...],True)*HD**-0.5).astype(bf)
        return carry
    lax.fori_loop(0,pairs,one,0)
    def flush(kb,carry):
        k=acck[kb]; v=accv[kb]
        k=jnp.where(lane,k+pltpu.roll(k,64,1),v+pltpu.roll(v,64,1))
        if join: dkvs[kb]=k
        else: dkv_ref[0,pl.ds(pl.multiple_of(kb*B,B),B),:]=k
        return carry
    lax.fori_loop(0,nkb,flush,0)
    if join:
        sums.one(1,part1)
        sums.two(1,part1)
    if comm: end()
    if join:
        sums.three(1,part1)
        for cp in before: cp.wait()

def attention(b,q,do,kv,cos,sin,comm,arrays,dp,cid,prev=()):
    S=kv.shape[1]; nkb=S//B; width=q.shape[1]; join=len(prev)>0
    assert not join or (b==1 and nkb==4)
    whole=lambda *shape: pl.BlockSpec(shape,lambda *_: (0,)*len(shape))
    blk=pl.BlockSpec((B,width),lambda *_: (b,0))
    kvs=pl.BlockSpec((1,S,128),lambda *_: (b,0,0))
    hbm=pl.BlockSpec(memory_space=pl.ANY)
    rows=2*B if join else B
    outs=[jax.ShapeDtypeStruct((rows,width),bf),jax.ShapeDtypeStruct((rows,width+128*join),bf)]+([] if join else [jax.ShapeDtypeStruct((1,S,128),f32)])
    params=dict(vmem_limit_bytes=62<<20)
    if comm: params.update(collective_id=cid,has_side_effects=True)
    return pl.pallas_call(functools.partial(attn_kernel,dp//2,width//128,comm,join,len(arrays)),
      grid_spec=pltpu.PrefetchScalarGridSpec(num_scalar_prefetch=0,grid=(1,),
        in_specs=[blk,blk,kvs,whole(B,128),whole(B,128)]+([hbm,hbm,whole(1,S,128)] if join else [])+(comm.ins if comm else []),
        out_specs=[whole(*t.shape) for t in outs]+(comm.outs if comm else []),
        scratch_shapes=[pltpu.VMEM((nkb,B,128),bf),pltpu.VMEM((nkb,B,128),bf),pltpu.VMEM((nkb,128,B),bf),pltpu.VMEM((nkb,B,128),f32),pltpu.VMEM((nkb,B,128),f32),
                        pltpu.VMEM((2,nkb,B,B),bf),pltpu.VMEM((2,nkb,1,B),f32),pltpu.VMEM((2,1,B),f32),pltpu.VMEM((2,1,B),f32),pltpu.VMEM((2,64,B),f32),pltpu.VMEM((2,64,B),f32)]
                       +([pltpu.VMEM((nkb,B,128),f32),pltpu.SemaphoreType.DMA((2,))]+Fold.scratch if join else [])
                       +(comm.scratch if comm else [])),
      out_shape=outs+(comm.shapes if comm else []),
      compiler_params=pltpu.CompilerParams(**params),name="attn")(q,do,kv,cos,sin,*prev,*arrays)


def kv_gather_kernel(nz, own_ref, full_ref, send, recv):
    pos = coords(nz)
    z, x, y, c = pos
    greet(pos, ["y", "c"], nz)
    nb = own_ref.shape[0]
    sent = []

    def go(b, m, src, kind):
        cp = pltpu.make_async_remote_copy(src, full_ref.at[b, m], send.at[len(sent)], recv.at[b, m],
                                          device_id=peer(pos, kind, nz), device_id_type=MESH)
        cp.start()
        sent.append(cp)

    def wait(b, m):
        pltpu.make_async_remote_copy(full_ref.at[b, m], full_ref.at[b, m], send.at[0], recv.at[b, m],
                                     device_id=peer(pos, "c", nz), device_id_type=MESH).wait_recv()

    for b in range(nb):
        go(b, y * 2 + c, own_ref.at[b], "y")
    for b in range(nb):
        go(b, y * 2 + c, own_ref.at[b], "c")
    for b in range(nb):
        full_ref[b, y * 2 + c] = own_ref[b]
    for b in range(nb):
        m = (1 - y) * 2 + c
        wait(b, m)
        go(b, m, full_ref.at[b, m], "c")
    for b in range(nb):
        wait(b, y * 2 + 1 - c)
        wait(b, (1 - y) * 2 + 1 - c)
    for cp in sent:
        cp.wait_send()


def kv_gather(own, dp, cid):
    nb, rows, w = own.shape
    return pl.pallas_call(
        functools.partial(kv_gather_kernel, dp // 2),
        in_specs=[pl.BlockSpec(memory_space=pltpu.VMEM)],
        out_specs=pl.BlockSpec(memory_space=pltpu.VMEM),
        out_shape=jax.ShapeDtypeStruct((nb, 4, rows, w), own.dtype),
        scratch_shapes=[pltpu.SemaphoreType.DMA((3 * nb,)), pltpu.SemaphoreType.DMA((nb, 4))],
        compiler_params=pltpu.CompilerParams(collective_id=cid, has_side_effects=True),
        name="gather_keyval",
    )(own)


def kv_reduce_kernel(nz, n, *refs):
    parts = refs[:n]
    cos_ref, sin_ref, out_ref, low, cbuf, ybuf, ysend, send, crecv, yrecv = refs[n:]
    pos = coords(nz)
    z, x, y, c = pos
    greet(pos, ["y", "c"], nz)
    sent = []

    def go(src, dst, sem, kind):
        cp = pltpu.make_async_remote_copy(src, dst, send.at[len(sent)], sem, device_id=peer(pos, kind, nz), device_id_type=MESH)
        cp.start()
        sent.append(cp)

    def wait(dst, sem):
        pltpu.make_async_remote_copy(dst, dst, send.at[0], sem, device_id=peer(pos, "c", nz), device_id_type=MESH).wait_recv()

    for ry in (1, 0):
        yy = 1 - y if ry else y
        for b in range(n):
            low[b, ry] = parts[b][yy * 2 + 1 - c].astype(bf)
            go(low.at[b, ry], cbuf.at[b, ry], crecv.at[b, ry], "c")
    for b in range(n):
        wait(cbuf.at[b, 1], crecv.at[b, 1])
        ysend[b] = (parts[b][(1 - y) * 2 + c] + cbuf[b, 1].astype(f32)).astype(bf)
        go(ysend.at[b], ybuf.at[b], yrecv.at[b], "y")
    for b in range(n):
        wait(cbuf.at[b, 0], crecv.at[b, 0])
        wait(ybuf.at[b], yrecv.at[b])
        v = parts[b][y * 2 + c] + cbuf[b, 0].astype(f32) + ybuf[b].astype(f32)
        out_ref[b] = turn(v, cos_ref[...], sin_ref[...], True, True).astype(bf)
    for cp in sent:
        cp.wait_send()


def kv_reduce(parts, cos, sin, dp, cid):
    nb = len(parts)
    mp, rows, w = parts[0].shape
    vm = pl.BlockSpec(memory_space=pltpu.VMEM)
    return pl.pallas_call(
        functools.partial(kv_reduce_kernel, dp // 2, nb),
        in_specs=[vm] * (nb + 2),
        out_specs=vm,
        out_shape=jax.ShapeDtypeStruct((nb, rows, w), bf),
        scratch_shapes=[pltpu.VMEM((nb, 2, rows, w), bf), pltpu.VMEM((nb, 2, rows, w), bf), pltpu.VMEM((nb, rows, w), bf),
                        pltpu.VMEM((nb, rows, w), bf), pltpu.SemaphoreType.DMA((3 * nb,)), pltpu.SemaphoreType.DMA((nb, 2)), pltpu.SemaphoreType.DMA((nb,))],
        compiler_params=pltpu.CompilerParams(collective_id=cid, has_side_effects=True),
        name="reduce_keyval",
    )(*parts, cos, sin)


def spread(arrays, inside, dp, mp):
    out = []
    for i, s in enumerate(arrays):
        if i in inside:
            out.append(lax.all_gather(s, "dp"))
        else:
            a = lax.all_gather(s, ("dp", "mp")).reshape((dp, mp) + s.shape)
            out.append(a.transpose(0, 2, 1, 3).reshape(dp, s.shape[0], -1))
    return out


def collect(parts, inside, dp, mp):
    out = []
    for i, p in enumerate(parts):
        p = p.astype(f32)
        if i in inside:
            out.append(lax.psum(lax.psum_scatter(p, "dp", scatter_dimension=0), "mp"))
        else:
            a = p.reshape(dp, p.shape[1], mp, -1).transpose(0, 2, 1, 3).reshape(dp * mp, p.shape[1], -1)
            out.append(lax.psum_scatter(a, ("dp", "mp"), scatter_dimension=0))
    return out


def rotary(position):
    lane = jnp.arange(2 * HD, dtype=jnp.int32)
    inside = lane % HD
    frequency = 10000.0 ** (-2.0 * (inside % (ROT // 2)).astype(f32) / ROT)
    angle = position[:, None].astype(f32) * frequency[None, :]
    turned = (inside < ROT)[None, :]
    return jnp.where(turned, jnp.cos(angle), 1.0), jnp.where(turned, jnp.sin(angle), 0.0)


def plain_prologue(tokens, cos, sin, wq, wo, wkv, gains, biases, dp, mp):
    nb, own, width = tokens.shape
    wq, wo, kvg = spread([wq, wo, jnp.concatenate([wkv, gains, biases], axis=1)], {2}, dp, mp)
    kvg = kvg.reshape(width, -1)
    small = kvg[:, 2 * HD :].astype(f32).T
    x = tokens.reshape(nb * own, width).astype(f32)
    centered = x - jnp.mean(x, axis=1, keepdims=True)
    normed = centered * lax.rsqrt(jnp.mean(centered * centered, axis=1, keepdims=True) + epsilon)
    ain = (normed * small[0] + small[2]).astype(bf)
    mlp_in = (normed * small[1] + small[3]).astype(bf)
    kv = jnp.dot(ain, kvg[:, : 2 * HD], preferred_element_type=f32).reshape(nb, own, 2 * HD)
    first, half = jnp.arange(2 * HD) < HD, ROT // 2
    other = jnp.where(jnp.arange(2 * HD) < half, -jnp.roll(kv, -half, axis=2), jnp.roll(kv, half, axis=2)) * sin
    kv = jnp.where(first, kv * cos + other, kv).astype(bf)
    wq = wq.reshape(width, width)
    q = jnp.dot(ain, wq, preferred_element_type=f32).reshape(nb, own, width // 128, 128)
    low = jnp.arange(128) % HD < half
    other = jnp.where(low, -jnp.roll(q, -half, axis=3), jnp.roll(q, half, axis=3)) * sin[:, None, :]
    q = ((q * cos[:, None, :] + other) * HD**-0.5).astype(bf).reshape(nb * own, width)
    return q, wo, jnp.concatenate([small, small]), normed, ain.T, mlp_in, kv_gather(kv, dp, 3), jnp.concatenate([wq, kvg[:, : 2 * HD]], axis=1)


def shards(tokens, norm_gains, norm_biases, w_query, w_keyval, w_output, w_up, w_down, cotangent, subset_ids, subset_weights):
    dp, mp = lax.axis_size("dp"), lax.axis_size("mp")
    me = lax.axis_index("mp")
    nb, own, width = tokens.shape
    rows = nb * own
    part, cols = w_query.shape
    ff = w_up.shape[1]
    mine = dp == 8
    dot = functools.partial(jnp.dot, preferred_element_type=f32)
    nt = lambda a, b: lax.dot_general(a, b, (((1,), (1,)), ((), ())), preferred_element_type=f32)
    tn = lambda a, b: lax.dot_general(a, b, (((0,), (0,)), ((), ())), preferred_element_type=f32)
    small_weights = (w_query, w_output, w_keyval, norm_gains, norm_biases)
    if mine:
        q, wo, small, normed, attn_in_t, mlp_in, kv, wqkv, cos, sin = prologue(tokens, *small_weights, dp, mp, 1)
    else:
        cos, sin = rotary(me * own + jnp.arange(own, dtype=jnp.int32))
        q, wo, small, normed, attn_in_t, mlp_in, kv, wqkv = plain_prologue(tokens, cos, sin, *small_weights, dp, mp)
    wo, wqkv = wo.reshape(width, width), wqkv.reshape(width, -1)
    kv_full = kv.reshape(nb, mp * own, 2 * HD)
    gain_a, gain_m = small[0], small[1]

    ids = lax.dynamic_slice_in_dim(subset_ids.reshape(nb, mp * own), me * own, own, 1).reshape(rows)
    matches = ids[:, None] == jnp.arange(subset_weights.shape[0], dtype=jnp.int32)[None, :]
    scale = jnp.sum(jnp.where(matches, subset_weights[None, :], 0.0), axis=1, keepdims=True)
    g = (cotangent.reshape(rows, width).astype(f32) * scale).astype(bf)

    grad_heads = dot(g, wo).astype(bf)
    mlp_plan = lambda a, b: [(0, 0, 768, a), (1, 0, 256, a), (1, 256, 768, b)]
    if mine:
        o0, dq0, dkv0, up, down = attention(0, q, grad_heads, kv_full, cos, sin, Gather([w_up, w_down], mlp_plan("zyx", "xzy"), dp, mp), [w_up, w_down], dp, 5)
    else:
        o0, dq0, dkv0 = attention(0, q, grad_heads, kv_full, cos, sin, None, [], dp, 5)
        up, down = spread([w_up, w_down], (), dp, mp)
    up = up.reshape(width, mp * ff)
    down = down.reshape(width, mp * ff)

    pre = dot(mlp_in, up)
    cdf = 0.5 * (1.0 + lax.erf(pre * sqrt_half))
    hidden = (pre * cdf).astype(bf)
    slope = (cdf + pre * (jnp.exp(-0.5 * pre * pre) * inv_sqrt_two_pi)).astype(bf)
    hidden, slope = lax.optimization_barrier((hidden, slope))
    dpre = (dot(g, down) * slope).astype(bf)
    gup = tn(mlp_in, dpre).astype(bf).reshape(dp, part, mp * ff)
    gdown = tn(g, hidden).astype(bf).reshape(dp, part, mp * ff)
    if mine:
        o, dqkv, grad_up, grad_down = attention(1, q, grad_heads, kv_full, cos, sin, Scatter([gup, gdown], mlp_plan("xyz", "yzx"), dp, mp), [gup, gdown], dp, 6, (o0, dq0, dkv0))
    else:
        o1, dq1, dkv1 = attention(1, q, grad_heads, kv_full, cos, sin, None, [], dp, 6)
        grad_up, grad_down = collect([gup, gdown], (), dp, mp)
        dkvp = kv_reduce([d.reshape(mp, own, 2 * HD) for d in (dkv0, dkv1)], cos, sin, dp, 4)
        o = jnp.concatenate([o0, o1])
        dqkv = jnp.concatenate([jnp.concatenate([dq0, dq1]), dkvp.reshape(rows, 2 * HD)], axis=1)

    dmlp = nt(dpre, up)
    dattn = nt(dqkv, wqkv)
    dnormed = dattn * gain_a + dmlp * gain_m
    sums = [jnp.sum(dattn * normed, axis=0), jnp.sum(dmlp * normed, axis=0), jnp.sum(dattn, axis=0), jnp.sum(dmlp, axis=0)]
    gq = dot(attn_in_t, dqkv).astype(bf).reshape(dp, part, -1)
    go = tn(g, o).astype(bf).reshape(dp, part, width)
    k = 2 * HD
    if mine:
        sums = jnp.concatenate([s[None] for s in sums] + [jnp.zeros((4, width), f32)])
        flat = lambda a: a.reshape(rows, width)
        grad_query, grad_output, grad_keyval, gb, out, input_grad = scatter_small(gq, go, sums, o, wo, hidden, down, flat(tokens), flat(cotangent), scale, dnormed, dp, mp, 2)
        grad_gains, grad_biases = gb[:2].T, gb[2:4].T
    else:
        x = tokens.reshape(rows, width).astype(f32)
        out = (x + nt(o, wo) + nt(hidden, down)).astype(bf)
        centered = x - jnp.mean(x, axis=1, keepdims=True)
        inverse = lax.rsqrt(jnp.mean(centered * centered, axis=1, keepdims=True) + epsilon)
        dx = (dnormed - jnp.mean(dnormed, axis=1, keepdims=True) - normed * jnp.mean(dnormed * normed, axis=1, keepdims=True)) * inverse
        input_grad = (cotangent.reshape(rows, width).astype(f32) * scale + dx).astype(bf)
        gq, gkv = gq[:, :, :width], gq[:, :, width:].astype(f32)
        gkvg = jnp.concatenate([gkv, jnp.stack(sums, axis=1).reshape(dp, part, 4)], axis=2)
        grad_query, grad_output, c = collect([gq, go, gkvg], {2}, dp, mp)
        grad_keyval, grad_gains, grad_biases = c[:, :k], c[:, k : k + 2], c[:, k + 2 : k + 4]
    return (
        out.reshape(tokens.shape),
        kv_full.reshape(-1, 2 * HD),
        input_grad.reshape(tokens.shape),
        grad_gains,
        grad_biases,
        grad_query,
        grad_keyval,
        grad_output,
        grad_up,
        grad_down,
    )


def solution(mesh):
    rows = P(None, ("dp", "mp"), None)
    d, dm = P("dp", None), P("dp", "mp")
    return jax.shard_map(
        shards,
        mesh=mesh,
        in_specs=(rows, d, d, dm, d, dm, dm, dm, rows, P("dp"), P()),
        out_specs=(rows, d, rows, d, d, dm, d, dm, dm, dm),
        check_vma=False,
    )
```
